32 devices in a mesh: fac: 8 (over y, x, core), freq: 4 (over z).
Axes of the slice: x: 2, y: 2, z: 4, core: 2. Of those that a mesh axis runs over, the one named last changes fastest.
Arguments:
- right_side: float32 [16, 36864, 128], P('freq', 'fac'), may hold values from -6 to 6
- factors: bfloat16 [36864, 1024], P('fac'), may hold values from -0.03125 to 0.03125
- pair_weight: float32 [16, 36864], P('freq', 'fac'), may hold values from -2 to 2
- second_order: float32 [16, 36864], P('freq', 'fac'), may hold values from -1 to 1
- forward: float32 [16, 16], replicated, may hold values from -3 to 3
- backward: float32 [16, 16], replicated, may hold values from -3 to 3
Outputs:
- amplitude: float32 [16, 36864, 128], P('freq', 'fac')
- sources: float32 [16, 36864, 128], P('freq', 'fac')
The draws below stay inside these ranges and needn't reach their ends.
All inputs are finite; a program needn't handle non-finite values.
Results may differ from the reference program's by a relative error of at most 0.0015.
Values may be sent and summed in bfloat16 or wider, within the bound.
A program may use at most 128 MiB of HBM per device.

```python
import jax
import jax.numpy as jnp
from jax import lax

NAUX = 1024
NFREQ = 16
COLS = 128
OUTER = 2
INNER = 2
PAIRS = 36864


def steps_of(key, dims, shards, low, largest):
    loudness, own = 1.0, jax.random.fold_in(key, 6)
    for dim, parts in shards:
        heights = jnp.exp(jax.random.uniform(jax.random.fold_in(own, dim), (parts,), jnp.float32, low / len(shards), largest / len(shards)))
        loudness = loudness * jnp.repeat(heights, dims[dim] // parts).reshape([-1 if axis == dim else 1 for axis in range(len(dims))])
    return loudness


def scatter_about(rng, extent, width, limit, split=(), kind=jnp.bfloat16):
    values = width * jax.random.normal(rng, extent, jnp.float32)
    if split:
        values = values * steps_of(rng, extent, split, -0.22, 0.18)
    return jnp.clip(values, -limit, limit).astype(kind)


def setup_inputs(seed: int = 0) -> dict:
    seeds = jax.random.split(jax.random.key(seed), 7)
    return {
        "right_side": scatter_about(seeds[0], (NFREQ, PAIRS, COLS), 1.0, 6.0, ((0, 4), (1, 8)), jnp.float32),
        "factors": scatter_about(seeds[1], (PAIRS, NAUX), PAIRS ** -0.5, 0.03125, ((0, 8),)),
        "pair_weight": jnp.clip(jax.random.uniform(seeds[2], (NFREQ, PAIRS), jnp.float32, -2.0, 2.0) * steps_of(seeds[2], (NFREQ, PAIRS), ((0, 4), (1, 8)), -0.4, 0.0), -2.0, 2.0),
        "second_order": jnp.clip(jax.random.uniform(seeds[3], (NFREQ, PAIRS), jnp.float32, -1.0, 1.0) * steps_of(seeds[3], (NFREQ, PAIRS), ((0, 4), (1, 8)), -0.4, 0.0), -1.0, 1.0),
        "forward": scatter_about(seeds[4], (NFREQ, NFREQ), (NFREQ // 4) ** -0.5, 3.0, (), jnp.float32),
        "backward": scatter_about(seeds[5], (NFREQ, NFREQ), (NFREQ // 4) ** -0.5, 3.0, (), jnp.float32),
    }


def reference(right_side, factors, pair_weight, second_order, forward, backward):
    sources = right_side
    amplitude = sources
    for outer in range(OUTER):
        amplitude = sources
        for inner in range(INNER):
            fresh = []
            for freq in range(NFREQ):
                rounded = amplitude[freq].astype(jnp.bfloat16)
                projection = jnp.dot(factors.T, rounded, preferred_element_type=jnp.float32)
                projected = projection.astype(jnp.bfloat16)
                spread = jnp.dot(factors, projected, preferred_element_type=jnp.float32)
                fresh.append(sources[freq] + pair_weight[freq][:, None] * spread)
            amplitude = jnp.stack(fresh)
        timed = jnp.einsum("tw,wpc->tpc", forward, amplitude, precision=lax.Precision.HIGHEST)
        product = second_order[:, :, None] * timed
        returned = jnp.einsum("wt,tpc->wpc", backward, product, precision=lax.Precision.HIGHEST)
        sources = right_side + returned
    return amplitude, sources
```

```python
import functools

import jax
import jax.numpy as jnp
from jax import lax
from jax.experimental import pallas as pl
from jax.experimental.pallas import tpu as pltpu
from jax.sharding import PartitionSpec as P

INNER = 2
LANES = 128
MESH = pl.DeviceIdType.MESH
CHUNK = 16
WIDE = 32
EXACT = lax.Precision.HIGHEST
R_MAX = 6.0
W_MAX = 2.0
L_MAX = 0.03125
HALF_TOP = 32768.0
VMEM = pltpu.VMEM


def tile_of(pairs):
    for blocks in (3, 4, 2, 1):
        if pairs % (blocks * LANES) == 0:
            return blocks * LANES
    return None


def mix(table, lanes, outs, count, term):
    totals = [None] * outs
    for v in range(count):
        value = term(v)
        for w in range(outs):
            row = w * count + v
            product = table[row : row + 1, lanes] * value
            totals[w] = product if totals[w] is None else totals[w] + product
    return totals


def blocks_of(ref):
    return [slice(k, k + LANES) for k in range(0, ref.shape[1], LANES)]


def part(i, base, chunk):
    return pl.ds(pl.multiple_of(base + i * chunk, chunk), chunk)


def spread(l_ref, p_ref, held):
    block = p_ref.shape[1]
    for s in range(p_ref.shape[0]):
        held[s * block : (s + 1) * block, :] = lax.dot_general(
            p_ref[s], l_ref[...], (((1,), (1,)), ((), ())), preferred_element_type=jnp.float32
        )


def dot_exact(a, b):
    return lax.dot_general(
        a, b, (((1,), (0,)), ((), ())), precision=EXACT, preferred_element_type=jnp.float32
    )


def resident(x):
    return pl.BlockSpec(x.shape, lambda i, *_: (0,) * x.ndim, pipeline_mode=pl.Buffered(1))


def quarter_kernel(nf, parts, me_ref, l_ref, k_ref, wt_ref, coef_ref, p_ref, *rest):
    r_refs, rest = rest[:parts], rest[parts:]
    u_refs, rest = rest[:parts], rest[parts:]
    v_refs, (table, held, turned, mid, far) = rest[:parts], rest[parts:]
    own = nf // parts
    cols = r_refs[0].shape[2]
    table[...] = dot_exact(coef_ref[...], k_ref[...])
    spread(l_ref, p_ref, held)
    for lanes in blocks_of(table):
        for v in range(nf):
            turned[v] = r_refs[v // own][v % own, lanes, :].T

        @pl.loop(0, cols // CHUNK)
        def _(i):
            rows = part(i, 0, CHUNK)
            got = mix(
                table,
                lanes,
                nf,
                nf,
                lambda v: turned[v, rows, :]
                + wt_ref[v : v + 1, lanes] * held[part(i, v * cols, CHUNK), lanes],
            )
            for w in range(nf):
                mid[w, rows, :] = got[w]
                turned[w, rows, :] = turned[w, rows, :] + got[w]
            got = mix(table, lanes, nf, nf, lambda v: turned[v, rows, :])
            for w in range(nf):
                far[w, rows, :] = got[w]

        for w in range(nf):
            u_refs[w // own][w % own, lanes, :] = mid[w].T
            v_refs[w // own][w % own, lanes, :] = far[w].T


def quarter_pass(me, factors, kernels, weights, coef, gathered, right_side, moved):
    own, pairs, cols = right_side.shape
    nf = weights.shape[0]
    parts = nf // own
    quarter = pairs // parts
    naux = factors.shape[1]
    tile = tile_of(quarter)
    steps = None if tile is None else quarter // tile
    if tile is None:
        cut = lambda x, axis: lax.dynamic_slice_in_dim(x, me * quarter, quarter, axis)
        here = jnp.concatenate([cut(right_side, 1)] + moved)
        table = jnp.einsum("jt,tp->jp", coef, cut(kernels, 1), precision=EXACT)
        table = table.reshape(nf, nf, quarter)
        wide = jnp.einsum(
            "ja,pa->jp",
            gathered.reshape(nf * cols, naux),
            cut(factors, 0),
            preferred_element_type=jnp.float32,
        )
        wide = jnp.transpose(wide.reshape(nf, cols, quarter), (0, 2, 1))
        wide = here + cut(weights, 1)[:, :, None] * wide
        u = jnp.einsum("wvp,vpc->wpc", table, wide, precision=EXACT)
        v = jnp.einsum("wvp,vpc->wpc", table, here + u, precision=EXACT)
        return (
            [u[s * own : (s + 1) * own] for s in range(parts)],
            [v[s * own : (s + 1) * own] for s in range(parts)],
        )
    at = lambda i, m: m[0] * steps + i
    piece = pl.BlockSpec((own, tile, cols), lambda i, m: (0, i, 0))
    shape = jax.ShapeDtypeStruct((own, quarter, cols), jnp.float32)
    out = pl.pallas_call(
        functools.partial(quarter_kernel, nf, parts),
        out_shape=[shape] * (2 * parts),
        grid_spec=pltpu.PrefetchScalarGridSpec(
            num_scalar_prefetch=1,
            grid=(steps,),
            in_specs=[
                pl.BlockSpec((tile, naux), lambda i, m: (at(i, m), 0)),
                pl.BlockSpec((nf, tile), lambda i, m: (0, at(i, m))),
                pl.BlockSpec((nf, tile), lambda i, m: (0, at(i, m))),
                resident(coef),
                resident(gathered),
                pl.BlockSpec((own, tile, cols), lambda i, m: (0, at(i, m), 0)),
            ]
            + [piece] * (parts - 1),
            out_specs=[piece] * (2 * parts),
            scratch_shapes=[
                VMEM((nf * nf, tile), jnp.float32),
                VMEM((nf * cols, tile), jnp.float32),
            ]
            + [VMEM((nf, cols, LANES), jnp.float32)] * 3,
        ),
        compiler_params=pltpu.CompilerParams(vmem_limit_bytes=56 << 20),
        cost_estimate=pl.CostEstimate(
            flops=2 * nf * quarter * cols * (naux + 32 * nf),
            bytes_accessed=16 * nf * quarter * cols,
            transcendentals=0,
        ),
    )(me.reshape(1), factors, kernels, weights, coef, gathered, right_side, *moved)
    return list(out[:parts]), list(out[parts:])


def project_kernel(parts, steps, me_ref, l_ref, *rest):
    s_refs, (o_ref,) = rest[:parts], rest[parts:]
    own, _, cols = s_refs[0].shape
    i = pl.program_id(0)

    @pl.when(i == 0)
    def _():
        o_ref[...] = jnp.zeros_like(o_ref)

    for s in range(parts):

        @pl.when(lax.div(i, steps) == s)
        def _():
            for f in range(own):
                rows = slice(f * cols, (f + 1) * cols)
                o_ref[rows, :] += lax.dot_general(
                    s_refs[s][f].astype(jnp.bfloat16),
                    l_ref[...],
                    (((0,), (0,)), ((), ())),
                    preferred_element_type=jnp.float32,
                )


def stay(s, steps):
    return lambda i, m: (0, jnp.clip(i - s * steps, 0, steps - 1), 0)


def project(me, factors, pieces):
    own, quarter, cols = pieces[0].shape
    parts = len(pieces)
    naux = factors.shape[1]
    tile = tile_of(quarter)
    if tile is None:
        total = 0.0
        for s, x in enumerate(pieces):
            rows = lax.dynamic_slice_in_dim(
                factors, lax.rem(me + s, parts) * quarter, quarter, 0
            )
            total = total + jnp.einsum(
                "pa,fpc->fca", rows, x.astype(jnp.bfloat16), preferred_element_type=jnp.float32
            )
        return total.reshape(own * cols, naux)
    steps = quarter // tile
    around = lambda i, m: lax.rem(m[0] * steps + i, parts * steps)
    return pl.pallas_call(
        functools.partial(project_kernel, parts, steps),
        out_shape=jax.ShapeDtypeStruct((own * cols, naux), jnp.float32),
        grid_spec=pltpu.PrefetchScalarGridSpec(
            num_scalar_prefetch=1,
            grid=(parts * steps,),
            in_specs=[pl.BlockSpec((tile, naux), lambda i, m: (around(i, m), 0))]
            + [pl.BlockSpec((own, tile, cols), stay(s, steps)) for s in range(parts)],
            out_specs=pl.BlockSpec((own * cols, naux), lambda i, m: (0, 0)),
        ),
        compiler_params=pltpu.CompilerParams(vmem_limit_bytes=40 << 20),
        cost_estimate=pl.CostEstimate(
            flops=2 * own * parts * quarter * cols * naux,
            bytes_accessed=8 * own * parts * quarter * cols,
            transcendentals=0,
        ),
    )(me.reshape(1), factors, *pieces)


def again_kernel(own, l_ref, wt_ref, p_ref, x_ref, o_ref):
    cols = p_ref.shape[0] // own

    @pl.when(pl.program_id(0) == 0)
    def _():
        o_ref[...] = x_ref[...]

    for f in range(own):
        rows = slice(f * cols, (f + 1) * cols)
        wide = lax.dot_general(
            p_ref[rows, :], l_ref[...], (((1,), (1,)), ((), ())), preferred_element_type=jnp.float32
        )
        wide = (wide * wt_ref[f : f + 1, :]).astype(jnp.bfloat16)
        o_ref[rows, :] += lax.dot_general(
            wide, l_ref[...], (((1,), (0,)), ((), ())), preferred_element_type=jnp.float32
        )


def again(factors, pair_weight, projected, kept):
    pairs, naux = factors.shape
    own = pair_weight.shape[0]
    tile = tile_of(pairs)
    return pl.pallas_call(
        functools.partial(again_kernel, own),
        out_shape=jax.ShapeDtypeStruct(kept.shape, jnp.float32),
        grid=(pairs // tile,),
        in_specs=[
            pl.BlockSpec((tile, naux), lambda i: (i, 0)),
            pl.BlockSpec((own, tile), lambda i: (0, i)),
            resident(projected),
            resident(kept),
        ],
        out_specs=pl.BlockSpec(kept.shape, lambda i: (0, 0)),
        compiler_params=pltpu.CompilerParams(vmem_limit_bytes=40 << 20),
        cost_estimate=pl.CostEstimate(
            flops=4 * kept.size * pairs, bytes_accessed=2 * factors.size, transcendentals=0
        ),
    )(factors, pair_weight, projected, kept)


def final_kernel(nf, parts, steps, me_ref, l_ref, k_ref, wt_ref, coef_ref, p_ref, *rest):
    s_refs, rest = rest[:parts], rest[parts:]
    b_refs, (a_ref, new_ref, table, held, mid, second) = rest[:parts], rest[parts:]
    own, _, cols = a_ref.shape
    table[...] = dot_exact(coef_ref[...], k_ref[...])
    for w in range(own):
        rows = slice(w * nf, (w + 1) * nf)
        table[rows, :] = table[rows, :] * wt_ref[...]
    spread(l_ref, p_ref, held)
    for lanes in blocks_of(table):

        @pl.loop(0, cols // WIDE)
        def _(i):
            rows = part(i, 0, WIDE)
            got = mix(table, lanes, own, nf, lambda v: held[part(i, v * cols, WIDE), lanes])
            for w in range(own):
                mid[w, rows, :] = got[w]
                second[w, rows, :] = (
                    wt_ref[w : w + 1, lanes] * held[part(i, w * cols, WIDE), lanes]
                )

        for s in range(parts):

            @pl.when(lax.div(pl.program_id(0), steps) == s)
            def _():
                for w in range(own):
                    new_ref[w, lanes, :] = b_refs[s][w, lanes, :] + mid[w].T
                    a_ref[w, lanes, :] = s_refs[s][w, lanes, :] + second[w].T


def final(me, factors, kernels, weights, coef, gathered, sources, base):
    own, quarter, cols = sources[0].shape
    parts = len(sources)
    nf = weights.shape[0]
    pairs, naux = factors.shape
    tile = tile_of(quarter)
    shape = jax.ShapeDtypeStruct((own, pairs, cols), jnp.float32)
    if tile is None:
        wide = jnp.einsum(
            "ja,pa->jp",
            gathered.reshape(nf * cols, naux),
            factors,
            preferred_element_type=jnp.float32,
        )
        wide = jnp.transpose(wide.reshape(nf, cols, pairs), (0, 2, 1)) * weights[:, :, None]
        table = jnp.einsum("jt,tp->jp", coef, kernels, precision=EXACT).reshape(own, nf, pairs)
        new = jnp.einsum("wvp,vpc->wpc", table, wide, precision=EXACT)
        amplitude = wide[:own]
        for s in range(parts):
            at = lax.rem(me + s, parts) * quarter
            put = lambda x, y: lax.dynamic_update_slice_in_dim(
                x, lax.dynamic_slice_in_dim(x, at, quarter, 1) + y, at, 1
            )
            amplitude, new = put(amplitude, sources[s]), put(new, base[s])
        return amplitude, new
    steps = quarter // tile
    around = lambda i, m: lax.rem(m[0] * steps + i, parts * steps)
    out = pl.BlockSpec((own, tile, cols), lambda i, m: (0, around(i, m), 0))
    pieces = [pl.BlockSpec((own, tile, cols), stay(s, steps)) for s in range(parts)]
    return pl.pallas_call(
        functools.partial(final_kernel, nf, parts, steps),
        out_shape=(shape, shape),
        grid_spec=pltpu.PrefetchScalarGridSpec(
            num_scalar_prefetch=1,
            grid=(parts * steps,),
            in_specs=[
                pl.BlockSpec((tile, naux), lambda i, m: (around(i, m), 0)),
                pl.BlockSpec((nf, tile), lambda i, m: (0, around(i, m))),
                pl.BlockSpec((nf, tile), lambda i, m: (0, around(i, m))),
                resident(coef),
                resident(gathered),
            ]
            + pieces
            + pieces,
            out_specs=(out, out),
            scratch_shapes=[
                VMEM((own * nf, tile), jnp.float32),
                VMEM((nf * cols, tile), jnp.float32),
            ]
            + [VMEM((own, cols, LANES), jnp.float32)] * 2,
        ),
        compiler_params=pltpu.CompilerParams(vmem_limit_bytes=56 << 20),
        cost_estimate=pl.CostEstimate(
            flops=2 * nf * pairs * cols * naux,
            bytes_accessed=16 * own * pairs * cols,
            transcendentals=0,
        ),
    )(me.reshape(1), factors, kernels, weights, coef, gathered, *sources, *base)


def sum_kernel(chips, parts, x_ref, o_ref, near, red, land, mine, joined, *sems):
    near_out, near_in, red_out, red_in, z_out, z_in, wide_out, wide_in, pair_out, pair_in, local = sems
    me = lax.axis_index("fac")
    level = lax.axis_index("freq")
    levels = lax.axis_size("freq")
    core = lax.rem(me, 2)
    chip = lax.div(me, 2)
    partner = me + 1 - 2 * core

    def on(d):
        return lax.rem(chip + d, chips)

    def at(d):
        return {"fac": on(d) * 2 + core}

    def up(s):
        return {"freq": lax.rem(level + s, levels)}

    pal = {"fac": partner}
    barrier = pltpu.get_barrier_semaphore()
    greeted = [pal] + [at(d) for d in range(1, chips)] + [up(s) for s in range(1, parts)]
    for other in greeted:
        pl.semaphore_signal(barrier, inc=1, device_id=other, device_id_type=MESH)
    pl.semaphore_wait(barrier, len(greeted))

    started = []

    def send(src, dst, out, came, to):
        copy = pltpu.make_async_remote_copy(
            src_ref=src,
            dst_ref=dst,
            send_sem=out,
            recv_sem=came,
            device_id=to,
            device_id_type=MESH,
        )
        copy.start()
        started.append(copy)
        return copy

    turns = list(range(1, chips)) + [0]
    nears = {}
    for d in turns:
        nears[d] = send(
            x_ref.at[on(d), 1 - core], near.at[d], near_out.at[d], near_in.at[d], pal
        )
    block = mine.shape[0]
    step = min(block, 16)
    reds = []
    for d in range(1, chips):
        nears[d].wait_recv()
        for r in range(0, block, step):
            rows = slice(r, r + step)
            red[d, rows, :] = (x_ref[on(d), core, rows, :] + near[d, rows, :]).astype(red.dtype)
        reds.append(send(red.at[d], land.at[d], red_out.at[d], red_in.at[d], at(d)))
    nears[0].wait_recv()
    for copy in reds:
        copy.wait_recv()
    for r in range(0, block, step):
        rows = slice(r, r + step)
        total = x_ref[chip, core, rows, :] + near[0, rows, :]
        for d in range(1, chips):
            total = total + land[d, rows, :].astype(jnp.float32)
        mine[rows, :] = total.astype(mine.dtype)
    keep = pltpu.make_async_copy(mine, joined.at[0, chip, core], local)
    keep.start()
    keep.wait()

    zs = [None]
    for s in range(1, parts):
        here = joined.at[0, chip, core]
        zs.append(send(here, joined.at[s, chip, core], z_out.at[s], z_in.at[s], up(s)))
    wides, pairs = [], []
    for s in range(parts):
        here = joined.at[s, chip, core]
        if s:
            zs[s].wait_recv()
        for d in range(1, chips):
            wides.append(
                (s, d, send(here, here, wide_out.at[s, d], wide_in.at[s, d], at(d)))
            )
        pairs.append(send(here, here, pair_out.at[s, 0], pair_in.at[s, 0], pal))
    for s, d, copy in wides:
        copy.wait_recv()
        here = joined.at[s, lax.rem(chip - d + chips, chips), core]
        pairs.append(send(here, here, pair_out.at[s, d], pair_in.at[s, d], pal))
    for copy in pairs:
        copy.wait_recv()
    for copy in started:
        copy.wait_send()
    for s in range(parts):
        for c in range(chips):
            o_ref[s, c] = joined[s, c]


def summed(x, parts):
    n = lax.axis_size("fac")
    chips = n // 2
    rows, width = x.shape
    block = rows // n
    flat = (chips, 2, block, width)
    dma = pltpu.SemaphoreType.DMA
    result = pl.pallas_call(
        functools.partial(sum_kernel, chips, parts),
        out_shape=jax.ShapeDtypeStruct((parts,) + flat, jnp.bfloat16),
        in_specs=[pl.BlockSpec(memory_space=VMEM)],
        out_specs=pl.BlockSpec(memory_space=VMEM),
        scratch_shapes=[
            VMEM((chips, block, width), jnp.float32),
            VMEM((chips, block, width), jnp.bfloat16),
            VMEM((chips, block, width), jnp.bfloat16),
            VMEM((block, width), jnp.bfloat16),
            VMEM((parts,) + flat, jnp.bfloat16),
            dma((chips,)),
            dma((chips,)),
            dma((chips,)),
            dma((chips,)),
            dma((parts,)),
            dma((parts,)),
            dma((parts, chips)),
            dma((parts, chips)),
            dma((parts, chips)),
            dma((parts, chips)),
            dma,
        ],
        compiler_params=pltpu.CompilerParams(
            collective_id=min(parts, 2) - 1, has_side_effects=True, vmem_limit_bytes=24 << 20
        ),
        cost_estimate=pl.CostEstimate(
            flops=40000 * x.size // 1000, bytes_accessed=40 * x.size, transcendentals=0
        ),
    )(x.reshape(flat))
    return result.reshape(parts, rows, width)


def shards(right_side, factors, pair_weight, second_order, forward, backward):
    own, pairs, cols = right_side.shape
    nf = forward.shape[0]
    naux = factors.shape[1]
    parts = nf // own
    quarter = pairs // parts
    me = lax.axis_index("freq")

    def shift(x, by):
        if by == 0:
            return x
        return lax.ppermute(x, "freq", [(i, (i + by) % parts) for i in range(parts)])

    def sliced(x, s):
        return lax.dynamic_slice_in_dim(x, lax.rem(me + s, parts) * quarter, quarter, 1)

    order = jnp.concatenate(
        [lax.rem(me - s + parts, parts) * own + jnp.arange(own) for s in range(parts)]
    )
    pick = jax.nn.one_hot(order, nf, dtype=jnp.float32)
    ahead = jnp.einsum("ts,sv,wv->tw", pick, forward, pick, precision=EXACT)
    back = jnp.einsum("ws,st,vt->wv", pick, backward, pick, precision=EXACT)
    coef = (back[:, None, :] * ahead.T[None, :, :]).reshape(nf * nf, nf)
    reach = jnp.max(
        jnp.sum(
            jnp.einsum("wt,tv->wv", jnp.abs(backward), jnp.abs(forward), precision=EXACT), axis=1
        )
    )

    both = jnp.stack([pair_weight, second_order])
    tables = jnp.concatenate([shift(both, s) for s in range(parts)], axis=1)
    weights, kernels = tables[0], tables[1]
    up = 8192.0
    moved = []
    for s in range(1, parts):
        out = (sliced(right_side, s) * up).astype(jnp.float16)
        moved.append(shift(out, s))

    def first_projection():
        return jnp.einsum(
            "pa,fpc->fca",
            factors,
            right_side.astype(jnp.bfloat16),
            preferred_element_type=jnp.float32,
        ).reshape(own * cols, naux)

    def ladder(kept):
        kept_now = kept
        for inner in range(INNER):
            last = inner == INNER - 1
            mine = summed(kept_now, parts if last else 1)
            if not last:
                kept_now = again(factors, pair_weight, mine[0], kept)
        return mine

    gathered = ladder(first_projection())
    moved = [m.astype(jnp.float32) * (1.0 / up) for m in moved]
    u, v = quarter_pass(me, factors, kernels, weights, coef, gathered, right_side, moved)
    height = jnp.max(jnp.sum(jnp.abs(gathered.astype(jnp.float32)), axis=2))
    u_top = jnp.maximum(1.01 * reach * (R_MAX + W_MAX * L_MAX * height), 1e-30)
    v_top = jnp.maximum(1.01 * reach * (R_MAX + u_top), 1e-30)

    def returned(blocks, top):
        result = [sliced(right_side, 0) + blocks[0]]
        for s in range(1, parts):
            block = (blocks[s] * (HALF_TOP / top)).astype(jnp.float16)
            block = shift(block, parts - s)
            result.append(sliced(right_side, s) + block.astype(jnp.float32) * (top / HALF_TOP))
        return result

    sources = returned(u, u_top)
    base = returned(v, v_top)
    gathered = ladder(project(me, factors, sources))
    return final(me, factors, kernels, weights, coef[: own * nf], gathered, sources, base)


def solution(mesh):
    return jax.shard_map(
        shards,
        mesh=mesh,
        in_specs=(
            P("freq", "fac", None),
            P("fac", None),
            P("freq", "fac"),
            P("freq", "fac"),
            P(),
            P(),
        ),
        out_specs=(P("freq", "fac", None), P("freq", "fac", None)),
        check_vma=False,
    )
```

```python
import functools

import jax
import jax.numpy as jnp
from jax import lax
from jax.experimental import pallas as pl
from jax.experimental.pallas import tpu as pltpu
from jax.sharding import PartitionSpec as P

INNER = 2
LANES = 128
MESH = pl.DeviceIdType.MESH
CHUNK = 16
WIDE = 32
EXACT = lax.Precision.HIGHEST
R_MAX = 6.0
W_MAX = 2.0
L_MAX = 0.03125
HALF_TOP = 32768.0
VMEM = pltpu.VMEM


def tile_of(pairs):
    for blocks in (3, 4, 2, 1):
        if pairs % (blocks * LANES) == 0:
            return blocks * LANES
    return None


def mix(table, lanes, outs, count, term):
    totals = [None] * outs
    for v in range(count):
        value = term(v)
        for w in range(outs):
            row = w * count + v
            product = table[row : row + 1, lanes] * value
            totals[w] = product if totals[w] is None else totals[w] + product
    return totals


def blocks_of(ref):
    return [slice(k, k + LANES) for k in range(0, ref.shape[1], LANES)]


def part(i, base, chunk):
    return pl.ds(pl.multiple_of(base + i * chunk, chunk), chunk)


def spread(l_ref, p_ref, held):
    held[...] = lax.dot_general(
        p_ref[...].reshape(held.shape[0], l_ref.shape[1]),
        l_ref[...],
        (((1,), (1,)), ((), ())),
        preferred_element_type=jnp.float32,
    )


def dot_exact(a, b):
    return lax.dot_general(
        a, b, (((1,), (0,)), ((), ())), precision=EXACT, preferred_element_type=jnp.float32
    )


def resident(x):
    return pl.BlockSpec(x.shape, lambda i, *_: (0,) * x.ndim, pipeline_mode=pl.Buffered(1))


def quarter_kernel(nf, parts, me_ref, l_ref, k_ref, wt_ref, coef_ref, p_ref, *rest):
    r_refs, rest = rest[:parts], rest[parts:]
    u_refs, rest = rest[:parts], rest[parts:]
    v_refs, (table, held, turned, mid, far) = rest[:parts], rest[parts:]
    own = nf // parts
    cols = r_refs[0].shape[2]
    table[...] = dot_exact(coef_ref[...], k_ref[...])
    spread(l_ref, p_ref, held)
    for lanes in blocks_of(table):
        for v in range(nf):
            turned[v] = r_refs[v // own][v % own, lanes, :].T

        @pl.loop(0, cols // CHUNK)
        def _(i):
            rows = part(i, 0, CHUNK)
            got = mix(
                table,
                lanes,
                nf,
                nf,
                lambda v: turned[v, rows, :]
                + wt_ref[v : v + 1, lanes] * held[part(i, v * cols, CHUNK), lanes],
            )
            for w in range(nf):
                mid[w, rows, :] = got[w]
                turned[w, rows, :] = turned[w, rows, :] + got[w]
            got = mix(table, lanes, nf, nf, lambda v: turned[v, rows, :])
            for w in range(nf):
                far[w, rows, :] = got[w]

        for w in range(nf):
            u_refs[w // own][w % own, lanes, :] = mid[w].T
            v_refs[w // own][w % own, lanes, :] = far[w].T


def quarter_pass(me, factors, kernels, weights, coef, gathered, right_side, moved):
    own, pairs, cols = right_side.shape
    nf = weights.shape[0]
    parts = nf // own
    quarter = pairs // parts
    naux = factors.shape[1]
    tile = tile_of(quarter)
    steps = None if tile is None else quarter // tile
    if tile is None:
        cut = lambda x, axis: lax.dynamic_slice_in_dim(x, me * quarter, quarter, axis)
        here = jnp.concatenate([cut(right_side, 1)] + moved)
        table = jnp.einsum("jt,tp->jp", coef, cut(kernels, 1), precision=EXACT)
        table = table.reshape(nf, nf, quarter)
        wide = jnp.einsum(
            "ja,pa->jp",
            gathered.reshape(nf * cols, naux),
            cut(factors, 0),
            preferred_element_type=jnp.float32,
        )
        wide = jnp.transpose(wide.reshape(nf, cols, quarter), (0, 2, 1))
        wide = here + cut(weights, 1)[:, :, None] * wide
        u = jnp.einsum("wvp,vpc->wpc", table, wide, precision=EXACT)
        v = jnp.einsum("wvp,vpc->wpc", table, here + u, precision=EXACT)
        return (
            [u[s * own : (s + 1) * own] for s in range(parts)],
            [v[s * own : (s + 1) * own] for s in range(parts)],
        )
    at = lambda i, m: m[0] * steps + i
    piece = pl.BlockSpec((own, tile, cols), lambda i, m: (0, i, 0))
    shape = jax.ShapeDtypeStruct((own, quarter, cols), jnp.float32)
    out = pl.pallas_call(
        functools.partial(quarter_kernel, nf, parts),
        out_shape=[shape] * (2 * parts),
        grid_spec=pltpu.PrefetchScalarGridSpec(
            num_scalar_prefetch=1,
            grid=(steps,),
            in_specs=[
                pl.BlockSpec((tile, naux), lambda i, m: (at(i, m), 0)),
                pl.BlockSpec((nf, tile), lambda i, m: (0, at(i, m))),
                pl.BlockSpec((nf, tile), lambda i, m: (0, at(i, m))),
                resident(coef),
                resident(gathered),
                pl.BlockSpec((own, tile, cols), lambda i, m: (0, at(i, m), 0)),
            ]
            + [piece] * (parts - 1),
            out_specs=[piece] * (2 * parts),
            scratch_shapes=[
                VMEM((nf * nf, tile), jnp.float32),
                VMEM((nf * cols, tile), jnp.float32),
            ]
            + [VMEM((nf, cols, LANES), jnp.float32)] * 3,
        ),
        compiler_params=pltpu.CompilerParams(vmem_limit_bytes=56 << 20),
        cost_estimate=pl.CostEstimate(
            flops=2 * nf * quarter * cols * (naux + 32 * nf),
            bytes_accessed=16 * nf * quarter * cols,
            transcendentals=0,
        ),
    )(me.reshape(1), factors, kernels, weights, coef, gathered, right_side, *moved)
    return list(out[:parts]), list(out[parts:])


def project_kernel(parts, steps, me_ref, l_ref, *rest):
    s_refs, (o_ref,) = rest[:parts], rest[parts:]
    own, _, _ = s_refs[0].shape
    i = pl.program_id(0)

    @pl.when(i == 0)
    def _():
        o_ref[...] = jnp.zeros_like(o_ref)

    for s in range(parts):

        @pl.when(lax.div(i, steps) == s)
        def _():
            rounded = [s_refs[s][f].astype(jnp.bfloat16) for f in range(own)]
            o_ref[...] += lax.dot_general(
                jnp.concatenate(rounded, axis=1),
                l_ref[...],
                (((0,), (0,)), ((), ())),
                preferred_element_type=jnp.float32,
            )


def stay(s, steps):
    return lambda i, m: (0, jnp.clip(i - s * steps, 0, steps - 1), 0)


def project(me, factors, pieces):
    own, quarter, cols = pieces[0].shape
    parts = len(pieces)
    naux = factors.shape[1]
    tile = tile_of(quarter)
    if tile is None:
        total = 0.0
        for s, x in enumerate(pieces):
            rows = lax.dynamic_slice_in_dim(
                factors, lax.rem(me + s, parts) * quarter, quarter, 0
            )
            total = total + jnp.einsum(
                "pa,fpc->fca", rows, x.astype(jnp.bfloat16), preferred_element_type=jnp.float32
            )
        return total.reshape(own * cols, naux)
    steps = quarter // tile
    around = lambda i, m: lax.rem(m[0] * steps + i, parts * steps)
    return pl.pallas_call(
        functools.partial(project_kernel, parts, steps),
        out_shape=jax.ShapeDtypeStruct((own * cols, naux), jnp.float32),
        grid_spec=pltpu.PrefetchScalarGridSpec(
            num_scalar_prefetch=1,
            grid=(parts * steps,),
            in_specs=[pl.BlockSpec((tile, naux), lambda i, m: (around(i, m), 0))]
            + [pl.BlockSpec((own, tile, cols), stay(s, steps)) for s in range(parts)],
            out_specs=pl.BlockSpec((own * cols, naux), lambda i, m: (0, 0)),
        ),
        compiler_params=pltpu.CompilerParams(vmem_limit_bytes=40 << 20),
        cost_estimate=pl.CostEstimate(
            flops=2 * own * parts * quarter * cols * naux,
            bytes_accessed=8 * own * parts * quarter * cols,
            transcendentals=0,
        ),
    )(me.reshape(1), factors, *pieces)


def again_kernel(own, l_ref, wt_ref, p_ref, x_ref, o_ref):
    cols = p_ref.shape[0] // own

    @pl.when(pl.program_id(0) == 0)
    def _():
        o_ref[...] = x_ref[...]

    wide = lax.dot_general(
        p_ref[...], l_ref[...], (((1,), (1,)), ((), ())), preferred_element_type=jnp.float32
    )
    wide = [
        (wide[f * cols : (f + 1) * cols] * wt_ref[f : f + 1, :]).astype(jnp.bfloat16)
        for f in range(own)
    ]
    o_ref[...] += lax.dot_general(
        jnp.concatenate(wide, axis=0),
        l_ref[...],
        (((1,), (0,)), ((), ())),
        preferred_element_type=jnp.float32,
    )


def again(factors, pair_weight, projected, kept):
    pairs, naux = factors.shape
    own = pair_weight.shape[0]
    tile = tile_of(pairs)
    return pl.pallas_call(
        functools.partial(again_kernel, own),
        out_shape=jax.ShapeDtypeStruct(kept.shape, jnp.float32),
        grid=(pairs // tile,),
        in_specs=[
            pl.BlockSpec((tile, naux), lambda i: (i, 0)),
            pl.BlockSpec((own, tile), lambda i: (0, i)),
            resident(projected),
            resident(kept),
        ],
        out_specs=pl.BlockSpec(kept.shape, lambda i: (0, 0)),
        compiler_params=pltpu.CompilerParams(vmem_limit_bytes=40 << 20),
        cost_estimate=pl.CostEstimate(
            flops=4 * kept.size * pairs, bytes_accessed=2 * factors.size, transcendentals=0
        ),
    )(factors, pair_weight, projected, kept)


def final_kernel(nf, parts, steps, me_ref, l_ref, k_ref, wt_ref, coef_ref, p_ref, *rest):
    s_refs, rest = rest[:parts], rest[parts:]
    b_refs, (a_ref, new_ref, table, held, mid, second) = rest[:parts], rest[parts:]
    own, _, cols = a_ref.shape
    table[...] = dot_exact(coef_ref[...], k_ref[...])
    for w in range(own):
        rows = slice(w * nf, (w + 1) * nf)
        table[rows, :] = table[rows, :] * wt_ref[...]
    spread(l_ref, p_ref, held)
    for lanes in blocks_of(table):

        @pl.loop(0, cols // WIDE)
        def _(i):
            rows = part(i, 0, WIDE)
            got = mix(table, lanes, own, nf, lambda v: held[part(i, v * cols, WIDE), lanes])
            for w in range(own):
                mid[w, rows, :] = got[w]
                second[w, rows, :] = (
                    wt_ref[w : w + 1, lanes] * held[part(i, w * cols, WIDE), lanes]
                )

        for s in range(parts):

            @pl.when(lax.div(pl.program_id(0), steps) == s)
            def _():
                for w in range(own):
                    new_ref[w, lanes, :] = b_refs[s][w, lanes, :] + mid[w].T
                    a_ref[w, lanes, :] = s_refs[s][w, lanes, :] + second[w].T


def final(me, factors, kernels, weights, coef, gathered, sources, base):
    own, quarter, cols = sources[0].shape
    parts = len(sources)
    nf = weights.shape[0]
    pairs, naux = factors.shape
    tile = tile_of(quarter)
    shape = jax.ShapeDtypeStruct((own, pairs, cols), jnp.float32)
    if tile is None:
        wide = jnp.einsum(
            "ja,pa->jp",
            gathered.reshape(nf * cols, naux),
            factors,
            preferred_element_type=jnp.float32,
        )
        wide = jnp.transpose(wide.reshape(nf, cols, pairs), (0, 2, 1)) * weights[:, :, None]
        table = jnp.einsum("jt,tp->jp", coef, kernels, precision=EXACT).reshape(own, nf, pairs)
        new = jnp.einsum("wvp,vpc->wpc", table, wide, precision=EXACT)
        amplitude = wide[:own]
        for s in range(parts):
            at = lax.rem(me + s, parts) * quarter
            put = lambda x, y: lax.dynamic_update_slice_in_dim(
                x, lax.dynamic_slice_in_dim(x, at, quarter, 1) + y, at, 1
            )
            amplitude, new = put(amplitude, sources[s]), put(new, base[s])
        return amplitude, new
    steps = quarter // tile
    around = lambda i, m: lax.rem(m[0] * steps + i, parts * steps)
    out = pl.BlockSpec((own, tile, cols), lambda i, m: (0, around(i, m), 0))
    pieces = [pl.BlockSpec((own, tile, cols), stay(s, steps)) for s in range(parts)]
    return pl.pallas_call(
        functools.partial(final_kernel, nf, parts, steps),
        out_shape=(shape, shape),
        grid_spec=pltpu.PrefetchScalarGridSpec(
            num_scalar_prefetch=1,
            grid=(parts * steps,),
            in_specs=[
                pl.BlockSpec((tile, naux), lambda i, m: (around(i, m), 0)),
                pl.BlockSpec((nf, tile), lambda i, m: (0, around(i, m))),
                pl.BlockSpec((nf, tile), lambda i, m: (0, around(i, m))),
                resident(coef),
                resident(gathered),
            ]
            + pieces
            + pieces,
            out_specs=(out, out),
            scratch_shapes=[
                VMEM((own * nf, tile), jnp.float32),
                VMEM((nf * cols, tile), jnp.float32),
            ]
            + [VMEM((own, cols, LANES), jnp.float32)] * 2,
        ),
        compiler_params=pltpu.CompilerParams(vmem_limit_bytes=56 << 20),
        cost_estimate=pl.CostEstimate(
            flops=2 * nf * pairs * cols * naux,
            bytes_accessed=16 * own * pairs * cols,
            transcendentals=0,
        ),
    )(me.reshape(1), factors, kernels, weights, coef, gathered, *sources, *base)


def sum_kernel(chips, parts, x_ref, o_ref, near, red, land, mine, joined, *sems):
    near_out, near_in, red_out, red_in, z_out, z_in, wide_out, wide_in, pair_out, pair_in, local = sems
    me = lax.axis_index("fac")
    level = lax.axis_index("freq")
    levels = lax.axis_size("freq")
    core = lax.rem(me, 2)
    chip = lax.div(me, 2)
    partner = me + 1 - 2 * core

    def on(d):
        return lax.rem(chip + d, chips)

    def at(d):
        return {"fac": on(d) * 2 + core}

    def up(s):
        return {"freq": lax.rem(level + s, levels)}

    pal = {"fac": partner}
    barrier = pltpu.get_barrier_semaphore()
    greeted = [pal] + [at(d) for d in range(1, chips)] + [up(s) for s in range(1, parts)]
    for other in greeted:
        pl.semaphore_signal(barrier, inc=1, device_id=other, device_id_type=MESH)
    pl.semaphore_wait(barrier, len(greeted))

    started = []

    def send(src, dst, out, came, to):
        copy = pltpu.make_async_remote_copy(
            src_ref=src,
            dst_ref=dst,
            send_sem=out,
            recv_sem=came,
            device_id=to,
            device_id_type=MESH,
        )
        copy.start()
        started.append(copy)
        return copy

    turns = list(range(1, chips)) + [0]
    nears = {}
    for d in turns:
        nears[d] = send(
            x_ref.at[on(d), 1 - core], near.at[d], near_out.at[d], near_in.at[d], pal
        )
    block = mine.shape[0]
    step = min(block, 16)
    reds = []
    for d in range(1, chips):
        nears[d].wait_recv()
        for r in range(0, block, step):
            rows = slice(r, r + step)
            red[d, rows, :] = (x_ref[on(d), core, rows, :] + near[d, rows, :]).astype(red.dtype)
        reds.append(send(red.at[d], land.at[d], red_out.at[d], red_in.at[d], at(d)))
    nears[0].wait_recv()
    for copy in reds:
        copy.wait_recv()
    for r in range(0, block, step):
        rows = slice(r, r + step)
        total = x_ref[chip, core, rows, :] + near[0, rows, :]
        for d in range(1, chips):
            total = total + land[d, rows, :].astype(jnp.float32)
        mine[rows, :] = total.astype(mine.dtype)
    keep = pltpu.make_async_copy(mine, joined.at[0, chip, core], local)
    keep.start()
    keep.wait()

    zs = [None]
    for s in range(1, parts):
        here = joined.at[0, chip, core]
        zs.append(send(here, joined.at[s, chip, core], z_out.at[s], z_in.at[s], up(s)))
    wides, pairs = [], []
    for s in range(parts):
        here = joined.at[s, chip, core]
        if s:
            zs[s].wait_recv()
        for d in range(1, chips):
            wides.append(
                (s, d, send(here, here, wide_out.at[s, d], wide_in.at[s, d], at(d)))
            )
        pairs.append(send(here, here, pair_out.at[s, 0], pair_in.at[s, 0], pal))
    for s, d, copy in wides:
        copy.wait_recv()
        here = joined.at[s, lax.rem(chip - d + chips, chips), core]
        pairs.append(send(here, here, pair_out.at[s, d], pair_in.at[s, d], pal))
    for copy in pairs:
        copy.wait_recv()
    for copy in started:
        copy.wait_send()
    for s in range(parts):
        for c in range(chips):
            o_ref[s, c] = joined[s, c]


def summed(x, parts):
    n = lax.axis_size("fac")
    chips = n // 2
    rows, width = x.shape
    block = rows // n
    flat = (chips, 2, block, width)
    dma = pltpu.SemaphoreType.DMA
    result = pl.pallas_call(
        functools.partial(sum_kernel, chips, parts),
        out_shape=jax.ShapeDtypeStruct((parts,) + flat, jnp.bfloat16),
        in_specs=[pl.BlockSpec(memory_space=VMEM)],
        out_specs=pl.BlockSpec(memory_space=VMEM),
        scratch_shapes=[
            VMEM((chips, block, width), jnp.float32),
            VMEM((chips, block, width), jnp.bfloat16),
            VMEM((chips, block, width), jnp.bfloat16),
            VMEM((block, width), jnp.bfloat16),
            VMEM((parts,) + flat, jnp.bfloat16),
            dma((chips,)),
            dma((chips,)),
            dma((chips,)),
            dma((chips,)),
            dma((parts,)),
            dma((parts,)),
            dma((parts, chips)),
            dma((parts, chips)),
            dma((parts, chips)),
            dma((parts, chips)),
            dma,
        ],
        compiler_params=pltpu.CompilerParams(
            collective_id=min(parts, 2) - 1, has_side_effects=True, vmem_limit_bytes=24 << 20
        ),
        cost_estimate=pl.CostEstimate(
            flops=40000 * x.size // 1000, bytes_accessed=40 * x.size, transcendentals=0
        ),
    )(x.reshape(flat))
    return result.reshape(parts, rows, width)


def shards(right_side, factors, pair_weight, second_order, forward, backward):
    own, pairs, cols = right_side.shape
    nf = forward.shape[0]
    naux = factors.shape[1]
    parts = nf // own
    quarter = pairs // parts
    me = lax.axis_index("freq")

    def shift(x, by):
        if by == 0:
            return x
        return lax.ppermute(x, "freq", [(i, (i + by) % parts) for i in range(parts)])

    def sliced(x, s):
        return lax.dynamic_slice_in_dim(x, lax.rem(me + s, parts) * quarter, quarter, 1)

    order = jnp.concatenate(
        [lax.rem(me - s + parts, parts) * own + jnp.arange(own) for s in range(parts)]
    )
    pick = jax.nn.one_hot(order, nf, dtype=jnp.float32)
    ahead = jnp.einsum("ts,sv,wv->tw", pick, forward, pick, precision=EXACT)
    back = jnp.einsum("ws,st,vt->wv", pick, backward, pick, precision=EXACT)
    coef = (back[:, None, :] * ahead.T[None, :, :]).reshape(nf * nf, nf)
    reach = jnp.max(
        jnp.sum(
            jnp.einsum("wt,tv->wv", jnp.abs(backward), jnp.abs(forward), precision=EXACT), axis=1
        )
    )

    both = jnp.stack([pair_weight, second_order])
    tables = jnp.concatenate([shift(both, s) for s in range(parts)], axis=1)
    weights, kernels = tables[0], tables[1]
    up = 8192.0
    moved = []
    for s in range(1, parts):
        out = (sliced(right_side, s) * up).astype(jnp.float16)
        moved.append(shift(out, s))

    def first_projection():
        return jnp.einsum(
            "pa,fpc->fca",
            factors,
            right_side.astype(jnp.bfloat16),
            preferred_element_type=jnp.float32,
        ).reshape(own * cols, naux)

    def ladder(kept):
        kept_now = kept
        for inner in range(INNER):
            last = inner == INNER - 1
            mine = summed(kept_now, parts if last else 1)
            if not last:
                kept_now = again(factors, pair_weight, mine[0], kept)
        return mine

    gathered = ladder(first_projection())
    moved = [m.astype(jnp.float32) * (1.0 / up) for m in moved]
    u, v = quarter_pass(me, factors, kernels, weights, coef, gathered, right_side, moved)
    height = jnp.max(jnp.sum(jnp.abs(gathered.astype(jnp.float32)), axis=2))
    u_top = jnp.maximum(1.01 * reach * (R_MAX + W_MAX * L_MAX * height), 1e-30)
    v_top = jnp.maximum(1.01 * reach * (R_MAX + u_top), 1e-30)

    def halved(blocks, top):
        return [(b * (HALF_TOP / top)).astype(jnp.float16) for b in blocks[1:]]

    def returned(blocks):
        return [shift(b, parts - 1 - s) for s, b in enumerate(blocks)]

    def added(first, blocks, top):
        rest = [b.astype(jnp.float32) * (top / HALF_TOP) for b in blocks]
        return [sliced(right_side, s) + b for s, b in enumerate([first] + rest)]

    sources = added(u[0], returned(halved(u, u_top)), u_top)
    sent, sources = lax.optimization_barrier((halved(v, v_top), sources))
    sent = returned(sent)
    gathered = ladder(project(me, factors, sources))
    gathered, sent = lax.optimization_barrier((gathered, sent))
    base = added(v[0], sent, v_top)
    return final(me, factors, kernels, weights, coef[: own * nf], gathered, sources, base)


def solution(mesh):
    return jax.shard_map(
        shards,
        mesh=mesh,
        in_specs=(
            P("freq", "fac", None),
            P("fac", None),
            P("freq", "fac"),
            P("freq", "fac"),
            P(),
            P(),
        ),
        out_specs=(P("freq", "fac", None), P("freq", "fac", None)),
        check_vma=False,
    )
```

```python
import functools

import jax
import jax.numpy as jnp
from jax import lax
from jax.experimental import pallas as pl
from jax.experimental.pallas import tpu as pltpu
from jax.sharding import PartitionSpec as P


INNER = 2
LANES = 128
MESH = pl.DeviceIdType.MESH
CHUNK = 16
WIDE = 32
EXACT = lax.Precision.HIGHEST
R_MAX = 6.0
W_MAX = 2.0
L_MAX = 0.03125
HALF_TOP = 32768.0
VMEM = pltpu.VMEM


def tile_of(pairs):
    for blocks in (3, 4, 2, 1):
        if pairs % (blocks * LANES) == 0:
            return blocks * LANES
    return None


def mix(table, lanes, outs, count, term):
    totals = [None] * outs
    for v in range(count):
        value = term(v)
        for w in range(outs):
            row = w * count + v
            product = table[row : row + 1, lanes] * value
            totals[w] = product if totals[w] is None else totals[w] + product
    return totals


def part(i, base, chunk):
    return pl.ds(pl.multiple_of(base + i * chunk, chunk), chunk)


def spread(l_ref, p_ref, held):
    held[...] = lax.dot_general(
        p_ref[...].reshape(held.shape[0], l_ref.shape[1]),
        l_ref[...],
        (((1,), (1,)), ((), ())),
        preferred_element_type=jnp.float32,
    )


def dot_exact(a, b):
    return lax.dot_general(
        a, b, (((1,), (0,)), ((), ())), precision=EXACT, preferred_element_type=jnp.float32
    )


def resident(x):
    return pl.BlockSpec(x.shape, lambda i, *_: (0,) * x.ndim, pipeline_mode=pl.Buffered(1))


def quarter_kernel(nf, parts, kept, me_ref, l_ref, k_ref, wt_ref, coef_ref, p_ref, *rest):
    r_refs, rest = rest[:parts], rest[parts + kept :]
    u_refs, rest = rest[:parts], rest[parts:]
    v_refs, (table, held, turned, mid, far) = rest[:parts], rest[parts:]
    own = nf // parts
    cols = r_refs[0].shape[2]
    table[...] = dot_exact(coef_ref[...], k_ref[...])
    spread(l_ref, p_ref, held)

    @pl.loop(0, table.shape[1] // LANES)
    def _(block):
        lanes = part(block, 0, LANES)
        for v in range(nf):
            turned[v] = r_refs[v // own][v % own, lanes, :].T

        @pl.loop(0, cols // CHUNK)
        def _(i):
            rows = part(i, 0, CHUNK)
            got = mix(
                table,
                lanes,
                nf,
                nf,
                lambda v: turned[v, rows, :]
                + wt_ref[v : v + 1, lanes] * held[part(i, v * cols, CHUNK), lanes],
            )
            for w in range(nf):
                mid[w, rows, :] = got[w]
                turned[w, rows, :] = turned[w, rows, :] + got[w]
            got = mix(table, lanes, nf, nf, lambda v: turned[v, rows, :])
            for w in range(nf):
                far[w, rows, :] = got[w]

        for w in range(nf):
            u_refs[w // own][w % own, lanes, :] = mid[w].T
            v_refs[w // own][w % own, lanes, :] = far[w].T


def quarter_pass(
    me, k, group, factors, kernels, weights, coef, gathered, right_side, moved, kept
):
    own, pairs, cols = right_side.shape
    nf = weights.shape[0]
    parts = nf // own
    quarter = pairs // parts
    naux = factors.shape[1]
    tile = tile_of(quarter)
    if tile is None:
        cut = lambda x, axis: lax.dynamic_slice_in_dim(x, me * quarter, quarter, axis)
        here = jnp.concatenate([cut(right_side, 1)] + moved)
        table = jnp.einsum("jt,tp->jp", coef, cut(kernels, 1), precision=EXACT)
        table = table.reshape(nf, nf, quarter)
        wide = jnp.einsum(
            "ja,pa->jp",
            gathered.reshape(nf * cols, naux),
            cut(factors, 0),
            preferred_element_type=jnp.float32,
        )
        wide = jnp.transpose(wide.reshape(nf, cols, quarter), (0, 2, 1))
        wide = here + cut(weights, 1)[:, :, None] * wide
        u = jnp.einsum("wvp,vpc->wpc", table, wide, precision=EXACT)
        v = jnp.einsum("wvp,vpc->wpc", table, here + u, precision=EXACT)
        return (
            [u[s * own : (s + 1) * own] for s in range(parts)],
            [v[s * own : (s + 1) * own] for s in range(parts)],
        )
    steps = quarter // tile
    at = lambda m: m[0] * steps + k
    came = pl.BlockSpec((own, tile, cols), lambda i, m: (0, k - group[0], 0))
    piece = pl.BlockSpec((own, tile, cols), lambda i, m: (0, 0, 0))
    shape = jax.ShapeDtypeStruct((own, tile, cols), jnp.float32)
    wide = jax.ShapeDtypeStruct((own, (group[1] - group[0]) * tile, cols), jnp.float32)
    out = pl.pallas_call(
        functools.partial(quarter_kernel, nf, parts, len(kept)),
        out_shape=[shape] * parts + [wide] * parts,
        grid_spec=pltpu.PrefetchScalarGridSpec(
            num_scalar_prefetch=1,
            grid=(1,),
            in_specs=[
                pl.BlockSpec((tile, naux), lambda i, m: (at(m), 0)),
                pl.BlockSpec((nf, tile), lambda i, m: (0, at(m))),
                pl.BlockSpec((nf, tile), lambda i, m: (0, at(m))),
                resident(coef),
                resident(gathered),
                pl.BlockSpec((own, tile, cols), lambda i, m: (0, at(m), 0)),
            ]
            + [came] * (parts - 1)
            + [pl.BlockSpec(memory_space=pl.ANY)] * len(kept),
            out_specs=[piece] * parts + [came] * parts,
            scratch_shapes=[
                VMEM((nf * nf, tile), jnp.float32),
                VMEM((nf * cols, tile), jnp.float32),
            ]
            + [VMEM((nf, cols, LANES), jnp.float32)] * 3,
        ),
        input_output_aliases={6 + parts + n: parts + n for n in range(len(kept))},
        compiler_params=pltpu.CompilerParams(vmem_limit_bytes=40 << 20),
        cost_estimate=pl.CostEstimate(
            flops=2 * nf * tile * cols * (naux + 32 * nf),
            bytes_accessed=16 * nf * tile * cols,
            transcendentals=0,
        ),
    )(me.reshape(1), factors, kernels, weights, coef, gathered, right_side, *moved, *kept)
    return list(out[:parts]), list(out[parts:])


def project_kernel(parts, me_ref, l_ref, *rest):
    s_refs, (x_ref, o_ref) = rest[:parts], rest[parts:]
    own, _, _ = s_refs[0].shape
    i = pl.program_id(0)

    @pl.when(i == 0)
    def _():
        o_ref[...] = x_ref[...]

    for s in range(parts):

        @pl.when(i == s)
        def _():
            rounded = [s_refs[s][f].astype(jnp.bfloat16) for f in range(own)]
            o_ref[...] += lax.dot_general(
                jnp.concatenate(rounded, axis=1),
                l_ref[...],
                (((0,), (0,)), ((), ())),
                preferred_element_type=jnp.float32,
            )


def around(parts, steps, k):
    return lambda i, m: lax.rem(m[0] + i, parts) * steps + k


def project(me, k, factors, pieces, total):
    own, size, cols = pieces[0].shape
    parts = len(pieces)
    pairs, naux = factors.shape
    quarter = pairs // parts
    if tile_of(quarter) is None:
        for s, x in enumerate(pieces):
            rows = lax.dynamic_slice_in_dim(
                factors, lax.rem(me + s, parts) * quarter, quarter, 0
            )
            total = total + jnp.einsum(
                "pa,fpc->fca", rows, x.astype(jnp.bfloat16), preferred_element_type=jnp.float32
            ).reshape(total.shape)
        return total
    at = around(parts, quarter // size, k)
    return pl.pallas_call(
        functools.partial(project_kernel, parts),
        out_shape=jax.ShapeDtypeStruct(total.shape, jnp.float32),
        grid_spec=pltpu.PrefetchScalarGridSpec(
            num_scalar_prefetch=1,
            grid=(parts,),
            in_specs=[pl.BlockSpec((size, naux), lambda i, m: (at(i, m), 0))]
            + [pl.BlockSpec((own, size, cols), lambda i, m: (0, 0, 0))] * parts
            + [resident(total)],
            out_specs=pl.BlockSpec(total.shape, lambda i, m: (0, 0)),
        ),
        compiler_params=pltpu.CompilerParams(vmem_limit_bytes=40 << 20),
        cost_estimate=pl.CostEstimate(
            flops=2 * own * parts * size * cols * naux,
            bytes_accessed=8 * own * parts * size * cols,
            transcendentals=0,
        ),
    )(me.reshape(1), factors, *pieces, total)


def again_kernel(own, l_ref, wt_ref, p_ref, x_ref, o_ref):
    cols = p_ref.shape[0] // own

    @pl.when(pl.program_id(0) == 0)
    def _():
        o_ref[...] = x_ref[...]

    wide = lax.dot_general(
        p_ref[...], l_ref[...], (((1,), (1,)), ((), ())), preferred_element_type=jnp.float32
    )
    wide = [
        (wide[f * cols : (f + 1) * cols] * wt_ref[f : f + 1, :]).astype(jnp.bfloat16)
        for f in range(own)
    ]
    o_ref[...] += lax.dot_general(
        jnp.concatenate(wide, axis=0),
        l_ref[...],
        (((1,), (0,)), ((), ())),
        preferred_element_type=jnp.float32,
    )


def again(factors, pair_weight, projected, kept):
    pairs, naux = factors.shape
    own = pair_weight.shape[0]
    tile = tile_of(pairs)
    return pl.pallas_call(
        functools.partial(again_kernel, own),
        out_shape=jax.ShapeDtypeStruct(kept.shape, jnp.float32),
        grid=(pairs // tile,),
        in_specs=[
            pl.BlockSpec((tile, naux), lambda i: (i, 0)),
            pl.BlockSpec((own, tile), lambda i: (0, i)),
            resident(projected),
            resident(kept),
        ],
        out_specs=pl.BlockSpec(kept.shape, lambda i: (0, 0)),
        compiler_params=pltpu.CompilerParams(vmem_limit_bytes=40 << 20),
        cost_estimate=pl.CostEstimate(
            flops=4 * kept.size * pairs, bytes_accessed=2 * factors.size, transcendentals=0
        ),
    )(factors, pair_weight, projected, kept)


def final_kernel(nf, parts, held_outs, me_ref, l_ref, k_ref, wt_ref, coef_ref, p_ref, *rest):
    s_refs, rest = rest[:parts], rest[parts:]
    b_refs, rest = rest[:parts], rest[parts + held_outs :]
    a_ref, new_ref, table, held, mid, second = rest
    own, _, cols = a_ref.shape
    table[...] = dot_exact(coef_ref[...], k_ref[...])
    for w in range(own):
        rows = slice(w * nf, (w + 1) * nf)
        table[rows, :] = table[rows, :] * wt_ref[...]
    spread(l_ref, p_ref, held)

    @pl.loop(0, table.shape[1] // LANES)
    def _(block):
        lanes = part(block, 0, LANES)

        @pl.loop(0, cols // WIDE)
        def _(i):
            rows = part(i, 0, WIDE)
            got = mix(table, lanes, own, nf, lambda v: held[part(i, v * cols, WIDE), lanes])
            for w in range(own):
                mid[w, rows, :] = got[w]
                second[w, rows, :] = (
                    wt_ref[w : w + 1, lanes] * held[part(i, w * cols, WIDE), lanes]
                )

        for s in range(parts):

            @pl.when(pl.program_id(0) == s)
            def _():
                for w in range(own):
                    new_ref[w, lanes, :] = b_refs[s][w, lanes, :] + mid[w].T
                    a_ref[w, lanes, :] = s_refs[s][w, lanes, :] + second[w].T


def final(me, k, factors, kernels, weights, coef, gathered, sources, base, outs):
    own, size, cols = sources[0].shape
    parts = len(sources)
    nf = weights.shape[0]
    pairs, naux = factors.shape
    quarter = pairs // parts
    tile = tile_of(quarter)
    shape = jax.ShapeDtypeStruct((own, pairs, cols), jnp.float32)
    if tile is None:
        wide = jnp.einsum(
            "ja,pa->jp",
            gathered.reshape(nf * cols, naux),
            factors,
            preferred_element_type=jnp.float32,
        )
        wide = jnp.transpose(wide.reshape(nf, cols, pairs), (0, 2, 1)) * weights[:, :, None]
        table = jnp.einsum("jt,tp->jp", coef, kernels, precision=EXACT).reshape(own, nf, pairs)
        new = jnp.einsum("wvp,vpc->wpc", table, wide, precision=EXACT)
        amplitude = wide[:own]
        for s in range(parts):
            at = lax.rem(me + s, parts) * quarter
            put = lambda x, y: lax.dynamic_update_slice_in_dim(
                x, lax.dynamic_slice_in_dim(x, at, quarter, 1) + y, at, 1
            )
            amplitude, new = put(amplitude, sources[s]), put(new, base[s])
        return amplitude, new
    at = around(parts, quarter // size, k)
    out = pl.BlockSpec((own, size, cols), lambda i, m: (0, at(i, m), 0))
    piece = pl.BlockSpec((own, size, cols), lambda i, m: (0, 0, 0))
    return pl.pallas_call(
        functools.partial(final_kernel, nf, parts, len(outs)),
        out_shape=(shape, shape),
        grid_spec=pltpu.PrefetchScalarGridSpec(
            num_scalar_prefetch=1,
            grid=(parts,),
            in_specs=[
                pl.BlockSpec((size, naux), lambda i, m: (at(i, m), 0)),
                pl.BlockSpec((nf, size), lambda i, m: (0, at(i, m))),
                pl.BlockSpec((nf, size), lambda i, m: (0, at(i, m))),
                resident(coef),
                resident(gathered),
            ]
            + [piece] * (2 * parts)
            + [pl.BlockSpec(memory_space=pl.ANY)] * len(outs),
            out_specs=(out, out),
            scratch_shapes=[
                VMEM((own * nf, size), jnp.float32),
                VMEM((nf * cols, size), jnp.float32),
            ]
            + [VMEM((own, cols, LANES), jnp.float32)] * 2,
        ),
        input_output_aliases={6 + 2 * parts + n: n for n in range(len(outs))},
        compiler_params=pltpu.CompilerParams(vmem_limit_bytes=48 << 20),
        cost_estimate=pl.CostEstimate(
            flops=2 * nf * parts * size * cols * naux,
            bytes_accessed=16 * own * parts * size * cols,
            transcendentals=0,
        ),
    )(me.reshape(1), factors, kernels, weights, coef, gathered, *sources, *base, *outs)


class Plane:
    def __init__(self, chips):
        self.chips = chips
        me = lax.axis_index("fac")
        self.core = lax.rem(me, 2)
        self.chip = lax.div(me, 2)
        self.pal = {"fac": me + 1 - 2 * self.core}
        self.started = []

    def on(self, d):
        return lax.rem(self.chip + d + self.chips, self.chips)

    def at(self, d):
        return {"fac": self.on(d) * 2 + self.core}

    def chip_at(self, chip):
        return {"fac": chip * 2 + self.core}

    def greet(self):
        barrier = pltpu.get_barrier_semaphore()
        for other in [self.pal] + [self.at(d) for d in range(1, self.chips)]:
            pl.semaphore_signal(barrier, inc=1, device_id=other, device_id_type=MESH)
        pl.semaphore_wait(barrier, self.chips)

    def send(self, src, dst, sems, at, to):
        copy = pltpu.make_async_remote_copy(
            src_ref=src,
            dst_ref=dst,
            send_sem=sems[0].at[at],
            recv_sem=sems[1].at[at],
            device_id=to,
            device_id_type=MESH,
        )
        copy.start()
        self.started.append(copy)
        return copy

    def end(self):
        for copy in self.started:
            copy.wait_send()


def reduced(plane, x_ref, near, red, land, mine, near_sems, red_sems):
    chips, chip, core, pal = plane.chips, plane.chip, plane.core, plane.pal
    nears = {}
    for d in list(range(1, chips)) + [0]:
        nears[d] = plane.send(x_ref.at[plane.on(d), 1 - core], near.at[d], near_sems, d, pal)
    block = mine.shape[0]
    step = min(block, 16)
    reds = []
    for d in range(1, chips):
        nears[d].wait_recv()
        for r in range(0, block, step):
            rows = slice(r, r + step)
            red[d, rows, :] = (x_ref[plane.on(d), core, rows, :] + near[d, rows, :]).astype(
                red.dtype
            )
        reds.append(plane.send(red.at[d], land.at[d], red_sems, d, plane.at(d)))
    nears[0].wait_recv()
    for copy in reds:
        copy.wait_recv()
    for r in range(0, block, step):
        rows = slice(r, r + step)
        total = x_ref[chip, core, rows, :] + near[0, rows, :]
        for d in range(1, chips):
            total = total + land[d, rows, :].astype(jnp.float32)
        mine[rows, :] = total.astype(mine.dtype)


def reduce_kernel(chips, x_ref, o_ref, near, red, land, *sems):
    plane = Plane(chips)
    plane.greet()
    reduced(plane, x_ref, near, red, land, o_ref, sems[0:2], sems[2:4])
    plane.end()


def sum_kernel(chips, x_ref, o_ref, near, red, land, mine, joined, *sems):
    plane = Plane(chips)
    chip, core = plane.chip, plane.core
    plane.greet()
    reduced(plane, x_ref, near, red, land, mine, sems[0:2], sems[2:4])
    here = joined.at[chip, core]
    keep = pltpu.make_async_copy(mine, here, sems[8])
    keep.start()
    keep.wait()
    wides = [plane.send(here, here, sems[4:6], d, plane.at(d)) for d in range(1, chips)]
    pairs = [plane.send(here, here, sems[6:8], 0, plane.pal)]
    for d, copy in enumerate(wides, 1):
        copy.wait_recv()
        there = joined.at[plane.on(-d), core]
        pairs.append(plane.send(there, there, sems[6:8], d, plane.pal))
    for copy in pairs:
        copy.wait_recv()
    plane.end()
    for c in range(chips):
        o_ref[c] = joined[c]


def gather_kernel(chips, parts, x_ref, o_ref, joined, *sems):
    plane = Plane(chips)
    chip, core, pal = plane.chip, plane.core, plane.pal
    plane.greet()
    wide_sems, pair_sems = sems[0:2], sems[2:4]
    pairs = []
    square = chips == 4
    column, row = lax.rem(chip, 2), lax.div(chip, 2)
    across, along = chip + 1 - 2 * column, chip + 2 - 4 * row
    corner = along + 1 - 2 * column
    wides = []
    for s in range(parts):
        src, dst = x_ref.at[s], joined.at[s, chip, core]
        if square:
            for n, to in enumerate((across, along)):
                copy = plane.send(src, dst, wide_sems, s * chips + n, plane.chip_at(to))
                wides.append((s, n, copy))
        else:
            for d in range(1, chips):
                copy = plane.send(src, dst, wide_sems, s * chips + d, plane.at(d))
                wides.append((s, d, copy))
    for s in range(parts):
        pairs.append(
            plane.send(x_ref.at[s], joined.at[s, chip, core], pair_sems, s * chips, pal)
        )
    late = []
    for s, d, copy in wides:
        copy.wait_recv()
        chip_from = (across, along)[d] if square else plane.on(-d)
        there = joined.at[s, chip_from, core]
        if square and d == s % 2:
            other = (along, across)[d]
            turned = plane.send(there, there, wide_sems, s * chips + 2, plane.chip_at(other))
            late.append((s, turned))
        at = s * chips + (1 + d if square else d)
        pairs.append(plane.send(there, there, pair_sems, at, pal))
    for s, copy in late:
        copy.wait_recv()
        there = joined.at[s, corner, core]
        pairs.append(plane.send(there, there, pair_sems, s * chips + 3, pal))
    for copy in pairs:
        copy.wait_recv()
    plane.end()
    for s in range(parts):
        for c in range(chips):
            o_ref[s, c] = joined[s, c]
        o_ref[s, chip, core] = x_ref[s]


def dmas(count, pairs):
    return [pltpu.SemaphoreType.DMA((count,))] * (2 * pairs)


def reach_params(cid):
    return pltpu.CompilerParams(
        collective_id=cid, has_side_effects=True, vmem_limit_bytes=24 << 20
    )


def reach_cost(size):
    return pl.CostEstimate(flops=40 * size, bytes_accessed=40 * size, transcendentals=0)


WHOLE = pl.BlockSpec(memory_space=VMEM)


def summed(x, all_blocks):
    n = lax.axis_size("fac")
    chips = n // 2
    rows, width = x.shape
    block = rows // n
    flat = (chips, 2, block, width)
    landing = [
        VMEM((chips, block, width), jnp.float32),
        VMEM((chips, block, width), jnp.bfloat16),
        VMEM((chips, block, width), jnp.bfloat16),
    ]
    if not all_blocks:
        return pl.pallas_call(
            functools.partial(reduce_kernel, chips),
            out_shape=jax.ShapeDtypeStruct((block, width), jnp.bfloat16),
            in_specs=[WHOLE],
            out_specs=WHOLE,
            scratch_shapes=landing + dmas(chips, 2),
            compiler_params=reach_params(1),
            cost_estimate=reach_cost(x.size // 2),
        )(x.reshape(flat))
    result = pl.pallas_call(
        functools.partial(sum_kernel, chips),
        out_shape=jax.ShapeDtypeStruct(flat, jnp.bfloat16),
        in_specs=[WHOLE],
        out_specs=WHOLE,
        scratch_shapes=landing
        + [VMEM((block, width), jnp.bfloat16), VMEM(flat, jnp.bfloat16)]
        + dmas(chips, 4)
        + [pltpu.SemaphoreType.DMA],
        compiler_params=reach_params(0),
        cost_estimate=reach_cost(x.size),
    )(x.reshape(flat))
    return result.reshape(rows, width)


def gathered_over(blocks):
    n = lax.axis_size("fac")
    chips = n // 2
    parts, block, width = blocks.shape
    flat = (parts, chips, 2, block, width)
    result = pl.pallas_call(
        functools.partial(gather_kernel, chips, parts),
        out_shape=jax.ShapeDtypeStruct(flat, jnp.bfloat16),
        in_specs=[WHOLE],
        out_specs=WHOLE,
        scratch_shapes=[VMEM(flat, jnp.bfloat16)] + dmas(parts * chips, 2),
        compiler_params=reach_params(2),
        cost_estimate=reach_cost(blocks.size * 8),
    )(blocks)
    return result.reshape(parts, n * block, width)


def shards(right_side, factors, pair_weight, second_order, forward, backward):
    own, pairs, cols = right_side.shape
    nf = forward.shape[0]
    naux = factors.shape[1]
    parts = nf // own
    quarter = pairs // parts
    me = lax.axis_index("freq")

    def shift(x, by):
        if by == 0:
            return x
        return lax.ppermute(x, "freq", [(i, (i + by) % parts) for i in range(parts)])

    order = jnp.concatenate(
        [lax.rem(me - s + parts, parts) * own + jnp.arange(own) for s in range(parts)]
    )
    pick = jax.nn.one_hot(order, nf, dtype=jnp.float32)
    ahead = jnp.einsum("ts,sv,wv->tw", pick, forward, pick, precision=EXACT)
    back = jnp.einsum("ws,st,vt->wv", pick, backward, pick, precision=EXACT)
    coef = (back[:, None, :] * ahead.T[None, :, :]).reshape(nf * nf, nf)
    reach = jnp.max(
        jnp.sum(
            jnp.einsum("wt,tv->wv", jnp.abs(backward), jnp.abs(forward), precision=EXACT), axis=1
        )
    )

    both = jnp.stack([pair_weight, second_order])
    tables = jnp.concatenate([shift(both, s) for s in range(parts)], axis=1)
    weights, kernels = tables[0], tables[1]
    size = tile_of(quarter) or quarter
    chunks = quarter // size
    early = max(chunks - 1, 1)
    groups = [(0, early)] + ([(early, chunks)] if early < chunks else [])
    tie = lax.optimization_barrier
    up = 8192.0

    def sliced(s, low, high):
        at = lax.rem(me + s, parts) * quarter + low * size
        return lax.dynamic_slice_in_dim(right_side, at, (high - low) * size, 1)

    def leaving(low, high):
        return [(sliced(s, low, high) * up).astype(jnp.float16) for s in range(1, parts)]

    def passed(blocks, back):
        return [
            shift(b, parts - 1 - s if back else s + 1) for s, b in enumerate(blocks)
        ]

    def first_projection():
        return jnp.einsum(
            "pa,fpc->fca",
            factors,
            right_side.astype(jnp.bfloat16),
            preferred_element_type=jnp.float32,
        ).reshape(own * cols, naux)

    def ladder(kept):
        total = kept
        for _ in range(INNER - 1):
            mine = summed(total, True)
            total = again(factors, pair_weight, mine, kept)
        block = summed(total, False)
        return jnp.stack([shift(block, s) for s in range(parts)])

    came = [passed(leaving(*groups[0]), False)]
    blocks = ladder(first_projection())
    if len(groups) > 1:
        blocks, out = tie((blocks, leaving(*groups[1])))
        came.append(passed(out, False))
    gathered = gathered_over(blocks)

    height = jnp.max(jnp.sum(jnp.abs(gathered.astype(jnp.float32)), axis=2))
    u_top = jnp.maximum(1.01 * reach * (R_MAX + W_MAX * L_MAX * height), 1e-30)
    v_top = jnp.maximum(1.01 * reach * (R_MAX + u_top), 1e-30)

    def halved(blocks, top):
        return [(b * (HALF_TOP / top)).astype(jnp.float16) for b in blocks[1:]]

    def added(first, rest, top, k):
        rest = [b.astype(jnp.float32) * (top / HALF_TOP) for b in rest]
        return [sliced(s, k, k + 1) + b for s, b in enumerate([first] + rest)]

    us, vs, inward = [], [], []
    for group, moved in zip(groups, came):
        moved = [m.astype(jnp.float32) * (1.0 / up) for m in moved]
        v = ()
        for k in range(*group):
            u, v = quarter_pass(
                me, k, group, factors, kernels, weights, coef, gathered, right_side, moved, v
            )
            inward.append(passed(halved(u, u_top), True))
            us.append(u)
        vs.append(v)
    sources = []
    total = jnp.zeros((own * cols, naux), jnp.float32)
    for k in range(chunks):
        if k:
            inward[k], total = tie((inward[k], total))
        sources.append(added(us[k][0], inward[k], u_top, k))
        total = project(me, k, factors, sources[k], total)

    out, total = tie((halved(vs[0], v_top), total))
    back = [passed(out, True)]
    blocks = ladder(total)
    if len(groups) > 1:
        blocks, out = tie((blocks, halved(vs[1], v_top)))
        back.append(passed(out, True))
    gathered = gathered_over(blocks)
    outs = ()
    for (low, high), first, moved in zip(groups, vs, back):
        gathered, moved, outs = tie((gathered, moved, outs))
        for k in range(low, high):
            rest = [m[:, (k - low) * size : (k - low + 1) * size] for m in [first[0]] + moved]
            base = added(rest[0], rest[1:], v_top, k)
            outs = final(
                me, k, factors, kernels, weights, coef[: own * nf], gathered, sources[k], base, outs
            )
    return outs


def solution(mesh):
    return jax.shard_map(
        shards,
        mesh=mesh,
        in_specs=(
            P("freq", "fac", None),
            P("fac", None),
            P("freq", "fac"),
            P("freq", "fac"),
            P(),
            P(),
        ),
        out_specs=(P("freq", "fac", None), P("freq", "fac", None)),
        check_vma=False,
    )
```

```python
import functools

import jax
import jax.numpy as jnp
from jax import lax
from jax.experimental import pallas as pl
from jax.experimental.pallas import tpu as pltpu
from jax.sharding import PartitionSpec as P


INNER = 2
LANES = 128
MESH = pl.DeviceIdType.MESH
CHUNK = 16
WIDE = 32
EXACT = lax.Precision.HIGHEST
R_MAX = 6.0
W_MAX = 2.0
L_MAX = 0.03125
HALF_TOP = 32768.0
VMEM = pltpu.VMEM


def tile_of(pairs):
    for blocks in (3, 4, 2, 1):
        if pairs % (blocks * LANES) == 0:
            return blocks * LANES
    return None


def wide_tile(pairs):
    for blocks in (6, 4, 3, 2, 1):
        if pairs % (blocks * LANES) == 0:
            return blocks * LANES
    return None


def mix(table, lanes, outs, count, term):
    totals = [None] * outs
    for v in range(count):
        value = term(v)
        for w in range(outs):
            row = w * count + v
            product = table[row : row + 1, lanes] * value
            totals[w] = product if totals[w] is None else totals[w] + product
    return totals


def part(i, base, chunk):
    return pl.ds(pl.multiple_of(base + i * chunk, chunk), chunk)


def rows_times(p_ref, l_ref):
    return lax.dot_general(
        p_ref[...], l_ref[...], (((1,), (1,)), ((), ())), preferred_element_type=jnp.float32
    )


def spread(l_ref, p_ref, far_ref, held):
    own = p_ref.shape[0]
    held[:own, :] = rows_times(p_ref, l_ref)
    held[own:, :] = rows_times(far_ref, l_ref)


def dot_exact(a, b):
    return lax.dot_general(
        a, b, (((1,), (0,)), ((), ())), precision=EXACT, preferred_element_type=jnp.float32
    )


def resident(x):
    return pl.BlockSpec(x.shape, lambda i, *_: (0,) * x.ndim, pipeline_mode=pl.Buffered(1))


def quarter_kernel(nf, parts, me_ref, l_ref, k_ref, wt_ref, coef_ref, p_ref, far_ref, *rest):
    r_refs, rest = rest[:parts], rest[parts:]
    u_refs, rest = rest[:parts], rest[parts:]
    v_refs, (table, held, turned, mid, far) = rest[:parts], rest[parts:]
    own = nf // parts
    cols = r_refs[0].shape[2]
    table[...] = dot_exact(coef_ref[...], k_ref[...])
    spread(l_ref, p_ref, far_ref, held)

    @pl.loop(0, table.shape[1] // LANES)
    def _(block):
        lanes = part(block, 0, LANES)
        for v in range(nf):
            turned[v] = r_refs[v // own][v % own, lanes, :].T

        @pl.loop(0, cols // CHUNK)
        def _(i):
            rows = part(i, 0, CHUNK)
            got = mix(
                table,
                lanes,
                nf,
                nf,
                lambda v: turned[v, rows, :]
                + wt_ref[v : v + 1, lanes] * held[part(i, v * cols, CHUNK), lanes],
            )
            for w in range(nf):
                mid[w, rows, :] = got[w]
                turned[w, rows, :] = turned[w, rows, :] + got[w]
            got = mix(table, lanes, nf, nf, lambda v: turned[v, rows, :])
            for w in range(nf):
                far[w, rows, :] = got[w]

        for w in range(nf):
            u_refs[w // own][w % own, lanes, :] = mid[w].T
            v_refs[w // own][w % own, lanes, :] = far[w].T


def quarter_pass(me, k, first, factors, kernels, weights, coef, near, far, right_side, moved):
    own, pairs, cols = right_side.shape
    nf = weights.shape[0]
    parts = nf // own
    quarter = pairs // parts
    naux = factors.shape[1]
    tile = tile_of(quarter)
    if tile is None:
        cut = lambda x, axis: lax.dynamic_slice_in_dim(x, me * quarter, quarter, axis)
        here = jnp.concatenate([cut(right_side, 1)] + moved)
        table = jnp.einsum("jt,tp->jp", coef, cut(kernels, 1), precision=EXACT)
        table = table.reshape(nf, nf, quarter)
        wide = jnp.einsum(
            "ja,pa->jp",
            jnp.concatenate([near, far]),
            cut(factors, 0),
            preferred_element_type=jnp.float32,
        )
        wide = jnp.transpose(wide.reshape(nf, cols, quarter), (0, 2, 1))
        wide = here + cut(weights, 1)[:, :, None] * wide
        u = jnp.einsum("wvp,vpc->wpc", table, wide, precision=EXACT)
        v = jnp.einsum("wvp,vpc->wpc", table, here + u, precision=EXACT)
        return (
            [u[s * own : (s + 1) * own] for s in range(parts)],
            [v[s * own : (s + 1) * own] for s in range(parts)],
        )
    steps = quarter // tile
    at = lambda m: m[0] * steps + k
    came = pl.BlockSpec((own, tile, cols), lambda i, m: (0, k - first, 0))
    piece = pl.BlockSpec((own, tile, cols), lambda i, m: (0, 0, 0))
    shape = jax.ShapeDtypeStruct((own, tile, cols), jnp.float32)
    out = pl.pallas_call(
        functools.partial(quarter_kernel, nf, parts),
        out_shape=[shape] * (2 * parts),
        grid_spec=pltpu.PrefetchScalarGridSpec(
            num_scalar_prefetch=1,
            grid=(1,),
            in_specs=[
                pl.BlockSpec((tile, naux), lambda i, m: (at(m), 0)),
                pl.BlockSpec((nf, tile), lambda i, m: (0, at(m))),
                pl.BlockSpec((nf, tile), lambda i, m: (0, at(m))),
                resident(coef),
                resident(near),
                resident(far),
                pl.BlockSpec((own, tile, cols), lambda i, m: (0, at(m), 0)),
            ]
            + [came] * (parts - 1),
            out_specs=[piece] * (2 * parts),
            scratch_shapes=[
                VMEM((nf * nf, tile), jnp.float32),
                VMEM((nf * cols, tile), jnp.float32),
            ]
            + [VMEM((nf, cols, LANES), jnp.float32)] * 3,
        ),
        compiler_params=pltpu.CompilerParams(vmem_limit_bytes=36 << 20),
        cost_estimate=pl.CostEstimate(
            flops=2 * nf * tile * cols * (naux + 32 * nf),
            bytes_accessed=16 * nf * tile * cols,
            transcendentals=0,
        ),
    )(me.reshape(1), factors, kernels, weights, coef, near, far, right_side, *moved)
    return list(out[:parts]), list(out[parts:])


def project_kernel(parts, me_ref, l_ref, *rest):
    s_refs, (x_ref, o_ref) = rest[:parts], rest[parts:]
    own, _, _ = s_refs[0].shape
    i = pl.program_id(0)

    @pl.when(i == 0)
    def _():
        o_ref[...] = x_ref[...]

    for s in range(parts):

        @pl.when(i == s)
        def _():
            rounded = [s_refs[s][f].astype(jnp.bfloat16) for f in range(own)]
            o_ref[...] += lax.dot_general(
                jnp.concatenate(rounded, axis=1),
                l_ref[...],
                (((0,), (0,)), ((), ())),
                preferred_element_type=jnp.float32,
            )


def around(parts, steps, k):
    return lambda i, m: lax.rem(m[0] + i, parts) * steps + k


def project(me, k, factors, pieces, total):
    own, size, cols = pieces[0].shape
    parts = len(pieces)
    pairs, naux = factors.shape
    quarter = pairs // parts
    if tile_of(quarter) is None:
        for s, x in enumerate(pieces):
            rows = lax.dynamic_slice_in_dim(
                factors, lax.rem(me + s, parts) * quarter, quarter, 0
            )
            total = total + jnp.einsum(
                "pa,fpc->fca", rows, x.astype(jnp.bfloat16), preferred_element_type=jnp.float32
            ).reshape(total.shape)
        return total
    at = around(parts, quarter // size, k)
    return pl.pallas_call(
        functools.partial(project_kernel, parts),
        out_shape=jax.ShapeDtypeStruct(total.shape, jnp.float32),
        grid_spec=pltpu.PrefetchScalarGridSpec(
            num_scalar_prefetch=1,
            grid=(parts,),
            in_specs=[pl.BlockSpec((size, naux), lambda i, m: (at(i, m), 0))]
            + [pl.BlockSpec((own, size, cols), lambda i, m: (0, 0, 0))] * parts
            + [resident(total)],
            out_specs=pl.BlockSpec(total.shape, lambda i, m: (0, 0)),
        ),
        compiler_params=pltpu.CompilerParams(vmem_limit_bytes=40 << 20),
        cost_estimate=pl.CostEstimate(
            flops=2 * own * parts * size * cols * naux,
            bytes_accessed=8 * own * parts * size * cols,
            transcendentals=0,
        ),
    )(me.reshape(1), factors, *pieces, total)


def again_kernel(own, l_ref, wt_ref, p_ref, x_ref, o_ref):
    cols = p_ref.shape[0] // own

    @pl.when(pl.program_id(0) == 0)
    def _():
        o_ref[...] = x_ref[...]

    wide = lax.dot_general(
        p_ref[...], l_ref[...], (((1,), (1,)), ((), ())), preferred_element_type=jnp.float32
    )
    wide = [
        (wide[f * cols : (f + 1) * cols] * wt_ref[f : f + 1, :]).astype(jnp.bfloat16)
        for f in range(own)
    ]
    o_ref[...] += lax.dot_general(
        jnp.concatenate(wide, axis=0),
        l_ref[...],
        (((1,), (0,)), ((), ())),
        preferred_element_type=jnp.float32,
    )


def again(factors, pair_weight, projected, kept):
    pairs, naux = factors.shape
    own = pair_weight.shape[0]
    tile = wide_tile(pairs)
    return pl.pallas_call(
        functools.partial(again_kernel, own),
        out_shape=jax.ShapeDtypeStruct(kept.shape, jnp.float32),
        grid=(pairs // tile,),
        in_specs=[
            pl.BlockSpec((tile, naux), lambda i: (i, 0)),
            pl.BlockSpec((own, tile), lambda i: (0, i)),
            resident(projected),
            resident(kept),
        ],
        out_specs=pl.BlockSpec(kept.shape, lambda i: (0, 0)),
        compiler_params=pltpu.CompilerParams(vmem_limit_bytes=40 << 20),
        cost_estimate=pl.CostEstimate(
            flops=4 * kept.size * pairs, bytes_accessed=2 * factors.size, transcendentals=0
        ),
    )(factors, pair_weight, projected, kept)


class Stream:
    def __init__(self, refs, buffer, sems):
        self.refs, self.buffer, self.sems = refs, buffer, sems
        self.step = pl.program_id(0)
        self.slot = lax.rem(self.step, 2)

    def copy(self, n):
        return pltpu.make_async_copy(self.refs[n], self.buffer.at[n % 2], self.sems.at[n % 2])

    def ahead(self):
        @pl.when(self.step == 0)
        def _():
            self.copy(0).start()

        for n in range(1, len(self.refs)):

            @pl.when(self.step == n - 1)
            def _():
                self.copy(n).start()

    def here(self):
        pltpu.make_async_copy(
            self.refs[0], self.buffer.at[self.slot], self.sems.at[self.slot]
        ).wait()
        return self.buffer.at[self.slot]


def stream_scratch(piece):
    return [VMEM((2,) + piece.shape, piece.dtype), pltpu.SemaphoreType.DMA((2,))]


ANYWHERE = pl.BlockSpec(memory_space=pl.ANY)


def amplitude_kernel(pieces, me_ref, l_ref, wt_ref, p_ref, *rest):
    refs, (a_ref, buffer, sems) = rest[:pieces], rest[pieces:]
    own, tile, cols = a_ref.shape
    stream = Stream(refs, buffer, sems)
    stream.ahead()
    wide = rows_times(p_ref, l_ref)
    here = stream.here()
    for f in range(own):
        scaled = wide[f * cols : (f + 1) * cols] * wt_ref[f : f + 1, :]
        for k in range(0, tile, LANES):
            lanes = slice(k, k + LANES)
            a_ref[f, lanes, :] = here[f, lanes, :] + scaled[:, lanes].T


def amplitude(me, factors, pair_weight, near, sources):
    own, size, cols = sources[0][0].shape
    parts = len(sources[0])
    pairs, naux = factors.shape
    quarter = pairs // parts
    if tile_of(quarter) is None:
        wide = jnp.einsum("ja,pa->jp", near, factors, preferred_element_type=jnp.float32)
        wide = jnp.transpose(wide.reshape(own, cols, pairs), (0, 2, 1))
        result = wide * pair_weight[:, :, None]
        for s in range(parts):
            at = lax.rem(me + s, parts) * quarter
            part_of = lax.dynamic_slice_in_dim(result, at, quarter, 1) + sources[0][s]
            result = lax.dynamic_update_slice_in_dim(result, part_of, at, 1)
        return result
    steps = quarter // size
    pieces = [x for chunk in sources for x in chunk]
    at = lambda i, m: lax.rem(m[0] + lax.rem(i, parts), parts) * steps + lax.div(i, parts)
    return pl.pallas_call(
        functools.partial(amplitude_kernel, len(pieces)),
        out_shape=jax.ShapeDtypeStruct((own, pairs, cols), jnp.float32),
        grid_spec=pltpu.PrefetchScalarGridSpec(
            num_scalar_prefetch=1,
            grid=(len(pieces),),
            in_specs=[
                pl.BlockSpec((size, naux), lambda i, m: (at(i, m), 0)),
                pl.BlockSpec((own, size), lambda i, m: (0, at(i, m))),
                resident(near),
            ]
            + [ANYWHERE] * len(pieces),
            out_specs=pl.BlockSpec((own, size, cols), lambda i, m: (0, at(i, m), 0)),
            scratch_shapes=stream_scratch(pieces[0]),
        ),
        compiler_params=pltpu.CompilerParams(vmem_limit_bytes=20 << 20),
        cost_estimate=pl.CostEstimate(
            flops=2 * own * pairs * cols * naux,
            bytes_accessed=8 * own * pairs * cols,
            transcendentals=0,
        ),
    )(me.reshape(1), factors, pair_weight, near, *pieces)


def final_kernel(nf, parts, held_outs, me_ref, l_ref, k_ref, wt_ref, coef_ref, p_ref, far_ref, *rest):
    b_refs, rest = rest[:parts], rest[parts + held_outs :]
    new_ref, table, held, mid, buffer, sems = rest
    own, _, cols = new_ref.shape
    stream = Stream(b_refs, buffer, sems)
    stream.ahead()
    table[...] = dot_exact(coef_ref[...], k_ref[...])
    for w in range(own):
        rows = slice(w * nf, (w + 1) * nf)
        table[rows, :] = table[rows, :] * wt_ref[...]
    spread(l_ref, p_ref, far_ref, held)
    here = stream.here()

    @pl.loop(0, table.shape[1] // LANES)
    def _(block):
        lanes = part(block, 0, LANES)

        @pl.loop(0, cols // WIDE)
        def _(i):
            rows = part(i, 0, WIDE)
            got = mix(table, lanes, own, nf, lambda v: held[part(i, v * cols, WIDE), lanes])
            for w in range(own):
                mid[w, rows, :] = got[w]

        for w in range(own):
            new_ref[w, lanes, :] = here[w, lanes, :] + mid[w].T


def final(me, k, factors, kernels, weights, coef, near, far, base, outs):
    own, size, cols = base[0].shape
    parts = len(base)
    nf = weights.shape[0]
    pairs, naux = factors.shape
    quarter = pairs // parts
    tile = tile_of(quarter)
    if tile is None:
        wide = jnp.einsum(
            "ja,pa->jp",
            jnp.concatenate([near, far]),
            factors,
            preferred_element_type=jnp.float32,
        )
        wide = jnp.transpose(wide.reshape(nf, cols, pairs), (0, 2, 1)) * weights[:, :, None]
        table = jnp.einsum("jt,tp->jp", coef, kernels, precision=EXACT).reshape(own, nf, pairs)
        new = jnp.einsum("wvp,vpc->wpc", table, wide, precision=EXACT)
        for s in range(parts):
            at = lax.rem(me + s, parts) * quarter
            part_of = lax.dynamic_slice_in_dim(new, at, quarter, 1) + base[s]
            new = lax.dynamic_update_slice_in_dim(new, part_of, at, 1)
        return [new]
    at = around(parts, quarter // size, k)
    result = pl.pallas_call(
        functools.partial(final_kernel, nf, parts, len(outs)),
        out_shape=jax.ShapeDtypeStruct((own, pairs, cols), jnp.float32),
        grid_spec=pltpu.PrefetchScalarGridSpec(
            num_scalar_prefetch=1,
            grid=(parts,),
            in_specs=[
                pl.BlockSpec((size, naux), lambda i, m: (at(i, m), 0)),
                pl.BlockSpec((nf, size), lambda i, m: (0, at(i, m))),
                pl.BlockSpec((nf, size), lambda i, m: (0, at(i, m))),
                resident(coef),
                resident(near),
                resident(far),
            ]
            + [ANYWHERE] * (parts + len(outs)),
            out_specs=pl.BlockSpec((own, size, cols), lambda i, m: (0, at(i, m), 0)),
            scratch_shapes=[
                VMEM((own * nf, size), jnp.float32),
                VMEM((nf * cols, size), jnp.float32),
                VMEM((own, cols, LANES), jnp.float32),
            ]
            + stream_scratch(base[0]),
        ),
        input_output_aliases={7 + parts + n: n for n in range(len(outs))},
        compiler_params=pltpu.CompilerParams(vmem_limit_bytes=26 << 20),
        cost_estimate=pl.CostEstimate(
            flops=2 * nf * parts * size * cols * naux,
            bytes_accessed=8 * own * parts * size * cols,
            transcendentals=0,
        ),
    )(me.reshape(1), factors, kernels, weights, coef, near, far, *base, *outs)
    return [result]


class Plane:
    def __init__(self, chips):
        self.chips = chips
        me = lax.axis_index("fac")
        self.core = lax.rem(me, 2)
        self.chip = lax.div(me, 2)
        self.pal = {"fac": me + 1 - 2 * self.core}
        self.started = []

    def on(self, d):
        return lax.rem(self.chip + d + self.chips, self.chips)

    def at(self, d):
        return {"fac": self.on(d) * 2 + self.core}

    def chip_at(self, chip):
        return {"fac": chip * 2 + self.core}

    def greet(self):
        barrier = pltpu.get_barrier_semaphore()
        for other in [self.pal] + [self.at(d) for d in range(1, self.chips)]:
            pl.semaphore_signal(barrier, inc=1, device_id=other, device_id_type=MESH)
        pl.semaphore_wait(barrier, self.chips)

    def send(self, src, dst, sems, at, to):
        copy = pltpu.make_async_remote_copy(
            src_ref=src,
            dst_ref=dst,
            send_sem=sems[0].at[at],
            recv_sem=sems[1].at[at],
            device_id=to,
            device_id_type=MESH,
        )
        copy.start()
        self.started.append(copy)
        return copy

    def end(self):
        for copy in self.started:
            copy.wait_send()


def reduced(plane, x_ref, near, red, land, mine, near_sems, red_sems):
    chips, chip, core, pal = plane.chips, plane.chip, plane.core, plane.pal
    nears = {}
    for d in list(range(1, chips)) + [0]:
        nears[d] = plane.send(x_ref.at[plane.on(d), 1 - core], near.at[d], near_sems, d, pal)
    block = mine.shape[0]
    step = min(block, 16)
    reds = []
    for d in range(1, chips):
        nears[d].wait_recv()
        for r in range(0, block, step):
            rows = slice(r, r + step)
            red[d, rows, :] = (x_ref[plane.on(d), core, rows, :] + near[d, rows, :]).astype(
                red.dtype
            )
        reds.append(plane.send(red.at[d], land.at[d], red_sems, d, plane.at(d)))
    nears[0].wait_recv()
    for copy in reds:
        copy.wait_recv()
    for r in range(0, block, step):
        rows = slice(r, r + step)
        total = x_ref[chip, core, rows, :] + near[0, rows, :]
        for d in range(1, chips):
            total = total + land[d, rows, :].astype(jnp.float32)
        mine[rows, :] = total.astype(mine.dtype)


def reduce_kernel(chips, x_ref, o_ref, near, red, land, *sems):
    plane = Plane(chips)
    plane.greet()
    reduced(plane, x_ref, near, red, land, o_ref, sems[0:2], sems[2:4])
    plane.end()


def sum_kernel(chips, x_ref, o_ref, near, red, land, mine, joined, *sems):
    plane = Plane(chips)
    chip, core = plane.chip, plane.core
    plane.greet()
    reduced(plane, x_ref, near, red, land, mine, sems[0:2], sems[2:4])
    here = joined.at[chip, core]
    keep = pltpu.make_async_copy(mine, here, sems[8])
    keep.start()
    keep.wait()
    wides = [plane.send(here, here, sems[4:6], d, plane.at(d)) for d in range(1, chips)]
    pairs = [plane.send(here, here, sems[6:8], 0, plane.pal)]
    for d, copy in enumerate(wides, 1):
        copy.wait_recv()
        there = joined.at[plane.on(-d), core]
        pairs.append(plane.send(there, there, sems[6:8], d, plane.pal))
    for copy in pairs:
        copy.wait_recv()
    plane.end()
    for c in range(chips):
        o_ref[c] = joined[c]


def gather_kernel(chips, parts, *refs):
    x_refs, (o_ref, joined, *sems) = refs[:parts], refs[parts:]
    plane = Plane(chips)
    chip, core, pal = plane.chip, plane.core, plane.pal
    plane.greet()
    wide_sems, pair_sems = sems[0:2], sems[2:4]
    pairs = []
    square = chips == 4
    column, row = lax.rem(chip, 2), lax.div(chip, 2)
    across, along = chip + 1 - 2 * column, chip + 2 - 4 * row
    corner = along + 1 - 2 * column
    wides = []
    for s in range(parts):
        src, dst = x_refs[s], joined.at[s, chip, core]
        if square:
            for n, to in enumerate((across, along)):
                copy = plane.send(src, dst, wide_sems, s * chips + n, plane.chip_at(to))
                wides.append((s, n, copy))
        else:
            for d in range(1, chips):
                copy = plane.send(src, dst, wide_sems, s * chips + d, plane.at(d))
                wides.append((s, d, copy))
    for s in range(parts):
        pairs.append(
            plane.send(x_refs[s], joined.at[s, chip, core], pair_sems, s * chips, pal)
        )
    late = []
    for s, d, copy in wides:
        copy.wait_recv()
        chip_from = (across, along)[d] if square else plane.on(-d)
        there = joined.at[s, chip_from, core]
        if square and d == s % 2:
            other = (along, across)[d]
            turned = plane.send(there, there, wide_sems, s * chips + 2, plane.chip_at(other))
            late.append((s, turned))
        at = s * chips + (1 + d if square else d)
        pairs.append(plane.send(there, there, pair_sems, at, pal))
    for s, copy in late:
        copy.wait_recv()
        there = joined.at[s, corner, core]
        pairs.append(plane.send(there, there, pair_sems, s * chips + 3, pal))
    for copy in pairs:
        copy.wait_recv()
    plane.end()
    for s in range(parts):
        for c in range(chips):
            o_ref[s, c] = joined[s, c]
        o_ref[s, chip, core] = x_refs[s][...]


def dmas(count, pairs):
    return [pltpu.SemaphoreType.DMA((count,))] * (2 * pairs)


def reach_params(cid):
    return pltpu.CompilerParams(
        collective_id=cid, has_side_effects=True, vmem_limit_bytes=24 << 20
    )


def reach_cost(size):
    return pl.CostEstimate(flops=40 * size, bytes_accessed=40 * size, transcendentals=0)


WHOLE = pl.BlockSpec(memory_space=VMEM)


def summed(x, all_blocks):
    n = lax.axis_size("fac")
    chips = n // 2
    rows, width = x.shape
    block = rows // n
    flat = (chips, 2, block, width)
    landing = [
        VMEM((chips, block, width), jnp.float32),
        VMEM((chips, block, width), jnp.bfloat16),
        VMEM((chips, block, width), jnp.bfloat16),
    ]
    if not all_blocks:
        return pl.pallas_call(
            functools.partial(reduce_kernel, chips),
            out_shape=jax.ShapeDtypeStruct((block, width), jnp.bfloat16),
            in_specs=[WHOLE],
            out_specs=WHOLE,
            scratch_shapes=landing + dmas(chips, 2),
            compiler_params=reach_params(1),
            cost_estimate=reach_cost(x.size // 2),
        )(x.reshape(flat))
    result = pl.pallas_call(
        functools.partial(sum_kernel, chips),
        out_shape=jax.ShapeDtypeStruct(flat, jnp.bfloat16),
        in_specs=[WHOLE],
        out_specs=WHOLE,
        scratch_shapes=landing
        + [VMEM((block, width), jnp.bfloat16), VMEM(flat, jnp.bfloat16)]
        + dmas(chips, 4)
        + [pltpu.SemaphoreType.DMA],
        compiler_params=reach_params(0),
        cost_estimate=reach_cost(x.size),
    )(x.reshape(flat))
    return result.reshape(rows, width)


def gathered_over(blocks):
    n = lax.axis_size("fac")
    chips = n // 2
    parts = len(blocks)
    block, width = blocks[0].shape
    flat = (parts, chips, 2, block, width)
    result = pl.pallas_call(
        functools.partial(gather_kernel, chips, parts),
        out_shape=jax.ShapeDtypeStruct(flat, jnp.bfloat16),
        in_specs=[WHOLE] * parts,
        out_specs=WHOLE,
        scratch_shapes=[VMEM(flat, jnp.bfloat16)] + dmas(parts * chips, 2),
        compiler_params=reach_params(2 if parts == 1 else 3),
        cost_estimate=reach_cost(block * width * parts * 8),
    )(*blocks)
    return result.reshape(parts * n * block, width)


def shards(right_side, factors, pair_weight, second_order, forward, backward):
    own, pairs, cols = right_side.shape
    nf = forward.shape[0]
    naux = factors.shape[1]
    parts = nf // own
    quarter = pairs // parts
    me = lax.axis_index("freq")

    def shift(x, by):
        if by == 0:
            return x
        return lax.ppermute(x, "freq", [(i, (i + by) % parts) for i in range(parts)])

    order = jnp.concatenate(
        [lax.rem(me - s + parts, parts) * own + jnp.arange(own) for s in range(parts)]
    )
    pick = jax.nn.one_hot(order, nf, dtype=jnp.float32)
    ahead = jnp.einsum("ts,sv,wv->tw", pick, forward, pick, precision=EXACT)
    back = jnp.einsum("ws,st,vt->wv", pick, backward, pick, precision=EXACT)
    coef = (back[:, None, :] * ahead.T[None, :, :]).reshape(nf * nf, nf)
    reach = jnp.max(
        jnp.sum(
            jnp.einsum("wt,tv->wv", jnp.abs(backward), jnp.abs(forward), precision=EXACT), axis=1
        )
    )

    both = jnp.stack([pair_weight, second_order])
    tables = jnp.concatenate([shift(both, s) for s in range(parts)], axis=1)
    weights, kernels = tables[0], tables[1]
    size = tile_of(quarter) or quarter
    chunks = quarter // size
    early = max(chunks - 1, 1)
    groups = [(0, early)] + ([(early, chunks)] if early < chunks else [])
    tie = lax.optimization_barrier
    up = 8192.0

    def sliced(x, s, low, high):
        at = lax.rem(me + s, parts) * quarter + low * size
        return lax.dynamic_slice_in_dim(x, at, (high - low) * size, 1)

    def leaving(low, high):
        return [(sliced(right_side, s, low, high) * up).astype(jnp.float16) for s in range(1, parts)]

    def passed(blocks, back):
        return [
            shift(b, parts - 1 - s if back else s + 1) for s, b in enumerate(blocks)
        ]

    def first_projection():
        return jnp.einsum(
            "pa,fpc->fca",
            factors,
            right_side.astype(jnp.bfloat16),
            preferred_element_type=jnp.float32,
        ).reshape(own * cols, naux)

    def ladder(kept):
        total = kept
        for _ in range(INNER - 1):
            mine = summed(total, True)
            total = again(factors, pair_weight, mine, kept)
        block = summed(total, False)
        far = [shift(block, s) for s in range(1, parts)]
        return gathered_over([block]), far

    leaves = [leaving(*g) for g in groups]
    right_late, leaves[-1] = tie((right_side, leaves[-1]))
    came = [passed(x, False) for x in leaves]
    near, blocks = ladder(first_projection())
    far = gathered_over(blocks)

    def tall(x):
        return jnp.max(jnp.sum(jnp.abs(x.astype(jnp.float32)), axis=1))

    height = jnp.maximum(tall(near), tall(far))
    u_top = jnp.maximum(1.01 * reach * (R_MAX + W_MAX * L_MAX * height), 1e-30)
    v_top = jnp.maximum(1.01 * reach * (R_MAX + u_top), 1e-30)

    def halved(blocks, top):
        return [(b * (HALF_TOP / top)).astype(jnp.float16) for b in blocks[1:]]

    def added(first, rest, top, k):
        rest = [b.astype(jnp.float32) * (top / HALF_TOP) for b in rest]
        return [sliced(right_late, s, k, k + 1) + b for s, b in enumerate([first] + rest)]

    us, vs, inward = [], [], []
    for group, moved in zip(groups, came):
        moved = [m.astype(jnp.float32) * (1.0 / up) for m in moved]
        for k in range(*group):
            u, v = quarter_pass(
                me, k, group[0], factors, kernels, weights, coef, near, far, right_side, moved
            )
            inward.append(passed(halved(u, u_top), True))
            us.append(u)
            vs.append(v)
    sources = []
    total = jnp.zeros((own * cols, naux), jnp.float32)
    for k in range(chunks):
        if k:
            inward[k], total = tie((inward[k], total))
        sources.append(added(us[k][0], inward[k], u_top, k))
        total = project(me, k, factors, sources[k], total)

    halves = []
    for v in vs:
        halves.append(halved(v, v_top))
    out, total = tie((halves[0], total))
    back = [passed(out, True)]
    near, blocks = ladder(total)
    for k in range(1, chunks):
        back.append(passed(halves[k], True))
    amplitudes = amplitude(me, factors, pair_weight, near, sources)
    far = gathered_over(blocks)
    outs = []
    for k in range(chunks):
        back[k], outs = tie((back[k], outs))
        base = added(vs[k][0], back[k], v_top, k)
        outs = final(
            me, k, factors, kernels, weights, coef[: own * nf], near, far, base, outs
        )
    return amplitudes, outs[0]


def solution(mesh):
    return jax.shard_map(
        shards,
        mesh=mesh,
        in_specs=(
            P("freq", "fac", None),
            P("fac", None),
            P("freq", "fac"),
            P("freq", "fac"),
            P(),
            P(),
        ),
        out_specs=(P("freq", "fac", None), P("freq", "fac", None)),
        check_vma=False,
    )
```

```python
import functools

import jax
import jax.numpy as jnp
from jax import lax
from jax.experimental import pallas as pl
from jax.experimental.pallas import tpu as pltpu
from jax.sharding import PartitionSpec as P


INNER = 2
LANES = 128
MESH = pl.DeviceIdType.MESH
CHUNK = 16
WIDE = 32
EXACT = lax.Precision.HIGHEST
R_MAX = 6.0
W_MAX = 2.0
L_MAX = 0.03125
HALF_TOP = 32768.0
VMEM = pltpu.VMEM


def tile_of(pairs):
    for blocks in (3, 4, 2, 1):
        if pairs % (blocks * LANES) == 0:
            return blocks * LANES
    return None


def wide_tile(pairs):
    for blocks in (6, 4, 3, 2, 1):
        if pairs % (blocks * LANES) == 0:
            return blocks * LANES
    return None


def mix(table, lanes, outs, count, term):
    totals = [None] * outs
    for v in range(count):
        value = term(v)
        for w in range(outs):
            row = w * count + v
            product = table[row : row + 1, lanes] * value
            totals[w] = product if totals[w] is None else totals[w] + product
    return totals


def part(i, base, chunk):
    return pl.ds(pl.multiple_of(base + i * chunk, chunk), chunk)


def rows_times(p_ref, l_ref):
    return lax.dot_general(
        p_ref[...], l_ref[...], (((1,), (1,)), ((), ())), preferred_element_type=jnp.float32
    )


def spread(l_ref, p_ref, far_ref, held):
    own = p_ref.shape[0]
    held[:own, :] = rows_times(p_ref, l_ref)
    held[own:, :] = rows_times(far_ref, l_ref)


def dot_exact(a, b):
    return lax.dot_general(
        a, b, (((1,), (0,)), ((), ())), precision=EXACT, preferred_element_type=jnp.float32
    )


def resident(x):
    return pl.BlockSpec(x.shape, lambda i, *_: (0,) * x.ndim, pipeline_mode=pl.Buffered(1))


def quarter_kernel(nf, parts, sets, me_ref, l_ref, k_ref, wt_ref, coef_ref, p_ref, far_ref, *rest):
    own_ref, rest = rest[0], rest[1:]
    came, rest = rest[: sets * (parts - 1)], rest[sets * (parts - 1) :]
    u_refs, rest = rest[:parts], rest[parts:]
    v_refs, (table, held, turned, mid, far) = rest[:parts], rest[parts:]
    own = nf // parts
    cols = own_ref.shape[2]
    table[...] = dot_exact(coef_ref[...], k_ref[...])
    spread(l_ref, p_ref, far_ref, held)

    @pl.loop(0, table.shape[1] // LANES)
    def _(block):
        lanes = part(block, 0, LANES)
        for v in range(own):
            turned[v] = own_ref[v, lanes, :].T
        for j in range(sets):

            @pl.when(pl.program_id(0) == j)
            def _():
                for v in range(own, nf):
                    turned[v] = came[j * (parts - 1) + v // own - 1][v % own, lanes, :].T

        @pl.loop(0, cols // CHUNK)
        def _(i):
            rows = part(i, 0, CHUNK)
            got = mix(
                table,
                lanes,
                nf,
                nf,
                lambda v: turned[v, rows, :]
                + wt_ref[v : v + 1, lanes] * held[part(i, v * cols, CHUNK), lanes],
            )
            for w in range(nf):
                mid[w, rows, :] = got[w]
                turned[w, rows, :] = turned[w, rows, :] + got[w]
            got = mix(table, lanes, nf, nf, lambda v: turned[v, rows, :])
            for w in range(nf):
                far[w, rows, :] = got[w]

        for w in range(nf):
            u_refs[w // own][w % own, lanes, :] = mid[w].T
            v_refs[w // own][w % own, lanes, :] = far[w].T


def quarter_pass(me, low, factors, kernels, weights, coef, near, far, right_side, moved):
    own, pairs, cols = right_side.shape
    nf = weights.shape[0]
    parts = nf // own
    quarter = pairs // parts
    naux = factors.shape[1]
    tile = tile_of(quarter)
    sets = len(moved)
    if tile is None:
        cut = lambda x, axis: lax.dynamic_slice_in_dim(x, me * quarter, quarter, axis)
        here = jnp.concatenate([cut(right_side, 1)] + moved[0][0])
        table = jnp.einsum("jt,tp->jp", coef, cut(kernels, 1), precision=EXACT)
        table = table.reshape(nf, nf, quarter)
        wide = jnp.einsum(
            "ja,pa->jp",
            jnp.concatenate([near, far]),
            cut(factors, 0),
            preferred_element_type=jnp.float32,
        )
        wide = jnp.transpose(wide.reshape(nf, cols, quarter), (0, 2, 1))
        wide = here + cut(weights, 1)[:, :, None] * wide
        u = jnp.einsum("wvp,vpc->wpc", table, wide, precision=EXACT)
        v = jnp.einsum("wvp,vpc->wpc", table, here + u, precision=EXACT)
        return (
            [u[s * own : (s + 1) * own] for s in range(parts)],
            [v[s * own : (s + 1) * own] for s in range(parts)],
        )
    steps = quarter // tile
    at = lambda i, m: m[0] * steps + low + i
    here = lambda n: pl.BlockSpec((own, tile, cols), lambda i, m: (0, n, 0))
    piece = pl.BlockSpec((own, tile, cols), lambda i, m: (0, i, 0))
    shape = jax.ShapeDtypeStruct((own, sets * tile, cols), jnp.float32)
    out = pl.pallas_call(
        functools.partial(quarter_kernel, nf, parts, sets),
        out_shape=[shape] * (2 * parts),
        grid_spec=pltpu.PrefetchScalarGridSpec(
            num_scalar_prefetch=1,
            grid=(sets,),
            in_specs=[
                pl.BlockSpec((tile, naux), lambda i, m: (at(i, m), 0)),
                pl.BlockSpec((nf, tile), lambda i, m: (0, at(i, m))),
                pl.BlockSpec((nf, tile), lambda i, m: (0, at(i, m))),
                resident(coef),
                resident(near),
                resident(far),
                pl.BlockSpec((own, tile, cols), lambda i, m: (0, at(i, m), 0)),
            ]
            + [here(n) for _, n in moved for _ in range(parts - 1)],
            out_specs=[piece] * (2 * parts),
            scratch_shapes=[
                VMEM((nf * nf, tile), jnp.float32),
                VMEM((nf * cols, tile), jnp.float32),
            ]
            + [VMEM((nf, cols, LANES), jnp.float32)] * 3,
        ),
        compiler_params=pltpu.CompilerParams(vmem_limit_bytes=(36 if sets == 1 else 46) << 20),
        cost_estimate=pl.CostEstimate(
            flops=2 * nf * sets * tile * cols * (naux + 32 * nf),
            bytes_accessed=16 * nf * sets * tile * cols,
            transcendentals=0,
        ),
    )(
        me.reshape(1),
        factors,
        kernels,
        weights,
        coef,
        near,
        far,
        right_side,
        *[x for xs, _ in moved for x in xs],
    )
    return list(out[:parts]), list(out[parts:])


def project_kernel(parts, sets, me_ref, l_ref, *rest):
    s_refs, (x_ref, o_ref) = rest[:parts], rest[parts:]
    own, _, _ = s_refs[0].shape
    i = pl.program_id(0)

    @pl.when(i == 0)
    def _():
        o_ref[...] = x_ref[...]

    for s in range(parts):

        @pl.when(lax.div(i, sets) == s)
        def _():
            rounded = [s_refs[s][f].astype(jnp.bfloat16) for f in range(own)]
            o_ref[...] += lax.dot_general(
                jnp.concatenate(rounded, axis=1),
                l_ref[...],
                (((0,), (0,)), ((), ())),
                preferred_element_type=jnp.float32,
            )


def around(parts, steps, low, sets):
    return lambda i, m: lax.rem(m[0] + lax.div(i, sets), parts) * steps + low + lax.rem(i, sets)


def project(me, low, factors, pieces, total):
    own, size, cols = pieces[0].shape
    parts = len(pieces)
    pairs, naux = factors.shape
    quarter = pairs // parts
    tile = tile_of(quarter)
    if tile is None:
        for s, x in enumerate(pieces):
            rows = lax.dynamic_slice_in_dim(
                factors, lax.rem(me + s, parts) * quarter, quarter, 0
            )
            total = total + jnp.einsum(
                "pa,fpc->fca", rows, x.astype(jnp.bfloat16), preferred_element_type=jnp.float32
            ).reshape(total.shape)
        return total
    sets = size // tile
    at = around(parts, quarter // tile, low, sets)
    stay = lambda s: lambda i, m: (0, jnp.clip(i - s * sets, 0, sets - 1), 0)
    return pl.pallas_call(
        functools.partial(project_kernel, parts, sets),
        out_shape=jax.ShapeDtypeStruct(total.shape, jnp.float32),
        grid_spec=pltpu.PrefetchScalarGridSpec(
            num_scalar_prefetch=1,
            grid=(parts * sets,),
            in_specs=[pl.BlockSpec((tile, naux), lambda i, m: (at(i, m), 0))]
            + [pl.BlockSpec((own, tile, cols), stay(s)) for s in range(parts)]
            + [resident(total)],
            out_specs=pl.BlockSpec(total.shape, lambda i, m: (0, 0)),
        ),
        compiler_params=pltpu.CompilerParams(vmem_limit_bytes=40 << 20),
        cost_estimate=pl.CostEstimate(
            flops=2 * own * parts * size * cols * naux,
            bytes_accessed=8 * own * parts * size * cols,
            transcendentals=0,
        ),
    )(me.reshape(1), factors, *pieces, total)


def again_kernel(own, l_ref, wt_ref, p_ref, x_ref, o_ref):
    cols = p_ref.shape[0] // own

    @pl.when(pl.program_id(0) == 0)
    def _():
        o_ref[...] = x_ref[...]

    wide = lax.dot_general(
        p_ref[...], l_ref[...], (((1,), (1,)), ((), ())), preferred_element_type=jnp.float32
    )
    wide = [
        (wide[f * cols : (f + 1) * cols] * wt_ref[f : f + 1, :]).astype(jnp.bfloat16)
        for f in range(own)
    ]
    o_ref[...] += lax.dot_general(
        jnp.concatenate(wide, axis=0),
        l_ref[...],
        (((1,), (0,)), ((), ())),
        preferred_element_type=jnp.float32,
    )


def again(factors, pair_weight, projected, kept):
    pairs, naux = factors.shape
    own = pair_weight.shape[0]
    tile = wide_tile(pairs)
    return pl.pallas_call(
        functools.partial(again_kernel, own),
        out_shape=jax.ShapeDtypeStruct(kept.shape, jnp.float32),
        grid=(pairs // tile,),
        in_specs=[
            pl.BlockSpec((tile, naux), lambda i: (i, 0)),
            pl.BlockSpec((own, tile), lambda i: (0, i)),
            resident(projected),
            resident(kept),
        ],
        out_specs=pl.BlockSpec(kept.shape, lambda i: (0, 0)),
        compiler_params=pltpu.CompilerParams(vmem_limit_bytes=40 << 20),
        cost_estimate=pl.CostEstimate(
            flops=4 * kept.size * pairs, bytes_accessed=2 * factors.size, transcendentals=0
        ),
    )(factors, pair_weight, projected, kept)


class Stream:
    def __init__(self, refs, buffer, sems):
        tile = buffer.shape[2]
        refs = [
            ref.at[:, n : n + tile, :] for ref in refs for n in range(0, ref.shape[1], tile)
        ]
        self.refs, self.buffer, self.sems = refs, buffer, sems
        self.step = pl.program_id(0)
        self.slot = lax.rem(self.step, 2)

    def copy(self, n):
        return pltpu.make_async_copy(self.refs[n], self.buffer.at[n % 2], self.sems.at[n % 2])

    def ahead(self):
        @pl.when(self.step == 0)
        def _():
            self.copy(0).start()

        for n in range(1, len(self.refs)):

            @pl.when(self.step == n - 1)
            def _():
                self.copy(n).start()

    def here(self):
        pltpu.make_async_copy(
            self.refs[0], self.buffer.at[self.slot], self.sems.at[self.slot]
        ).wait()
        return self.buffer.at[self.slot]


def stream_scratch(own, tile, cols):
    return [VMEM((2, own, tile, cols), jnp.float32), pltpu.SemaphoreType.DMA((2,))]


ANYWHERE = pl.BlockSpec(memory_space=pl.ANY)


def amplitude_kernel(pieces, me_ref, l_ref, wt_ref, p_ref, *rest):
    refs, (a_ref, buffer, sems) = rest[:pieces], rest[pieces:]
    own, tile, cols = a_ref.shape
    stream = Stream(refs, buffer, sems)
    stream.ahead()
    wide = rows_times(p_ref, l_ref)
    here = stream.here()
    for f in range(own):
        scaled = wide[f * cols : (f + 1) * cols] * wt_ref[f : f + 1, :]
        for k in range(0, tile, LANES):
            lanes = slice(k, k + LANES)
            a_ref[f, lanes, :] = here[f, lanes, :] + scaled[:, lanes].T


def amplitude(me, factors, pair_weight, near, sources):
    own, _, cols = sources[0][0].shape
    parts = len(sources[0])
    pairs, naux = factors.shape
    quarter = pairs // parts
    size = tile_of(quarter)
    if size is None:
        wide = jnp.einsum("ja,pa->jp", near, factors, preferred_element_type=jnp.float32)
        wide = jnp.transpose(wide.reshape(own, cols, pairs), (0, 2, 1))
        result = wide * pair_weight[:, :, None]
        for s in range(parts):
            at = lax.rem(me + s, parts) * quarter
            part_of = lax.dynamic_slice_in_dim(result, at, quarter, 1) + sources[0][s]
            result = lax.dynamic_update_slice_in_dim(result, part_of, at, 1)
        return result
    steps = quarter // size
    pieces = [x for group in sources for x in group]
    first = parts * (sources[0][0].shape[1] // size)
    ranks = [around(parts, steps, 0, first // parts)]
    if len(sources) > 1:
        ranks.append(around(parts, steps, first // parts, steps - first // parts))

    def at(i, m):
        place = ranks[0](i, m)
        if len(ranks) > 1:
            place = jnp.where(i < first, place, ranks[1](jnp.maximum(i - first, 0), m))
        return place

    return pl.pallas_call(
        functools.partial(amplitude_kernel, len(pieces)),
        out_shape=jax.ShapeDtypeStruct((own, pairs, cols), jnp.float32),
        grid_spec=pltpu.PrefetchScalarGridSpec(
            num_scalar_prefetch=1,
            grid=(parts * steps,),
            in_specs=[
                pl.BlockSpec((size, naux), lambda i, m: (at(i, m), 0)),
                pl.BlockSpec((own, size), lambda i, m: (0, at(i, m))),
                resident(near),
            ]
            + [ANYWHERE] * len(pieces),
            out_specs=pl.BlockSpec((own, size, cols), lambda i, m: (0, at(i, m), 0)),
            scratch_shapes=stream_scratch(own, size, cols),
        ),
        compiler_params=pltpu.CompilerParams(vmem_limit_bytes=20 << 20),
        cost_estimate=pl.CostEstimate(
            flops=2 * own * pairs * cols * naux,
            bytes_accessed=8 * own * pairs * cols,
            transcendentals=0,
        ),
    )(me.reshape(1), factors, pair_weight, near, *pieces)


def final_kernel(nf, parts, held_outs, me_ref, l_ref, k_ref, wt_ref, coef_ref, p_ref, far_ref, *rest):
    b_refs, rest = rest[:parts], rest[parts + held_outs :]
    new_ref, table, held, mid, buffer, sems = rest
    own, _, cols = new_ref.shape
    stream = Stream(b_refs, buffer, sems)
    stream.ahead()
    table[...] = dot_exact(coef_ref[...], k_ref[...])
    for w in range(own):
        rows = slice(w * nf, (w + 1) * nf)
        table[rows, :] = table[rows, :] * wt_ref[...]
    spread(l_ref, p_ref, far_ref, held)
    here = stream.here()

    @pl.loop(0, table.shape[1] // LANES)
    def _(block):
        lanes = part(block, 0, LANES)

        @pl.loop(0, cols // WIDE)
        def _(i):
            rows = part(i, 0, WIDE)
            got = mix(table, lanes, own, nf, lambda v: held[part(i, v * cols, WIDE), lanes])
            for w in range(own):
                mid[w, rows, :] = got[w]

        for w in range(own):
            new_ref[w, lanes, :] = here[w, lanes, :] + mid[w].T


def final(me, low, factors, kernels, weights, coef, near, far, base, outs):
    own, span, cols = base[0].shape
    parts = len(base)
    nf = weights.shape[0]
    pairs, naux = factors.shape
    quarter = pairs // parts
    tile = tile_of(quarter)
    if tile is None:
        wide = jnp.einsum(
            "ja,pa->jp",
            jnp.concatenate([near, far]),
            factors,
            preferred_element_type=jnp.float32,
        )
        wide = jnp.transpose(wide.reshape(nf, cols, pairs), (0, 2, 1)) * weights[:, :, None]
        table = jnp.einsum("jt,tp->jp", coef, kernels, precision=EXACT).reshape(own, nf, pairs)
        new = jnp.einsum("wvp,vpc->wpc", table, wide, precision=EXACT)
        for s in range(parts):
            at = lax.rem(me + s, parts) * quarter
            part_of = lax.dynamic_slice_in_dim(new, at, quarter, 1) + base[s]
            new = lax.dynamic_update_slice_in_dim(new, part_of, at, 1)
        return [new]
    size = tile
    sets = span // size
    at = around(parts, quarter // size, low, sets)
    result = pl.pallas_call(
        functools.partial(final_kernel, nf, parts, len(outs)),
        out_shape=jax.ShapeDtypeStruct((own, pairs, cols), jnp.float32),
        grid_spec=pltpu.PrefetchScalarGridSpec(
            num_scalar_prefetch=1,
            grid=(parts * sets,),
            in_specs=[
                pl.BlockSpec((size, naux), lambda i, m: (at(i, m), 0)),
                pl.BlockSpec((nf, size), lambda i, m: (0, at(i, m))),
                pl.BlockSpec((nf, size), lambda i, m: (0, at(i, m))),
                resident(coef),
                resident(near),
                resident(far),
            ]
            + [ANYWHERE] * (parts + len(outs)),
            out_specs=pl.BlockSpec((own, size, cols), lambda i, m: (0, at(i, m), 0)),
            scratch_shapes=[
                VMEM((own * nf, size), jnp.float32),
                VMEM((nf * cols, size), jnp.float32),
                VMEM((own, cols, LANES), jnp.float32),
            ]
            + stream_scratch(own, size, cols),
        ),
        input_output_aliases={7 + parts + n: n for n in range(len(outs))},
        compiler_params=pltpu.CompilerParams(vmem_limit_bytes=26 << 20),
        cost_estimate=pl.CostEstimate(
            flops=2 * nf * parts * span * cols * naux,
            bytes_accessed=8 * own * parts * span * cols,
            transcendentals=0,
        ),
    )(me.reshape(1), factors, kernels, weights, coef, near, far, *base, *outs)
    return [result]


class Plane:
    def __init__(self, chips):
        self.chips = chips
        me = lax.axis_index("fac")
        self.core = lax.rem(me, 2)
        self.chip = lax.div(me, 2)
        self.pal = {"fac": me + 1 - 2 * self.core}
        self.started = []

    def on(self, d):
        return lax.rem(self.chip + d + self.chips, self.chips)

    def at(self, d):
        return {"fac": self.on(d) * 2 + self.core}

    def chip_at(self, chip):
        return {"fac": chip * 2 + self.core}

    def greet(self):
        barrier = pltpu.get_barrier_semaphore()
        for other in [self.pal] + [self.at(d) for d in range(1, self.chips)]:
            pl.semaphore_signal(barrier, inc=1, device_id=other, device_id_type=MESH)
        pl.semaphore_wait(barrier, self.chips)

    def send(self, src, dst, sems, at, to):
        copy = pltpu.make_async_remote_copy(
            src_ref=src,
            dst_ref=dst,
            send_sem=sems[0].at[at],
            recv_sem=sems[1].at[at],
            device_id=to,
            device_id_type=MESH,
        )
        copy.start()
        self.started.append(copy)
        return copy

    def end(self):
        for copy in self.started:
            copy.wait_send()


def reduced(plane, x_ref, near, red, land, mine, near_sems, red_sems):
    chips, chip, core, pal = plane.chips, plane.chip, plane.core, plane.pal
    nears = {}
    for d in list(range(1, chips)) + [0]:
        nears[d] = plane.send(x_ref.at[plane.on(d), 1 - core], near.at[d], near_sems, d, pal)
    block = mine.shape[0]
    step = min(block, 16)
    reds = []
    for d in range(1, chips):
        nears[d].wait_recv()
        for r in range(0, block, step):
            rows = slice(r, r + step)
            red[d, rows, :] = (x_ref[plane.on(d), core, rows, :] + near[d, rows, :]).astype(
                red.dtype
            )
        reds.append(plane.send(red.at[d], land.at[d], red_sems, d, plane.at(d)))
    nears[0].wait_recv()
    for copy in reds:
        copy.wait_recv()
    for r in range(0, block, step):
        rows = slice(r, r + step)
        total = x_ref[chip, core, rows, :] + near[0, rows, :]
        for d in range(1, chips):
            total = total + land[d, rows, :].astype(jnp.float32)
        mine[rows, :] = total.astype(mine.dtype)


def reduce_kernel(chips, x_ref, o_ref, near, red, land, *sems):
    plane = Plane(chips)
    plane.greet()
    reduced(plane, x_ref, near, red, land, o_ref, sems[0:2], sems[2:4])
    plane.end()


def sum_kernel(chips, x_ref, o_ref, near, red, land, mine, joined, *sems):
    plane = Plane(chips)
    chip, core = plane.chip, plane.core
    plane.greet()
    reduced(plane, x_ref, near, red, land, mine, sems[0:2], sems[2:4])
    here = joined.at[chip, core]
    keep = pltpu.make_async_copy(mine, here, sems[8])
    keep.start()
    keep.wait()
    wides = [plane.send(here, here, sems[4:6], d, plane.at(d)) for d in range(1, chips)]
    pairs = [plane.send(here, here, sems[6:8], 0, plane.pal)]
    for d, copy in enumerate(wides, 1):
        copy.wait_recv()
        there = joined.at[plane.on(-d), core]
        pairs.append(plane.send(there, there, sems[6:8], d, plane.pal))
    for copy in pairs:
        copy.wait_recv()
    plane.end()
    for c in range(chips):
        o_ref[c] = joined[c]


def gather_kernel(chips, parts, *refs):
    x_refs, (o_ref, joined, *sems) = refs[:parts], refs[parts:]
    kept = sems[4]
    plane = Plane(chips)
    chip, core, pal = plane.chip, plane.core, plane.pal
    plane.greet()
    wide_sems, pair_sems = sems[0:2], sems[2:4]
    pairs = []
    copies = []
    for s in range(parts):
        copies.append(
            pltpu.make_async_copy(x_refs[s], joined.at[s, chip, core], kept.at[s])
        )
        copies[-1].start()
    square = chips == 4
    column, row = lax.rem(chip, 2), lax.div(chip, 2)
    across, along = chip + 1 - 2 * column, chip + 2 - 4 * row
    corner = along + 1 - 2 * column
    wides = []
    for s in range(parts):
        src, dst = x_refs[s], joined.at[s, chip, core]
        if square:
            for n, to in enumerate((across, along)):
                copy = plane.send(src, dst, wide_sems, s * chips + n, plane.chip_at(to))
                wides.append((s, n, copy))
        else:
            for d in range(1, chips):
                copy = plane.send(src, dst, wide_sems, s * chips + d, plane.at(d))
                wides.append((s, d, copy))
    for s in range(parts):
        pairs.append(
            plane.send(x_refs[s], joined.at[s, chip, core], pair_sems, s * chips, pal)
        )
    late = []
    for s, d, copy in wides:
        copy.wait_recv()
        chip_from = (across, along)[d] if square else plane.on(-d)
        there = joined.at[s, chip_from, core]
        if square and d == s % 2:
            other = (along, across)[d]
            turned = plane.send(there, there, wide_sems, s * chips + 2, plane.chip_at(other))
            late.append((s, turned))
        at = s * chips + (1 + d if square else d)
        pairs.append(plane.send(there, there, pair_sems, at, pal))
    for s, copy in late:
        copy.wait_recv()
        there = joined.at[s, corner, core]
        pairs.append(plane.send(there, there, pair_sems, s * chips + 3, pal))
    for copy in pairs:
        copy.wait_recv()
    plane.end()
    for copy in copies:
        copy.wait()
    for s in range(parts):
        for c in range(chips):
            o_ref[s, c] = joined[s, c]


def dmas(count, pairs):
    return [pltpu.SemaphoreType.DMA((count,))] * (2 * pairs)


def reach_params(cid):
    return pltpu.CompilerParams(
        collective_id=cid, has_side_effects=True, vmem_limit_bytes=24 << 20
    )


def reach_cost(size):
    return pl.CostEstimate(flops=40 * size, bytes_accessed=40 * size, transcendentals=0)


WHOLE = pl.BlockSpec(memory_space=VMEM)


def summed(x, all_blocks):
    n = lax.axis_size("fac")
    chips = n // 2
    rows, width = x.shape
    block = rows // n
    flat = (chips, 2, block, width)
    landing = [
        VMEM((chips, block, width), jnp.float32),
        VMEM((chips, block, width), jnp.bfloat16),
        VMEM((chips, block, width), jnp.bfloat16),
    ]
    if not all_blocks:
        return pl.pallas_call(
            functools.partial(reduce_kernel, chips),
            out_shape=jax.ShapeDtypeStruct((block, width), jnp.bfloat16),
            in_specs=[WHOLE],
            out_specs=WHOLE,
            scratch_shapes=landing + dmas(chips, 2),
            compiler_params=reach_params(1),
            cost_estimate=reach_cost(x.size // 2),
        )(x.reshape(flat))
    result = pl.pallas_call(
        functools.partial(sum_kernel, chips),
        out_shape=jax.ShapeDtypeStruct(flat, jnp.bfloat16),
        in_specs=[WHOLE],
        out_specs=WHOLE,
        scratch_shapes=landing
        + [VMEM((block, width), jnp.bfloat16), VMEM(flat, jnp.bfloat16)]
        + dmas(chips, 4)
        + [pltpu.SemaphoreType.DMA],
        compiler_params=reach_params(0),
        cost_estimate=reach_cost(x.size),
    )(x.reshape(flat))
    return result.reshape(rows, width)


def gathered_over(blocks):
    n = lax.axis_size("fac")
    chips = n // 2
    parts = len(blocks)
    block, width = blocks[0].shape
    flat = (parts, chips, 2, block, width)
    result = pl.pallas_call(
        functools.partial(gather_kernel, chips, parts),
        out_shape=jax.ShapeDtypeStruct(flat, jnp.bfloat16),
        in_specs=[pl.BlockSpec(memory_space=pl.ANY)] * parts,
        out_specs=WHOLE,
        scratch_shapes=[VMEM(flat, jnp.bfloat16)]
        + dmas(parts * chips, 2)
        + [pltpu.SemaphoreType.DMA((parts,))],
        compiler_params=reach_params(2 if parts == 1 else 3),
        cost_estimate=reach_cost(block * width * parts * 8),
    )(*blocks)
    return result.reshape(parts * n * block, width)


def shards(right_side, factors, pair_weight, second_order, forward, backward):
    own, pairs, cols = right_side.shape
    nf = forward.shape[0]
    naux = factors.shape[1]
    parts = nf // own
    quarter = pairs // parts
    me = lax.axis_index("freq")

    def shift(x, by):
        if by == 0:
            return x
        return lax.ppermute(x, "freq", [(i, (i + by) % parts) for i in range(parts)])

    order = jnp.concatenate(
        [lax.rem(me - s + parts, parts) * own + jnp.arange(own) for s in range(parts)]
    )
    pick = jax.nn.one_hot(order, nf, dtype=jnp.float32)
    ahead = jnp.einsum("ts,sv,wv->tw", pick, forward, pick, precision=EXACT)
    back = jnp.einsum("ws,st,vt->wv", pick, backward, pick, precision=EXACT)
    coef = (back[:, None, :] * ahead.T[None, :, :]).reshape(nf * nf, nf)
    reach = jnp.max(
        jnp.sum(
            jnp.einsum("wt,tv->wv", jnp.abs(backward), jnp.abs(forward), precision=EXACT), axis=1
        )
    )

    both = jnp.stack([pair_weight, second_order])
    tables = jnp.concatenate([shift(both, s) for s in range(parts)], axis=1)
    weights, kernels = tables[0], tables[1]
    size = tile_of(quarter) or quarter
    chunks = quarter // size
    early = max(chunks - 1, 1)
    groups = [(0, early)] + ([(early, chunks)] if early < chunks else [])
    calls = [(0, 1)] + ([(1, chunks)] if chunks > 1 else [])
    tie = lax.optimization_barrier
    up = 8192.0

    def sliced(x, s, low, high):
        at = lax.rem(me + s, parts) * quarter + low * size
        return lax.dynamic_slice_in_dim(x, at, (high - low) * size, 1)

    def leaving(low, high):
        return [(sliced(right_side, s, low, high) * up).astype(jnp.float16) for s in range(1, parts)]

    def passed(blocks, back):
        return [
            shift(b, parts - 1 - s if back else s + 1) for s, b in enumerate(blocks)
        ]

    def first_projection():
        return jnp.einsum(
            "pa,fpc->fca",
            factors,
            right_side.astype(jnp.bfloat16),
            preferred_element_type=jnp.float32,
        ).reshape(own * cols, naux)

    def ladder(kept):
        total = kept
        for _ in range(INNER - 1):
            mine = summed(total, True)
            total = again(factors, pair_weight, mine, kept)
        block = summed(total, False)
        far = [shift(block, s) for s in range(1, parts)]
        return gathered_over([block]), far

    leaves = [leaving(*g) for g in groups]
    right_late, leaves[-1] = tie((right_side, leaves[-1]))
    came = [passed(x, False) for x in leaves]
    near, blocks = ladder(first_projection())
    far = gathered_over(blocks)

    def tall(x):
        return jnp.max(jnp.sum(jnp.abs(x.astype(jnp.float32)), axis=1))

    height = jnp.maximum(tall(near), tall(far))
    u_top = jnp.maximum(1.01 * reach * (R_MAX + W_MAX * L_MAX * height), 1e-30)
    v_top = jnp.maximum(1.01 * reach * (R_MAX + u_top), 1e-30)

    def halved(blocks, top):
        return [(b * (HALF_TOP / top)).astype(jnp.float16) for b in blocks[1:]]

    def added(first, rest, top, group):
        rest = [b.astype(jnp.float32) * (top / HALF_TOP) for b in rest]
        return [sliced(right_late, s, *group) + b for s, b in enumerate([first] + rest)]

    placed = []
    for group, moved in zip(groups, came):
        moved = [m.astype(jnp.float32) * (1.0 / up) for m in moved]
        placed += [(moved, k - group[0]) for k in range(*group)]
    us, vs, inward, halves = [], [], [], []
    for low, high in calls:
        u, v = quarter_pass(
            me,
            low,
            factors,
            kernels,
            weights,
            coef,
            near,
            far,
            right_side,
            placed[low:high],
        )
        inward.append(passed(halved(u, u_top), True))
        halves.append(halved(v, v_top))
        us.append(u)
        vs.append(v)
    sources = []
    total = jnp.zeros((own * cols, naux), jnp.float32)
    for n, group in enumerate(calls):
        if n:
            inward[n], total = tie((inward[n], total))
        sources.append(added(us[n][0], inward[n], u_top, group))
        total = project(me, group[0], factors, sources[n], total)

    out, total = tie((halves[0], total))
    back = [passed(out, True)]
    near, blocks = ladder(total)
    for n in range(1, len(calls)):
        back.append(passed(halves[n], True))
    amplitudes = amplitude(me, factors, pair_weight, near, sources)
    far = gathered_over(blocks)
    outs = []
    for n, group in enumerate(calls):
        back[n], outs = tie((back[n], outs))
        base = added(vs[n][0], back[n], v_top, group)
        outs = final(
            me,
            group[0],
            factors,
            kernels,
            weights,
            coef[: own * nf],
            near,
            far,
            base,
            outs,
        )
    return amplitudes, outs[0]


def solution(mesh):
    return jax.shard_map(
        shards,
        mesh=mesh,
        in_specs=(
            P("freq", "fac", None),
            P("fac", None),
            P("freq", "fac"),
            P("freq", "fac"),
            P(),
            P(),
        ),
        out_specs=(P("freq", "fac", None), P("freq", "fac", None)),
        check_vma=False,
    )
```

```python
import functools

import jax
import jax.numpy as jnp
from jax import lax
from jax.experimental import pallas as pl
from jax.experimental.pallas import tpu as pltpu
from jax.sharding import PartitionSpec as P


INNER = 2
LANES = 128
MESH = pl.DeviceIdType.MESH
CHUNK = 16
WIDE = 32
EXACT = lax.Precision.HIGHEST
R_MAX = 6.0
W_MAX = 2.0
L_MAX = 0.03125
HALF_TOP = 32768.0
VMEM = pltpu.VMEM


def tile_of(pairs):
    for blocks in (3, 4, 2, 1):
        if pairs % (blocks * LANES) == 0:
            return blocks * LANES
    return None


def wide_tile(pairs):
    for blocks in (6, 4, 3, 2, 1):
        if pairs % (blocks * LANES) == 0:
            return blocks * LANES
    return None


def mix(table, lanes, outs, count, term):
    totals = [None] * outs
    for v in range(count):
        value = term(v)
        for w in range(outs):
            row = w * count + v
            product = table[row : row + 1, lanes] * value
            totals[w] = product if totals[w] is None else totals[w] + product
    return totals


def part(i, base, chunk):
    return pl.ds(pl.multiple_of(base + i * chunk, chunk), chunk)


def rows_times(p_ref, l_ref):
    return lax.dot_general(
        p_ref[...], l_ref[...], (((1,), (1,)), ((), ())), preferred_element_type=jnp.float32
    )


def spread(l_ref, p_ref, far_ref, held):
    own = p_ref.shape[0]
    held[:own, :] = rows_times(p_ref, l_ref)
    held[own:, :] = rows_times(far_ref, l_ref)


def dot_exact(a, b):
    return lax.dot_general(
        a, b, (((1,), (0,)), ((), ())), precision=EXACT, preferred_element_type=jnp.float32
    )


def resident(x):
    return pl.BlockSpec(x.shape, lambda i, *_: (0,) * x.ndim, pipeline_mode=pl.Buffered(1))


def quarter_kernel(nf, parts, sets, me_ref, l_ref, k_ref, wt_ref, coef_ref, p_ref, far_ref, *rest):
    own_ref, rest = rest[0], rest[1:]
    came, rest = rest[: sets * (parts - 1)], rest[sets * (parts - 1) :]
    u_refs, rest = rest[:parts], rest[parts:]
    v_refs, (table, held, turned, mid, far) = rest[:parts], rest[parts:]
    own = nf // parts
    cols = own_ref.shape[2]
    table[...] = dot_exact(coef_ref[...], k_ref[...])
    spread(l_ref, p_ref, far_ref, held)

    @pl.loop(0, table.shape[1] // LANES)
    def _(block):
        lanes = part(block, 0, LANES)
        for v in range(own):
            turned[v] = own_ref[v, lanes, :].T
        for j in range(sets):

            @pl.when(pl.program_id(0) == j)
            def _():
                for v in range(own, nf):
                    turned[v] = came[j * (parts - 1) + v // own - 1][v % own, lanes, :].T

        @pl.loop(0, cols // CHUNK)
        def _(i):
            rows = part(i, 0, CHUNK)
            got = mix(
                table,
                lanes,
                nf,
                nf,
                lambda v: turned[v, rows, :]
                + wt_ref[v : v + 1, lanes] * held[part(i, v * cols, CHUNK), lanes],
            )
            for w in range(nf):
                mid[w, rows, :] = got[w]
                turned[w, rows, :] = turned[w, rows, :] + got[w]
            got = mix(table, lanes, nf, nf, lambda v: turned[v, rows, :])
            for w in range(nf):
                far[w, rows, :] = got[w]

        for w in range(nf):
            u_refs[w // own][w % own, lanes, :] = mid[w].T
            v_refs[w // own][w % own, lanes, :] = far[w].T


def quarter_pass(me, low, factors, kernels, weights, coef, near, far, right_side, moved):
    own, pairs, cols = right_side.shape
    nf = weights.shape[0]
    parts = nf // own
    quarter = pairs // parts
    naux = factors.shape[1]
    tile = tile_of(quarter)
    sets = len(moved)
    if tile is None:
        cut = lambda x, axis: lax.dynamic_slice_in_dim(x, me * quarter, quarter, axis)
        here = jnp.concatenate([cut(right_side, 1)] + moved[0][0])
        table = jnp.einsum("jt,tp->jp", coef, cut(kernels, 1), precision=EXACT)
        table = table.reshape(nf, nf, quarter)
        wide = jnp.einsum(
            "ja,pa->jp",
            jnp.concatenate([near, far]),
            cut(factors, 0),
            preferred_element_type=jnp.float32,
        )
        wide = jnp.transpose(wide.reshape(nf, cols, quarter), (0, 2, 1))
        wide = here + cut(weights, 1)[:, :, None] * wide
        u = jnp.einsum("wvp,vpc->wpc", table, wide, precision=EXACT)
        v = jnp.einsum("wvp,vpc->wpc", table, here + u, precision=EXACT)
        return (
            [u[s * own : (s + 1) * own] for s in range(parts)],
            [v[s * own : (s + 1) * own] for s in range(parts)],
        )
    steps = quarter // tile
    at = lambda i, m: m[0] * steps + low + i
    here = lambda n: pl.BlockSpec((own, tile, cols), lambda i, m: (0, n, 0))
    piece = pl.BlockSpec((own, tile, cols), lambda i, m: (0, i, 0))
    shape = jax.ShapeDtypeStruct((own, sets * tile, cols), jnp.float32)
    out = pl.pallas_call(
        functools.partial(quarter_kernel, nf, parts, sets),
        out_shape=[shape] * (2 * parts),
        grid_spec=pltpu.PrefetchScalarGridSpec(
            num_scalar_prefetch=1,
            grid=(sets,),
            in_specs=[
                pl.BlockSpec((tile, naux), lambda i, m: (at(i, m), 0)),
                pl.BlockSpec((nf, tile), lambda i, m: (0, at(i, m))),
                pl.BlockSpec((nf, tile), lambda i, m: (0, at(i, m))),
                resident(coef),
                resident(near),
                resident(far),
                pl.BlockSpec((own, tile, cols), lambda i, m: (0, at(i, m), 0)),
            ]
            + [here(n) for _, n in moved for _ in range(parts - 1)],
            out_specs=[piece] * (2 * parts),
            scratch_shapes=[
                VMEM((nf * nf, tile), jnp.float32),
                VMEM((nf * cols, tile), jnp.float32),
            ]
            + [VMEM((nf, cols, LANES), jnp.float32)] * 3,
        ),
        compiler_params=pltpu.CompilerParams(vmem_limit_bytes=(36 if sets == 1 else 46) << 20),
        cost_estimate=pl.CostEstimate(
            flops=2 * nf * sets * tile * cols * (naux + 32 * nf),
            bytes_accessed=16 * nf * sets * tile * cols,
            transcendentals=0,
        ),
    )(
        me.reshape(1),
        factors,
        kernels,
        weights,
        coef,
        near,
        far,
        right_side,
        *[x for xs, _ in moved for x in xs],
    )
    return list(out[:parts]), list(out[parts:])


def project_kernel(parts, sets, me_ref, l_ref, *rest):
    s_refs, (x_ref, o_ref) = rest[:parts], rest[parts:]
    own, _, _ = s_refs[0].shape
    i = pl.program_id(0)

    @pl.when(i == 0)
    def _():
        o_ref[...] = x_ref[...]

    for s in range(parts):

        @pl.when(lax.div(i, sets) == s)
        def _():
            rounded = [s_refs[s][f].astype(jnp.bfloat16) for f in range(own)]
            o_ref[...] += lax.dot_general(
                jnp.concatenate(rounded, axis=1),
                l_ref[...],
                (((0,), (0,)), ((), ())),
                preferred_element_type=jnp.float32,
            )


def around(parts, steps, low, sets):
    return lambda i, m: lax.rem(m[0] + lax.div(i, sets), parts) * steps + low + lax.rem(i, sets)


def project(me, low, factors, pieces, total):
    own, size, cols = pieces[0].shape
    parts = len(pieces)
    pairs, naux = factors.shape
    quarter = pairs // parts
    tile = tile_of(quarter)
    if tile is None:
        for s, x in enumerate(pieces):
            rows = lax.dynamic_slice_in_dim(
                factors, lax.rem(me + s, parts) * quarter, quarter, 0
            )
            total = total + jnp.einsum(
                "pa,fpc->fca", rows, x.astype(jnp.bfloat16), preferred_element_type=jnp.float32
            ).reshape(total.shape)
        return total
    sets = size // tile
    at = around(parts, quarter // tile, low, sets)
    stay = lambda s: lambda i, m: (0, jnp.clip(i - s * sets, 0, sets - 1), 0)
    return pl.pallas_call(
        functools.partial(project_kernel, parts, sets),
        out_shape=jax.ShapeDtypeStruct(total.shape, jnp.float32),
        grid_spec=pltpu.PrefetchScalarGridSpec(
            num_scalar_prefetch=1,
            grid=(parts * sets,),
            in_specs=[pl.BlockSpec((tile, naux), lambda i, m: (at(i, m), 0))]
            + [pl.BlockSpec((own, tile, cols), stay(s)) for s in range(parts)]
            + [resident(total)],
            out_specs=pl.BlockSpec(total.shape, lambda i, m: (0, 0)),
        ),
        compiler_params=pltpu.CompilerParams(vmem_limit_bytes=40 << 20),
        cost_estimate=pl.CostEstimate(
            flops=2 * own * parts * size * cols * naux,
            bytes_accessed=8 * own * parts * size * cols,
            transcendentals=0,
        ),
    )(me.reshape(1), factors, *pieces, total)


def again_kernel(own, l_ref, wt_ref, p_ref, x_ref, o_ref):
    cols = p_ref.shape[0] // own

    @pl.when(pl.program_id(0) == 0)
    def _():
        o_ref[...] = x_ref[...]

    wide = lax.dot_general(
        p_ref[...], l_ref[...], (((1,), (1,)), ((), ())), preferred_element_type=jnp.float32
    )
    wide = [
        (wide[f * cols : (f + 1) * cols] * wt_ref[f : f + 1, :]).astype(jnp.bfloat16)
        for f in range(own)
    ]
    o_ref[...] += lax.dot_general(
        jnp.concatenate(wide, axis=0),
        l_ref[...],
        (((1,), (0,)), ((), ())),
        preferred_element_type=jnp.float32,
    )


def again(factors, pair_weight, projected, kept):
    pairs, naux = factors.shape
    own = pair_weight.shape[0]
    tile = wide_tile(pairs)
    return pl.pallas_call(
        functools.partial(again_kernel, own),
        out_shape=jax.ShapeDtypeStruct(kept.shape, jnp.float32),
        grid=(pairs // tile,),
        in_specs=[
            pl.BlockSpec((tile, naux), lambda i: (i, 0)),
            pl.BlockSpec((own, tile), lambda i: (0, i)),
            resident(projected),
            resident(kept),
        ],
        out_specs=pl.BlockSpec(kept.shape, lambda i: (0, 0)),
        compiler_params=pltpu.CompilerParams(vmem_limit_bytes=40 << 20),
        cost_estimate=pl.CostEstimate(
            flops=4 * kept.size * pairs, bytes_accessed=2 * factors.size, transcendentals=0
        ),
    )(factors, pair_weight, projected, kept)


class Stream:
    def __init__(self, refs, buffer, sems):
        tile = buffer.shape[2]
        refs = [
            ref.at[:, n : n + tile, :] for ref in refs for n in range(0, ref.shape[1], tile)
        ]
        self.refs, self.buffer, self.sems = refs, buffer, sems
        self.step = pl.program_id(0)
        self.slot = lax.rem(self.step, 2)

    def copy(self, n):
        return pltpu.make_async_copy(self.refs[n], self.buffer.at[n % 2], self.sems.at[n % 2])

    def ahead(self):
        @pl.when(self.step == 0)
        def _():
            self.copy(0).start()

        for n in range(1, len(self.refs)):

            @pl.when(self.step == n - 1)
            def _():
                self.copy(n).start()

    def here(self):
        pltpu.make_async_copy(
            self.refs[0], self.buffer.at[self.slot], self.sems.at[self.slot]
        ).wait()
        return self.buffer.at[self.slot]


def stream_scratch(own, tile, cols):
    return [VMEM((2, own, tile, cols), jnp.float32), pltpu.SemaphoreType.DMA((2,))]


ANYWHERE = pl.BlockSpec(memory_space=pl.ANY)


def amplitude_kernel(pieces, me_ref, l_ref, wt_ref, p_ref, *rest):
    refs, (a_ref, buffer, sems) = rest[:pieces], rest[pieces:]
    own, tile, cols = a_ref.shape
    stream = Stream(refs, buffer, sems)
    stream.ahead()
    wide = rows_times(p_ref, l_ref)
    here = stream.here()
    for f in range(own):
        scaled = wide[f * cols : (f + 1) * cols] * wt_ref[f : f + 1, :]
        for k in range(0, tile, LANES):
            lanes = slice(k, k + LANES)
            a_ref[f, lanes, :] = here[f, lanes, :] + scaled[:, lanes].T


def amplitude(me, factors, pair_weight, near, sources):
    own, _, cols = sources[0][0].shape
    parts = len(sources[0])
    pairs, naux = factors.shape
    quarter = pairs // parts
    size = tile_of(quarter)
    if size is None:
        wide = jnp.einsum("ja,pa->jp", near, factors, preferred_element_type=jnp.float32)
        wide = jnp.transpose(wide.reshape(own, cols, pairs), (0, 2, 1))
        result = wide * pair_weight[:, :, None]
        for s in range(parts):
            at = lax.rem(me + s, parts) * quarter
            part_of = lax.dynamic_slice_in_dim(result, at, quarter, 1) + sources[0][s]
            result = lax.dynamic_update_slice_in_dim(result, part_of, at, 1)
        return result
    steps = quarter // size
    pieces = [x for group in sources for x in group]
    at = lambda i, m: lax.rem(m[0] + lax.rem(i, parts), parts) * steps + lax.div(i, parts)
    return pl.pallas_call(
        functools.partial(amplitude_kernel, len(pieces)),
        out_shape=jax.ShapeDtypeStruct((own, pairs, cols), jnp.float32),
        grid_spec=pltpu.PrefetchScalarGridSpec(
            num_scalar_prefetch=1,
            grid=(parts * steps,),
            in_specs=[
                pl.BlockSpec((size, naux), lambda i, m: (at(i, m), 0)),
                pl.BlockSpec((own, size), lambda i, m: (0, at(i, m))),
                resident(near),
            ]
            + [ANYWHERE] * len(pieces),
            out_specs=pl.BlockSpec((own, size, cols), lambda i, m: (0, at(i, m), 0)),
            scratch_shapes=stream_scratch(own, size, cols),
        ),
        compiler_params=pltpu.CompilerParams(vmem_limit_bytes=20 << 20),
        cost_estimate=pl.CostEstimate(
            flops=2 * own * pairs * cols * naux,
            bytes_accessed=8 * own * pairs * cols,
            transcendentals=0,
        ),
    )(me.reshape(1), factors, pair_weight, near, *pieces)


def final_kernel(nf, parts, held_outs, me_ref, l_ref, k_ref, wt_ref, coef_ref, p_ref, far_ref, *rest):
    b_refs, rest = rest[:parts], rest[parts + held_outs :]
    new_ref, table, held, mid, buffer, sems = rest
    own, _, cols = new_ref.shape
    stream = Stream(b_refs, buffer, sems)
    stream.ahead()
    table[...] = dot_exact(coef_ref[...], k_ref[...])
    for w in range(own):
        rows = slice(w * nf, (w + 1) * nf)
        table[rows, :] = table[rows, :] * wt_ref[...]
    spread(l_ref, p_ref, far_ref, held)
    here = stream.here()

    @pl.loop(0, table.shape[1] // LANES)
    def _(block):
        lanes = part(block, 0, LANES)

        @pl.loop(0, cols // WIDE)
        def _(i):
            rows = part(i, 0, WIDE)
            got = mix(table, lanes, own, nf, lambda v: held[part(i, v * cols, WIDE), lanes])
            for w in range(own):
                mid[w, rows, :] = got[w]

        for w in range(own):
            new_ref[w, lanes, :] = here[w, lanes, :] + mid[w].T


def final(me, low, factors, kernels, weights, coef, near, far, base, outs):
    own, span, cols = base[0].shape
    parts = len(base)
    nf = weights.shape[0]
    pairs, naux = factors.shape
    quarter = pairs // parts
    tile = tile_of(quarter)
    if tile is None:
        wide = jnp.einsum(
            "ja,pa->jp",
            jnp.concatenate([near, far]),
            factors,
            preferred_element_type=jnp.float32,
        )
        wide = jnp.transpose(wide.reshape(nf, cols, pairs), (0, 2, 1)) * weights[:, :, None]
        table = jnp.einsum("jt,tp->jp", coef, kernels, precision=EXACT).reshape(own, nf, pairs)
        new = jnp.einsum("wvp,vpc->wpc", table, wide, precision=EXACT)
        for s in range(parts):
            at = lax.rem(me + s, parts) * quarter
            part_of = lax.dynamic_slice_in_dim(new, at, quarter, 1) + base[s]
            new = lax.dynamic_update_slice_in_dim(new, part_of, at, 1)
        return [new]
    size = tile
    sets = span // size
    at = around(parts, quarter // size, low, sets)
    result = pl.pallas_call(
        functools.partial(final_kernel, nf, parts, len(outs)),
        out_shape=jax.ShapeDtypeStruct((own, pairs, cols), jnp.float32),
        grid_spec=pltpu.PrefetchScalarGridSpec(
            num_scalar_prefetch=1,
            grid=(parts * sets,),
            in_specs=[
                pl.BlockSpec((size, naux), lambda i, m: (at(i, m), 0)),
                pl.BlockSpec((nf, size), lambda i, m: (0, at(i, m))),
                pl.BlockSpec((nf, size), lambda i, m: (0, at(i, m))),
                resident(coef),
                resident(near),
                resident(far),
            ]
            + [ANYWHERE] * (parts + len(outs)),
            out_specs=pl.BlockSpec((own, size, cols), lambda i, m: (0, at(i, m), 0)),
            scratch_shapes=[
                VMEM((own * nf, size), jnp.float32),
                VMEM((nf * cols, size), jnp.float32),
                VMEM((own, cols, LANES), jnp.float32),
            ]
            + stream_scratch(own, size, cols),
        ),
        input_output_aliases={7 + parts + n: n for n in range(len(outs))},
        compiler_params=pltpu.CompilerParams(vmem_limit_bytes=26 << 20),
        cost_estimate=pl.CostEstimate(
            flops=2 * nf * parts * span * cols * naux,
            bytes_accessed=8 * own * parts * span * cols,
            transcendentals=0,
        ),
    )(me.reshape(1), factors, kernels, weights, coef, near, far, *base, *outs)
    return [result]


class Plane:
    def __init__(self, chips):
        self.chips = chips
        me = lax.axis_index("fac")
        self.core = lax.rem(me, 2)
        self.chip = lax.div(me, 2)
        self.pal = {"fac": me + 1 - 2 * self.core}
        self.started = []

    def on(self, d):
        return lax.rem(self.chip + d + self.chips, self.chips)

    def at(self, d):
        return {"fac": self.on(d) * 2 + self.core}

    def chip_at(self, chip):
        return {"fac": chip * 2 + self.core}

    def greet(self):
        barrier = pltpu.get_barrier_semaphore()
        for other in [self.pal] + [self.at(d) for d in range(1, self.chips)]:
            pl.semaphore_signal(barrier, inc=1, device_id=other, device_id_type=MESH)
        pl.semaphore_wait(barrier, self.chips)

    def send(self, src, dst, sems, at, to):
        copy = pltpu.make_async_remote_copy(
            src_ref=src,
            dst_ref=dst,
            send_sem=sems[0].at[at],
            recv_sem=sems[1].at[at],
            device_id=to,
            device_id_type=MESH,
        )
        copy.start()
        self.started.append(copy)
        return copy

    def end(self):
        for copy in self.started:
            copy.wait_send()


def reduced(plane, x_ref, near, red, land, mine, near_sems, red_sems):
    chips, chip, core, pal = plane.chips, plane.chip, plane.core, plane.pal
    nears = {}
    for d in list(range(1, chips)) + [0]:
        nears[d] = plane.send(x_ref.at[plane.on(d), 1 - core], near.at[d], near_sems, d, pal)
    block = mine.shape[0]
    step = min(block, 16)
    reds = []
    for d in range(1, chips):
        nears[d].wait_recv()
        for r in range(0, block, step):
            rows = slice(r, r + step)
            red[d, rows, :] = (x_ref[plane.on(d), core, rows, :] + near[d, rows, :]).astype(
                red.dtype
            )
        reds.append(plane.send(red.at[d], land.at[d], red_sems, d, plane.at(d)))
    nears[0].wait_recv()
    for copy in reds:
        copy.wait_recv()
    for r in range(0, block, step):
        rows = slice(r, r + step)
        total = x_ref[chip, core, rows, :] + near[0, rows, :]
        for d in range(1, chips):
            total = total + land[d, rows, :].astype(jnp.float32)
        mine[rows, :] = total.astype(mine.dtype)


def reduce_kernel(chips, x_ref, o_ref, near, red, land, *sems):
    plane = Plane(chips)
    plane.greet()
    reduced(plane, x_ref, near, red, land, o_ref, sems[0:2], sems[2:4])
    plane.end()


def sum_kernel(chips, x_ref, o_ref, near, red, land, mine, joined, *sems):
    plane = Plane(chips)
    chip, core = plane.chip, plane.core
    plane.greet()
    reduced(plane, x_ref, near, red, land, mine, sems[0:2], sems[2:4])
    here = joined.at[chip, core]
    keep = pltpu.make_async_copy(mine, here, sems[8])
    keep.start()
    keep.wait()
    wides = [plane.send(here, here, sems[4:6], d, plane.at(d)) for d in range(1, chips)]
    pairs = [plane.send(here, here, sems[6:8], 0, plane.pal)]
    for d, copy in enumerate(wides, 1):
        copy.wait_recv()
        there = joined.at[plane.on(-d), core]
        pairs.append(plane.send(there, there, sems[6:8], d, plane.pal))
    for copy in pairs:
        copy.wait_recv()
    plane.end()
    for c in range(chips):
        o_ref[c] = joined[c]


def gather_kernel(chips, parts, *refs):
    x_ref, o_ref, joined, *sems = refs
    x_refs = [x_ref.at[s] for s in range(parts)]
    kept = sems[4]
    plane = Plane(chips)
    chip, core, pal = plane.chip, plane.core, plane.pal
    plane.greet()
    wide_sems, pair_sems = sems[0:2], sems[2:4]
    pairs = []
    copies = []
    for s in range(parts):
        copies.append(
            pltpu.make_async_copy(x_refs[s], joined.at[s, chip, core], kept.at[s])
        )
        copies[-1].start()
    square = chips == 4
    column, row = lax.rem(chip, 2), lax.div(chip, 2)
    across, along = chip + 1 - 2 * column, chip + 2 - 4 * row
    corner = along + 1 - 2 * column
    wides = []
    for s in range(parts):
        src, dst = x_refs[s], joined.at[s, chip, core]
        if square:
            for n, to in enumerate((across, along)):
                copy = plane.send(src, dst, wide_sems, s * chips + n, plane.chip_at(to))
                wides.append((s, n, copy))
        else:
            for d in range(1, chips):
                copy = plane.send(src, dst, wide_sems, s * chips + d, plane.at(d))
                wides.append((s, d, copy))
    for s in range(parts):
        pairs.append(
            plane.send(x_refs[s], joined.at[s, chip, core], pair_sems, s * chips, pal)
        )
    late = []
    for s, d, copy in wides:
        copy.wait_recv()
        chip_from = (across, along)[d] if square else plane.on(-d)
        there = joined.at[s, chip_from, core]
        if square and d == s % 2:
            other = (along, across)[d]
            turned = plane.send(there, there, wide_sems, s * chips + 2, plane.chip_at(other))
            late.append((s, turned))
        at = s * chips + (1 + d if square else d)
        pairs.append(plane.send(there, there, pair_sems, at, pal))
    for s, copy in late:
        copy.wait_recv()
        there = joined.at[s, corner, core]
        pairs.append(plane.send(there, there, pair_sems, s * chips + 3, pal))
    for copy in pairs:
        copy.wait_recv()
    plane.end()
    for copy in copies:
        copy.wait()
    for s in range(parts):
        for c in range(chips):
            o_ref[s, c] = joined[s, c]


def dmas(count, pairs):
    return [pltpu.SemaphoreType.DMA((count,))] * (2 * pairs)


def reach_params(cid):
    return pltpu.CompilerParams(
        collective_id=cid, has_side_effects=True, vmem_limit_bytes=24 << 20
    )


def reach_cost(size):
    return pl.CostEstimate(flops=40 * size, bytes_accessed=40 * size, transcendentals=0)


WHOLE = pl.BlockSpec(memory_space=VMEM)


def summed(x, all_blocks):
    n = lax.axis_size("fac")
    chips = n // 2
    rows, width = x.shape
    block = rows // n
    flat = (chips, 2, block, width)
    landing = [
        VMEM((chips, block, width), jnp.float32),
        VMEM((chips, block, width), jnp.bfloat16),
        VMEM((chips, block, width), jnp.bfloat16),
    ]
    if not all_blocks:
        return pl.pallas_call(
            functools.partial(reduce_kernel, chips),
            out_shape=jax.ShapeDtypeStruct((block, width), jnp.bfloat16),
            in_specs=[WHOLE],
            out_specs=WHOLE,
            scratch_shapes=landing + dmas(chips, 2),
            compiler_params=reach_params(1),
            cost_estimate=reach_cost(x.size // 2),
        )(x.reshape(flat))
    result = pl.pallas_call(
        functools.partial(sum_kernel, chips),
        out_shape=jax.ShapeDtypeStruct(flat, jnp.bfloat16),
        in_specs=[WHOLE],
        out_specs=WHOLE,
        scratch_shapes=landing
        + [VMEM((block, width), jnp.bfloat16), VMEM(flat, jnp.bfloat16)]
        + dmas(chips, 4)
        + [pltpu.SemaphoreType.DMA],
        compiler_params=reach_params(0),
        cost_estimate=reach_cost(x.size),
    )(x.reshape(flat))
    return result.reshape(rows, width)


def gathered_over(blocks):
    n = lax.axis_size("fac")
    chips = n // 2
    parts, block, width = blocks.shape
    flat = (parts, chips, 2, block, width)
    result = pl.pallas_call(
        functools.partial(gather_kernel, chips, parts),
        out_shape=jax.ShapeDtypeStruct(flat, jnp.bfloat16),
        in_specs=[WHOLE],
        out_specs=WHOLE,
        scratch_shapes=[VMEM(flat, jnp.bfloat16)]
        + dmas(parts * chips, 2)
        + [pltpu.SemaphoreType.DMA((parts,))],
        compiler_params=reach_params(2 if parts == 1 else 3),
        cost_estimate=reach_cost(block * width * parts * 8),
    )(blocks)
    return result.reshape(parts * n * block, width)


def shards(right_side, factors, pair_weight, second_order, forward, backward):
    own, pairs, cols = right_side.shape
    nf = forward.shape[0]
    naux = factors.shape[1]
    parts = nf // own
    quarter = pairs // parts
    me = lax.axis_index("freq")

    def shift(x, by):
        if by == 0:
            return x
        return lax.ppermute(x, "freq", [(i, (i + by) % parts) for i in range(parts)])

    order = jnp.concatenate(
        [lax.rem(me - s + parts, parts) * own + jnp.arange(own) for s in range(parts)]
    )
    pick = jax.nn.one_hot(order, nf, dtype=jnp.float32)
    ahead = jnp.einsum("ts,sv,wv->tw", pick, forward, pick, precision=EXACT)
    back = jnp.einsum("ws,st,vt->wv", pick, backward, pick, precision=EXACT)
    coef = (back[:, None, :] * ahead.T[None, :, :]).reshape(nf * nf, nf)
    reach = jnp.max(
        jnp.sum(
            jnp.einsum("wt,tv->wv", jnp.abs(backward), jnp.abs(forward), precision=EXACT), axis=1
        )
    )

    both = jnp.stack([pair_weight, second_order])
    fine = HALF_TOP / 2.0
    slim = (both * fine).astype(jnp.float16)
    came = [shift(slim, s) for s in range(1, parts)]
    tables = [both] + [x.astype(jnp.float32) * (1.0 / fine) for x in came]
    weights, kernels = [jnp.concatenate([x[n] for x in tables]) for n in range(2)]
    size = tile_of(quarter) or quarter
    chunks = quarter // size
    early = max(chunks - 1, 1)
    groups = [(0, early)] + ([(early, chunks)] if early < chunks else [])
    calls = [(k, k + 1) for k in range(chunks)]
    tie = lax.optimization_barrier
    up = 8192.0

    def sliced(x, s, low, high):
        at = lax.rem(me + s, parts) * quarter + low * size
        return lax.dynamic_slice_in_dim(x, at, (high - low) * size, 1)

    def leaving(low, high):
        return [(sliced(right_side, s, low, high) * up).astype(jnp.float16) for s in range(1, parts)]

    def passed(blocks, back):
        return [
            shift(b, parts - 1 - s if back else s + 1) for s, b in enumerate(blocks)
        ]

    def first_projection():
        return jnp.einsum(
            "pa,fpc->fca",
            factors,
            right_side.astype(jnp.bfloat16),
            preferred_element_type=jnp.float32,
        ).reshape(own * cols, naux)

    def ladder(kept):
        total = kept
        for _ in range(INNER - 1):
            mine = summed(total, True)
            total = again(factors, pair_weight, mine, kept)
        block = summed(total, False)
        far = [shift(block, s) for s in range(1, parts)]
        return gathered_over(block[None]), far

    def joined(blocks):
        blocks = jnp.stack(blocks)
        return gathered_over(blocks)

    leaves = []
    for g in groups:
        leaves.append(leaving(*g))
    right_late, leaves[-1] = tie((right_side, leaves[-1]))
    came = [passed(x, False) for x in leaves]
    near, blocks = ladder(first_projection())
    far = joined(blocks)

    def tall(x):
        return jnp.max(jnp.sum(jnp.abs(x.astype(jnp.float32)), axis=1))

    height = jnp.maximum(tall(near), tall(far))
    u_top = jnp.maximum(1.01 * reach * (R_MAX + W_MAX * L_MAX * height), 1e-30)
    v_top = jnp.maximum(1.01 * reach * (R_MAX + u_top), 1e-30)

    def halved(blocks, top):
        return [(b * (HALF_TOP / top)).astype(jnp.float16) for b in blocks[1:]]

    def added(first, rest, top, group):
        rest = [b.astype(jnp.float32) * (top / HALF_TOP) for b in rest]
        return [sliced(right_late, s, *group) + b for s, b in enumerate([first] + rest)]

    placed = []
    for group, moved in zip(groups, came):
        moved = [m.astype(jnp.float32) * (1.0 / up) for m in moved]
        placed += [(moved, k - group[0]) for k in range(*group)]
    us, vs, inward, halves = [], [], [], []
    for low, high in calls:
        u, v = quarter_pass(
            me,
            low,
            factors,
            kernels,
            weights,
            coef,
            near,
            far,
            right_side,
            placed[low:high],
        )
        inward.append(passed(halved(u, u_top), True))
        halves.append(halved(v, v_top))
        us.append(u)
        vs.append(v)
    sources = []
    total = jnp.zeros((own * cols, naux), jnp.float32)
    for n, group in enumerate(calls):
        if n:
            inward[n], total = tie((inward[n], total))
        sources.append(added(us[n][0], inward[n], u_top, group))
        total = project(me, group[0], factors, sources[n], total)

    out, total = tie((halves[0], total))
    back = [passed(out, True)]
    near, blocks = ladder(total)
    for n in range(1, len(calls)):
        back.append(passed(halves[n], True))
    amplitudes = amplitude(me, factors, pair_weight, near, sources)
    far = joined(blocks)
    outs = []
    for n, group in enumerate(calls):
        back[n], outs = tie((back[n], outs))
        base = added(vs[n][0], back[n], v_top, group)
        outs = final(
            me,
            group[0],
            factors,
            kernels,
            weights,
            coef[: own * nf],
            near,
            far,
            base,
            outs,
        )
    return amplitudes, outs[0]


def solution(mesh):
    return jax.shard_map(
        shards,
        mesh=mesh,
        in_specs=(
            P("freq", "fac", None),
            P("fac", None),
            P("freq", "fac"),
            P("freq", "fac"),
            P(),
            P(),
        ),
        out_specs=(P("freq", "fac", None), P("freq", "fac", None)),
        check_vma=False,
    )
```

```python
import functools

import jax
import jax.numpy as jnp
from jax import lax
from jax.experimental import pallas as pl
from jax.experimental.pallas import tpu as pltpu
from jax.sharding import PartitionSpec as P


INNER = 2
LANES = 128
MESH = pl.DeviceIdType.MESH
CHUNK = 16
EXACT = lax.Precision.HIGHEST
R_MAX = 6.0
W_MAX = 2.0
L_MAX = 0.03125
HALF_TOP = 32768.0
VMEM = pltpu.VMEM


def tile_of(pairs):
    for blocks in (3, 4, 2, 1):
        if pairs % (blocks * LANES) == 0:
            return blocks * LANES
    return None


def wide_tile(pairs):
    for blocks in (6, 4, 3, 2, 1):
        if pairs % (blocks * LANES) == 0:
            return blocks * LANES
    return None


def mix(table, lanes, outs, count, term):
    totals = [None] * outs
    for v in range(count):
        value = term(v)
        for w in range(outs):
            row = w * count + v
            product = table[row : row + 1, lanes] * value
            totals[w] = product if totals[w] is None else totals[w] + product
    return totals


def part(i, base, chunk):
    return pl.ds(pl.multiple_of(base + i * chunk, chunk), chunk)


def rows_times(p_ref, l_ref):
    return lax.dot_general(
        p_ref[...], l_ref[...], (((1,), (1,)), ((), ())), preferred_element_type=jnp.float32
    )


def dot_exact(a, b):
    return lax.dot_general(
        a, b, (((1,), (0,)), ((), ())), precision=EXACT, preferred_element_type=jnp.float32
    )


def resident(x):
    return pl.BlockSpec(x.shape, lambda i, *_: (0,) * x.ndim, pipeline_mode=pl.Buffered(1))


def quarter_kernel(nf, parts, sets, me_ref, l_ref, k_ref, wt_ref, coef_ref, p_ref, *rest):
    own_ref, rest = rest[0], rest[1:]
    came, rest = rest[: sets * (parts - 1)], rest[sets * (parts - 1) :]
    u_refs, rest = rest[:parts], rest[parts:]
    v_refs, (table, held, turned, mid, far) = rest[:parts], rest[parts:]
    own = nf // parts
    cols = own_ref.shape[2]
    table[...] = dot_exact(coef_ref[...], k_ref[...])
    held[...] = rows_times(p_ref, l_ref)

    @pl.loop(0, table.shape[1] // LANES)
    def _(block):
        lanes = part(block, 0, LANES)
        for v in range(own):
            turned[v] = own_ref[v, lanes, :].T
        for j in range(sets):

            @pl.when(pl.program_id(0) == j)
            def _():
                for v in range(own, nf):
                    turned[v] = came[j * (parts - 1) + v // own - 1][v % own, lanes, :].T

        @pl.loop(0, cols // CHUNK)
        def _(i):
            rows = part(i, 0, CHUNK)
            got = mix(
                table,
                lanes,
                nf,
                nf,
                lambda v: turned[v, rows, :]
                + wt_ref[v : v + 1, lanes] * held[part(i, v * cols, CHUNK), lanes],
            )
            for w in range(nf):
                mid[w, rows, :] = got[w]
                turned[w, rows, :] = turned[w, rows, :] + got[w]
            got = mix(table, lanes, nf, nf, lambda v: turned[v, rows, :])
            for w in range(nf):
                far[w, rows, :] = got[w]

        for w in range(nf):
            u_refs[w // own][w % own, lanes, :] = mid[w].T
            v_refs[w // own][w % own, lanes, :] = far[w].T


def quarter_pass(me, low, factors, kernels, weights, coef, gathered, right_side, moved):
    own, pairs, cols = right_side.shape
    nf = weights.shape[0]
    parts = nf // own
    quarter = pairs // parts
    naux = factors.shape[1]
    tile = tile_of(quarter)
    sets = len(moved)
    if tile is None:
        cut = lambda x, axis: lax.dynamic_slice_in_dim(x, me * quarter, quarter, axis)
        here = jnp.concatenate([cut(right_side, 1)] + moved[0][0])
        table = jnp.einsum("jt,tp->jp", coef, cut(kernels, 1), precision=EXACT)
        table = table.reshape(nf, nf, quarter)
        wide = jnp.einsum(
            "ja,pa->jp",
            gathered,
            cut(factors, 0),
            preferred_element_type=jnp.float32,
        )
        wide = jnp.transpose(wide.reshape(nf, cols, quarter), (0, 2, 1))
        wide = here + cut(weights, 1)[:, :, None] * wide
        u = jnp.einsum("wvp,vpc->wpc", table, wide, precision=EXACT)
        v = jnp.einsum("wvp,vpc->wpc", table, here + u, precision=EXACT)
        return (
            [u[s * own : (s + 1) * own] for s in range(parts)],
            [v[s * own : (s + 1) * own] for s in range(parts)],
        )
    steps = quarter // tile
    at = lambda i, m: m[0] * steps + low + i
    here = lambda n: pl.BlockSpec((own, tile, cols), lambda i, m: (0, n, 0))
    piece = pl.BlockSpec((own, tile, cols), lambda i, m: (0, i, 0))
    shape = jax.ShapeDtypeStruct((own, sets * tile, cols), jnp.float32)
    out = pl.pallas_call(
        functools.partial(quarter_kernel, nf, parts, sets),
        out_shape=[shape] * (2 * parts),
        grid_spec=pltpu.PrefetchScalarGridSpec(
            num_scalar_prefetch=1,
            grid=(sets,),
            in_specs=[
                pl.BlockSpec((tile, naux), lambda i, m: (at(i, m), 0)),
                pl.BlockSpec((nf, tile), lambda i, m: (0, at(i, m))),
                pl.BlockSpec((nf, tile), lambda i, m: (0, at(i, m))),
                resident(coef),
                resident(gathered),
                pl.BlockSpec((own, tile, cols), lambda i, m: (0, at(i, m), 0)),
            ]
            + [here(n) for _, n in moved for _ in range(parts - 1)],
            out_specs=[piece] * (2 * parts),
            scratch_shapes=[
                VMEM((nf * nf, tile), jnp.float32),
                VMEM((nf * cols, tile), jnp.float32),
            ]
            + [VMEM((nf, cols, LANES), jnp.float32)] * 3,
        ),
        compiler_params=pltpu.CompilerParams(vmem_limit_bytes=54 << 20),
        cost_estimate=pl.CostEstimate(
            flops=2 * nf * sets * tile * cols * (naux + 32 * nf),
            bytes_accessed=16 * nf * sets * tile * cols,
            transcendentals=0,
        ),
    )(
        me.reshape(1),
        factors,
        kernels,
        weights,
        coef,
        gathered,
        right_side,
        *[x for xs, _ in moved for x in xs],
    )
    return list(out[:parts]), list(out[parts:])


def project_kernel(parts, sets, me_ref, l_ref, *rest):
    s_refs, (x_ref, o_ref) = rest[:parts], rest[parts:]
    own, _, _ = s_refs[0].shape
    i = pl.program_id(0)

    @pl.when(i == 0)
    def _():
        o_ref[...] = x_ref[...]

    for s in range(parts):

        @pl.when(lax.div(i, sets) == s)
        def _():
            rounded = [s_refs[s][f].astype(jnp.bfloat16) for f in range(own)]
            o_ref[...] += lax.dot_general(
                jnp.concatenate(rounded, axis=1),
                l_ref[...],
                (((0,), (0,)), ((), ())),
                preferred_element_type=jnp.float32,
            )


def around(parts, steps, low, sets):
    return lambda i, m: lax.rem(m[0] + lax.div(i, sets), parts) * steps + low + lax.rem(i, sets)


def project(me, low, factors, pieces, total):
    own, size, cols = pieces[0].shape
    parts = len(pieces)
    pairs, naux = factors.shape
    quarter = pairs // parts
    tile = tile_of(quarter)
    if tile is None:
        for s, x in enumerate(pieces):
            rows = lax.dynamic_slice_in_dim(
                factors, lax.rem(me + s, parts) * quarter, quarter, 0
            )
            total = total + jnp.einsum(
                "pa,fpc->fca", rows, x.astype(jnp.bfloat16), preferred_element_type=jnp.float32
            ).reshape(total.shape)
        return total
    sets = size // tile
    at = around(parts, quarter // tile, low, sets)
    stay = lambda s: lambda i, m: (0, jnp.clip(i - s * sets, 0, sets - 1), 0)
    return pl.pallas_call(
        functools.partial(project_kernel, parts, sets),
        out_shape=jax.ShapeDtypeStruct(total.shape, jnp.float32),
        grid_spec=pltpu.PrefetchScalarGridSpec(
            num_scalar_prefetch=1,
            grid=(parts * sets,),
            in_specs=[pl.BlockSpec((tile, naux), lambda i, m: (at(i, m), 0))]
            + [pl.BlockSpec((own, tile, cols), stay(s)) for s in range(parts)]
            + [resident(total)],
            out_specs=pl.BlockSpec(total.shape, lambda i, m: (0, 0)),
        ),
        compiler_params=pltpu.CompilerParams(vmem_limit_bytes=40 << 20),
        cost_estimate=pl.CostEstimate(
            flops=2 * own * parts * size * cols * naux,
            bytes_accessed=8 * own * parts * size * cols,
            transcendentals=0,
        ),
    )(me.reshape(1), factors, *pieces, total)


def again_kernel(own, l_ref, wt_ref, p_ref, x_ref, o_ref):
    cols = p_ref.shape[0] // own

    @pl.when(pl.program_id(0) == 0)
    def _():
        o_ref[...] = x_ref[...]

    wide = lax.dot_general(
        p_ref[...], l_ref[...], (((1,), (1,)), ((), ())), preferred_element_type=jnp.float32
    )
    wide = [
        (wide[f * cols : (f + 1) * cols] * wt_ref[f : f + 1, :]).astype(jnp.bfloat16)
        for f in range(own)
    ]
    o_ref[...] += lax.dot_general(
        jnp.concatenate(wide, axis=0),
        l_ref[...],
        (((1,), (0,)), ((), ())),
        preferred_element_type=jnp.float32,
    )


def again(factors, pair_weight, projected, kept):
    pairs, naux = factors.shape
    own = pair_weight.shape[0]
    tile = wide_tile(pairs)
    return pl.pallas_call(
        functools.partial(again_kernel, own),
        out_shape=jax.ShapeDtypeStruct(kept.shape, jnp.float32),
        grid=(pairs // tile,),
        in_specs=[
            pl.BlockSpec((tile, naux), lambda i: (i, 0)),
            pl.BlockSpec((own, tile), lambda i: (0, i)),
            resident(projected),
            resident(kept),
        ],
        out_specs=pl.BlockSpec(kept.shape, lambda i: (0, 0)),
        compiler_params=pltpu.CompilerParams(vmem_limit_bytes=40 << 20),
        cost_estimate=pl.CostEstimate(
            flops=4 * kept.size * pairs, bytes_accessed=2 * factors.size, transcendentals=0
        ),
    )(factors, pair_weight, projected, kept)


class Stream:
    def __init__(self, refs, buffer, sems, step):
        tile = buffer.shape[2]
        refs = [
            ref.at[:, n : n + tile, :] for ref in refs for n in range(0, ref.shape[1], tile)
        ]
        self.refs, self.buffer, self.sems = refs, buffer, sems
        self.step = step
        self.slot = lax.rem(step + 2, 2)

    def copy(self, n):
        return pltpu.make_async_copy(self.refs[n], self.buffer.at[n % 2], self.sems.at[n % 2])

    def ahead(self):
        @pl.when(pl.program_id(0) == 0)
        def _():
            self.copy(0).start()

        for n in range(1, len(self.refs)):

            @pl.when(self.step == n - 1)
            def _():
                self.copy(n).start()

    def here(self):
        pltpu.make_async_copy(
            self.refs[0], self.buffer.at[self.slot], self.sems.at[self.slot]
        ).wait()
        return self.buffer.at[self.slot]


def stream_scratch(own, tile, cols):
    return [VMEM((2, own, tile, cols), jnp.float32), pltpu.SemaphoreType.DMA((2,))]


ANYWHERE = pl.BlockSpec(memory_space=pl.ANY)


def amplitude_kernel(pieces, me_ref, l_ref, wt_ref, p_ref, *rest):
    refs, (a_ref, buffer, sems) = rest[:pieces], rest[pieces:]
    own, tile, cols = a_ref.shape
    stream = Stream(refs, buffer, sems, pl.program_id(0))
    stream.ahead()
    wide = rows_times(p_ref, l_ref)
    here = stream.here()
    for f in range(own):
        scaled = wide[f * cols : (f + 1) * cols] * wt_ref[f : f + 1, :]
        for k in range(0, tile, LANES):
            lanes = slice(k, k + LANES)
            a_ref[f, lanes, :] = here[f, lanes, :] + scaled[:, lanes].T


def amplitude(me, factors, pair_weight, near, sources):
    own, _, cols = sources[0][0].shape
    parts = len(sources[0])
    pairs, naux = factors.shape
    quarter = pairs // parts
    size = tile_of(quarter)
    if size is None:
        wide = jnp.einsum("ja,pa->jp", near, factors, preferred_element_type=jnp.float32)
        wide = jnp.transpose(wide.reshape(own, cols, pairs), (0, 2, 1))
        result = wide * pair_weight[:, :, None]
        for s in range(parts):
            at = lax.rem(me + s, parts) * quarter
            part_of = lax.dynamic_slice_in_dim(result, at, quarter, 1) + sources[0][s]
            result = lax.dynamic_update_slice_in_dim(result, part_of, at, 1)
        return result
    steps = quarter // size
    pieces = [x for group in sources for x in group]
    at = lambda i, m: lax.rem(m[0] + lax.rem(i, parts), parts) * steps + lax.div(i, parts)
    return pl.pallas_call(
        functools.partial(amplitude_kernel, len(pieces)),
        out_shape=jax.ShapeDtypeStruct((own, pairs, cols), jnp.float32),
        grid_spec=pltpu.PrefetchScalarGridSpec(
            num_scalar_prefetch=1,
            grid=(parts * steps,),
            in_specs=[
                pl.BlockSpec((size, naux), lambda i, m: (at(i, m), 0)),
                pl.BlockSpec((own, size), lambda i, m: (0, at(i, m))),
                resident(near),
            ]
            + [ANYWHERE] * len(pieces),
            out_specs=pl.BlockSpec((own, size, cols), lambda i, m: (0, at(i, m), 0)),
            scratch_shapes=stream_scratch(own, size, cols),
        ),
        compiler_params=pltpu.CompilerParams(vmem_limit_bytes=20 << 20),
        cost_estimate=pl.CostEstimate(
            flops=2 * own * pairs * cols * naux,
            bytes_accessed=8 * own * pairs * cols,
            transcendentals=0,
        ),
    )(me.reshape(1), factors, pair_weight, near, *pieces)


def final_kernel(nf, held_outs, me_ref, l_ref, k_ref, wt_ref, coef_ref, p_ref, *rest):
    parts = len(rest) - held_outs - 6
    b_refs, rest = rest[:parts], rest[parts + held_outs :]
    new_ref, table, held, mid, buffer, sems = rest
    own, tile, cols = new_ref.shape
    i = pl.program_id(0)
    count = pl.num_programs(0) - 1
    stream = Stream(b_refs, buffer, sems, i - 1)
    turns = cols // CHUNK
    share = p_ref.shape[0] // turns
    ahead, now = lax.rem(i, 2), lax.rem(i + 1, 2)

    def multiply(r):
        rows = part(r, 0, share)
        held[ahead, rows, :] = lax.dot_general(
            p_ref[rows, :], l_ref[...], (((1,), (1,)), ((), ())), preferred_element_type=jnp.float32
        )

    def blend(r):
        rows = part(r, 0, CHUNK)
        for k in range(0, tile, LANES):
            lanes = slice(k, k + LANES)
            got = mix(table, lanes, own, nf, lambda v: held[now, part(r, v * cols, CHUNK), lanes])
            for w in range(own):
                mid[w, rows, lanes] = got[w]

    stream.ahead()

    @pl.when(i > 0)
    def _():
        table[...] = dot_exact(coef_ref[...], k_ref[...])
        for w in range(own):
            rows = slice(w * nf, (w + 1) * nf)
            table[rows, :] = table[rows, :] * wt_ref[...]

    @pl.when(i == 0)
    def _():
        pl.loop(0, turns)(multiply)

    @pl.when((i > 0) & (i < count))
    def _():
        @pl.loop(0, turns)
        def _(r):
            blend(r)
            multiply(r)

    @pl.when(i == count)
    def _():
        pl.loop(0, turns)(blend)

    @pl.when(i > 0)
    def _():
        here = stream.here()
        for w in range(own):
            for k in range(0, tile, LANES):
                lanes = slice(k, k + LANES)
                new_ref[w, lanes, :] = here[w, lanes, :] + mid[w, :, lanes].T


def final(me, low, factors, kernels, weights, coef, gathered, base, outs):
    own, span, cols = base[0].shape
    parts = len(base)
    nf = weights.shape[0]
    pairs, naux = factors.shape
    quarter = pairs // parts
    tile = tile_of(quarter)
    if tile is None:
        wide = jnp.einsum(
            "ja,pa->jp",
            gathered,
            factors,
            preferred_element_type=jnp.float32,
        )
        wide = jnp.transpose(wide.reshape(nf, cols, pairs), (0, 2, 1)) * weights[:, :, None]
        table = jnp.einsum("jt,tp->jp", coef, kernels, precision=EXACT).reshape(own, nf, pairs)
        new = jnp.einsum("wvp,vpc->wpc", table, wide, precision=EXACT)
        for s in range(parts):
            at = lax.rem(me + s, parts) * quarter
            part_of = lax.dynamic_slice_in_dim(new, at, quarter, 1) + base[s]
            new = lax.dynamic_update_slice_in_dim(new, part_of, at, 1)
        return [new]
    size = tile
    sets = span // size
    at = around(parts, quarter // size, low, sets)
    count = parts * sets
    ahead = lambda i, m: at(jnp.minimum(i, count - 1), m)
    now = lambda i, m: at(jnp.maximum(i - 1, 0), m)
    result = pl.pallas_call(
        functools.partial(final_kernel, nf, len(outs)),
        out_shape=jax.ShapeDtypeStruct((own, pairs, cols), jnp.float32),
        grid_spec=pltpu.PrefetchScalarGridSpec(
            num_scalar_prefetch=1,
            grid=(count + 1,),
            in_specs=[
                pl.BlockSpec((size, naux), lambda i, m: (ahead(i, m), 0)),
                pl.BlockSpec((nf, size), lambda i, m: (0, now(i, m))),
                pl.BlockSpec((nf, size), lambda i, m: (0, now(i, m))),
                resident(coef),
                resident(gathered),
            ]
            + [ANYWHERE] * (parts + len(outs)),
            out_specs=pl.BlockSpec((own, size, cols), lambda i, m: (0, now(i, m), 0)),
            scratch_shapes=[
                VMEM((own * nf, size), jnp.float32),
                VMEM((2, nf * cols, size), jnp.float32),
                VMEM((own, cols, size), jnp.float32),
            ]
            + stream_scratch(own, size, cols),
        ),
        input_output_aliases={6 + parts + n: n for n in range(len(outs))},
        compiler_params=pltpu.CompilerParams(vmem_limit_bytes=30 << 20),
        cost_estimate=pl.CostEstimate(
            flops=2 * nf * parts * span * cols * naux,
            bytes_accessed=8 * own * parts * span * cols,
            transcendentals=0,
        ),
    )(me.reshape(1), factors, kernels, weights, coef, gathered, *base, *outs)
    return [result]


class Plane:
    def __init__(self, chips):
        self.chips = chips
        me = lax.axis_index("fac")
        self.core = lax.rem(me, 2)
        self.chip = lax.div(me, 2)
        self.pal = {"fac": me + 1 - 2 * self.core}
        self.started = []

    def on(self, d):
        return lax.rem(self.chip + d + self.chips, self.chips)

    def at(self, d):
        return {"fac": self.on(d) * 2 + self.core}

    def chip_at(self, chip):
        return {"fac": chip * 2 + self.core}

    def greet(self):
        barrier = pltpu.get_barrier_semaphore()
        for other in [self.pal] + [self.at(d) for d in range(1, self.chips)]:
            pl.semaphore_signal(barrier, inc=1, device_id=other, device_id_type=MESH)
        pl.semaphore_wait(barrier, self.chips)

    def send(self, src, dst, sems, at, to):
        copy = pltpu.make_async_remote_copy(
            src_ref=src,
            dst_ref=dst,
            send_sem=sems[0].at[at],
            recv_sem=sems[1].at[at],
            device_id=to,
            device_id_type=MESH,
        )
        copy.start()
        self.started.append(copy)
        return copy

    def end(self):
        for copy in self.started:
            copy.wait_send()


def reduced(plane, x_ref, near, red, land, mine, near_sems, red_sems):
    chips, chip, core, pal = plane.chips, plane.chip, plane.core, plane.pal
    nears = {}
    for d in list(range(1, chips)) + [0]:
        nears[d] = plane.send(x_ref.at[plane.on(d), 1 - core], near.at[d], near_sems, d, pal)
    block = mine.shape[0]
    step = min(block, 16)
    reds = []
    for d in range(1, chips):
        nears[d].wait_recv()
        for r in range(0, block, step):
            rows = slice(r, r + step)
            red[d, rows, :] = (x_ref[plane.on(d), core, rows, :] + near[d, rows, :]).astype(
                red.dtype
            )
        reds.append(plane.send(red.at[d], land.at[d], red_sems, d, plane.at(d)))
    nears[0].wait_recv()
    for copy in reds:
        copy.wait_recv()
    for r in range(0, block, step):
        rows = slice(r, r + step)
        total = x_ref[chip, core, rows, :] + near[0, rows, :]
        for d in range(1, chips):
            total = total + land[d, rows, :].astype(jnp.float32)
        mine[rows, :] = total.astype(mine.dtype)


def reduce_kernel(chips, x_ref, o_ref, near, red, land, *sems):
    plane = Plane(chips)
    plane.greet()
    reduced(plane, x_ref, near, red, land, o_ref, sems[0:2], sems[2:4])
    plane.end()


def sum_kernel(chips, x_ref, o_ref, near, red, land, mine, joined, *sems):
    plane = Plane(chips)
    chip, core = plane.chip, plane.core
    plane.greet()
    reduced(plane, x_ref, near, red, land, mine, sems[0:2], sems[2:4])
    here = joined.at[chip, core]
    keep = pltpu.make_async_copy(mine, here, sems[8])
    keep.start()
    keep.wait()
    wides = [plane.send(here, here, sems[4:6], d, plane.at(d)) for d in range(1, chips)]
    pairs = [plane.send(here, here, sems[6:8], 0, plane.pal)]
    for d, copy in enumerate(wides, 1):
        copy.wait_recv()
        there = joined.at[plane.on(-d), core]
        pairs.append(plane.send(there, there, sems[6:8], d, plane.pal))
    for copy in pairs:
        copy.wait_recv()
    plane.end()
    for c in range(chips):
        o_ref[c] = joined[c]


def gather_kernel(chips, parts, x_ref, *refs):
    near_ref = None
    if len(refs) > 8:
        near_ref, refs = refs[0], refs[1:]
    o_ref, top_ref, joined, *sems = refs
    skip = 0 if near_ref is None else 1
    x_refs = [x_ref.at[s] for s in range(parts)]
    kept = sems[4]
    plane = Plane(chips)
    chip, core, pal = plane.chip, plane.core, plane.pal
    plane.greet()
    wide_sems, pair_sems = sems[0:2], sems[2:4]
    pairs = []
    copies = []
    for s in range(parts):
        copies.append(
            pltpu.make_async_copy(x_refs[s], joined.at[s, chip, core], kept.at[s])
        )
        copies[-1].start()
    square = chips == 4
    column, row = lax.rem(chip, 2), lax.div(chip, 2)
    across, along = chip + 1 - 2 * column, chip + 2 - 4 * row
    corner = along + 1 - 2 * column
    wides = []
    for s in range(parts):
        src, dst = x_refs[s], joined.at[s, chip, core]
        if square:
            for n, to in enumerate((across, along)):
                copy = plane.send(src, dst, wide_sems, s * chips + n, plane.chip_at(to))
                wides.append((s, n, copy))
        else:
            for d in range(1, chips):
                copy = plane.send(src, dst, wide_sems, s * chips + d, plane.at(d))
                wides.append((s, d, copy))
    for s in range(parts):
        pairs.append(
            plane.send(x_refs[s], joined.at[s, chip, core], pair_sems, s * chips, pal)
        )
    late = []
    for s, d, copy in wides:
        copy.wait_recv()
        chip_from = (across, along)[d] if square else plane.on(-d)
        there = joined.at[s, chip_from, core]
        if square and d == s % 2:
            other = (along, across)[d]
            turned = plane.send(there, there, wide_sems, s * chips + 2, plane.chip_at(other))
            late.append((s, turned))
        at = s * chips + (1 + d if square else d)
        pairs.append(plane.send(there, there, pair_sems, at, pal))
    for s, copy in late:
        copy.wait_recv()
        there = joined.at[s, corner, core]
        pairs.append(plane.send(there, there, pair_sems, s * chips + 3, pal))
    for copy in pairs:
        copy.wait_recv()
    plane.end()
    for copy in copies:
        copy.wait()
    if skip:
        o_ref[0] = near_ref[...]
    top = jnp.zeros(top_ref.shape, jnp.float32)
    for s in range(parts):

        def fold(c, top):
            here = joined[s, c]
            o_ref[s + skip, c] = here
            here = jnp.abs(here.astype(jnp.float32))
            sums = here[..., :LANES]
            for k in range(LANES, here.shape[-1], LANES):
                sums = sums + here[..., k : k + LANES]
            return jnp.maximum(top, jnp.max(sums.reshape((-1,) + top.shape), axis=0))

        top = lax.fori_loop(0, chips, fold, top)
    top_ref[...] = top


def dmas(count, pairs):
    return [pltpu.SemaphoreType.DMA((count,))] * (2 * pairs)


def reach_params(cid):
    return pltpu.CompilerParams(
        collective_id=cid, has_side_effects=True, vmem_limit_bytes=24 << 20
    )


def reach_cost(size):
    return pl.CostEstimate(flops=40 * size, bytes_accessed=40 * size, transcendentals=0)


WHOLE = pl.BlockSpec(memory_space=VMEM)


def summed(x, all_blocks):
    n = lax.axis_size("fac")
    chips = n // 2
    rows, width = x.shape
    block = rows // n
    flat = (chips, 2, block, width)
    landing = [
        VMEM((chips, block, width), jnp.float32),
        VMEM((chips, block, width), jnp.bfloat16),
        VMEM((chips, block, width), jnp.bfloat16),
    ]
    if not all_blocks:
        return pl.pallas_call(
            functools.partial(reduce_kernel, chips),
            out_shape=jax.ShapeDtypeStruct((block, width), jnp.bfloat16),
            in_specs=[WHOLE],
            out_specs=WHOLE,
            scratch_shapes=landing + dmas(chips, 2),
            compiler_params=reach_params(1),
            cost_estimate=reach_cost(x.size // 2),
        )(x.reshape(flat))
    result = pl.pallas_call(
        functools.partial(sum_kernel, chips),
        out_shape=jax.ShapeDtypeStruct(flat, jnp.bfloat16),
        in_specs=[WHOLE],
        out_specs=WHOLE,
        scratch_shapes=landing
        + [VMEM((block, width), jnp.bfloat16), VMEM(flat, jnp.bfloat16)]
        + dmas(chips, 4)
        + [pltpu.SemaphoreType.DMA],
        compiler_params=reach_params(0),
        cost_estimate=reach_cost(x.size),
    )(x.reshape(flat))
    return result.reshape(rows, width)


def gathered_over(blocks, near=None):
    n = lax.axis_size("fac")
    chips = n // 2
    parts, block, width = blocks.shape
    flat = (chips, 2, block, width)
    result, top = pl.pallas_call(
        functools.partial(gather_kernel, chips, parts),
        out_shape=(
            jax.ShapeDtypeStruct((parts + (near is not None),) + flat, jnp.bfloat16),
            jax.ShapeDtypeStruct((8, LANES), jnp.float32),
        ),
        in_specs=[WHOLE] * (1 if near is None else 2),
        out_specs=(WHOLE, WHOLE),
        scratch_shapes=[VMEM((parts,) + flat, jnp.bfloat16)]
        + dmas(parts * chips, 2)
        + [pltpu.SemaphoreType.DMA((parts,))],
        compiler_params=reach_params(2 if parts == 1 else 3),
        cost_estimate=reach_cost(block * width * parts * 8),
    )(blocks, *(() if near is None else (near.reshape(flat),)))
    return result.reshape(-1, width), top


def shards(right_side, factors, pair_weight, second_order, forward, backward):
    own, pairs, cols = right_side.shape
    nf = forward.shape[0]
    naux = factors.shape[1]
    parts = nf // own
    quarter = pairs // parts
    me = lax.axis_index("freq")

    def shift(x, by):
        if by == 0:
            return x
        return lax.ppermute(x, "freq", [(i, (i + by) % parts) for i in range(parts)])

    order = jnp.concatenate(
        [lax.rem(me - s + parts, parts) * own + jnp.arange(own) for s in range(parts)]
    )
    pick = jax.nn.one_hot(order, nf, dtype=jnp.float32)
    ahead = jnp.einsum("ts,sv,wv->tw", pick, forward, pick, precision=EXACT)
    back = jnp.einsum("ws,st,vt->wv", pick, backward, pick, precision=EXACT)
    coef = (back[:, None, :] * ahead.T[None, :, :]).reshape(nf * nf, nf)
    reach = jnp.max(
        jnp.sum(
            jnp.einsum("wt,tv->wv", jnp.abs(backward), jnp.abs(forward), precision=EXACT), axis=1
        )
    )

    both = jnp.stack([pair_weight, second_order])
    fine = HALF_TOP / 2.0
    slim = (both * fine).astype(jnp.float16)
    came = [shift(slim, s) for s in range(1, parts)]
    tables = [both] + [x.astype(jnp.float32) * (1.0 / fine) for x in came]
    weights, kernels = [jnp.concatenate([x[n] for x in tables]) for n in range(2)]
    size = tile_of(quarter) or quarter
    chunks = quarter // size
    early = max(chunks - 1, 1)
    groups = [(0, early)] + ([(early, chunks)] if early < chunks else [])
    calls = [(k, k + 1) for k in range(chunks)]
    tie = lax.optimization_barrier
    up = 8192.0

    def sliced(x, s, low, high):
        at = lax.rem(me + s, parts) * quarter + low * size
        return lax.dynamic_slice_in_dim(x, at, (high - low) * size, 1)

    def leaving(low, high):
        return [(sliced(right_side, s, low, high) * up).astype(jnp.float16) for s in range(1, parts)]

    def passed(blocks, back):
        return [
            shift(b, parts - 1 - s if back else s + 1) for s, b in enumerate(blocks)
        ]

    def first_projection():
        return jnp.einsum(
            "pa,fpc->fca",
            factors,
            right_side.astype(jnp.bfloat16),
            preferred_element_type=jnp.float32,
        ).reshape(own * cols, naux)

    def ladder(kept):
        total = kept
        for _ in range(INNER - 1):
            mine = summed(total, True)
            total = again(factors, pair_weight, mine, kept)
        block = summed(total, False)
        far = [shift(block, s) for s in range(1, parts)]
        return *gathered_over(block[None]), far

    def joined(blocks, near):
        blocks = jnp.stack(blocks)
        return gathered_over(blocks, near)

    leaves = []
    for g in groups:
        leaves.append(leaving(*g))
    right_late, leaves[-1] = tie((right_side, leaves[-1]))
    came = [passed(x, False) for x in leaves]
    near, near_top, blocks = ladder(first_projection())
    gathered, far_top = joined(blocks, near)
    height = jnp.sum(jnp.max(jnp.maximum(near_top, far_top), axis=0))
    u_top = jnp.maximum(1.01 * reach * (R_MAX + W_MAX * L_MAX * height), 1e-30)
    v_top = jnp.maximum(1.01 * reach * (R_MAX + u_top), 1e-30)

    def halved(blocks, top):
        return [(b * (HALF_TOP / top)).astype(jnp.float16) for b in blocks[1:]]

    def added(first, rest, top, group):
        rest = [b.astype(jnp.float32) * (top / HALF_TOP) for b in rest]
        return [sliced(right_late, s, *group) + b for s, b in enumerate([first] + rest)]

    placed = []
    for group, moved in zip(groups, came):
        moved = [m.astype(jnp.float32) * (1.0 / up) for m in moved]
        placed += [(moved, k - group[0]) for k in range(*group)]
    us, vs, inward, halves = [], [], [], []
    for low, high in calls:
        u, v = quarter_pass(
            me,
            low,
            factors,
            kernels,
            weights,
            coef,
            gathered,
            right_side,
            placed[low:high],
        )
        inward.append(passed(halved(u, u_top), True))
        halves.append(halved(v, v_top))
        us.append(u)
        vs.append(v)
    sources = []
    total = jnp.zeros((own * cols, naux), jnp.float32)
    for n, group in enumerate(calls):
        if n:
            inward[n], total = tie((inward[n], total))
        sources.append(added(us[n][0], inward[n], u_top, group))
        total = project(me, group[0], factors, sources[n], total)

    out, total = tie((halves[0], total))
    back = [passed(out, True)]
    near, _, blocks = ladder(total)
    for n in range(1, len(calls)):
        back.append(passed(halves[n], True))
    amplitudes = amplitude(me, factors, pair_weight, near, sources)
    gathered, _ = joined(blocks, near)
    outs = []
    for n, group in enumerate(calls):
        back[n], outs = tie((back[n], outs))
        base = added(vs[n][0], back[n], v_top, group)
        outs = final(
            me,
            group[0],
            factors,
            kernels,
            weights,
            coef[: own * nf],
            gathered,
            base,
            outs,
        )
    return amplitudes, outs[0]


def solution(mesh):
    return jax.shard_map(
        shards,
        mesh=mesh,
        in_specs=(
            P("freq", "fac", None),
            P("fac", None),
            P("freq", "fac"),
            P("freq", "fac"),
            P(),
            P(),
        ),
        out_specs=(P("freq", "fac", None), P("freq", "fac", None)),
        check_vma=False,
    )
```

```python
import functools

import jax
import jax.numpy as jnp
from jax import lax
from jax.experimental import pallas as pl
from jax.experimental.pallas import tpu as pltpu
from jax.sharding import PartitionSpec as P


INNER = 2
LANES = 128
MESH = pl.DeviceIdType.MESH
CHUNK = 16
WIDE = 32
EXACT = lax.Precision.HIGHEST
R_MAX = 6.0
W_MAX = 2.0
L_MAX = 0.03125
HALF_TOP = 32768.0
VMEM = pltpu.VMEM


def tile_of(pairs):
    for blocks in (3, 4, 2, 1):
        if pairs % (blocks * LANES) == 0:
            return blocks * LANES
    return None


def wide_tile(pairs):
    for blocks in (6, 4, 3, 2, 1):
        if pairs % (blocks * LANES) == 0:
            return blocks * LANES
    return None


def mix(table, lanes, outs, count, term):
    totals = [None] * outs
    for v in range(count):
        value = term(v)
        for w in range(outs):
            row = w * count + v
            product = table[row : row + 1, lanes] * value
            totals[w] = product if totals[w] is None else totals[w] + product
    return totals


def part(i, base, chunk):
    return pl.ds(pl.multiple_of(base + i * chunk, chunk), chunk)


def rows_times(p_ref, l_ref):
    return lax.dot_general(
        p_ref[...], l_ref[...], (((1,), (1,)), ((), ())), preferred_element_type=jnp.float32
    )


def dot_exact(a, b):
    return lax.dot_general(
        a, b, (((1,), (0,)), ((), ())), precision=EXACT, preferred_element_type=jnp.float32
    )


def resident(x):
    return pl.BlockSpec(x.shape, lambda i, *_: (0,) * x.ndim, pipeline_mode=pl.Buffered(1))


def quarter_kernel(nf, parts, sets, me_ref, l_ref, k_ref, wt_ref, coef_ref, p_ref, *rest):
    own_ref, rest = rest[0], rest[1:]
    came, rest = rest[: sets * (parts - 1)], rest[sets * (parts - 1) :]
    u_refs, rest = rest[:parts], rest[parts:]
    v_refs, (table, held, turned, mid, far) = rest[:parts], rest[parts:]
    own = nf // parts
    cols = own_ref.shape[2]
    table[...] = dot_exact(coef_ref[...], k_ref[...])
    held[...] = rows_times(p_ref, l_ref)

    @pl.loop(0, table.shape[1] // LANES)
    def _(block):
        lanes = part(block, 0, LANES)
        for v in range(own):
            turned[v] = own_ref[v, lanes, :].T
        for j in range(sets):

            @pl.when(pl.program_id(0) == j)
            def _():
                for v in range(own, nf):
                    turned[v] = came[j * (parts - 1) + v // own - 1][v % own, lanes, :].T

        @pl.loop(0, cols // CHUNK)
        def _(i):
            rows = part(i, 0, CHUNK)
            got = mix(
                table,
                lanes,
                nf,
                nf,
                lambda v: turned[v, rows, :]
                + wt_ref[v : v + 1, lanes] * held[part(i, v * cols, CHUNK), lanes],
            )
            for w in range(nf):
                mid[w, rows, :] = got[w]
                turned[w, rows, :] = turned[w, rows, :] + got[w]
            got = mix(table, lanes, nf, nf, lambda v: turned[v, rows, :])
            for w in range(nf):
                far[w, rows, :] = got[w]

        for w in range(nf):
            u_refs[w // own][w % own, lanes, :] = mid[w].T
            v_refs[w // own][w % own, lanes, :] = far[w].T


def quarter_pass(me, low, factors, kernels, weights, coef, gathered, right_side, moved):
    own, pairs, cols = right_side.shape
    nf = weights.shape[0]
    parts = nf // own
    quarter = pairs // parts
    naux = factors.shape[1]
    tile = tile_of(quarter)
    sets = len(moved)
    if tile is None:
        cut = lambda x, axis: lax.dynamic_slice_in_dim(x, me * quarter, quarter, axis)
        here = jnp.concatenate([cut(right_side, 1)] + moved[0][0])
        table = jnp.einsum("jt,tp->jp", coef, cut(kernels, 1), precision=EXACT)
        table = table.reshape(nf, nf, quarter)
        wide = jnp.einsum(
            "ja,pa->jp",
            gathered,
            cut(factors, 0),
            preferred_element_type=jnp.float32,
        )
        wide = jnp.transpose(wide.reshape(nf, cols, quarter), (0, 2, 1))
        wide = here + cut(weights, 1)[:, :, None] * wide
        u = jnp.einsum("wvp,vpc->wpc", table, wide, precision=EXACT)
        v = jnp.einsum("wvp,vpc->wpc", table, here + u, precision=EXACT)
        return (
            [u[s * own : (s + 1) * own] for s in range(parts)],
            [v[s * own : (s + 1) * own] for s in range(parts)],
        )
    steps = quarter // tile
    at = lambda i, m: m[0] * steps + low + i
    here = lambda n: pl.BlockSpec((own, tile, cols), lambda i, m: (0, n, 0))
    piece = pl.BlockSpec((own, tile, cols), lambda i, m: (0, i, 0))
    shape = jax.ShapeDtypeStruct((own, sets * tile, cols), jnp.float32)
    out = pl.pallas_call(
        functools.partial(quarter_kernel, nf, parts, sets),
        out_shape=[shape] * parts + [pltpu.HBM(shape.shape, shape.dtype)] * parts,
        grid_spec=pltpu.PrefetchScalarGridSpec(
            num_scalar_prefetch=1,
            grid=(sets,),
            in_specs=[
                pl.BlockSpec((tile, naux), lambda i, m: (at(i, m), 0)),
                pl.BlockSpec((nf, tile), lambda i, m: (0, at(i, m))),
                pl.BlockSpec((nf, tile), lambda i, m: (0, at(i, m))),
                resident(coef),
                resident(gathered),
                pl.BlockSpec((own, tile, cols), lambda i, m: (0, at(i, m), 0)),
            ]
            + [here(n) for _, n in moved for _ in range(parts - 1)],
            out_specs=[piece] * (2 * parts),
            scratch_shapes=[
                VMEM((nf * nf, tile), jnp.float32),
                VMEM((nf * cols, tile), jnp.float32),
            ]
            + [VMEM((nf, cols, LANES), jnp.float32)] * 3,
        ),
        compiler_params=pltpu.CompilerParams(vmem_limit_bytes=36 << 20),
        cost_estimate=pl.CostEstimate(
            flops=2 * nf * sets * tile * cols * (naux + 32 * nf),
            bytes_accessed=16 * nf * sets * tile * cols,
            transcendentals=0,
        ),
    )(
        me.reshape(1),
        factors,
        kernels,
        weights,
        coef,
        gathered,
        right_side,
        *[x for xs, _ in moved for x in xs],
    )
    return list(out[:parts]), list(out[parts:])


def project_kernel(parts, sets, me_ref, l_ref, *rest):
    s_refs, (x_ref, o_ref) = rest[:parts], rest[parts:]
    own, _, _ = s_refs[0].shape
    i = pl.program_id(0)

    @pl.when(i == 0)
    def _():
        o_ref[...] = x_ref[...]

    for s in range(parts):

        @pl.when(lax.div(i, sets) == s)
        def _():
            rounded = [s_refs[s][f].astype(jnp.bfloat16) for f in range(own)]
            o_ref[...] += lax.dot_general(
                jnp.concatenate(rounded, axis=1),
                l_ref[...],
                (((0,), (0,)), ((), ())),
                preferred_element_type=jnp.float32,
            )


def around(parts, steps, low, sets):
    return lambda i, m: lax.rem(m[0] + lax.div(i, sets), parts) * steps + low + lax.rem(i, sets)


def project(me, low, factors, pieces, total):
    own, size, cols = pieces[0].shape
    parts = len(pieces)
    pairs, naux = factors.shape
    quarter = pairs // parts
    tile = tile_of(quarter)
    if tile is None:
        for s, x in enumerate(pieces):
            rows = lax.dynamic_slice_in_dim(
                factors, lax.rem(me + s, parts) * quarter, quarter, 0
            )
            total = total + jnp.einsum(
                "pa,fpc->fca", rows, x.astype(jnp.bfloat16), preferred_element_type=jnp.float32
            ).reshape(total.shape)
        return total
    sets = size // tile
    at = around(parts, quarter // tile, low, sets)
    stay = lambda s: lambda i, m: (0, jnp.clip(i - s * sets, 0, sets - 1), 0)
    return pl.pallas_call(
        functools.partial(project_kernel, parts, sets),
        out_shape=jax.ShapeDtypeStruct(total.shape, jnp.float32),
        grid_spec=pltpu.PrefetchScalarGridSpec(
            num_scalar_prefetch=1,
            grid=(parts * sets,),
            in_specs=[pl.BlockSpec((tile, naux), lambda i, m: (at(i, m), 0))]
            + [pl.BlockSpec((own, tile, cols), stay(s)) for s in range(parts)]
            + [resident(total)],
            out_specs=pl.BlockSpec(total.shape, lambda i, m: (0, 0)),
        ),
        compiler_params=pltpu.CompilerParams(vmem_limit_bytes=40 << 20),
        cost_estimate=pl.CostEstimate(
            flops=2 * own * parts * size * cols * naux,
            bytes_accessed=8 * own * parts * size * cols,
            transcendentals=0,
        ),
    )(me.reshape(1), factors, *pieces, total)


def again_kernel(own, l_ref, wt_ref, p_ref, x_ref, o_ref):
    cols = p_ref.shape[0] // own

    @pl.when(pl.program_id(0) == 0)
    def _():
        o_ref[...] = x_ref[...]

    wide = lax.dot_general(
        p_ref[...], l_ref[...], (((1,), (1,)), ((), ())), preferred_element_type=jnp.float32
    )
    wide = [
        (wide[f * cols : (f + 1) * cols] * wt_ref[f : f + 1, :]).astype(jnp.bfloat16)
        for f in range(own)
    ]
    o_ref[...] += lax.dot_general(
        jnp.concatenate(wide, axis=0),
        l_ref[...],
        (((1,), (0,)), ((), ())),
        preferred_element_type=jnp.float32,
    )


def again(factors, pair_weight, projected, kept):
    pairs, naux = factors.shape
    own = pair_weight.shape[0]
    tile = wide_tile(pairs)
    return pl.pallas_call(
        functools.partial(again_kernel, own),
        out_shape=jax.ShapeDtypeStruct(kept.shape, jnp.float32),
        grid=(pairs // tile,),
        in_specs=[
            pl.BlockSpec((tile, naux), lambda i: (i, 0)),
            pl.BlockSpec((own, tile), lambda i: (0, i)),
            resident(projected),
            resident(kept),
        ],
        out_specs=pl.BlockSpec(kept.shape, lambda i: (0, 0)),
        compiler_params=pltpu.CompilerParams(vmem_limit_bytes=40 << 20),
        cost_estimate=pl.CostEstimate(
            flops=4 * kept.size * pairs, bytes_accessed=2 * factors.size, transcendentals=0
        ),
    )(factors, pair_weight, projected, kept)


class Stream:
    def __init__(self, refs, buffer, sems, step):
        tile = buffer.shape[2]
        refs = [
            ref.at[:, n : n + tile, :] for ref in refs for n in range(0, ref.shape[1], tile)
        ]
        self.refs, self.buffer, self.sems = refs, buffer, sems
        self.step = step
        self.slot = lax.rem(step + 2, 2)

    def copy(self, n):
        return pltpu.make_async_copy(self.refs[n], self.buffer.at[n % 2], self.sems.at[n % 2])

    def ahead(self):
        @pl.when(pl.program_id(0) == 0)
        def _():
            self.copy(0).start()

        for n in range(1, len(self.refs)):

            @pl.when(self.step == n - 1)
            def _():
                self.copy(n).start()

    def here(self):
        pltpu.make_async_copy(
            self.refs[0], self.buffer.at[self.slot], self.sems.at[self.slot]
        ).wait()
        return self.buffer.at[self.slot]


def stream_scratch(own, tile, cols):
    return [VMEM((2, own, tile, cols), jnp.float32), pltpu.SemaphoreType.DMA((2,))]


ANYWHERE = pl.BlockSpec(memory_space=pl.ANY)


def amplitude_kernel(pieces, me_ref, l_ref, wt_ref, p_ref, *rest):
    refs, (a_ref, buffer, sems) = rest[:pieces], rest[pieces:]
    own, tile, cols = a_ref.shape
    stream = Stream(refs, buffer, sems, pl.program_id(0))
    stream.ahead()
    wide = rows_times(p_ref, l_ref)
    here = stream.here()
    for f in range(own):
        scaled = wide[f * cols : (f + 1) * cols] * wt_ref[f : f + 1, :]
        for k in range(0, tile, LANES):
            lanes = slice(k, k + LANES)
            a_ref[f, lanes, :] = here[f, lanes, :] + scaled[:, lanes].T


def amplitude(me, factors, pair_weight, near, sources):
    own, _, cols = sources[0][0].shape
    parts = len(sources[0])
    pairs, naux = factors.shape
    quarter = pairs // parts
    size = tile_of(quarter)
    if size is None:
        wide = jnp.einsum("ja,pa->jp", near, factors, preferred_element_type=jnp.float32)
        wide = jnp.transpose(wide.reshape(own, cols, pairs), (0, 2, 1))
        result = wide * pair_weight[:, :, None]
        for s in range(parts):
            at = lax.rem(me + s, parts) * quarter
            part_of = lax.dynamic_slice_in_dim(result, at, quarter, 1) + sources[0][s]
            result = lax.dynamic_update_slice_in_dim(result, part_of, at, 1)
        return result
    steps = quarter // size
    pieces = [x for group in sources for x in group]
    at = lambda i, m: lax.rem(m[0] + lax.rem(i, parts), parts) * steps + lax.div(i, parts)
    return pl.pallas_call(
        functools.partial(amplitude_kernel, len(pieces)),
        out_shape=jax.ShapeDtypeStruct((own, pairs, cols), jnp.float32),
        grid_spec=pltpu.PrefetchScalarGridSpec(
            num_scalar_prefetch=1,
            grid=(parts * steps,),
            in_specs=[
                pl.BlockSpec((size, naux), lambda i, m: (at(i, m), 0)),
                pl.BlockSpec((own, size), lambda i, m: (0, at(i, m))),
                resident(near),
            ]
            + [ANYWHERE] * len(pieces),
            out_specs=pl.BlockSpec((own, size, cols), lambda i, m: (0, at(i, m), 0)),
            scratch_shapes=stream_scratch(own, size, cols),
        ),
        compiler_params=pltpu.CompilerParams(vmem_limit_bytes=20 << 20),
        cost_estimate=pl.CostEstimate(
            flops=2 * own * pairs * cols * naux,
            bytes_accessed=8 * own * pairs * cols,
            transcendentals=0,
        ),
    )(me.reshape(1), factors, pair_weight, near, *pieces)


def final_kernel(nf, parts, held_outs, me_ref, l_ref, k_ref, wt_ref, coef_ref, p_ref, *rest):
    b_refs, rest = rest[:parts], rest[parts + held_outs :]
    new_ref, table, held, mid, buffer, sems = rest
    own, _, cols = new_ref.shape
    stream = Stream(b_refs, buffer, sems, pl.program_id(0))
    stream.ahead()
    table[...] = dot_exact(coef_ref[...], k_ref[...])
    for w in range(own):
        rows = slice(w * nf, (w + 1) * nf)
        table[rows, :] = table[rows, :] * wt_ref[...]
    held[...] = rows_times(p_ref, l_ref)
    here = stream.here()

    @pl.loop(0, table.shape[1] // LANES)
    def _(block):
        lanes = part(block, 0, LANES)

        @pl.loop(0, cols // WIDE)
        def _(i):
            rows = part(i, 0, WIDE)
            got = mix(table, lanes, own, nf, lambda v: held[part(i, v * cols, WIDE), lanes])
            for w in range(own):
                mid[w, rows, :] = got[w]

        for w in range(own):
            new_ref[w, lanes, :] = here[w, lanes, :] + mid[w].T


def final(me, low, factors, kernels, weights, coef, gathered, base, outs):
    own, span, cols = base[0].shape
    parts = len(base)
    nf = weights.shape[0]
    pairs, naux = factors.shape
    quarter = pairs // parts
    tile = tile_of(quarter)
    if tile is None:
        wide = jnp.einsum(
            "ja,pa->jp",
            gathered,
            factors,
            preferred_element_type=jnp.float32,
        )
        wide = jnp.transpose(wide.reshape(nf, cols, pairs), (0, 2, 1)) * weights[:, :, None]
        table = jnp.einsum("jt,tp->jp", coef, kernels, precision=EXACT).reshape(own, nf, pairs)
        new = jnp.einsum("wvp,vpc->wpc", table, wide, precision=EXACT)
        for s in range(parts):
            at = lax.rem(me + s, parts) * quarter
            part_of = lax.dynamic_slice_in_dim(new, at, quarter, 1) + base[s]
            new = lax.dynamic_update_slice_in_dim(new, part_of, at, 1)
        return [new]
    size = tile
    sets = span // size
    at = around(parts, quarter // size, low, sets)
    result = pl.pallas_call(
        functools.partial(final_kernel, nf, parts, len(outs)),
        out_shape=jax.ShapeDtypeStruct((own, pairs, cols), jnp.float32),
        grid_spec=pltpu.PrefetchScalarGridSpec(
            num_scalar_prefetch=1,
            grid=(parts * sets,),
            in_specs=[
                pl.BlockSpec((size, naux), lambda i, m: (at(i, m), 0)),
                pl.BlockSpec((nf, size), lambda i, m: (0, at(i, m))),
                pl.BlockSpec((nf, size), lambda i, m: (0, at(i, m))),
                resident(coef),
                resident(gathered),
            ]
            + [ANYWHERE] * (parts + len(outs)),
            out_specs=pl.BlockSpec((own, size, cols), lambda i, m: (0, at(i, m), 0)),
            scratch_shapes=[
                VMEM((own * nf, size), jnp.float32),
                VMEM((nf * cols, size), jnp.float32),
                VMEM((own, cols, LANES), jnp.float32),
            ]
            + stream_scratch(own, size, cols),
        ),
        input_output_aliases={6 + parts + n: n for n in range(len(outs))},
        compiler_params=pltpu.CompilerParams(vmem_limit_bytes=26 << 20),
        cost_estimate=pl.CostEstimate(
            flops=2 * nf * parts * span * cols * naux,
            bytes_accessed=8 * own * parts * span * cols,
            transcendentals=0,
        ),
    )(me.reshape(1), factors, kernels, weights, coef, gathered, *base, *outs)
    return [result]


class Plane:
    def __init__(self, chips):
        self.chips = chips
        me = lax.axis_index("fac")
        self.core = lax.rem(me, 2)
        self.chip = lax.div(me, 2)
        self.pal = {"fac": me + 1 - 2 * self.core}
        self.started = []

    def on(self, d):
        return lax.rem(self.chip + d + self.chips, self.chips)

    def at(self, d):
        return {"fac": self.on(d) * 2 + self.core}

    def chip_at(self, chip):
        return {"fac": chip * 2 + self.core}

    def greet(self):
        barrier = pltpu.get_barrier_semaphore()
        for other in [self.pal] + [self.at(d) for d in range(1, self.chips)]:
            pl.semaphore_signal(barrier, inc=1, device_id=other, device_id_type=MESH)
        pl.semaphore_wait(barrier, self.chips)

    def send(self, src, dst, sems, at, to):
        copy = pltpu.make_async_remote_copy(
            src_ref=src,
            dst_ref=dst,
            send_sem=sems[0].at[at],
            recv_sem=sems[1].at[at],
            device_id=to,
            device_id_type=MESH,
        )
        copy.start()
        self.started.append(copy)
        return copy

    def end(self):
        for copy in self.started:
            copy.wait_send()


def reduced(plane, x_ref, near, red, land, mine, near_sems, red_sems):
    chips, chip, core, pal = plane.chips, plane.chip, plane.core, plane.pal
    nears = {}
    for d in list(range(1, chips)) + [0]:
        nears[d] = plane.send(x_ref.at[plane.on(d), 1 - core], near.at[d], near_sems, d, pal)
    block = mine.shape[0]
    step = min(block, 16)
    reds = []
    for d in range(1, chips):
        nears[d].wait_recv()
        for r in range(0, block, step):
            rows = slice(r, r + step)
            red[d, rows, :] = (x_ref[plane.on(d), core, rows, :] + near[d, rows, :]).astype(
                red.dtype
            )
        reds.append(plane.send(red.at[d], land.at[d], red_sems, d, plane.at(d)))
    nears[0].wait_recv()
    for copy in reds:
        copy.wait_recv()
    for r in range(0, block, step):
        rows = slice(r, r + step)
        total = x_ref[chip, core, rows, :] + near[0, rows, :]
        for d in range(1, chips):
            total = total + land[d, rows, :].astype(jnp.float32)
        mine[rows, :] = total.astype(mine.dtype)


def reduce_kernel(chips, x_ref, o_ref, near, red, land, *sems):
    plane = Plane(chips)
    plane.greet()
    reduced(plane, x_ref, near, red, land, o_ref, sems[0:2], sems[2:4])
    plane.end()


def sum_kernel(chips, x_ref, o_ref, near, red, land, mine, joined, *sems):
    plane = Plane(chips)
    chip, core = plane.chip, plane.core
    plane.greet()
    reduced(plane, x_ref, near, red, land, mine, sems[0:2], sems[2:4])
    here = joined.at[chip, core]
    keep = pltpu.make_async_copy(mine, here, sems[8])
    keep.start()
    keep.wait()
    wides = [plane.send(here, here, sems[4:6], d, plane.at(d)) for d in range(1, chips)]
    pairs = [plane.send(here, here, sems[6:8], 0, plane.pal)]
    for d, copy in enumerate(wides, 1):
        copy.wait_recv()
        there = joined.at[plane.on(-d), core]
        pairs.append(plane.send(there, there, sems[6:8], d, plane.pal))
    for copy in pairs:
        copy.wait_recv()
    plane.end()
    for c in range(chips):
        o_ref[c] = joined[c]


def gather_kernel(chips, parts, x_ref, *refs):
    near_ref = None
    if len(refs) > 8:
        near_ref, refs = refs[0], refs[1:]
    o_ref, top_ref, joined, *sems = refs
    skip = 0 if near_ref is None else 1
    x_refs = [x_ref.at[s] for s in range(parts)]
    kept = sems[4]
    plane = Plane(chips)
    chip, core, pal = plane.chip, plane.core, plane.pal
    plane.greet()
    wide_sems, pair_sems = sems[0:2], sems[2:4]
    pairs = []
    copies = []
    for s in range(parts):
        copies.append(
            pltpu.make_async_copy(x_refs[s], joined.at[s, chip, core], kept.at[s])
        )
        copies[-1].start()
    square = chips == 4
    column, row = lax.rem(chip, 2), lax.div(chip, 2)
    across, along = chip + 1 - 2 * column, chip + 2 - 4 * row
    corner = along + 1 - 2 * column
    wides = []
    for s in range(parts):
        src, dst = x_refs[s], joined.at[s, chip, core]
        if square:
            for n, to in enumerate((across, along)):
                copy = plane.send(src, dst, wide_sems, s * chips + n, plane.chip_at(to))
                wides.append((s, n, copy))
        else:
            for d in range(1, chips):
                copy = plane.send(src, dst, wide_sems, s * chips + d, plane.at(d))
                wides.append((s, d, copy))
    for s in range(parts):
        pairs.append(
            plane.send(x_refs[s], joined.at[s, chip, core], pair_sems, s * chips, pal)
        )
    late = []
    for s, d, copy in wides:
        copy.wait_recv()
        chip_from = (across, along)[d] if square else plane.on(-d)
        there = joined.at[s, chip_from, core]
        if square and d == s % 2:
            other = (along, across)[d]
            turned = plane.send(there, there, wide_sems, s * chips + 2, plane.chip_at(other))
            late.append((s, turned))
        at = s * chips + (1 + d if square else d)
        pairs.append(plane.send(there, there, pair_sems, at, pal))
    for s, copy in late:
        copy.wait_recv()
        there = joined.at[s, corner, core]
        pairs.append(plane.send(there, there, pair_sems, s * chips + 3, pal))
    for copy in pairs:
        copy.wait_recv()
    plane.end()
    for copy in copies:
        copy.wait()
    if skip:
        o_ref[0] = near_ref[...]
    top = jnp.zeros(top_ref.shape, jnp.float32)
    for s in range(parts):

        def fold(c, top):
            here = joined[s, c]
            o_ref[s + skip, c] = here
            here = jnp.abs(here.astype(jnp.float32))
            sums = here[..., :LANES]
            for k in range(LANES, here.shape[-1], LANES):
                sums = sums + here[..., k : k + LANES]
            return jnp.maximum(top, jnp.max(sums.reshape((-1,) + top.shape), axis=0))

        top = lax.fori_loop(0, chips, fold, top)
    top_ref[...] = top


def dmas(count, pairs):
    return [pltpu.SemaphoreType.DMA((count,))] * (2 * pairs)


def reach_params(cid):
    return pltpu.CompilerParams(
        collective_id=cid, has_side_effects=True, vmem_limit_bytes=24 << 20
    )


def reach_cost(size):
    return pl.CostEstimate(flops=40 * size, bytes_accessed=40 * size, transcendentals=0)


WHOLE = pl.BlockSpec(memory_space=VMEM)


def summed(x, all_blocks):
    n = lax.axis_size("fac")
    chips = n // 2
    rows, width = x.shape
    block = rows // n
    flat = (chips, 2, block, width)
    landing = [
        VMEM((chips, block, width), jnp.float32),
        VMEM((chips, block, width), jnp.bfloat16),
        VMEM((chips, block, width), jnp.bfloat16),
    ]
    if not all_blocks:
        return pl.pallas_call(
            functools.partial(reduce_kernel, chips),
            out_shape=jax.ShapeDtypeStruct((block, width), jnp.bfloat16),
            in_specs=[WHOLE],
            out_specs=WHOLE,
            scratch_shapes=landing + dmas(chips, 2),
            compiler_params=reach_params(1),
            cost_estimate=reach_cost(x.size // 2),
        )(x.reshape(flat))
    result = pl.pallas_call(
        functools.partial(sum_kernel, chips),
        out_shape=jax.ShapeDtypeStruct(flat, jnp.bfloat16),
        in_specs=[WHOLE],
        out_specs=WHOLE,
        scratch_shapes=landing
        + [VMEM((block, width), jnp.bfloat16), VMEM(flat, jnp.bfloat16)]
        + dmas(chips, 4)
        + [pltpu.SemaphoreType.DMA],
        compiler_params=reach_params(0),
        cost_estimate=reach_cost(x.size),
    )(x.reshape(flat))
    return result.reshape(rows, width)


def gathered_over(blocks, near=None):
    n = lax.axis_size("fac")
    chips = n // 2
    parts, block, width = blocks.shape
    flat = (chips, 2, block, width)
    result, top = pl.pallas_call(
        functools.partial(gather_kernel, chips, parts),
        out_shape=(
            jax.ShapeDtypeStruct((parts + (near is not None),) + flat, jnp.bfloat16),
            jax.ShapeDtypeStruct((8, LANES), jnp.float32),
        ),
        in_specs=[WHOLE] * (1 if near is None else 2),
        out_specs=(WHOLE, WHOLE),
        scratch_shapes=[VMEM((parts,) + flat, jnp.bfloat16)]
        + dmas(parts * chips, 2)
        + [pltpu.SemaphoreType.DMA((parts,))],
        compiler_params=reach_params(2 if parts == 1 else 3),
        cost_estimate=reach_cost(block * width * parts * 8),
    )(blocks, *(() if near is None else (near.reshape(flat),)))
    return result.reshape(-1, width), top


def shards(right_side, factors, pair_weight, second_order, forward, backward):
    own, pairs, cols = right_side.shape
    nf = forward.shape[0]
    naux = factors.shape[1]
    parts = nf // own
    quarter = pairs // parts
    me = lax.axis_index("freq")

    def shift(x, by):
        if by == 0:
            return x
        return lax.ppermute(x, "freq", [(i, (i + by) % parts) for i in range(parts)])

    order = jnp.concatenate(
        [lax.rem(me - s + parts, parts) * own + jnp.arange(own) for s in range(parts)]
    )
    pick = jax.nn.one_hot(order, nf, dtype=jnp.float32)
    ahead = jnp.einsum("ts,sv,wv->tw", pick, forward, pick, precision=EXACT)
    back = jnp.einsum("ws,st,vt->wv", pick, backward, pick, precision=EXACT)
    coef = (back[:, None, :] * ahead.T[None, :, :]).reshape(nf * nf, nf)
    reach = jnp.max(
        jnp.sum(
            jnp.einsum("wt,tv->wv", jnp.abs(backward), jnp.abs(forward), precision=EXACT), axis=1
        )
    )

    both = jnp.stack([pair_weight, second_order])
    fine = HALF_TOP / 2.0
    slim = (both * fine).astype(jnp.float16)
    came = [shift(slim, s) for s in range(1, parts)]
    tables = [both] + [x.astype(jnp.float32) * (1.0 / fine) for x in came]
    weights, kernels = [jnp.concatenate([x[n] for x in tables]) for n in range(2)]
    size = tile_of(quarter) or quarter
    chunks = quarter // size
    early = max(chunks - 1, 1)
    groups = [(0, early)] + ([(early, chunks)] if early < chunks else [])
    calls = [(k, k + 1) for k in range(chunks)]
    tie = lax.optimization_barrier
    up = 8192.0

    def sliced(x, s, low, high):
        at = lax.rem(me + s, parts) * quarter + low * size
        return lax.dynamic_slice_in_dim(x, at, (high - low) * size, 1)

    def leaving(low, high):
        return [(sliced(right_side, s, low, high) * up).astype(jnp.float16) for s in range(1, parts)]

    def passed(blocks, back):
        return [
            shift(b, parts - 1 - s if back else s + 1) for s, b in enumerate(blocks)
        ]

    def first_projection():
        return jnp.einsum(
            "pa,fpc->fca",
            factors,
            right_side.astype(jnp.bfloat16),
            preferred_element_type=jnp.float32,
        ).reshape(own * cols, naux)

    def ladder(kept):
        total = kept
        for _ in range(INNER - 1):
            mine = summed(total, True)
            total = again(factors, pair_weight, mine, kept)
        block = summed(total, False)
        far = [shift(block, s) for s in range(1, parts)]
        return *gathered_over(block[None]), far

    def joined(blocks, near):
        blocks = jnp.stack(blocks)
        return gathered_over(blocks, near)

    leaves = []
    for g in groups:
        leaves.append(leaving(*g))
    right_late, leaves[-1] = tie((right_side, leaves[-1]))
    came = [passed(x, False) for x in leaves]
    near, near_top, blocks = ladder(first_projection())
    gathered, far_top = joined(blocks, near)
    height = jnp.sum(jnp.max(jnp.maximum(near_top, far_top), axis=0))
    u_top = jnp.maximum(1.01 * reach * (R_MAX + W_MAX * L_MAX * height), 1e-30)
    v_top = jnp.maximum(1.01 * reach * (R_MAX + u_top), 1e-30)

    def halved(blocks, top):
        return [(b * (HALF_TOP / top)).astype(jnp.float16) for b in blocks[1:]]

    def added(first, rest, top, group):
        rest = [b.astype(jnp.float32) * (top / HALF_TOP) for b in rest]
        return [sliced(right_late, s, *group) + b for s, b in enumerate([first] + rest)]

    placed = []
    for group, moved in zip(groups, came):
        moved = [m.astype(jnp.float32) * (1.0 / up) for m in moved]
        placed += [(moved, k - group[0]) for k in range(*group)]
    us, vs, inward, halves = [], [], [], []
    for low, high in calls:
        u, v = quarter_pass(
            me,
            low,
            factors,
            kernels,
            weights,
            coef,
            gathered,
            right_side,
            placed[low:high],
        )
        inward.append(passed(halved(u, u_top), True))
        halves.append(halved(v, v_top))
        us.append(u)
        vs.append(v)
    sources = []
    total = jnp.zeros((own * cols, naux), jnp.float32)
    for n, group in enumerate(calls):
        if n:
            inward[n], total = tie((inward[n], total))
        sources.append(added(us[n][0], inward[n], u_top, group))
        total = project(me, group[0], factors, sources[n], total)

    out, total = tie((halves[0], total))
    back = [passed(out, True)]
    near, _, blocks = ladder(total)
    for n in range(1, len(calls)):
        back.append(passed(halves[n], True))
    amplitudes = amplitude(me, factors, pair_weight, near, sources)
    gathered, _ = joined(blocks, near)
    outs = []
    for n, group in enumerate(calls):
        back[n], outs = tie((back[n], outs))
        base = added(vs[n][0], back[n], v_top, group)
        outs = final(
            me,
            group[0],
            factors,
            kernels,
            weights,
            coef[: own * nf],
            gathered,
            base,
            outs,
        )
    return amplitudes, outs[0]


def solution(mesh):
    return jax.shard_map(
        shards,
        mesh=mesh,
        in_specs=(
            P("freq", "fac", None),
            P("fac", None),
            P("freq", "fac"),
            P("freq", "fac"),
            P(),
            P(),
        ),
        out_specs=(P("freq", "fac", None), P("freq", "fac", None)),
        check_vma=False,
    )
```

```python
import functools

import jax
import jax.numpy as jnp
from jax import lax
from jax.experimental import pallas as pl
from jax.experimental.pallas import tpu as pltpu
from jax.sharding import PartitionSpec as P


INNER = 2
LANES = 128
MESH = pl.DeviceIdType.MESH
CHUNK = 16
WIDE = 32
EXACT = lax.Precision.HIGHEST
R_MAX = 6.0
W_MAX = 2.0
L_MAX = 0.03125
HALF_TOP = 32768.0
VMEM = pltpu.VMEM


def tile_of(pairs):
    for blocks in (3, 4, 2, 1):
        if pairs % (blocks * LANES) == 0:
            return blocks * LANES
    return None


def wide_tile(pairs):
    for blocks in (6, 4, 3, 2, 1):
        if pairs % (blocks * LANES) == 0:
            return blocks * LANES
    return None


def mix(table, lanes, outs, count, term):
    totals = [None] * outs
    for v in range(count):
        value = term(v)
        for w in range(outs):
            row = w * count + v
            product = table[row : row + 1, lanes] * value
            totals[w] = product if totals[w] is None else totals[w] + product
    return totals


def part(i, base, chunk):
    return pl.ds(pl.multiple_of(base + i * chunk, chunk), chunk)


def rows_times(p_ref, l_ref):
    return lax.dot_general(
        p_ref[...], l_ref[...], (((1,), (1,)), ((), ())), preferred_element_type=jnp.float32
    )


def dot_exact(a, b):
    return lax.dot_general(
        a, b, (((1,), (0,)), ((), ())), precision=EXACT, preferred_element_type=jnp.float32
    )


def resident(x):
    return pl.BlockSpec(x.shape, lambda i, *_: (0,) * x.ndim, pipeline_mode=pl.Buffered(1))


def quarter_kernel(nf, parts, sets, me_ref, l_ref, k_ref, wt_ref, coef_ref, p_ref, *rest):
    own_ref, rest = rest[0], rest[1:]
    came, rest = rest[: sets * (parts - 1)], rest[sets * (parts - 1) :]
    mine_u, far_u, mine_v, far_v, table, held, turned, mid, far = rest
    own = nf // parts
    cols = own_ref.shape[2]
    table[...] = dot_exact(coef_ref[...], k_ref[...])
    held[...] = rows_times(p_ref, l_ref)

    @pl.loop(0, table.shape[1] // LANES)
    def _(block):
        lanes = part(block, 0, LANES)
        for v in range(own):
            turned[v] = own_ref[v, lanes, :].T
        for j in range(sets):

            @pl.when(pl.program_id(0) == j)
            def _():
                for v in range(own, nf):
                    turned[v] = came[j * (parts - 1) + v // own - 1][v % own, lanes, :].T

        @pl.loop(0, cols // CHUNK)
        def _(i):
            rows = part(i, 0, CHUNK)
            got = mix(
                table,
                lanes,
                nf,
                nf,
                lambda v: turned[v, rows, :]
                + wt_ref[v : v + 1, lanes] * held[part(i, v * cols, CHUNK), lanes],
            )
            for w in range(nf):
                mid[w, rows, :] = got[w]
                turned[w, rows, :] = turned[w, rows, :] + got[w]
            got = mix(table, lanes, nf, nf, lambda v: turned[v, rows, :])
            for w in range(nf):
                far[w, rows, :] = got[w]

        for w in range(nf):
            u_ref, v_ref, row = (mine_u, mine_v, w) if w < own else (far_u, far_v, w - own)
            u_ref[row, lanes, :] = mid[w].T
            v_ref[row, lanes, :] = far[w].T


def quarter_pass(me, low, factors, kernels, weights, coef, gathered, right_side, moved):
    own, pairs, cols = right_side.shape
    nf = weights.shape[0]
    parts = nf // own
    quarter = pairs // parts
    naux = factors.shape[1]
    tile = tile_of(quarter)
    sets = len(moved)
    if tile is None:
        cut = lambda x, axis: lax.dynamic_slice_in_dim(x, me * quarter, quarter, axis)
        here = jnp.concatenate([cut(right_side, 1)] + moved[0][0])
        table = jnp.einsum("jt,tp->jp", coef, cut(kernels, 1), precision=EXACT)
        table = table.reshape(nf, nf, quarter)
        wide = jnp.einsum(
            "ja,pa->jp",
            gathered,
            cut(factors, 0),
            preferred_element_type=jnp.float32,
        )
        wide = jnp.transpose(wide.reshape(nf, cols, quarter), (0, 2, 1))
        wide = here + cut(weights, 1)[:, :, None] * wide
        u = jnp.einsum("wvp,vpc->wpc", table, wide, precision=EXACT)
        v = jnp.einsum("wvp,vpc->wpc", table, here + u, precision=EXACT)
        return u[:own], u[own:], v[:own], v[own:]
    steps = quarter // tile
    at = lambda i, m: m[0] * steps + low + i
    here = lambda n: pl.BlockSpec((own, tile, cols), lambda i, m: (0, n, 0))
    outs = [(rows, sets * tile, cols) for rows in (own, nf - own)]
    pieces = [pl.BlockSpec((x[0], tile, cols), lambda i, m: (0, i, 0)) for x in outs]
    return pl.pallas_call(
        functools.partial(quarter_kernel, nf, parts, sets),
        out_shape=[jax.ShapeDtypeStruct(x, jnp.float32) for x in outs]
        + [pltpu.HBM(x, jnp.float32) for x in outs],
        grid_spec=pltpu.PrefetchScalarGridSpec(
            num_scalar_prefetch=1,
            grid=(sets,),
            in_specs=[
                pl.BlockSpec((tile, naux), lambda i, m: (at(i, m), 0)),
                pl.BlockSpec((nf, tile), lambda i, m: (0, at(i, m))),
                pl.BlockSpec((nf, tile), lambda i, m: (0, at(i, m))),
                resident(coef),
                resident(gathered),
                pl.BlockSpec((own, tile, cols), lambda i, m: (0, at(i, m), 0)),
            ]
            + [here(n) for _, n in moved for _ in range(parts - 1)],
            out_specs=pieces * 2,
            scratch_shapes=[
                VMEM((nf * nf, tile), jnp.float32),
                VMEM((nf * cols, tile), jnp.float32),
            ]
            + [VMEM((nf, cols, LANES), jnp.float32)] * 3,
        ),
        compiler_params=pltpu.CompilerParams(vmem_limit_bytes=36 << 20),
        cost_estimate=pl.CostEstimate(
            flops=2 * nf * sets * tile * cols * (naux + 32 * nf),
            bytes_accessed=16 * nf * sets * tile * cols,
            transcendentals=0,
        ),
    )(
        me.reshape(1),
        factors,
        kernels,
        weights,
        coef,
        gathered,
        right_side,
        *[x for xs, _ in moved for x in xs],
    )


def project_kernel(parts, sets, me_ref, l_ref, *rest):
    s_refs, (x_ref, o_ref) = rest[:parts], rest[parts:]
    own, _, _ = s_refs[0].shape
    i = pl.program_id(0)

    @pl.when(i == 0)
    def _():
        o_ref[...] = x_ref[...]

    for s in range(parts):

        @pl.when(lax.div(i, sets) == s)
        def _():
            rounded = [s_refs[s][f].astype(jnp.bfloat16) for f in range(own)]
            o_ref[...] += lax.dot_general(
                jnp.concatenate(rounded, axis=1),
                l_ref[...],
                (((0,), (0,)), ((), ())),
                preferred_element_type=jnp.float32,
            )


def around(parts, steps, low, sets):
    return lambda i, m: lax.rem(m[0] + lax.div(i, sets), parts) * steps + low + lax.rem(i, sets)


def project(me, low, factors, pieces, total):
    own, size, cols = pieces[0].shape
    parts = len(pieces)
    pairs, naux = factors.shape
    quarter = pairs // parts
    tile = tile_of(quarter)
    if tile is None:
        for s, x in enumerate(pieces):
            rows = lax.dynamic_slice_in_dim(
                factors, lax.rem(me + s, parts) * quarter, quarter, 0
            )
            total = total + jnp.einsum(
                "pa,fpc->fca", rows, x.astype(jnp.bfloat16), preferred_element_type=jnp.float32
            ).reshape(total.shape)
        return total
    sets = size // tile
    at = around(parts, quarter // tile, low, sets)
    stay = lambda s: lambda i, m: (0, jnp.clip(i - s * sets, 0, sets - 1), 0)
    return pl.pallas_call(
        functools.partial(project_kernel, parts, sets),
        out_shape=jax.ShapeDtypeStruct(total.shape, jnp.float32),
        grid_spec=pltpu.PrefetchScalarGridSpec(
            num_scalar_prefetch=1,
            grid=(parts * sets,),
            in_specs=[pl.BlockSpec((tile, naux), lambda i, m: (at(i, m), 0))]
            + [pl.BlockSpec((own, tile, cols), stay(s)) for s in range(parts)]
            + [resident(total)],
            out_specs=pl.BlockSpec(total.shape, lambda i, m: (0, 0)),
        ),
        compiler_params=pltpu.CompilerParams(vmem_limit_bytes=40 << 20),
        cost_estimate=pl.CostEstimate(
            flops=2 * own * parts * size * cols * naux,
            bytes_accessed=8 * own * parts * size * cols,
            transcendentals=0,
        ),
    )(me.reshape(1), factors, *pieces, total)


def again_kernel(own, l_ref, wt_ref, p_ref, x_ref, o_ref):
    cols = p_ref.shape[0] // own

    @pl.when(pl.program_id(0) == 0)
    def _():
        o_ref[...] = x_ref[...]

    wide = lax.dot_general(
        p_ref[...], l_ref[...], (((1,), (1,)), ((), ())), preferred_element_type=jnp.float32
    )
    wide = [
        (wide[f * cols : (f + 1) * cols] * wt_ref[f : f + 1, :]).astype(jnp.bfloat16)
        for f in range(own)
    ]
    o_ref[...] += lax.dot_general(
        jnp.concatenate(wide, axis=0),
        l_ref[...],
        (((1,), (0,)), ((), ())),
        preferred_element_type=jnp.float32,
    )


def again(factors, pair_weight, projected, kept):
    pairs, naux = factors.shape
    own = pair_weight.shape[0]
    tile = wide_tile(pairs)
    return pl.pallas_call(
        functools.partial(again_kernel, own),
        out_shape=jax.ShapeDtypeStruct(kept.shape, jnp.float32),
        grid=(pairs // tile,),
        in_specs=[
            pl.BlockSpec((tile, naux), lambda i: (i, 0)),
            pl.BlockSpec((own, tile), lambda i: (0, i)),
            resident(projected),
            resident(kept),
        ],
        out_specs=pl.BlockSpec(kept.shape, lambda i: (0, 0)),
        compiler_params=pltpu.CompilerParams(vmem_limit_bytes=40 << 20),
        cost_estimate=pl.CostEstimate(
            flops=4 * kept.size * pairs, bytes_accessed=2 * factors.size, transcendentals=0
        ),
    )(factors, pair_weight, projected, kept)


class Stream:
    def __init__(self, refs, buffer, sems, step):
        tile = buffer.shape[2]
        refs = [
            ref.at[:, n : n + tile, :] for ref in refs for n in range(0, ref.shape[1], tile)
        ]
        self.refs, self.buffer, self.sems = refs, buffer, sems
        self.step = step
        self.slot = lax.rem(step + 2, 2)

    def copy(self, n):
        return pltpu.make_async_copy(self.refs[n], self.buffer.at[n % 2], self.sems.at[n % 2])

    def ahead(self):
        @pl.when(pl.program_id(0) == 0)
        def _():
            self.copy(0).start()

        for n in range(1, len(self.refs)):

            @pl.when(self.step == n - 1)
            def _():
                self.copy(n).start()

    def here(self):
        pltpu.make_async_copy(
            self.refs[0], self.buffer.at[self.slot], self.sems.at[self.slot]
        ).wait()
        return self.buffer.at[self.slot]


def stream_scratch(own, tile, cols):
    return [VMEM((2, own, tile, cols), jnp.float32), pltpu.SemaphoreType.DMA((2,))]


ANYWHERE = pl.BlockSpec(memory_space=pl.ANY)


def amplitude_kernel(pieces, me_ref, l_ref, wt_ref, p_ref, *rest):
    refs, (a_ref, buffer, sems) = rest[:pieces], rest[pieces:]
    own, tile, cols = a_ref.shape
    stream = Stream(refs, buffer, sems, pl.program_id(0))
    stream.ahead()
    wide = rows_times(p_ref, l_ref)
    here = stream.here()
    for f in range(own):
        scaled = wide[f * cols : (f + 1) * cols] * wt_ref[f : f + 1, :]
        for k in range(0, tile, LANES):
            lanes = slice(k, k + LANES)
            a_ref[f, lanes, :] = here[f, lanes, :] + scaled[:, lanes].T


def amplitude(me, factors, pair_weight, near, sources):
    own, _, cols = sources[0][0].shape
    parts = len(sources[0])
    pairs, naux = factors.shape
    quarter = pairs // parts
    size = tile_of(quarter)
    if size is None:
        wide = jnp.einsum("ja,pa->jp", near, factors, preferred_element_type=jnp.float32)
        wide = jnp.transpose(wide.reshape(own, cols, pairs), (0, 2, 1))
        result = wide * pair_weight[:, :, None]
        for s in range(parts):
            at = lax.rem(me + s, parts) * quarter
            part_of = lax.dynamic_slice_in_dim(result, at, quarter, 1) + sources[0][s]
            result = lax.dynamic_update_slice_in_dim(result, part_of, at, 1)
        return result
    steps = quarter // size
    pieces = [x for group in sources for x in group]
    at = lambda i, m: lax.rem(m[0] + lax.rem(i, parts), parts) * steps + lax.div(i, parts)
    return pl.pallas_call(
        functools.partial(amplitude_kernel, len(pieces)),
        out_shape=jax.ShapeDtypeStruct((own, pairs, cols), jnp.float32),
        grid_spec=pltpu.PrefetchScalarGridSpec(
            num_scalar_prefetch=1,
            grid=(parts * steps,),
            in_specs=[
                pl.BlockSpec((size, naux), lambda i, m: (at(i, m), 0)),
                pl.BlockSpec((own, size), lambda i, m: (0, at(i, m))),
                resident(near),
            ]
            + [ANYWHERE] * len(pieces),
            out_specs=pl.BlockSpec((own, size, cols), lambda i, m: (0, at(i, m), 0)),
            scratch_shapes=stream_scratch(own, size, cols),
        ),
        compiler_params=pltpu.CompilerParams(vmem_limit_bytes=20 << 20),
        cost_estimate=pl.CostEstimate(
            flops=2 * own * pairs * cols * naux,
            bytes_accessed=8 * own * pairs * cols,
            transcendentals=0,
        ),
    )(me.reshape(1), factors, pair_weight, near, *pieces)


def final_kernel(nf, parts, held_outs, me_ref, l_ref, k_ref, wt_ref, coef_ref, p_ref, *rest):
    b_refs, rest = rest[:parts], rest[parts + held_outs :]
    new_ref, table, held, mid, buffer, sems = rest
    own, _, cols = new_ref.shape
    stream = Stream(b_refs, buffer, sems, pl.program_id(0))
    stream.ahead()
    table[...] = dot_exact(coef_ref[...], k_ref[...])
    for w in range(own):
        rows = slice(w * nf, (w + 1) * nf)
        table[rows, :] = table[rows, :] * wt_ref[...]
    held[...] = rows_times(p_ref, l_ref)
    here = stream.here()

    @pl.loop(0, table.shape[1] // LANES)
    def _(block):
        lanes = part(block, 0, LANES)

        @pl.loop(0, cols // WIDE)
        def _(i):
            rows = part(i, 0, WIDE)
            got = mix(table, lanes, own, nf, lambda v: held[part(i, v * cols, WIDE), lanes])
            for w in range(own):
                mid[w, rows, :] = got[w]

        for w in range(own):
            new_ref[w, lanes, :] = here[w, lanes, :] + mid[w].T


def final(me, low, factors, kernels, weights, coef, gathered, base, outs):
    own, span, cols = base[0].shape
    parts = len(base)
    nf = weights.shape[0]
    pairs, naux = factors.shape
    quarter = pairs // parts
    tile = tile_of(quarter)
    if tile is None:
        wide = jnp.einsum(
            "ja,pa->jp",
            gathered,
            factors,
            preferred_element_type=jnp.float32,
        )
        wide = jnp.transpose(wide.reshape(nf, cols, pairs), (0, 2, 1)) * weights[:, :, None]
        table = jnp.einsum("jt,tp->jp", coef, kernels, precision=EXACT).reshape(own, nf, pairs)
        new = jnp.einsum("wvp,vpc->wpc", table, wide, precision=EXACT)
        for s in range(parts):
            at = lax.rem(me + s, parts) * quarter
            part_of = lax.dynamic_slice_in_dim(new, at, quarter, 1) + base[s]
            new = lax.dynamic_update_slice_in_dim(new, part_of, at, 1)
        return [new]
    size = tile
    sets = span // size
    at = around(parts, quarter // size, low, sets)
    result = pl.pallas_call(
        functools.partial(final_kernel, nf, parts, len(outs)),
        out_shape=jax.ShapeDtypeStruct((own, pairs, cols), jnp.float32),
        grid_spec=pltpu.PrefetchScalarGridSpec(
            num_scalar_prefetch=1,
            grid=(parts * sets,),
            in_specs=[
                pl.BlockSpec((size, naux), lambda i, m: (at(i, m), 0)),
                pl.BlockSpec((nf, size), lambda i, m: (0, at(i, m))),
                pl.BlockSpec((nf, size), lambda i, m: (0, at(i, m))),
                resident(coef),
                resident(gathered),
            ]
            + [ANYWHERE] * (parts + len(outs)),
            out_specs=pl.BlockSpec((own, size, cols), lambda i, m: (0, at(i, m), 0)),
            scratch_shapes=[
                VMEM((own * nf, size), jnp.float32),
                VMEM((nf * cols, size), jnp.float32),
                VMEM((own, cols, LANES), jnp.float32),
            ]
            + stream_scratch(own, size, cols),
        ),
        input_output_aliases={6 + parts + n: n for n in range(len(outs))},
        compiler_params=pltpu.CompilerParams(vmem_limit_bytes=26 << 20),
        cost_estimate=pl.CostEstimate(
            flops=2 * nf * parts * span * cols * naux,
            bytes_accessed=8 * own * parts * span * cols,
            transcendentals=0,
        ),
    )(me.reshape(1), factors, kernels, weights, coef, gathered, *base, *outs)
    return [result]


class Plane:
    def __init__(self, chips):
        self.chips = chips
        me = lax.axis_index("fac")
        self.core = lax.rem(me, 2)
        self.chip = lax.div(me, 2)
        self.pal = {"fac": me + 1 - 2 * self.core}
        self.started = []

    def on(self, d):
        return lax.rem(self.chip + d + self.chips, self.chips)

    def at(self, d):
        return {"fac": self.on(d) * 2 + self.core}

    def chip_at(self, chip):
        return {"fac": chip * 2 + self.core}

    def greet(self):
        barrier = pltpu.get_barrier_semaphore()
        for other in [self.pal] + [self.at(d) for d in range(1, self.chips)]:
            pl.semaphore_signal(barrier, inc=1, device_id=other, device_id_type=MESH)
        pl.semaphore_wait(barrier, self.chips)

    def send(self, src, dst, sems, at, to):
        copy = pltpu.make_async_remote_copy(
            src_ref=src,
            dst_ref=dst,
            send_sem=sems[0].at[at],
            recv_sem=sems[1].at[at],
            device_id=to,
            device_id_type=MESH,
        )
        copy.start()
        self.started.append(copy)
        return copy

    def end(self):
        for copy in self.started:
            copy.wait_send()


def reduced(plane, x_ref, near, red, land, mine, near_sems, red_sems):
    chips, chip, core, pal = plane.chips, plane.chip, plane.core, plane.pal
    nears = {}
    for d in list(range(1, chips)) + [0]:
        nears[d] = plane.send(x_ref.at[plane.on(d), 1 - core], near.at[d], near_sems, d, pal)
    block = mine.shape[0]
    step = min(block, 16)
    reds = []
    for d in range(1, chips):
        nears[d].wait_recv()
        for r in range(0, block, step):
            rows = slice(r, r + step)
            red[d, rows, :] = (x_ref[plane.on(d), core, rows, :] + near[d, rows, :]).astype(
                red.dtype
            )
        reds.append(plane.send(red.at[d], land.at[d], red_sems, d, plane.at(d)))
    nears[0].wait_recv()
    for copy in reds:
        copy.wait_recv()
    for r in range(0, block, step):
        rows = slice(r, r + step)
        total = x_ref[chip, core, rows, :] + near[0, rows, :]
        for d in range(1, chips):
            total = total + land[d, rows, :].astype(jnp.float32)
        mine[rows, :] = total.astype(mine.dtype)


def reduce_kernel(chips, x_ref, o_ref, near, red, land, *sems):
    plane = Plane(chips)
    plane.greet()
    reduced(plane, x_ref, near, red, land, o_ref, sems[0:2], sems[2:4])
    plane.end()


def sum_kernel(chips, x_ref, o_ref, near, red, land, mine, joined, *sems):
    plane = Plane(chips)
    chip, core = plane.chip, plane.core
    plane.greet()
    reduced(plane, x_ref, near, red, land, mine, sems[0:2], sems[2:4])
    here = joined.at[chip, core]
    keep = pltpu.make_async_copy(mine, here, sems[8])
    keep.start()
    keep.wait()
    wides = [plane.send(here, here, sems[4:6], d, plane.at(d)) for d in range(1, chips)]
    pairs = [plane.send(here, here, sems[6:8], 0, plane.pal)]
    for d, copy in enumerate(wides, 1):
        copy.wait_recv()
        there = joined.at[plane.on(-d), core]
        pairs.append(plane.send(there, there, sems[6:8], d, plane.pal))
    for copy in pairs:
        copy.wait_recv()
    plane.end()
    for c in range(chips):
        o_ref[c] = joined[c]


def gather_kernel(chips, parts, x_ref, *refs):
    near_ref = None
    if len(refs) > 8:
        near_ref, refs = refs[0], refs[1:]
    o_ref, top_ref, joined, *sems = refs
    skip = 0 if near_ref is None else 1
    x_refs = [x_ref.at[s] for s in range(parts)]
    kept = sems[4]
    plane = Plane(chips)
    chip, core, pal = plane.chip, plane.core, plane.pal
    plane.greet()
    wide_sems, pair_sems = sems[0:2], sems[2:4]
    pairs = []
    copies = []
    for s in range(parts):
        copies.append(
            pltpu.make_async_copy(x_refs[s], joined.at[s, chip, core], kept.at[s])
        )
        copies[-1].start()
    square = chips == 4
    column, row = lax.rem(chip, 2), lax.div(chip, 2)
    across, along = chip + 1 - 2 * column, chip + 2 - 4 * row
    corner = along + 1 - 2 * column
    wides = []
    for s in range(parts):
        src, dst = x_refs[s], joined.at[s, chip, core]
        if square:
            for n, to in enumerate((across, along)):
                copy = plane.send(src, dst, wide_sems, s * chips + n, plane.chip_at(to))
                wides.append((s, n, copy))
        else:
            for d in range(1, chips):
                copy = plane.send(src, dst, wide_sems, s * chips + d, plane.at(d))
                wides.append((s, d, copy))
    for s in range(parts):
        pairs.append(
            plane.send(x_refs[s], joined.at[s, chip, core], pair_sems, s * chips, pal)
        )
    late = []
    for s, d, copy in wides:
        copy.wait_recv()
        chip_from = (across, along)[d] if square else plane.on(-d)
        there = joined.at[s, chip_from, core]
        if square and d == s % 2:
            other = (along, across)[d]
            turned = plane.send(there, there, wide_sems, s * chips + 2, plane.chip_at(other))
            late.append((s, turned))
        at = s * chips + (1 + d if square else d)
        pairs.append(plane.send(there, there, pair_sems, at, pal))
    for s, copy in late:
        copy.wait_recv()
        there = joined.at[s, corner, core]
        pairs.append(plane.send(there, there, pair_sems, s * chips + 3, pal))
    for copy in pairs:
        copy.wait_recv()
    plane.end()
    for copy in copies:
        copy.wait()
    if skip:
        o_ref[0] = near_ref[...]
    top = jnp.zeros(top_ref.shape, jnp.float32)
    for s in range(parts):

        def fold(c, top):
            here = joined[s, c]
            o_ref[s + skip, c] = here
            here = jnp.abs(here.astype(jnp.float32))
            sums = here[..., :LANES]
            for k in range(LANES, here.shape[-1], LANES):
                sums = sums + here[..., k : k + LANES]
            return jnp.maximum(top, jnp.max(sums.reshape((-1,) + top.shape), axis=0))

        top = lax.fori_loop(0, chips, fold, top)
    top_ref[...] = top


def dmas(count, pairs):
    return [pltpu.SemaphoreType.DMA((count,))] * (2 * pairs)


def reach_params(cid):
    return pltpu.CompilerParams(
        collective_id=cid, has_side_effects=True, vmem_limit_bytes=24 << 20
    )


def reach_cost(size):
    return pl.CostEstimate(flops=40 * size, bytes_accessed=40 * size, transcendentals=0)


WHOLE = pl.BlockSpec(memory_space=VMEM)


def summed(x, all_blocks):
    n = lax.axis_size("fac")
    chips = n // 2
    rows, width = x.shape
    block = rows // n
    flat = (chips, 2, block, width)
    landing = [
        VMEM((chips, block, width), jnp.float32),
        VMEM((chips, block, width), jnp.bfloat16),
        VMEM((chips, block, width), jnp.bfloat16),
    ]
    if not all_blocks:
        return pl.pallas_call(
            functools.partial(reduce_kernel, chips),
            out_shape=jax.ShapeDtypeStruct((block, width), jnp.bfloat16),
            in_specs=[WHOLE],
            out_specs=WHOLE,
            scratch_shapes=landing + dmas(chips, 2),
            compiler_params=reach_params(1),
            cost_estimate=reach_cost(x.size // 2),
        )(x.reshape(flat))
    result = pl.pallas_call(
        functools.partial(sum_kernel, chips),
        out_shape=jax.ShapeDtypeStruct(flat, jnp.bfloat16),
        in_specs=[WHOLE],
        out_specs=WHOLE,
        scratch_shapes=landing
        + [VMEM((block, width), jnp.bfloat16), VMEM(flat, jnp.bfloat16)]
        + dmas(chips, 4)
        + [pltpu.SemaphoreType.DMA],
        compiler_params=reach_params(0),
        cost_estimate=reach_cost(x.size),
    )(x.reshape(flat))
    return result.reshape(rows, width)


def gathered_over(blocks, near=None):
    n = lax.axis_size("fac")
    chips = n // 2
    parts, block, width = blocks.shape
    flat = (chips, 2, block, width)
    result, top = pl.pallas_call(
        functools.partial(gather_kernel, chips, parts),
        out_shape=(
            jax.ShapeDtypeStruct((parts + (near is not None),) + flat, jnp.bfloat16),
            jax.ShapeDtypeStruct((8, LANES), jnp.float32),
        ),
        in_specs=[WHOLE] * (1 if near is None else 2),
        out_specs=(WHOLE, WHOLE),
        scratch_shapes=[VMEM((parts,) + flat, jnp.bfloat16)]
        + dmas(parts * chips, 2)
        + [pltpu.SemaphoreType.DMA((parts,))],
        compiler_params=reach_params(2 if parts == 1 else 3),
        cost_estimate=reach_cost(block * width * parts * 8),
    )(blocks, *(() if near is None else (near.reshape(flat),)))
    return result.reshape(-1, width), top


def shards(right_side, factors, pair_weight, second_order, forward, backward):
    own, pairs, cols = right_side.shape
    nf = forward.shape[0]
    naux = factors.shape[1]
    parts = nf // own
    quarter = pairs // parts
    me = lax.axis_index("freq")

    def shift(x, by):
        if by == 0:
            return x
        return lax.ppermute(x, "freq", [(i, (i + by) % parts) for i in range(parts)])

    order = jnp.concatenate(
        [lax.rem(me - s + parts, parts) * own + jnp.arange(own) for s in range(parts)]
    )
    pick = jax.nn.one_hot(order, nf, dtype=jnp.float32)
    ahead = jnp.einsum("ts,sv,wv->tw", pick, forward, pick, precision=EXACT)
    back = jnp.einsum("ws,st,vt->wv", pick, backward, pick, precision=EXACT)
    coef = (back[:, None, :] * ahead.T[None, :, :]).reshape(nf * nf, nf)
    reach = jnp.max(
        jnp.sum(
            jnp.einsum("wt,tv->wv", jnp.abs(backward), jnp.abs(forward), precision=EXACT), axis=1
        )
    )

    both = jnp.stack([pair_weight, second_order])
    fine = HALF_TOP / 2.0
    slim = (both * fine).astype(jnp.float16)
    came = [shift(slim, s) for s in range(1, parts)]
    tables = [both] + [x.astype(jnp.float32) * (1.0 / fine) for x in came]
    weights, kernels = [jnp.concatenate([x[n] for x in tables]) for n in range(2)]
    size = tile_of(quarter) or quarter
    chunks = quarter // size
    early = max(chunks - 1, 1)
    groups = [(0, early)] + ([(early, chunks)] if early < chunks else [])
    calls = [(k, k + 1) for k in range(chunks)]
    tie = lax.optimization_barrier
    up = 8192.0

    def sliced(x, s, low, high):
        at = lax.rem(me + s, parts) * quarter + low * size
        return lax.dynamic_slice_in_dim(x, at, (high - low) * size, 1)

    def leaving(low, high):
        return [(sliced(right_side, s, low, high) * up).astype(jnp.float16) for s in range(1, parts)]

    def passed(blocks, back):
        return [
            shift(b, parts - 1 - s if back else s + 1) for s, b in enumerate(blocks)
        ]

    def first_projection():
        return jnp.einsum(
            "pa,fpc->fca",
            factors,
            right_side.astype(jnp.bfloat16),
            preferred_element_type=jnp.float32,
        ).reshape(own * cols, naux)

    def ladder(kept):
        total = kept
        for _ in range(INNER - 1):
            mine = summed(total, True)
            total = again(factors, pair_weight, mine, kept)
        block = summed(total, False)
        far = [shift(block, s) for s in range(1, parts)]
        return *gathered_over(block[None]), far

    def joined(blocks, near):
        blocks = jnp.stack(blocks)
        return gathered_over(blocks, near)

    leaves = []
    for g in groups:
        leaves.append(leaving(*g))
    right_late, leaves[-1] = tie((right_side, leaves[-1]))
    came = [passed(x, False) for x in leaves]
    near, near_top, blocks = ladder(first_projection())
    gathered, far_top = joined(blocks, near)
    height = jnp.sum(jnp.max(jnp.maximum(near_top, far_top), axis=0))
    u_top = jnp.maximum(1.01 * reach * (R_MAX + W_MAX * L_MAX * height), 1e-30)
    v_top = jnp.maximum(1.01 * reach * (R_MAX + u_top), 1e-30)

    def halved(far, top):
        blocks = [far[s * own : (s + 1) * own] for s in range(parts - 1)]
        return [(b * (HALF_TOP / top)).astype(jnp.float16) for b in blocks]

    def added(first, rest, top, group):
        rest = [b.astype(jnp.float32) * (top / HALF_TOP) for b in rest]
        return [sliced(right_late, s, *group) + b for s, b in enumerate([first] + rest)]

    us, vs, inward, halves = [], [], [], []
    for n, (low, high) in enumerate(calls):
        at = next(g for g, (first, end) in enumerate(groups) if first <= low < end)
        moved = came[at]
        if n:
            moved, _ = tie((moved, us[-1][1]))
        start = (low - groups[at][0]) * size
        moved = [
            m[:, start : start + size].astype(jnp.float32) * (1.0 / up) for m in moved
        ]
        mine_u, far_u, mine_v, far_v = quarter_pass(
            me,
            low,
            factors,
            kernels,
            weights,
            coef,
            gathered,
            right_side,
            [(moved, 0)],
        )
        inward.append(passed(halved(far_u, u_top), True))
        halves.append(halved(far_v, v_top))
        us.append((mine_u, far_u))
        vs.append((mine_v, far_v))
    sources = []
    total = jnp.zeros((own * cols, naux), jnp.float32)
    for n, group in enumerate(calls):
        if n:
            inward[n], total = tie((inward[n], total))
        sources.append(added(us[n][0], inward[n], u_top, group))
        total = project(me, group[0], factors, sources[n], total)

    near, _, blocks = ladder(total)
    back = [passed(x, True) for x in halves]
    amplitudes = amplitude(me, factors, pair_weight, near, sources)
    gathered, _ = joined(blocks, near)
    outs = []
    for n, group in enumerate(calls):
        back[n], outs, gathered = tie((back[n], outs, gathered))
        base = added(vs[n][0], back[n], v_top, group)
        outs = final(
            me,
            group[0],
            factors,
            kernels,
            weights,
            coef[: own * nf],
            gathered,
            base,
            outs,
        )
    return amplitudes, outs[0]


def solution(mesh):
    return jax.shard_map(
        shards,
        mesh=mesh,
        in_specs=(
            P("freq", "fac", None),
            P("fac", None),
            P("freq", "fac"),
            P("freq", "fac"),
            P(),
            P(),
        ),
        out_specs=(P("freq", "fac", None), P("freq", "fac", None)),
        check_vma=False,
    )
```

```python
import functools

import jax
import jax.numpy as jnp
from jax import lax
from jax.experimental import pallas as pl
from jax.experimental.pallas import tpu as pltpu
from jax.sharding import PartitionSpec as P


INNER = 2
LANES = 128
MESH = pl.DeviceIdType.MESH
CHUNK = 16
WIDE = 32
EXACT = lax.Precision.HIGHEST
R_MAX = 6.0
W_MAX = 2.0
L_MAX = 0.03125
HALF_TOP = 32768.0
VMEM = pltpu.VMEM


def tile_of(pairs):
    for blocks in (3, 4, 2, 1):
        if pairs % (blocks * LANES) == 0:
            return blocks * LANES
    return None


def wide_tile(pairs):
    for blocks in (6, 4, 3, 2, 1):
        if pairs % (blocks * LANES) == 0:
            return blocks * LANES
    return None


def mix(table, lanes, outs, count, term):
    totals = [None] * outs
    for v in range(count):
        value = term(v)
        for w in range(outs):
            row = w * count + v
            product = table[row : row + 1, lanes] * value
            totals[w] = product if totals[w] is None else totals[w] + product
    return totals


def part(i, base, chunk):
    return pl.ds(pl.multiple_of(base + i * chunk, chunk), chunk)


def rows_times(p_ref, l_ref):
    return lax.dot_general(
        p_ref[...], l_ref[...], (((1,), (1,)), ((), ())), preferred_element_type=jnp.float32
    )


def dot_exact(a, b):
    return lax.dot_general(
        a, b, (((1,), (0,)), ((), ())), precision=EXACT, preferred_element_type=jnp.float32
    )


def resident(x):
    return pl.BlockSpec(x.shape, lambda i, *_: (0,) * x.ndim, pipeline_mode=pl.Buffered(1))


def quarter_kernel(nf, parts, sets, me_ref, l_ref, k_ref, wt_ref, coef_ref, p_ref, *rest):
    own_ref, rest = rest[0], rest[1:]
    came, rest = rest[: sets * (parts - 1)], rest[sets * (parts - 1) :]
    mine_u, far_u, mine_v, far_v, table, held, turned, mid, far = rest
    own = nf // parts
    cols = own_ref.shape[2]
    table[...] = dot_exact(coef_ref[...], k_ref[...])
    held[...] = rows_times(p_ref, l_ref)

    @pl.loop(0, table.shape[1] // LANES)
    def _(block):
        lanes = part(block, 0, LANES)
        for v in range(own):
            turned[v] = own_ref[v, lanes, :].T
        for j in range(sets):

            @pl.when(pl.program_id(0) == j)
            def _():
                for v in range(own, nf):
                    turned[v] = came[j * (parts - 1) + v // own - 1][v % own, lanes, :].T

        @pl.loop(0, cols // CHUNK)
        def _(i):
            rows = part(i, 0, CHUNK)
            got = mix(
                table,
                lanes,
                nf,
                nf,
                lambda v: turned[v, rows, :]
                + wt_ref[v : v + 1, lanes] * held[part(i, v * cols, CHUNK), lanes],
            )
            for w in range(nf):
                mid[w, rows, :] = got[w]
                turned[w, rows, :] = turned[w, rows, :] + got[w]
            got = mix(table, lanes, nf, nf, lambda v: turned[v, rows, :])
            for w in range(nf):
                far[w, rows, :] = got[w]

        for w in range(nf):
            u_ref, v_ref, row = (mine_u, mine_v, w) if w < own else (far_u, far_v, w - own)
            u_ref[row, lanes, :] = mid[w].T
            v_ref[row, lanes, :] = far[w].T


def quarter_pass(me, low, factors, kernels, weights, coef, gathered, right_side, moved):
    own, pairs, cols = right_side.shape
    nf = weights.shape[0]
    parts = nf // own
    quarter = pairs // parts
    naux = factors.shape[1]
    tile = tile_of(quarter)
    sets = len(moved)
    if tile is None:
        cut = lambda x, axis: lax.dynamic_slice_in_dim(x, me * quarter, quarter, axis)
        here = jnp.concatenate([cut(right_side, 1)] + moved[0][0])
        table = jnp.einsum("jt,tp->jp", coef, cut(kernels, 1), precision=EXACT)
        table = table.reshape(nf, nf, quarter)
        wide = jnp.einsum(
            "ja,pa->jp",
            gathered,
            cut(factors, 0),
            preferred_element_type=jnp.float32,
        )
        wide = jnp.transpose(wide.reshape(nf, cols, quarter), (0, 2, 1))
        wide = here + cut(weights, 1)[:, :, None] * wide
        u = jnp.einsum("wvp,vpc->wpc", table, wide, precision=EXACT)
        v = jnp.einsum("wvp,vpc->wpc", table, here + u, precision=EXACT)
        return u[:own], u[own:], v[:own], v[own:]
    steps = quarter // tile
    at = lambda i, m: m[0] * steps + low + i
    here = lambda n: pl.BlockSpec((own, tile, cols), lambda i, m: (0, n, 0))
    outs = [(rows, sets * tile, cols) for rows in (own, nf - own)]
    pieces = [pl.BlockSpec((x[0], tile, cols), lambda i, m: (0, i, 0)) for x in outs]
    return pl.pallas_call(
        functools.partial(quarter_kernel, nf, parts, sets),
        out_shape=[jax.ShapeDtypeStruct(x, jnp.float32) for x in outs]
        + [pltpu.HBM(x, jnp.float32) for x in outs],
        grid_spec=pltpu.PrefetchScalarGridSpec(
            num_scalar_prefetch=1,
            grid=(sets,),
            in_specs=[
                pl.BlockSpec((tile, naux), lambda i, m: (at(i, m), 0)),
                pl.BlockSpec((nf, tile), lambda i, m: (0, at(i, m))),
                pl.BlockSpec((nf, tile), lambda i, m: (0, at(i, m))),
                resident(coef),
                resident(gathered),
                pl.BlockSpec((own, tile, cols), lambda i, m: (0, at(i, m), 0)),
            ]
            + [here(n) for _, n in moved for _ in range(parts - 1)],
            out_specs=pieces * 2,
            scratch_shapes=[
                VMEM((nf * nf, tile), jnp.float32),
                VMEM((nf * cols, tile), jnp.float32),
            ]
            + [VMEM((nf, cols, LANES), jnp.float32)] * 3,
        ),
        compiler_params=pltpu.CompilerParams(vmem_limit_bytes=36 << 20),
        cost_estimate=pl.CostEstimate(
            flops=2 * nf * sets * tile * cols * (naux + 32 * nf),
            bytes_accessed=16 * nf * sets * tile * cols,
            transcendentals=0,
        ),
    )(
        me.reshape(1),
        factors,
        kernels,
        weights,
        coef,
        gathered,
        right_side,
        *[x for xs, _ in moved for x in xs],
    )


def project_kernel(parts, sets, me_ref, l_ref, *rest):
    s_refs, (x_ref, o_ref) = rest[:parts], rest[parts:]
    own, _, _ = s_refs[0].shape
    i = pl.program_id(0)

    @pl.when(i == 0)
    def _():
        o_ref[...] = x_ref[...]

    for s in range(parts):

        @pl.when(lax.div(i, sets) == s)
        def _():
            rounded = [s_refs[s][f].astype(jnp.bfloat16) for f in range(own)]
            o_ref[...] += lax.dot_general(
                jnp.concatenate(rounded, axis=1),
                l_ref[...],
                (((0,), (0,)), ((), ())),
                preferred_element_type=jnp.float32,
            )


def around(parts, steps, low, sets):
    return lambda i, m: lax.rem(m[0] + lax.div(i, sets), parts) * steps + low + lax.rem(i, sets)


def project(me, low, factors, pieces, total):
    own, size, cols = pieces[0].shape
    parts = len(pieces)
    pairs, naux = factors.shape
    quarter = pairs // parts
    tile = tile_of(quarter)
    if tile is None:
        for s, x in enumerate(pieces):
            rows = lax.dynamic_slice_in_dim(
                factors, lax.rem(me + s, parts) * quarter, quarter, 0
            )
            total = total + jnp.einsum(
                "pa,fpc->fca", rows, x.astype(jnp.bfloat16), preferred_element_type=jnp.float32
            ).reshape(total.shape)
        return total
    sets = size // tile
    at = around(parts, quarter // tile, low, sets)
    stay = lambda s: lambda i, m: (0, jnp.clip(i - s * sets, 0, sets - 1), 0)
    return pl.pallas_call(
        functools.partial(project_kernel, parts, sets),
        out_shape=jax.ShapeDtypeStruct(total.shape, jnp.float32),
        grid_spec=pltpu.PrefetchScalarGridSpec(
            num_scalar_prefetch=1,
            grid=(parts * sets,),
            in_specs=[pl.BlockSpec((tile, naux), lambda i, m: (at(i, m), 0))]
            + [pl.BlockSpec((own, tile, cols), stay(s)) for s in range(parts)]
            + [resident(total)],
            out_specs=pl.BlockSpec(total.shape, lambda i, m: (0, 0)),
        ),
        compiler_params=pltpu.CompilerParams(vmem_limit_bytes=40 << 20),
        cost_estimate=pl.CostEstimate(
            flops=2 * own * parts * size * cols * naux,
            bytes_accessed=8 * own * parts * size * cols,
            transcendentals=0,
        ),
    )(me.reshape(1), factors, *pieces, total)


def again_kernel(own, l_ref, wt_ref, p_ref, x_ref, o_ref):
    cols = p_ref.shape[0] // own

    @pl.when(pl.program_id(0) == 0)
    def _():
        o_ref[...] = x_ref[...]

    wide = lax.dot_general(
        p_ref[...], l_ref[...], (((1,), (1,)), ((), ())), preferred_element_type=jnp.float32
    )
    wide = [
        (wide[f * cols : (f + 1) * cols] * wt_ref[f : f + 1, :]).astype(jnp.bfloat16)
        for f in range(own)
    ]
    o_ref[...] += lax.dot_general(
        jnp.concatenate(wide, axis=0),
        l_ref[...],
        (((1,), (0,)), ((), ())),
        preferred_element_type=jnp.float32,
    )


def again(factors, pair_weight, projected, kept):
    pairs, naux = factors.shape
    own = pair_weight.shape[0]
    tile = wide_tile(pairs)
    return pl.pallas_call(
        functools.partial(again_kernel, own),
        out_shape=jax.ShapeDtypeStruct(kept.shape, jnp.float32),
        grid=(pairs // tile,),
        in_specs=[
            pl.BlockSpec((tile, naux), lambda i: (i, 0)),
            pl.BlockSpec((own, tile), lambda i: (0, i)),
            resident(projected),
            resident(kept),
        ],
        out_specs=pl.BlockSpec(kept.shape, lambda i: (0, 0)),
        compiler_params=pltpu.CompilerParams(vmem_limit_bytes=40 << 20),
        cost_estimate=pl.CostEstimate(
            flops=4 * kept.size * pairs, bytes_accessed=2 * factors.size, transcendentals=0
        ),
    )(factors, pair_weight, projected, kept)


class Stream:
    def __init__(self, refs, buffer, sems, step):
        tile = buffer.shape[2]
        refs = [
            ref.at[:, n : n + tile, :] for ref in refs for n in range(0, ref.shape[1], tile)
        ]
        self.refs, self.buffer, self.sems = refs, buffer, sems
        self.step = step
        self.slot = lax.rem(step + 2, 2)

    def copy(self, n):
        return pltpu.make_async_copy(self.refs[n], self.buffer.at[n % 2], self.sems.at[n % 2])

    def ahead(self):
        @pl.when(pl.program_id(0) == 0)
        def _():
            self.copy(0).start()

        for n in range(1, len(self.refs)):

            @pl.when(self.step == n - 1)
            def _():
                self.copy(n).start()

    def here(self):
        pltpu.make_async_copy(
            self.refs[0], self.buffer.at[self.slot], self.sems.at[self.slot]
        ).wait()
        return self.buffer.at[self.slot]


def stream_scratch(own, tile, cols):
    return [VMEM((2, own, tile, cols), jnp.float32), pltpu.SemaphoreType.DMA((2,))]


ANYWHERE = pl.BlockSpec(memory_space=pl.ANY)


def amplitude_kernel(pieces, me_ref, l_ref, wt_ref, p_ref, *rest):
    refs, (a_ref, buffer, sems) = rest[:pieces], rest[pieces:]
    own, tile, cols = a_ref.shape
    stream = Stream(refs, buffer, sems, pl.program_id(0))
    stream.ahead()
    wide = rows_times(p_ref, l_ref)
    here = stream.here()
    for f in range(own):
        scaled = wide[f * cols : (f + 1) * cols] * wt_ref[f : f + 1, :]
        for k in range(0, tile, LANES):
            lanes = slice(k, k + LANES)
            a_ref[f, lanes, :] = here[f, lanes, :] + scaled[:, lanes].T


def amplitude(me, factors, pair_weight, near, sources):
    own, _, cols = sources[0][0].shape
    parts = len(sources[0])
    pairs, naux = factors.shape
    quarter = pairs // parts
    size = tile_of(quarter)
    if size is None:
        wide = jnp.einsum("ja,pa->jp", near, factors, preferred_element_type=jnp.float32)
        wide = jnp.transpose(wide.reshape(own, cols, pairs), (0, 2, 1))
        result = wide * pair_weight[:, :, None]
        for s in range(parts):
            at = lax.rem(me + s, parts) * quarter
            part_of = lax.dynamic_slice_in_dim(result, at, quarter, 1) + sources[0][s]
            result = lax.dynamic_update_slice_in_dim(result, part_of, at, 1)
        return result
    steps = quarter // size
    pieces = [x for group in sources for x in group]
    at = lambda i, m: lax.rem(m[0] + lax.rem(i, parts), parts) * steps + lax.div(i, parts)
    return pl.pallas_call(
        functools.partial(amplitude_kernel, len(pieces)),
        out_shape=jax.ShapeDtypeStruct((own, pairs, cols), jnp.float32),
        grid_spec=pltpu.PrefetchScalarGridSpec(
            num_scalar_prefetch=1,
            grid=(parts * steps,),
            in_specs=[
                pl.BlockSpec((size, naux), lambda i, m: (at(i, m), 0)),
                pl.BlockSpec((own, size), lambda i, m: (0, at(i, m))),
                resident(near),
            ]
            + [ANYWHERE] * len(pieces),
            out_specs=pl.BlockSpec((own, size, cols), lambda i, m: (0, at(i, m), 0)),
            scratch_shapes=stream_scratch(own, size, cols),
        ),
        compiler_params=pltpu.CompilerParams(vmem_limit_bytes=20 << 20),
        cost_estimate=pl.CostEstimate(
            flops=2 * own * pairs * cols * naux,
            bytes_accessed=8 * own * pairs * cols,
            transcendentals=0,
        ),
    )(me.reshape(1), factors, pair_weight, near, *pieces)


def final_kernel(nf, parts, held_outs, me_ref, l_ref, k_ref, wt_ref, coef_ref, p_ref, *rest):
    b_refs, rest = rest[:parts], rest[parts + held_outs :]
    new_ref, table, held, mid, buffer, sems = rest
    own, _, cols = new_ref.shape
    stream = Stream(b_refs, buffer, sems, pl.program_id(0))
    stream.ahead()
    table[...] = dot_exact(coef_ref[...], k_ref[...])
    for w in range(own):
        rows = slice(w * nf, (w + 1) * nf)
        table[rows, :] = table[rows, :] * wt_ref[...]
    held[...] = rows_times(p_ref, l_ref)
    here = stream.here()

    @pl.loop(0, table.shape[1] // LANES)
    def _(block):
        lanes = part(block, 0, LANES)

        @pl.loop(0, cols // WIDE)
        def _(i):
            rows = part(i, 0, WIDE)
            got = mix(table, lanes, own, nf, lambda v: held[part(i, v * cols, WIDE), lanes])
            for w in range(own):
                mid[w, rows, :] = got[w]

        for w in range(own):
            new_ref[w, lanes, :] = here[w, lanes, :] + mid[w].T


def final(me, low, factors, kernels, weights, coef, gathered, base, outs):
    own, span, cols = base[0].shape
    parts = len(base)
    nf = weights.shape[0]
    pairs, naux = factors.shape
    quarter = pairs // parts
    tile = tile_of(quarter)
    if tile is None:
        wide = jnp.einsum(
            "ja,pa->jp",
            gathered,
            factors,
            preferred_element_type=jnp.float32,
        )
        wide = jnp.transpose(wide.reshape(nf, cols, pairs), (0, 2, 1)) * weights[:, :, None]
        table = jnp.einsum("jt,tp->jp", coef, kernels, precision=EXACT).reshape(own, nf, pairs)
        new = jnp.einsum("wvp,vpc->wpc", table, wide, precision=EXACT)
        for s in range(parts):
            at = lax.rem(me + s, parts) * quarter
            part_of = lax.dynamic_slice_in_dim(new, at, quarter, 1) + base[s]
            new = lax.dynamic_update_slice_in_dim(new, part_of, at, 1)
        return [new]
    size = tile
    sets = span // size
    at = around(parts, quarter // size, low, sets)
    result = pl.pallas_call(
        functools.partial(final_kernel, nf, parts, len(outs)),
        out_shape=jax.ShapeDtypeStruct((own, pairs, cols), jnp.float32),
        grid_spec=pltpu.PrefetchScalarGridSpec(
            num_scalar_prefetch=1,
            grid=(parts * sets,),
            in_specs=[
                pl.BlockSpec((size, naux), lambda i, m: (at(i, m), 0)),
                pl.BlockSpec((nf, size), lambda i, m: (0, at(i, m))),
                pl.BlockSpec((nf, size), lambda i, m: (0, at(i, m))),
                resident(coef),
                resident(gathered),
            ]
            + [ANYWHERE] * (parts + len(outs)),
            out_specs=pl.BlockSpec((own, size, cols), lambda i, m: (0, at(i, m), 0)),
            scratch_shapes=[
                VMEM((own * nf, size), jnp.float32),
                VMEM((nf * cols, size), jnp.float32),
                VMEM((own, cols, LANES), jnp.float32),
            ]
            + stream_scratch(own, size, cols),
        ),
        input_output_aliases={6 + parts + n: n for n in range(len(outs))},
        compiler_params=pltpu.CompilerParams(vmem_limit_bytes=26 << 20),
        cost_estimate=pl.CostEstimate(
            flops=2 * nf * parts * span * cols * naux,
            bytes_accessed=8 * own * parts * span * cols,
            transcendentals=0,
        ),
    )(me.reshape(1), factors, kernels, weights, coef, gathered, *base, *outs)
    return [result]


class Plane:
    def __init__(self, chips):
        self.chips = chips
        me = lax.axis_index("fac")
        self.core = lax.rem(me, 2)
        self.chip = lax.div(me, 2)
        self.pal = {"fac": me + 1 - 2 * self.core}
        self.started = []

    def on(self, d):
        return lax.rem(self.chip + d + self.chips, self.chips)

    def at(self, d):
        return {"fac": self.on(d) * 2 + self.core}

    def chip_at(self, chip):
        return {"fac": chip * 2 + self.core}

    def greet(self):
        barrier = pltpu.get_barrier_semaphore()
        for other in [self.pal] + [self.at(d) for d in range(1, self.chips)]:
            pl.semaphore_signal(barrier, inc=1, device_id=other, device_id_type=MESH)
        pl.semaphore_wait(barrier, self.chips)

    def send(self, src, dst, sems, at, to):
        copy = pltpu.make_async_remote_copy(
            src_ref=src,
            dst_ref=dst,
            send_sem=sems[0].at[at],
            recv_sem=sems[1].at[at],
            device_id=to,
            device_id_type=MESH,
        )
        copy.start()
        self.started.append(copy)
        return copy

    def end(self):
        for copy in self.started:
            copy.wait_send()


def reduced(plane, x_ref, near, red, land, mine, near_sems, red_sems):
    chips, chip, core, pal = plane.chips, plane.chip, plane.core, plane.pal
    nears = {}
    for d in list(range(1, chips)) + [0]:
        nears[d] = plane.send(x_ref.at[plane.on(d), 1 - core], near.at[d], near_sems, d, pal)
    block = mine.shape[0]
    step = min(block, 16)
    reds = []
    for d in range(1, chips):
        nears[d].wait_recv()
        for r in range(0, block, step):
            rows = slice(r, r + step)
            red[d, rows, :] = (x_ref[plane.on(d), core, rows, :] + near[d, rows, :]).astype(
                red.dtype
            )
        reds.append(plane.send(red.at[d], land.at[d], red_sems, d, plane.at(d)))
    nears[0].wait_recv()
    for copy in reds:
        copy.wait_recv()
    for r in range(0, block, step):
        rows = slice(r, r + step)
        total = x_ref[chip, core, rows, :] + near[0, rows, :]
        for d in range(1, chips):
            total = total + land[d, rows, :].astype(jnp.float32)
        mine[rows, :] = total.astype(mine.dtype)


def reduce_kernel(chips, x_ref, o_ref, near, red, land, *sems):
    plane = Plane(chips)
    plane.greet()
    reduced(plane, x_ref, near, red, land, o_ref, sems[0:2], sems[2:4])
    plane.end()


def sum_kernel(chips, x_ref, o_ref, near, red, land, mine, joined, *sems):
    plane = Plane(chips)
    chip, core = plane.chip, plane.core
    plane.greet()
    reduced(plane, x_ref, near, red, land, mine, sems[0:2], sems[2:4])
    here = joined.at[chip, core]
    keep = pltpu.make_async_copy(mine, here, sems[8])
    keep.start()
    keep.wait()
    wides = [plane.send(here, here, sems[4:6], d, plane.at(d)) for d in range(1, chips)]
    pairs = [plane.send(here, here, sems[6:8], 0, plane.pal)]
    for d, copy in enumerate(wides, 1):
        copy.wait_recv()
        there = joined.at[plane.on(-d), core]
        pairs.append(plane.send(there, there, sems[6:8], d, plane.pal))
    for copy in pairs:
        copy.wait_recv()
    plane.end()
    for c in range(chips):
        o_ref[c] = joined[c]


def gather_kernel(chips, parts, x_ref, *refs):
    near_ref = None
    if len(refs) > 8:
        near_ref, refs = refs[0], refs[1:]
    o_ref, top_ref, joined, *sems = refs
    skip = 0 if near_ref is None else 1
    x_refs = [x_ref.at[s] for s in range(parts)]
    kept = sems[4]
    plane = Plane(chips)
    chip, core, pal = plane.chip, plane.core, plane.pal
    plane.greet()
    wide_sems, pair_sems = sems[0:2], sems[2:4]
    pairs = []
    copies = []
    for s in range(parts):
        copies.append(
            pltpu.make_async_copy(x_refs[s], joined.at[s, chip, core], kept.at[s])
        )
        copies[-1].start()
    square = chips == 4
    column, row = lax.rem(chip, 2), lax.div(chip, 2)
    across, along = chip + 1 - 2 * column, chip + 2 - 4 * row
    corner = along + 1 - 2 * column
    wides = []
    for s in range(parts):
        src, dst = x_refs[s], joined.at[s, chip, core]
        if square:
            for n, to in enumerate((across, along)):
                copy = plane.send(src, dst, wide_sems, s * chips + n, plane.chip_at(to))
                wides.append((s, n, copy))
        else:
            for d in range(1, chips):
                copy = plane.send(src, dst, wide_sems, s * chips + d, plane.at(d))
                wides.append((s, d, copy))
    for s in range(parts):
        pairs.append(
            plane.send(x_refs[s], joined.at[s, chip, core], pair_sems, s * chips, pal)
        )
    late = []
    for s, d, copy in wides:
        copy.wait_recv()
        chip_from = (across, along)[d] if square else plane.on(-d)
        there = joined.at[s, chip_from, core]
        if square and d == s % 2:
            other = (along, across)[d]
            turned = plane.send(there, there, wide_sems, s * chips + 2, plane.chip_at(other))
            late.append((s, turned))
        at = s * chips + (1 + d if square else d)
        pairs.append(plane.send(there, there, pair_sems, at, pal))
    for s, copy in late:
        copy.wait_recv()
        there = joined.at[s, corner, core]
        pairs.append(plane.send(there, there, pair_sems, s * chips + 3, pal))
    for copy in pairs:
        copy.wait_recv()
    plane.end()
    for copy in copies:
        copy.wait()
    if skip:
        o_ref[0] = near_ref[...]
    top = jnp.zeros(top_ref.shape, jnp.float32)
    for s in range(parts):

        def fold(c, top):
            here = joined[s, c]
            o_ref[s + skip, c] = here
            here = jnp.abs(here.astype(jnp.float32))
            sums = here[..., :LANES]
            for k in range(LANES, here.shape[-1], LANES):
                sums = sums + here[..., k : k + LANES]
            return jnp.maximum(top, jnp.max(sums.reshape((-1,) + top.shape), axis=0))

        top = lax.fori_loop(0, chips, fold, top)
    top_ref[...] = top


def dmas(count, pairs):
    return [pltpu.SemaphoreType.DMA((count,))] * (2 * pairs)


def reach_params(cid):
    return pltpu.CompilerParams(
        collective_id=cid, has_side_effects=True, vmem_limit_bytes=24 << 20
    )


def reach_cost(size):
    return pl.CostEstimate(flops=40 * size, bytes_accessed=40 * size, transcendentals=0)


WHOLE = pl.BlockSpec(memory_space=VMEM)


def summed(x, all_blocks):
    n = lax.axis_size("fac")
    chips = n // 2
    rows, width = x.shape
    block = rows // n
    flat = (chips, 2, block, width)
    landing = [
        VMEM((chips, block, width), jnp.float32),
        VMEM((chips, block, width), jnp.bfloat16),
        VMEM((chips, block, width), jnp.bfloat16),
    ]
    if not all_blocks:
        return pl.pallas_call(
            functools.partial(reduce_kernel, chips),
            out_shape=jax.ShapeDtypeStruct((block, width), jnp.bfloat16),
            in_specs=[WHOLE],
            out_specs=WHOLE,
            scratch_shapes=landing + dmas(chips, 2),
            compiler_params=reach_params(1),
            cost_estimate=reach_cost(x.size // 2),
        )(x.reshape(flat))
    result = pl.pallas_call(
        functools.partial(sum_kernel, chips),
        out_shape=jax.ShapeDtypeStruct(flat, jnp.bfloat16),
        in_specs=[WHOLE],
        out_specs=WHOLE,
        scratch_shapes=landing
        + [VMEM((block, width), jnp.bfloat16), VMEM(flat, jnp.bfloat16)]
        + dmas(chips, 4)
        + [pltpu.SemaphoreType.DMA],
        compiler_params=reach_params(0),
        cost_estimate=reach_cost(x.size),
    )(x.reshape(flat))
    return result.reshape(rows, width)


def gathered_over(blocks, near=None):
    n = lax.axis_size("fac")
    chips = n // 2
    parts, block, width = blocks.shape
    flat = (chips, 2, block, width)
    result, top = pl.pallas_call(
        functools.partial(gather_kernel, chips, parts),
        out_shape=(
            jax.ShapeDtypeStruct((parts + (near is not None),) + flat, jnp.bfloat16),
            jax.ShapeDtypeStruct((8, LANES), jnp.float32),
        ),
        in_specs=[WHOLE] * (1 if near is None else 2),
        out_specs=(WHOLE, WHOLE),
        scratch_shapes=[VMEM((parts,) + flat, jnp.bfloat16)]
        + dmas(parts * chips, 2)
        + [pltpu.SemaphoreType.DMA((parts,))],
        compiler_params=reach_params(2 if parts == 1 else 3),
        cost_estimate=reach_cost(block * width * parts * 8),
    )(blocks, *(() if near is None else (near.reshape(flat),)))
    return result.reshape(-1, width), top


def shards(right_side, factors, pair_weight, second_order, forward, backward):
    own, pairs, cols = right_side.shape
    nf = forward.shape[0]
    naux = factors.shape[1]
    parts = nf // own
    quarter = pairs // parts
    me = lax.axis_index("freq")

    def shift(x, by):
        if by == 0:
            return x
        return lax.ppermute(x, "freq", [(i, (i + by) % parts) for i in range(parts)])

    order = jnp.concatenate(
        [lax.rem(me - s + parts, parts) * own + jnp.arange(own) for s in range(parts)]
    )
    pick = jax.nn.one_hot(order, nf, dtype=jnp.float32)
    ahead = jnp.einsum("ts,sv,wv->tw", pick, forward, pick, precision=EXACT)
    back = jnp.einsum("ws,st,vt->wv", pick, backward, pick, precision=EXACT)
    coef = (back[:, None, :] * ahead.T[None, :, :]).reshape(nf * nf, nf)
    reach = jnp.max(
        jnp.sum(
            jnp.einsum("wt,tv->wv", jnp.abs(backward), jnp.abs(forward), precision=EXACT), axis=1
        )
    )

    both = jnp.stack([pair_weight, second_order])
    fine = HALF_TOP / 2.0
    slim = (both * fine).astype(jnp.float16)
    came = [shift(slim, s) for s in range(1, parts)]
    tables = [both] + [x.astype(jnp.float32) * (1.0 / fine) for x in came]
    weights, kernels = [jnp.concatenate([x[n] for x in tables]) for n in range(2)]
    size = tile_of(quarter) or quarter
    chunks = quarter // size
    early = max(chunks - 1, 1)
    groups = [(0, early)] + ([(early, chunks)] if early < chunks else [])
    calls = [(k, k + 1) for k in range(chunks)]
    tie = lax.optimization_barrier
    up = 8192.0

    def sliced(x, s, low, high):
        at = lax.rem(me + s, parts) * quarter + low * size
        return lax.dynamic_slice_in_dim(x, at, (high - low) * size, 1)

    def leaving(low, high):
        return [(sliced(right_side, s, low, high) * up).astype(jnp.float16) for s in range(1, parts)]

    def passed(blocks, back):
        return [
            shift(b, parts - 1 - s if back else s + 1) for s, b in enumerate(blocks)
        ]

    def first_projection():
        return jnp.einsum(
            "pa,fpc->fca",
            factors,
            right_side.astype(jnp.bfloat16),
            preferred_element_type=jnp.float32,
        ).reshape(own * cols, naux)

    def ladder(kept):
        total = kept
        for _ in range(INNER - 1):
            mine = summed(total, True)
            total = again(factors, pair_weight, mine, kept)
        block = summed(total, False)
        far = [shift(block, s) for s in range(1, parts)]
        return *gathered_over(block[None]), far

    def joined(blocks, near):
        blocks = jnp.stack(blocks)
        return gathered_over(blocks, near)

    leaves = []
    for g in groups:
        leaves.append(leaving(*g))
    right_late, leaves[-1] = tie((right_side, leaves[-1]))
    came = [passed(x, False) for x in leaves]
    near, near_top, blocks = ladder(first_projection())
    gathered, far_top = joined(blocks, near)
    height = jnp.sum(jnp.max(jnp.maximum(near_top, far_top), axis=0))
    u_top = jnp.maximum(1.01 * reach * (R_MAX + W_MAX * L_MAX * height), 1e-30)
    v_top = jnp.maximum(1.01 * reach * (R_MAX + u_top), 1e-30)

    def halved(far, top):
        blocks = [far[s * own : (s + 1) * own] for s in range(parts - 1)]
        return [(b * (HALF_TOP / top)).astype(jnp.float16) for b in blocks]

    def added(first, rest, top, group):
        rest = [b.astype(jnp.float32) * (top / HALF_TOP) for b in rest]
        return [sliced(right_late, s, *group) + b for s, b in enumerate([first] + rest)]

    us, vs, inward = [], [], []
    for n, (low, high) in enumerate(calls):
        at = next(g for g, (first, end) in enumerate(groups) if first <= low < end)
        moved = came[at]
        if n:
            moved, _ = tie((moved, us[-1][1]))
        start = (low - groups[at][0]) * size
        moved = [
            m[:, start : start + size].astype(jnp.float32) * (1.0 / up) for m in moved
        ]
        mine_u, far_u, mine_v, far_v = quarter_pass(
            me,
            low,
            factors,
            kernels,
            weights,
            coef,
            gathered,
            right_side,
            [(moved, 0)],
        )
        inward.append(passed(halved(far_u, u_top), True))
        us.append((mine_u, far_u))
        vs.append((mine_v, far_v))
    sources = []
    total = jnp.zeros((own * cols, naux), jnp.float32)
    for n, group in enumerate(calls):
        if n:
            inward[n], total = tie((inward[n], total))
        sources.append(added(us[n][0], inward[n], u_top, group))
        total = project(me, group[0], factors, sources[n], total)

    order = [*range(1, chunks), 0]
    lots = [order[:-1], order[-1:]] if chunks > 1 else [order]
    halves, back = [], {}
    for lot in lots:
        halves.append(halved(jnp.concatenate([vs[k][1] for k in lot], axis=1), v_top))

    def returned(n):
        back[n] = passed(halves[n], True)

    halves[0], total = tie((halves[0], total))
    returned(0)
    near, _, blocks = ladder(total)
    if len(lots) > 1:
        returned(1)
    amplitudes = amplitude(me, factors, pair_weight, near, sources)
    gathered, _ = joined(blocks, near)
    outs = []
    for n, j, k in [(n, j, k) for n, lot in enumerate(lots) for j, k in enumerate(lot)]:
        back[n], outs, gathered = tie((back[n], outs, gathered))
        base = [m[:, j * size : (j + 1) * size] for m in back[n]]
        base = added(vs[k][0], base, v_top, calls[k])
        outs = final(
            me,
            k,
            factors,
            kernels,
            weights,
            coef[: own * nf],
            gathered,
            base,
            outs,
        )
    return amplitudes, outs[0]


def solution(mesh):
    return jax.shard_map(
        shards,
        mesh=mesh,
        in_specs=(
            P("freq", "fac", None),
            P("fac", None),
            P("freq", "fac"),
            P("freq", "fac"),
            P(),
            P(),
        ),
        out_specs=(P("freq", "fac", None), P("freq", "fac", None)),
        check_vma=False,
    )
```

```python
import functools

import jax
import jax.numpy as jnp
from jax import lax
from jax.experimental import pallas as pl
from jax.experimental.pallas import tpu as pltpu
from jax.sharding import PartitionSpec as P


INNER = 2
LANES = 128
MESH = pl.DeviceIdType.MESH
CHUNK = 16
WIDE = 32
EXACT = lax.Precision.HIGHEST
R_MAX = 6.0
W_MAX = 2.0
L_MAX = 0.03125
HALF_TOP = 32768.0
VMEM = pltpu.VMEM


def tile_of(pairs):
    for blocks in (3, 4, 2, 1):
        if pairs % (blocks * LANES) == 0:
            return blocks * LANES
    return None


def wide_tile(pairs):
    for blocks in (6, 4, 3, 2, 1):
        if pairs % (blocks * LANES) == 0:
            return blocks * LANES
    return None


def mix(table, lanes, outs, count, term):
    totals = [None] * outs
    for v in range(count):
        value = term(v)
        for w in range(outs):
            row = w * count + v
            product = table[row : row + 1, lanes] * value
            totals[w] = product if totals[w] is None else totals[w] + product
    return totals


def part(i, base, chunk):
    return pl.ds(pl.multiple_of(base + i * chunk, chunk), chunk)


def rows_times(p_ref, l_ref):
    return lax.dot_general(
        p_ref[...], l_ref[...], (((1,), (1,)), ((), ())), preferred_element_type=jnp.float32
    )


def dot_exact(a, b):
    return lax.dot_general(
        a, b, (((1,), (0,)), ((), ())), precision=EXACT, preferred_element_type=jnp.float32
    )


def resident(x):
    return pl.BlockSpec(x.shape, lambda i, *_: (0,) * x.ndim, pipeline_mode=pl.Buffered(1))


def quarter_kernel(nf, parts, sets, me_ref, l_ref, k_ref, wt_ref, coef_ref, p_ref, *rest):
    own_ref, rest = rest[0], rest[1:]
    came, rest = rest[: sets * (parts - 1)], rest[sets * (parts - 1) :]
    mine_u, far_u, mine_v, far_v, table, held, turned, mid, far = rest
    own = nf // parts
    cols = own_ref.shape[2]
    table[...] = dot_exact(coef_ref[...], k_ref[...])
    held[...] = rows_times(p_ref, l_ref)

    @pl.loop(0, table.shape[1] // LANES)
    def _(block):
        lanes = part(block, 0, LANES)
        for v in range(own):
            turned[v] = own_ref[v, lanes, :].T
        for j in range(sets):

            @pl.when(pl.program_id(0) == j)
            def _():
                for v in range(own, nf):
                    turned[v] = came[j * (parts - 1) + v // own - 1][v % own, lanes, :].T

        @pl.loop(0, cols // CHUNK)
        def _(i):
            rows = part(i, 0, CHUNK)
            got = mix(
                table,
                lanes,
                nf,
                nf,
                lambda v: turned[v, rows, :]
                + wt_ref[v : v + 1, lanes] * held[part(i, v * cols, CHUNK), lanes],
            )
            for w in range(nf):
                mid[w, rows, :] = got[w]
                turned[w, rows, :] = turned[w, rows, :] + got[w]
            got = mix(table, lanes, nf, nf, lambda v: turned[v, rows, :])
            for w in range(nf):
                far[w, rows, :] = got[w]

        for w in range(nf):
            u_ref, v_ref, row = (mine_u, mine_v, w) if w < own else (far_u, far_v, w - own)
            u_ref[row, lanes, :] = mid[w].T
            v_ref[row, lanes, :] = far[w].T


def quarter_pass(me, low, factors, kernels, weights, coef, gathered, right_side, moved):
    own, pairs, cols = right_side.shape
    nf = weights.shape[0]
    parts = nf // own
    quarter = pairs // parts
    naux = factors.shape[1]
    tile = tile_of(quarter)
    sets = len(moved)
    if tile is None:
        cut = lambda x, axis: lax.dynamic_slice_in_dim(x, me * quarter, quarter, axis)
        here = jnp.concatenate([cut(right_side, 1)] + moved[0][0])
        table = jnp.einsum("jt,tp->jp", coef, cut(kernels, 1), precision=EXACT)
        table = table.reshape(nf, nf, quarter)
        wide = jnp.einsum(
            "ja,pa->jp",
            gathered,
            cut(factors, 0),
            preferred_element_type=jnp.float32,
        )
        wide = jnp.transpose(wide.reshape(nf, cols, quarter), (0, 2, 1))
        wide = here + cut(weights, 1)[:, :, None] * wide
        u = jnp.einsum("wvp,vpc->wpc", table, wide, precision=EXACT)
        v = jnp.einsum("wvp,vpc->wpc", table, here + u, precision=EXACT)
        return u[:own], u[own:], v[:own], v[own:]
    steps = quarter // tile
    at = lambda i, m: m[0] * steps + low + i
    here = lambda n: pl.BlockSpec((own, tile, cols), lambda i, m: (0, n, 0))
    outs = [(rows, sets * tile, cols) for rows in (own, nf - own)]
    pieces = [pl.BlockSpec((x[0], tile, cols), lambda i, m: (0, i, 0)) for x in outs]
    return pl.pallas_call(
        functools.partial(quarter_kernel, nf, parts, sets),
        out_shape=[jax.ShapeDtypeStruct(x, jnp.float32) for x in outs]
        + [pltpu.HBM(x, jnp.float32) for x in outs],
        grid_spec=pltpu.PrefetchScalarGridSpec(
            num_scalar_prefetch=1,
            grid=(sets,),
            in_specs=[
                pl.BlockSpec((tile, naux), lambda i, m: (at(i, m), 0)),
                pl.BlockSpec((nf, tile), lambda i, m: (0, at(i, m))),
                pl.BlockSpec((nf, tile), lambda i, m: (0, at(i, m))),
                resident(coef),
                resident(gathered),
                pl.BlockSpec((own, tile, cols), lambda i, m: (0, at(i, m), 0)),
            ]
            + [here(n) for _, n in moved for _ in range(parts - 1)],
            out_specs=pieces * 2,
            scratch_shapes=[
                VMEM((nf * nf, tile), jnp.float32),
                VMEM((nf * cols, tile), jnp.float32),
            ]
            + [VMEM((nf, cols, LANES), jnp.float32)] * 3,
        ),
        compiler_params=pltpu.CompilerParams(vmem_limit_bytes=36 << 20),
        cost_estimate=pl.CostEstimate(
            flops=2 * nf * sets * tile * cols * (naux + 32 * nf),
            bytes_accessed=16 * nf * sets * tile * cols,
            transcendentals=0,
        ),
    )(
        me.reshape(1),
        factors,
        kernels,
        weights,
        coef,
        gathered,
        right_side,
        *[x for xs, _ in moved for x in xs],
    )


def project_kernel(parts, sets, me_ref, l_ref, *rest):
    s_refs, (x_ref, o_ref) = rest[:parts], rest[parts:]
    own, _, _ = s_refs[0].shape
    i = pl.program_id(0)

    @pl.when(i == 0)
    def _():
        o_ref[...] = x_ref[...]

    for s in range(parts):

        @pl.when(lax.div(i, sets) == s)
        def _():
            rounded = [s_refs[s][f].astype(jnp.bfloat16) for f in range(own)]
            o_ref[...] += lax.dot_general(
                jnp.concatenate(rounded, axis=1),
                l_ref[...],
                (((0,), (0,)), ((), ())),
                preferred_element_type=jnp.float32,
            )


def around(parts, steps, low, sets):
    return lambda i, m: lax.rem(m[0] + lax.div(i, sets), parts) * steps + low + lax.rem(i, sets)


def project(me, low, factors, pieces, total):
    own, size, cols = pieces[0].shape
    parts = len(pieces)
    pairs, naux = factors.shape
    quarter = pairs // parts
    tile = tile_of(quarter)
    if tile is None:
        for s, x in enumerate(pieces):
            rows = lax.dynamic_slice_in_dim(
                factors, lax.rem(me + s, parts) * quarter, quarter, 0
            )
            total = total + jnp.einsum(
                "pa,fpc->fca", rows, x.astype(jnp.bfloat16), preferred_element_type=jnp.float32
            ).reshape(total.shape)
        return total
    sets = size // tile
    at = around(parts, quarter // tile, low, sets)
    stay = lambda s: lambda i, m: (0, jnp.clip(i - s * sets, 0, sets - 1), 0)
    return pl.pallas_call(
        functools.partial(project_kernel, parts, sets),
        out_shape=jax.ShapeDtypeStruct(total.shape, jnp.float32),
        grid_spec=pltpu.PrefetchScalarGridSpec(
            num_scalar_prefetch=1,
            grid=(parts * sets,),
            in_specs=[pl.BlockSpec((tile, naux), lambda i, m: (at(i, m), 0))]
            + [pl.BlockSpec((own, tile, cols), stay(s)) for s in range(parts)]
            + [resident(total)],
            out_specs=pl.BlockSpec(total.shape, lambda i, m: (0, 0)),
        ),
        compiler_params=pltpu.CompilerParams(vmem_limit_bytes=40 << 20),
        cost_estimate=pl.CostEstimate(
            flops=2 * own * parts * size * cols * naux,
            bytes_accessed=8 * own * parts * size * cols,
            transcendentals=0,
        ),
    )(me.reshape(1), factors, *pieces, total)


def again_kernel(own, l_ref, wt_ref, p_ref, x_ref, o_ref):
    cols = p_ref.shape[0] // own

    @pl.when(pl.program_id(0) == 0)
    def _():
        o_ref[...] = x_ref[...]

    wide = lax.dot_general(
        p_ref[...], l_ref[...], (((1,), (1,)), ((), ())), preferred_element_type=jnp.float32
    )
    wide = [
        (wide[f * cols : (f + 1) * cols] * wt_ref[f : f + 1, :]).astype(jnp.bfloat16)
        for f in range(own)
    ]
    o_ref[...] += lax.dot_general(
        jnp.concatenate(wide, axis=0),
        l_ref[...],
        (((1,), (0,)), ((), ())),
        preferred_element_type=jnp.float32,
    )


def again(factors, pair_weight, projected, kept):
    pairs, naux = factors.shape
    own = pair_weight.shape[0]
    tile = wide_tile(pairs)
    return pl.pallas_call(
        functools.partial(again_kernel, own),
        out_shape=jax.ShapeDtypeStruct(kept.shape, jnp.float32),
        grid=(pairs // tile,),
        in_specs=[
            pl.BlockSpec((tile, naux), lambda i: (i, 0)),
            pl.BlockSpec((own, tile), lambda i: (0, i)),
            resident(projected),
            resident(kept),
        ],
        out_specs=pl.BlockSpec(kept.shape, lambda i: (0, 0)),
        compiler_params=pltpu.CompilerParams(vmem_limit_bytes=40 << 20),
        cost_estimate=pl.CostEstimate(
            flops=4 * kept.size * pairs, bytes_accessed=2 * factors.size, transcendentals=0
        ),
    )(factors, pair_weight, projected, kept)


class Stream:
    def __init__(self, refs, buffer, sems, step):
        tile = buffer.shape[2]
        refs = [
            ref.at[:, n : n + tile, :] for ref in refs for n in range(0, ref.shape[1], tile)
        ]
        self.refs, self.buffer, self.sems = refs, buffer, sems
        self.step = step
        self.slot = lax.rem(step + 2, 2)

    def copy(self, n):
        return pltpu.make_async_copy(self.refs[n], self.buffer.at[n % 2], self.sems.at[n % 2])

    def ahead(self):
        @pl.when(pl.program_id(0) == 0)
        def _():
            self.copy(0).start()

        for n in range(1, len(self.refs)):

            @pl.when(self.step == n - 1)
            def _():
                self.copy(n).start()

    def here(self):
        pltpu.make_async_copy(
            self.refs[0], self.buffer.at[self.slot], self.sems.at[self.slot]
        ).wait()
        return self.buffer.at[self.slot]


def stream_scratch(own, tile, cols):
    return [VMEM((2, own, tile, cols), jnp.float32), pltpu.SemaphoreType.DMA((2,))]


ANYWHERE = pl.BlockSpec(memory_space=pl.ANY)


def amplitude_kernel(pieces, me_ref, l_ref, wt_ref, p_ref, *rest):
    refs, (a_ref, buffer, sems) = rest[:pieces], rest[pieces:]
    own, tile, cols = a_ref.shape
    stream = Stream(refs, buffer, sems, pl.program_id(0))
    stream.ahead()
    wide = rows_times(p_ref, l_ref)
    here = stream.here()
    for f in range(own):
        scaled = wide[f * cols : (f + 1) * cols] * wt_ref[f : f + 1, :]
        for k in range(0, tile, LANES):
            lanes = slice(k, k + LANES)
            a_ref[f, lanes, :] = here[f, lanes, :] + scaled[:, lanes].T


def amplitude(me, factors, pair_weight, near, sources):
    own, _, cols = sources[0][0].shape
    parts = len(sources[0])
    pairs, naux = factors.shape
    quarter = pairs // parts
    size = tile_of(quarter)
    if size is None:
        wide = jnp.einsum("ja,pa->jp", near, factors, preferred_element_type=jnp.float32)
        wide = jnp.transpose(wide.reshape(own, cols, pairs), (0, 2, 1))
        result = wide * pair_weight[:, :, None]
        for s in range(parts):
            at = lax.rem(me + s, parts) * quarter
            part_of = lax.dynamic_slice_in_dim(result, at, quarter, 1) + sources[0][s]
            result = lax.dynamic_update_slice_in_dim(result, part_of, at, 1)
        return result
    steps = quarter // size
    pieces = [x for group in sources for x in group]
    at = lambda i, m: lax.rem(m[0] + lax.rem(i, parts), parts) * steps + lax.div(i, parts)
    return pl.pallas_call(
        functools.partial(amplitude_kernel, len(pieces)),
        out_shape=jax.ShapeDtypeStruct((own, pairs, cols), jnp.float32),
        grid_spec=pltpu.PrefetchScalarGridSpec(
            num_scalar_prefetch=1,
            grid=(parts * steps,),
            in_specs=[
                pl.BlockSpec((size, naux), lambda i, m: (at(i, m), 0)),
                pl.BlockSpec((own, size), lambda i, m: (0, at(i, m))),
                resident(near),
            ]
            + [ANYWHERE] * len(pieces),
            out_specs=pl.BlockSpec((own, size, cols), lambda i, m: (0, at(i, m), 0)),
            scratch_shapes=stream_scratch(own, size, cols),
        ),
        compiler_params=pltpu.CompilerParams(vmem_limit_bytes=20 << 20),
        cost_estimate=pl.CostEstimate(
            flops=2 * own * pairs * cols * naux,
            bytes_accessed=8 * own * pairs * cols,
            transcendentals=0,
        ),
    )(me.reshape(1), factors, pair_weight, near, *pieces)


def final_kernel(nf, parts, held_outs, me_ref, l_ref, k_ref, wt_ref, coef_ref, p_ref, *rest):
    b_refs, rest = rest[:parts], rest[parts + held_outs :]
    new_ref, table, held, mid, buffer, sems = rest
    own, _, cols = new_ref.shape
    stream = Stream(b_refs, buffer, sems, pl.program_id(0))
    stream.ahead()
    table[...] = dot_exact(coef_ref[...], k_ref[...])
    for w in range(own):
        rows = slice(w * nf, (w + 1) * nf)
        table[rows, :] = table[rows, :] * wt_ref[...]
    held[...] = rows_times(p_ref, l_ref)
    here = stream.here()

    @pl.loop(0, table.shape[1] // LANES)
    def _(block):
        lanes = part(block, 0, LANES)

        @pl.loop(0, cols // WIDE)
        def _(i):
            rows = part(i, 0, WIDE)
            got = mix(table, lanes, own, nf, lambda v: held[part(i, v * cols, WIDE), lanes])
            for w in range(own):
                mid[w, rows, :] = got[w]

        for w in range(own):
            new_ref[w, lanes, :] = here[w, lanes, :] + mid[w].T


def final(me, low, factors, kernels, weights, coef, gathered, base, outs):
    own, span, cols = base[0].shape
    parts = len(base)
    nf = weights.shape[0]
    pairs, naux = factors.shape
    quarter = pairs // parts
    tile = tile_of(quarter)
    if tile is None:
        wide = jnp.einsum(
            "ja,pa->jp",
            gathered,
            factors,
            preferred_element_type=jnp.float32,
        )
        wide = jnp.transpose(wide.reshape(nf, cols, pairs), (0, 2, 1)) * weights[:, :, None]
        table = jnp.einsum("jt,tp->jp", coef, kernels, precision=EXACT).reshape(own, nf, pairs)
        new = jnp.einsum("wvp,vpc->wpc", table, wide, precision=EXACT)
        for s in range(parts):
            at = lax.rem(me + s, parts) * quarter
            part_of = lax.dynamic_slice_in_dim(new, at, quarter, 1) + base[s]
            new = lax.dynamic_update_slice_in_dim(new, part_of, at, 1)
        return [new]
    size = tile
    sets = span // size
    at = around(parts, quarter // size, low, sets)
    result = pl.pallas_call(
        functools.partial(final_kernel, nf, parts, len(outs)),
        out_shape=jax.ShapeDtypeStruct((own, pairs, cols), jnp.float32),
        grid_spec=pltpu.PrefetchScalarGridSpec(
            num_scalar_prefetch=1,
            grid=(parts * sets,),
            in_specs=[
                pl.BlockSpec((size, naux), lambda i, m: (at(i, m), 0)),
                pl.BlockSpec((nf, size), lambda i, m: (0, at(i, m))),
                pl.BlockSpec((nf, size), lambda i, m: (0, at(i, m))),
                resident(coef),
                resident(gathered),
            ]
            + [ANYWHERE] * (parts + len(outs)),
            out_specs=pl.BlockSpec((own, size, cols), lambda i, m: (0, at(i, m), 0)),
            scratch_shapes=[
                VMEM((own * nf, size), jnp.float32),
                VMEM((nf * cols, size), jnp.float32),
                VMEM((own, cols, LANES), jnp.float32),
            ]
            + stream_scratch(own, size, cols),
        ),
        input_output_aliases={6 + parts + n: n for n in range(len(outs))},
        compiler_params=pltpu.CompilerParams(vmem_limit_bytes=26 << 20),
        cost_estimate=pl.CostEstimate(
            flops=2 * nf * parts * span * cols * naux,
            bytes_accessed=8 * own * parts * span * cols,
            transcendentals=0,
        ),
    )(me.reshape(1), factors, kernels, weights, coef, gathered, *base, *outs)
    return [result]


class Plane:
    def __init__(self, chips):
        self.chips = chips
        me = lax.axis_index("fac")
        self.core = lax.rem(me, 2)
        self.chip = lax.div(me, 2)
        self.pal = {"fac": me + 1 - 2 * self.core}
        self.started = []

    def on(self, d):
        return lax.rem(self.chip + d + self.chips, self.chips)

    def at(self, d):
        return {"fac": self.on(d) * 2 + self.core}

    def chip_at(self, chip):
        return {"fac": chip * 2 + self.core}

    def greet(self):
        barrier = pltpu.get_barrier_semaphore()
        for other in [self.pal] + [self.at(d) for d in range(1, self.chips)]:
            pl.semaphore_signal(barrier, inc=1, device_id=other, device_id_type=MESH)
        pl.semaphore_wait(barrier, self.chips)

    def send(self, src, dst, sems, at, to):
        copy = pltpu.make_async_remote_copy(
            src_ref=src,
            dst_ref=dst,
            send_sem=sems[0].at[at],
            recv_sem=sems[1].at[at],
            device_id=to,
            device_id_type=MESH,
        )
        copy.start()
        self.started.append(copy)
        return copy

    def end(self):
        for copy in self.started:
            copy.wait_send()


def reduced(plane, x_ref, near, red, land, mine, near_sems, red_sems):
    chips, chip, core, pal = plane.chips, plane.chip, plane.core, plane.pal
    nears = {}
    for d in list(range(1, chips)) + [0]:
        nears[d] = plane.send(x_ref.at[plane.on(d), 1 - core], near.at[d], near_sems, d, pal)
    block = mine.shape[0]
    step = min(block, 16)
    reds = []
    for d in range(1, chips):
        nears[d].wait_recv()
        for r in range(0, block, step):
            rows = slice(r, r + step)
            red[d, rows, :] = (x_ref[plane.on(d), core, rows, :] + near[d, rows, :]).astype(
                red.dtype
            )
        reds.append(plane.send(red.at[d], land.at[d], red_sems, d, plane.at(d)))
    nears[0].wait_recv()
    for copy in reds:
        copy.wait_recv()
    for r in range(0, block, step):
        rows = slice(r, r + step)
        total = x_ref[chip, core, rows, :] + near[0, rows, :]
        for d in range(1, chips):
            total = total + land[d, rows, :].astype(jnp.float32)
        mine[rows, :] = total.astype(mine.dtype)


def reduce_kernel(chips, x_ref, o_ref, near, red, land, *sems):
    plane = Plane(chips)
    plane.greet()
    reduced(plane, x_ref, near, red, land, o_ref, sems[0:2], sems[2:4])
    plane.end()


def sum_kernel(chips, x_ref, o_ref, near, red, land, mine, joined, *sems):
    plane = Plane(chips)
    chip, core = plane.chip, plane.core
    plane.greet()
    reduced(plane, x_ref, near, red, land, mine, sems[0:2], sems[2:4])
    here = joined.at[chip, core]
    keep = pltpu.make_async_copy(mine, here, sems[8])
    keep.start()
    keep.wait()
    wides = [plane.send(here, here, sems[4:6], d, plane.at(d)) for d in range(1, chips)]
    pairs = [plane.send(here, here, sems[6:8], 0, plane.pal)]
    for d, copy in enumerate(wides, 1):
        copy.wait_recv()
        there = joined.at[plane.on(-d), core]
        pairs.append(plane.send(there, there, sems[6:8], d, plane.pal))
    for copy in pairs:
        copy.wait_recv()
    plane.end()
    for c in range(chips):
        o_ref[c] = joined[c]


def gather_kernel(chips, parts, x_ref, *refs):
    near_ref = None
    if len(refs) > 8:
        near_ref, refs = refs[0], refs[1:]
    o_ref, top_ref, joined, *sems = refs
    skip = 0 if near_ref is None else 1
    x_refs = [x_ref.at[s] for s in range(parts)]
    kept = sems[4]
    plane = Plane(chips)
    chip, core, pal = plane.chip, plane.core, plane.pal
    plane.greet()
    wide_sems, pair_sems = sems[0:2], sems[2:4]
    pairs = []
    copies = []
    for s in range(parts):
        copies.append(
            pltpu.make_async_copy(x_refs[s], joined.at[s, chip, core], kept.at[s])
        )
        copies[-1].start()
    square = chips == 4
    column, row = lax.rem(chip, 2), lax.div(chip, 2)
    across, along = chip + 1 - 2 * column, chip + 2 - 4 * row
    corner = along + 1 - 2 * column
    wides = []
    for s in range(parts):
        src, dst = x_refs[s], joined.at[s, chip, core]
        if square:
            for n, to in enumerate((across, along)):
                copy = plane.send(src, dst, wide_sems, s * chips + n, plane.chip_at(to))
                wides.append((s, n, copy))
        else:
            for d in range(1, chips):
                copy = plane.send(src, dst, wide_sems, s * chips + d, plane.at(d))
                wides.append((s, d, copy))
    for s in range(parts):
        pairs.append(
            plane.send(x_refs[s], joined.at[s, chip, core], pair_sems, s * chips, pal)
        )
    late = []
    for s, d, copy in wides:
        copy.wait_recv()
        chip_from = (across, along)[d] if square else plane.on(-d)
        there = joined.at[s, chip_from, core]
        if square and d == s % 2:
            other = (along, across)[d]
            turned = plane.send(there, there, wide_sems, s * chips + 2, plane.chip_at(other))
            late.append((s, turned))
        at = s * chips + (1 + d if square else d)
        pairs.append(plane.send(there, there, pair_sems, at, pal))
    for s, copy in late:
        copy.wait_recv()
        there = joined.at[s, corner, core]
        pairs.append(plane.send(there, there, pair_sems, s * chips + 3, pal))
    for copy in pairs:
        copy.wait_recv()
    plane.end()
    for copy in copies:
        copy.wait()
    if skip:
        o_ref[0] = near_ref[...]
    top = jnp.zeros(top_ref.shape, jnp.float32)
    for s in range(parts):

        def fold(c, top):
            here = joined[s, c]
            o_ref[s + skip, c] = here
            here = jnp.abs(here.astype(jnp.float32))
            sums = here[..., :LANES]
            for k in range(LANES, here.shape[-1], LANES):
                sums = sums + here[..., k : k + LANES]
            return jnp.maximum(top, jnp.max(sums.reshape((-1,) + top.shape), axis=0))

        top = lax.fori_loop(0, chips, fold, top)
    top_ref[...] = top


def dmas(count, pairs):
    return [pltpu.SemaphoreType.DMA((count,))] * (2 * pairs)


def reach_params(cid):
    return pltpu.CompilerParams(
        collective_id=cid, has_side_effects=True, vmem_limit_bytes=24 << 20
    )


def reach_cost(size):
    return pl.CostEstimate(flops=40 * size, bytes_accessed=40 * size, transcendentals=0)


WHOLE = pl.BlockSpec(memory_space=VMEM)


def summed(x, all_blocks):
    n = lax.axis_size("fac")
    chips = n // 2
    rows, width = x.shape
    block = rows // n
    flat = (chips, 2, block, width)
    landing = [
        VMEM((chips, block, width), jnp.float32),
        VMEM((chips, block, width), jnp.bfloat16),
        VMEM((chips, block, width), jnp.bfloat16),
    ]
    if not all_blocks:
        return pl.pallas_call(
            functools.partial(reduce_kernel, chips),
            out_shape=jax.ShapeDtypeStruct((block, width), jnp.bfloat16),
            in_specs=[WHOLE],
            out_specs=WHOLE,
            scratch_shapes=landing + dmas(chips, 2),
            compiler_params=reach_params(1),
            cost_estimate=reach_cost(x.size // 2),
        )(x.reshape(flat))
    result = pl.pallas_call(
        functools.partial(sum_kernel, chips),
        out_shape=jax.ShapeDtypeStruct(flat, jnp.bfloat16),
        in_specs=[WHOLE],
        out_specs=WHOLE,
        scratch_shapes=landing
        + [VMEM((block, width), jnp.bfloat16), VMEM(flat, jnp.bfloat16)]
        + dmas(chips, 4)
        + [pltpu.SemaphoreType.DMA],
        compiler_params=reach_params(0),
        cost_estimate=reach_cost(x.size),
    )(x.reshape(flat))
    return result.reshape(rows, width)


def gathered_over(blocks, near=None):
    n = lax.axis_size("fac")
    chips = n // 2
    parts, block, width = blocks.shape
    flat = (chips, 2, block, width)
    result, top = pl.pallas_call(
        functools.partial(gather_kernel, chips, parts),
        out_shape=(
            jax.ShapeDtypeStruct((parts + (near is not None),) + flat, jnp.bfloat16),
            jax.ShapeDtypeStruct((8, LANES), jnp.float32),
        ),
        in_specs=[WHOLE] * (1 if near is None else 2),
        out_specs=(WHOLE, WHOLE),
        scratch_shapes=[VMEM((parts,) + flat, jnp.bfloat16)]
        + dmas(parts * chips, 2)
        + [pltpu.SemaphoreType.DMA((parts,))],
        compiler_params=reach_params(2 if parts == 1 else 3),
        cost_estimate=reach_cost(block * width * parts * 8),
    )(blocks, *(() if near is None else (near.reshape(flat),)))
    return result.reshape(-1, width), top


def shards(right_side, factors, pair_weight, second_order, forward, backward):
    own, pairs, cols = right_side.shape
    nf = forward.shape[0]
    naux = factors.shape[1]
    parts = nf // own
    quarter = pairs // parts
    me = lax.axis_index("freq")

    def shift(x, by):
        if by == 0:
            return x
        return lax.ppermute(x, "freq", [(i, (i + by) % parts) for i in range(parts)])

    order = jnp.concatenate(
        [lax.rem(me - s + parts, parts) * own + jnp.arange(own) for s in range(parts)]
    )
    pick = jax.nn.one_hot(order, nf, dtype=jnp.float32)
    ahead = jnp.einsum("ts,sv,wv->tw", pick, forward, pick, precision=EXACT)
    back = jnp.einsum("ws,st,vt->wv", pick, backward, pick, precision=EXACT)
    coef = (back[:, None, :] * ahead.T[None, :, :]).reshape(nf * nf, nf)
    reach = jnp.max(
        jnp.sum(
            jnp.einsum("wt,tv->wv", jnp.abs(backward), jnp.abs(forward), precision=EXACT), axis=1
        )
    )

    both = jnp.stack([pair_weight, second_order])
    fine = HALF_TOP / 2.0
    slim = (both * fine).astype(jnp.float16)
    came = [shift(slim, s) for s in range(1, parts)]
    tables = [both] + [x.astype(jnp.float32) * (1.0 / fine) for x in came]
    weights, kernels = [jnp.concatenate([x[n] for x in tables]) for n in range(2)]
    size = tile_of(quarter) or quarter
    chunks = quarter // size
    early = max(chunks - 1, 1)
    groups = [(0, early)] + ([(early, chunks)] if early < chunks else [])
    calls = [(k, k + 1) for k in range(chunks)]
    tie = lax.optimization_barrier
    up = 8192.0

    def sliced(x, s, low, high):
        at = lax.rem(me + s, parts) * quarter + low * size
        return lax.dynamic_slice_in_dim(x, at, (high - low) * size, 1)

    def leaving(low, high):
        return [(sliced(right_side, s, low, high) * up).astype(jnp.float16) for s in range(1, parts)]

    def passed(blocks, back):
        return [
            shift(b, parts - 1 - s if back else s + 1) for s, b in enumerate(blocks)
        ]

    def first_projection():
        return jnp.einsum(
            "pa,fpc->fca",
            factors,
            right_side.astype(jnp.bfloat16),
            preferred_element_type=jnp.float32,
        ).reshape(own * cols, naux)

    def ladder(kept):
        total = kept
        for _ in range(INNER - 1):
            mine = summed(total, True)
            total = again(factors, pair_weight, mine, kept)
        block = summed(total, False)
        far = [shift(block, s) for s in range(1, parts)]
        return *gathered_over(block[None]), far

    def joined(blocks, near):
        blocks = jnp.stack(blocks)
        return gathered_over(blocks, near)

    leaves = []
    for g in groups:
        leaves.append(leaving(*g))
    right_late, leaves[-1] = tie((right_side, leaves[-1]))
    came = [passed(x, False) for x in leaves]
    near, near_top, blocks = ladder(first_projection())
    gathered, far_top = joined(blocks, near)
    height = jnp.sum(jnp.max(jnp.maximum(near_top, far_top), axis=0))
    u_top = jnp.maximum(1.01 * reach * (R_MAX + W_MAX * L_MAX * height), 1e-30)
    v_top = jnp.maximum(1.01 * reach * (R_MAX + u_top), 1e-30)

    def halved(far, top):
        blocks = [far[s * own : (s + 1) * own] for s in range(parts - 1)]
        return [(b * (HALF_TOP / top)).astype(jnp.float16) for b in blocks]

    def added(first, rest, top, group):
        rest = [b.astype(jnp.float32) * (top / HALF_TOP) for b in rest]
        return [sliced(right_late, s, *group) + b for s, b in enumerate([first] + rest)]

    us, vs, inward = [], [], []
    for n, (low, high) in enumerate(calls):
        at = next(g for g, (first, end) in enumerate(groups) if first <= low < end)
        moved = came[at]
        if n:
            moved, _ = tie((moved, us[-1][1]))
        start = (low - groups[at][0]) * size
        moved = [
            m[:, start : start + size].astype(jnp.float32) * (1.0 / up) for m in moved
        ]
        mine_u, far_u, mine_v, far_v = quarter_pass(
            me,
            low,
            factors,
            kernels,
            weights,
            coef,
            gathered,
            right_side,
            [(moved, 0)],
        )
        inward.append(passed(halved(far_u, u_top), True))
        us.append((mine_u, far_u))
        vs.append((mine_v, far_v))
    sources = []
    total = jnp.zeros((own * cols, naux), jnp.float32)
    for n, group in enumerate(calls):
        if n:
            inward[n], total = tie((inward[n], total))
        sources.append(added(us[n][0], inward[n], u_top, group))
        total = project(me, group[0], factors, sources[n], total)

    halves, back = [], {}
    for n in range(chunks):
        halves.append(halved(vs[n][1], v_top))

    def returned(n):
        back[n] = passed(halves[n], True)

    halves[0], total = tie((halves[0], total))
    returned(0)
    near, _, blocks = ladder(total)
    for n in range(1, chunks):
        returned(n)
    amplitudes = amplitude(me, factors, pair_weight, near, sources)
    gathered, _ = joined(blocks, near)
    outs = []
    for k in range(chunks):
        back[k], outs = tie((back[k], outs))
        base = added(vs[k][0], back[k], v_top, calls[k])
        outs = final(
            me,
            k,
            factors,
            kernels,
            weights,
            coef[: own * nf],
            gathered,
            base,
            outs,
        )
    return amplitudes, outs[0]


def solution(mesh):
    return jax.shard_map(
        shards,
        mesh=mesh,
        in_specs=(
            P("freq", "fac", None),
            P("fac", None),
            P("freq", "fac"),
            P("freq", "fac"),
            P(),
            P(),
        ),
        out_specs=(P("freq", "fac", None), P("freq", "fac", None)),
        check_vma=False,
    )
```

```python
import functools

import jax
import jax.numpy as jnp
from jax import lax
from jax.experimental import pallas as pl
from jax.experimental.pallas import tpu as pltpu
from jax.sharding import PartitionSpec as P


INNER = 2
LANES = 128
MESH = pl.DeviceIdType.MESH
CHUNK = 16
WIDE = 32
EXACT = lax.Precision.HIGHEST
R_MAX = 6.0
W_MAX = 2.0
L_MAX = 0.03125
HALF_TOP = 32768.0
VMEM = pltpu.VMEM


def tile_of(pairs):
    for blocks in (3, 4, 2, 1):
        if pairs % (blocks * LANES) == 0:
            return blocks * LANES
    return None


def wide_tile(pairs):
    for blocks in (6, 4, 3, 2, 1):
        if pairs % (blocks * LANES) == 0:
            return blocks * LANES
    return None


def mix(table, lanes, outs, count, term):
    totals = [None] * outs
    for v in range(count):
        value = term(v)
        for w in range(outs):
            row = w * count + v
            product = table[row : row + 1, lanes] * value
            totals[w] = product if totals[w] is None else totals[w] + product
    return totals


def part(i, base, chunk):
    return pl.ds(pl.multiple_of(base + i * chunk, chunk), chunk)


def rows_times(p_ref, l_ref):
    return lax.dot_general(
        p_ref[...], l_ref[...], (((1,), (1,)), ((), ())), preferred_element_type=jnp.float32
    )


def dot_exact(a, b):
    return lax.dot_general(
        a, b, (((1,), (0,)), ((), ())), precision=EXACT, preferred_element_type=jnp.float32
    )


def resident(x):
    return pl.BlockSpec(x.shape, lambda i, *_: (0,) * x.ndim, pipeline_mode=pl.Buffered(1))


def quarter_kernel(nf, parts, sets, me_ref, l_ref, k_ref, wt_ref, coef_ref, p_ref, *rest):
    own_ref, rest = rest[0], rest[1:]
    came, rest = rest[: sets * (parts - 1)], rest[sets * (parts - 1) :]
    mine_u, far_u, mine_v, far_v, table, held, turned, mid, far = rest
    own = nf // parts
    cols = own_ref.shape[2]
    table[...] = dot_exact(coef_ref[...], k_ref[...])
    held[...] = rows_times(p_ref, l_ref)

    @pl.loop(0, table.shape[1] // LANES)
    def _(block):
        lanes = part(block, 0, LANES)
        for v in range(own):
            turned[v] = own_ref[v, lanes, :].T
        for j in range(sets):

            @pl.when(pl.program_id(0) == j)
            def _():
                for v in range(own, nf):
                    turned[v] = came[j * (parts - 1) + v // own - 1][v % own, lanes, :].T

        @pl.loop(0, cols // CHUNK)
        def _(i):
            rows = part(i, 0, CHUNK)
            got = mix(
                table,
                lanes,
                nf,
                nf,
                lambda v: turned[v, rows, :]
                + wt_ref[v : v + 1, lanes] * held[part(i, v * cols, CHUNK), lanes],
            )
            for w in range(nf):
                mid[w, rows, :] = got[w]
                turned[w, rows, :] = turned[w, rows, :] + got[w]
            got = mix(table, lanes, nf, nf, lambda v: turned[v, rows, :])
            for w in range(nf):
                far[w, rows, :] = got[w]

        for w in range(nf):
            u_ref, v_ref, row = (mine_u, mine_v, w) if w < own else (far_u, far_v, w - own)
            u_ref[row, lanes, :] = mid[w].T
            v_ref[row, lanes, :] = far[w].T


def quarter_pass(me, low, factors, kernels, weights, coef, gathered, right_side, moved):
    own, pairs, cols = right_side.shape
    nf = weights.shape[0]
    parts = nf // own
    quarter = pairs // parts
    naux = factors.shape[1]
    tile = tile_of(quarter)
    sets = len(moved)
    if tile is None:
        cut = lambda x, axis: lax.dynamic_slice_in_dim(x, me * quarter, quarter, axis)
        here = jnp.concatenate([cut(right_side, 1)] + moved[0][0])
        table = jnp.einsum("jt,tp->jp", coef, cut(kernels, 1), precision=EXACT)
        table = table.reshape(nf, nf, quarter)
        wide = jnp.einsum(
            "ja,pa->jp",
            gathered,
            cut(factors, 0),
            preferred_element_type=jnp.float32,
        )
        wide = jnp.transpose(wide.reshape(nf, cols, quarter), (0, 2, 1))
        wide = here + cut(weights, 1)[:, :, None] * wide
        u = jnp.einsum("wvp,vpc->wpc", table, wide, precision=EXACT)
        v = jnp.einsum("wvp,vpc->wpc", table, here + u, precision=EXACT)
        return u[:own], u[own:], v[:own], v[own:]
    steps = quarter // tile
    at = lambda i, m: m[0] * steps + low + i
    here = lambda n: pl.BlockSpec((own, tile, cols), lambda i, m: (0, n, 0))
    outs = [(rows, sets * tile, cols) for rows in (own, nf - own)]
    pieces = [pl.BlockSpec((x[0], tile, cols), lambda i, m: (0, i, 0)) for x in outs]
    return pl.pallas_call(
        functools.partial(quarter_kernel, nf, parts, sets),
        out_shape=[jax.ShapeDtypeStruct(x, jnp.float32) for x in outs]
        + [pltpu.HBM(x, jnp.float32) for x in outs],
        grid_spec=pltpu.PrefetchScalarGridSpec(
            num_scalar_prefetch=1,
            grid=(sets,),
            in_specs=[
                pl.BlockSpec((tile, naux), lambda i, m: (at(i, m), 0)),
                pl.BlockSpec((nf, tile), lambda i, m: (0, at(i, m))),
                pl.BlockSpec((nf, tile), lambda i, m: (0, at(i, m))),
                resident(coef),
                resident(gathered),
                pl.BlockSpec((own, tile, cols), lambda i, m: (0, at(i, m), 0)),
            ]
            + [here(n) for _, n in moved for _ in range(parts - 1)],
            out_specs=pieces * 2,
            scratch_shapes=[
                VMEM((nf * nf, tile), jnp.float32),
                VMEM((nf * cols, tile), jnp.float32),
            ]
            + [VMEM((nf, cols, LANES), jnp.float32)] * 3,
        ),
        compiler_params=pltpu.CompilerParams(vmem_limit_bytes=36 << 20),
        cost_estimate=pl.CostEstimate(
            flops=2 * nf * sets * tile * cols * (naux + 32 * nf),
            bytes_accessed=16 * nf * sets * tile * cols,
            transcendentals=0,
        ),
    )(
        me.reshape(1),
        factors,
        kernels,
        weights,
        coef,
        gathered,
        right_side,
        *[x for xs, _ in moved for x in xs],
    )


def project_kernel(parts, sets, me_ref, l_ref, *rest):
    s_refs, (x_ref, o_ref) = rest[:parts], rest[parts:]
    own, _, _ = s_refs[0].shape
    i = pl.program_id(0)

    @pl.when(i == 0)
    def _():
        o_ref[...] = x_ref[...]

    for s in range(parts):

        @pl.when(lax.div(i, sets) == s)
        def _():
            rounded = [s_refs[s][f].astype(jnp.bfloat16) for f in range(own)]
            o_ref[...] += lax.dot_general(
                jnp.concatenate(rounded, axis=1),
                l_ref[...],
                (((0,), (0,)), ((), ())),
                preferred_element_type=jnp.float32,
            )


def around(parts, steps, low, sets):
    return lambda i, m: lax.rem(m[0] + lax.div(i, sets), parts) * steps + low + lax.rem(i, sets)


def project(me, low, factors, pieces, total):
    own, size, cols = pieces[0].shape
    parts = len(pieces)
    pairs, naux = factors.shape
    quarter = pairs // parts
    tile = tile_of(quarter)
    if tile is None:
        for s, x in enumerate(pieces):
            rows = lax.dynamic_slice_in_dim(
                factors, lax.rem(me + s, parts) * quarter, quarter, 0
            )
            total = total + jnp.einsum(
                "pa,fpc->fca", rows, x.astype(jnp.bfloat16), preferred_element_type=jnp.float32
            ).reshape(total.shape)
        return total
    sets = size // tile
    at = around(parts, quarter // tile, low, sets)
    stay = lambda s: lambda i, m: (0, jnp.clip(i - s * sets, 0, sets - 1), 0)
    return pl.pallas_call(
        functools.partial(project_kernel, parts, sets),
        out_shape=jax.ShapeDtypeStruct(total.shape, jnp.float32),
        grid_spec=pltpu.PrefetchScalarGridSpec(
            num_scalar_prefetch=1,
            grid=(parts * sets,),
            in_specs=[pl.BlockSpec((tile, naux), lambda i, m: (at(i, m), 0))]
            + [pl.BlockSpec((own, tile, cols), stay(s)) for s in range(parts)]
            + [resident(total)],
            out_specs=pl.BlockSpec(total.shape, lambda i, m: (0, 0)),
        ),
        compiler_params=pltpu.CompilerParams(vmem_limit_bytes=18 << 20),
        cost_estimate=pl.CostEstimate(
            flops=2 * own * parts * size * cols * naux,
            bytes_accessed=8 * own * parts * size * cols,
            transcendentals=0,
        ),
    )(me.reshape(1), factors, *pieces, total)


def again_kernel(own, l_ref, wt_ref, p_ref, x_ref, o_ref):
    cols = p_ref.shape[0] // own

    @pl.when(pl.program_id(0) == 0)
    def _():
        o_ref[...] = x_ref[...]

    wide = lax.dot_general(
        p_ref[...], l_ref[...], (((1,), (1,)), ((), ())), preferred_element_type=jnp.float32
    )
    wide = [
        (wide[f * cols : (f + 1) * cols] * wt_ref[f : f + 1, :]).astype(jnp.bfloat16)
        for f in range(own)
    ]
    o_ref[...] += lax.dot_general(
        jnp.concatenate(wide, axis=0),
        l_ref[...],
        (((1,), (0,)), ((), ())),
        preferred_element_type=jnp.float32,
    )


def again(factors, pair_weight, projected, kept):
    pairs, naux = factors.shape
    own = pair_weight.shape[0]
    tile = wide_tile(pairs)
    return pl.pallas_call(
        functools.partial(again_kernel, own),
        out_shape=jax.ShapeDtypeStruct(kept.shape, jnp.float32),
        grid=(pairs // tile,),
        in_specs=[
            pl.BlockSpec((tile, naux), lambda i: (i, 0)),
            pl.BlockSpec((own, tile), lambda i: (0, i)),
            resident(projected),
            resident(kept),
        ],
        out_specs=pl.BlockSpec(kept.shape, lambda i: (0, 0)),
        compiler_params=pltpu.CompilerParams(vmem_limit_bytes=18 << 20),
        cost_estimate=pl.CostEstimate(
            flops=4 * kept.size * pairs, bytes_accessed=2 * factors.size, transcendentals=0
        ),
    )(factors, pair_weight, projected, kept)


class Stream:
    def __init__(self, refs, buffer, sems, step):
        tile = buffer.shape[2]
        refs = [
            ref.at[:, n : n + tile, :] for ref in refs for n in range(0, ref.shape[1], tile)
        ]
        self.refs, self.buffer, self.sems = refs, buffer, sems
        self.step = step
        self.slot = lax.rem(step + 2, 2)

    def copy(self, n):
        return pltpu.make_async_copy(self.refs[n], self.buffer.at[n % 2], self.sems.at[n % 2])

    def ahead(self):
        @pl.when(pl.program_id(0) == 0)
        def _():
            self.copy(0).start()

        for n in range(1, len(self.refs)):

            @pl.when(self.step == n - 1)
            def _():
                self.copy(n).start()

    def here(self):
        pltpu.make_async_copy(
            self.refs[0], self.buffer.at[self.slot], self.sems.at[self.slot]
        ).wait()
        return self.buffer.at[self.slot]


def stream_scratch(own, tile, cols):
    return [VMEM((2, own, tile, cols), jnp.float32), pltpu.SemaphoreType.DMA((2,))]


ANYWHERE = pl.BlockSpec(memory_space=pl.ANY)


def amplitude_kernel(pieces, me_ref, l_ref, wt_ref, p_ref, *rest):
    refs, (a_ref, buffer, sems) = rest[:pieces], rest[pieces:]
    own, tile, cols = a_ref.shape
    stream = Stream(refs, buffer, sems, pl.program_id(0))
    stream.ahead()
    wide = rows_times(p_ref, l_ref)
    here = stream.here()
    for f in range(own):
        scaled = wide[f * cols : (f + 1) * cols] * wt_ref[f : f + 1, :]
        for k in range(0, tile, LANES):
            lanes = slice(k, k + LANES)
            a_ref[f, lanes, :] = here[f, lanes, :] + scaled[:, lanes].T


def amplitude(me, factors, pair_weight, near, sources):
    own, _, cols = sources[0][0].shape
    parts = len(sources[0])
    pairs, naux = factors.shape
    quarter = pairs // parts
    size = tile_of(quarter)
    if size is None:
        wide = jnp.einsum("ja,pa->jp", near, factors, preferred_element_type=jnp.float32)
        wide = jnp.transpose(wide.reshape(own, cols, pairs), (0, 2, 1))
        result = wide * pair_weight[:, :, None]
        for s in range(parts):
            at = lax.rem(me + s, parts) * quarter
            part_of = lax.dynamic_slice_in_dim(result, at, quarter, 1) + sources[0][s]
            result = lax.dynamic_update_slice_in_dim(result, part_of, at, 1)
        return result
    steps = quarter // size
    pieces = [x for group in sources for x in group]
    at = lambda i, m: lax.rem(m[0] + lax.rem(i, parts), parts) * steps + lax.div(i, parts)
    return pl.pallas_call(
        functools.partial(amplitude_kernel, len(pieces)),
        out_shape=jax.ShapeDtypeStruct((own, pairs, cols), jnp.float32),
        grid_spec=pltpu.PrefetchScalarGridSpec(
            num_scalar_prefetch=1,
            grid=(parts * steps,),
            in_specs=[
                pl.BlockSpec((size, naux), lambda i, m: (at(i, m), 0)),
                pl.BlockSpec((own, size), lambda i, m: (0, at(i, m))),
                resident(near),
            ]
            + [ANYWHERE] * len(pieces),
            out_specs=pl.BlockSpec((own, size, cols), lambda i, m: (0, at(i, m), 0)),
            scratch_shapes=stream_scratch(own, size, cols),
        ),
        compiler_params=pltpu.CompilerParams(vmem_limit_bytes=13 << 20),
        cost_estimate=pl.CostEstimate(
            flops=2 * own * pairs * cols * naux,
            bytes_accessed=8 * own * pairs * cols,
            transcendentals=0,
        ),
    )(me.reshape(1), factors, pair_weight, near, *pieces)


def final_kernel(nf, parts, held_outs, me_ref, l_ref, k_ref, wt_ref, coef_ref, p_ref, *rest):
    b_refs, rest = rest[:parts], rest[parts + held_outs :]
    new_ref, table, held, mid, buffer, sems = rest
    own, _, cols = new_ref.shape
    stream = Stream(b_refs, buffer, sems, pl.program_id(0))
    stream.ahead()
    table[...] = dot_exact(coef_ref[...], k_ref[...])
    for w in range(own):
        rows = slice(w * nf, (w + 1) * nf)
        table[rows, :] = table[rows, :] * wt_ref[...]
    held[...] = rows_times(p_ref, l_ref)
    here = stream.here()

    @pl.loop(0, table.shape[1] // LANES)
    def _(block):
        lanes = part(block, 0, LANES)

        @pl.loop(0, cols // WIDE)
        def _(i):
            rows = part(i, 0, WIDE)
            got = mix(table, lanes, own, nf, lambda v: held[part(i, v * cols, WIDE), lanes])
            for w in range(own):
                mid[w, rows, :] = got[w]

        for w in range(own):
            new_ref[w, lanes, :] = here[w, lanes, :] + mid[w].T


def final(me, low, factors, kernels, weights, coef, gathered, base, outs):
    own, span, cols = base[0].shape
    parts = len(base)
    nf = weights.shape[0]
    pairs, naux = factors.shape
    quarter = pairs // parts
    tile = tile_of(quarter)
    if tile is None:
        wide = jnp.einsum(
            "ja,pa->jp",
            gathered,
            factors,
            preferred_element_type=jnp.float32,
        )
        wide = jnp.transpose(wide.reshape(nf, cols, pairs), (0, 2, 1)) * weights[:, :, None]
        table = jnp.einsum("jt,tp->jp", coef, kernels, precision=EXACT).reshape(own, nf, pairs)
        new = jnp.einsum("wvp,vpc->wpc", table, wide, precision=EXACT)
        for s in range(parts):
            at = lax.rem(me + s, parts) * quarter
            part_of = lax.dynamic_slice_in_dim(new, at, quarter, 1) + base[s]
            new = lax.dynamic_update_slice_in_dim(new, part_of, at, 1)
        return [new]
    size = tile
    sets = span // size
    at = around(parts, quarter // size, low, sets)
    result = pl.pallas_call(
        functools.partial(final_kernel, nf, parts, len(outs)),
        out_shape=jax.ShapeDtypeStruct((own, pairs, cols), jnp.float32),
        grid_spec=pltpu.PrefetchScalarGridSpec(
            num_scalar_prefetch=1,
            grid=(parts * sets,),
            in_specs=[
                pl.BlockSpec((size, naux), lambda i, m: (at(i, m), 0)),
                pl.BlockSpec((nf, size), lambda i, m: (0, at(i, m))),
                pl.BlockSpec((nf, size), lambda i, m: (0, at(i, m))),
                resident(coef),
                resident(gathered),
            ]
            + [ANYWHERE] * (parts + len(outs)),
            out_specs=pl.BlockSpec((own, size, cols), lambda i, m: (0, at(i, m), 0)),
            scratch_shapes=[
                VMEM((own * nf, size), jnp.float32),
                VMEM((nf * cols, size), jnp.float32),
                VMEM((own, cols, LANES), jnp.float32),
            ]
            + stream_scratch(own, size, cols),
        ),
        input_output_aliases={6 + parts + n: n for n in range(len(outs))},
        compiler_params=pltpu.CompilerParams(vmem_limit_bytes=18 << 20),
        cost_estimate=pl.CostEstimate(
            flops=2 * nf * parts * span * cols * naux,
            bytes_accessed=8 * own * parts * span * cols,
            transcendentals=0,
        ),
    )(me.reshape(1), factors, kernels, weights, coef, gathered, *base, *outs)
    return [result]


class Plane:
    def __init__(self, chips):
        self.chips = chips
        me = lax.axis_index("fac")
        self.core = lax.rem(me, 2)
        self.chip = lax.div(me, 2)
        self.pal = {"fac": me + 1 - 2 * self.core}
        self.started = []

    def on(self, d):
        return lax.rem(self.chip + d + self.chips, self.chips)

    def at(self, d):
        return {"fac": self.on(d) * 2 + self.core}

    def chip_at(self, chip):
        return {"fac": chip * 2 + self.core}

    def greet(self):
        barrier = pltpu.get_barrier_semaphore()
        for other in [self.pal] + [self.at(d) for d in range(1, self.chips)]:
            pl.semaphore_signal(barrier, inc=1, device_id=other, device_id_type=MESH)
        pl.semaphore_wait(barrier, self.chips)

    def send(self, src, dst, sems, at, to):
        copy = pltpu.make_async_remote_copy(
            src_ref=src,
            dst_ref=dst,
            send_sem=sems[0].at[at],
            recv_sem=sems[1].at[at],
            device_id=to,
            device_id_type=MESH,
        )
        copy.start()
        self.started.append(copy)
        return copy

    def end(self):
        for copy in self.started:
            copy.wait_send()


def reduced(plane, x_ref, near, red, land, mine, near_sems, red_sems):
    chips, chip, core, pal = plane.chips, plane.chip, plane.core, plane.pal
    nears = {}
    for d in list(range(1, chips)) + [0]:
        nears[d] = plane.send(x_ref.at[plane.on(d), 1 - core], near.at[d], near_sems, d, pal)
    block = mine.shape[0]
    step = min(block, 16)
    reds = []
    for d in range(1, chips):
        nears[d].wait_recv()
        for r in range(0, block, step):
            rows = slice(r, r + step)
            red[d, rows, :] = (x_ref[plane.on(d), core, rows, :] + near[d, rows, :]).astype(
                red.dtype
            )
        reds.append(plane.send(red.at[d], land.at[d], red_sems, d, plane.at(d)))
    nears[0].wait_recv()
    for copy in reds:
        copy.wait_recv()
    for r in range(0, block, step):
        rows = slice(r, r + step)
        total = x_ref[chip, core, rows, :] + near[0, rows, :]
        for d in range(1, chips):
            total = total + land[d, rows, :].astype(jnp.float32)
        mine[rows, :] = total.astype(mine.dtype)


def reduce_kernel(chips, x_ref, o_ref, near, red, land, *sems):
    plane = Plane(chips)
    plane.greet()
    reduced(plane, x_ref, near, red, land, o_ref, sems[0:2], sems[2:4])
    plane.end()


def sum_kernel(chips, x_ref, o_ref, near, red, land, joined, *sems):
    plane = Plane(chips)
    chip, core = plane.chip, plane.core
    plane.greet()
    here = joined.at[chip, core]
    reduced(plane, x_ref, near, red, land, here, sems[0:2], sems[2:4])
    wides = [plane.send(here, here, sems[4:6], d, plane.at(d)) for d in range(1, chips)]
    pairs = [plane.send(here, here, sems[6:8], 0, plane.pal)]
    for d, copy in enumerate(wides, 1):
        copy.wait_recv()
        there = joined.at[plane.on(-d), core]
        pairs.append(plane.send(there, there, sems[6:8], d, plane.pal))
    for copy in pairs:
        copy.wait_recv()
    plane.end()
    for c in range(chips):
        o_ref[c] = joined[c]


def gather_kernel(chips, parts, x_ref, *refs):
    near_ref = None
    if len(refs) > 8:
        near_ref, refs = refs[0], refs[1:]
    o_ref, top_ref, joined, *sems = refs
    skip = 0 if near_ref is None else 1
    x_refs = [x_ref.at[s] for s in range(parts)]
    kept = sems[4]
    plane = Plane(chips)
    chip, core, pal = plane.chip, plane.core, plane.pal
    plane.greet()
    wide_sems, pair_sems = sems[0:2], sems[2:4]
    pairs = []
    copies = []
    for s in range(parts):
        copies.append(
            pltpu.make_async_copy(x_refs[s], joined.at[s, chip, core], kept.at[s])
        )
        copies[-1].start()
    square = chips == 4
    column, row = lax.rem(chip, 2), lax.div(chip, 2)
    across, along = chip + 1 - 2 * column, chip + 2 - 4 * row
    corner = along + 1 - 2 * column
    wides = []
    for s in range(parts):
        src, dst = x_refs[s], joined.at[s, chip, core]
        if square:
            for n, to in enumerate((across, along)):
                copy = plane.send(src, dst, wide_sems, s * chips + n, plane.chip_at(to))
                wides.append((s, n, copy))
        else:
            for d in range(1, chips):
                copy = plane.send(src, dst, wide_sems, s * chips + d, plane.at(d))
                wides.append((s, d, copy))
    for s in range(parts):
        pairs.append(
            plane.send(x_refs[s], joined.at[s, chip, core], pair_sems, s * chips, pal)
        )
    late = []
    for s, d, copy in wides:
        copy.wait_recv()
        chip_from = (across, along)[d] if square else plane.on(-d)
        there = joined.at[s, chip_from, core]
        if square and d == s % 2:
            other = (along, across)[d]
            turned = plane.send(there, there, wide_sems, s * chips + 2, plane.chip_at(other))
            late.append((s, turned))
        at = s * chips + (1 + d if square else d)
        pairs.append(plane.send(there, there, pair_sems, at, pal))
    for s, copy in late:
        copy.wait_recv()
        there = joined.at[s, corner, core]
        pairs.append(plane.send(there, there, pair_sems, s * chips + 3, pal))
    for copy in pairs:
        copy.wait_recv()
    plane.end()
    for copy in copies:
        copy.wait()
    if skip:
        o_ref[0] = near_ref[...]
    top = jnp.zeros(top_ref.shape, jnp.float32)
    for s in range(parts):

        def fold(c, top):
            here = joined[s, c]
            o_ref[s + skip, c] = here
            here = jnp.abs(here.astype(jnp.float32))
            sums = here[..., :LANES]
            for k in range(LANES, here.shape[-1], LANES):
                sums = sums + here[..., k : k + LANES]
            return jnp.maximum(top, jnp.max(sums.reshape((-1,) + top.shape), axis=0))

        top = lax.fori_loop(0, chips, fold, top)
    top_ref[...] = top


def dmas(count, pairs):
    return [pltpu.SemaphoreType.DMA((count,))] * (2 * pairs)


def reach_params(cid):
    return pltpu.CompilerParams(
        collective_id=cid, has_side_effects=True, vmem_limit_bytes=24 << 20
    )


def reach_cost(size):
    return pl.CostEstimate(flops=40 * size, bytes_accessed=40 * size, transcendentals=0)


WHOLE = pl.BlockSpec(memory_space=VMEM)


def summed(x, all_blocks):
    n = lax.axis_size("fac")
    chips = n // 2
    rows, width = x.shape
    block = rows // n
    flat = (chips, 2, block, width)
    landing = [
        VMEM((chips, block, width), jnp.float32),
        VMEM((chips, block, width), jnp.bfloat16),
        VMEM((chips, block, width), jnp.bfloat16),
    ]
    if not all_blocks:
        return pl.pallas_call(
            functools.partial(reduce_kernel, chips),
            out_shape=jax.ShapeDtypeStruct((block, width), jnp.bfloat16),
            in_specs=[WHOLE],
            out_specs=WHOLE,
            scratch_shapes=landing + dmas(chips, 2),
            compiler_params=reach_params(1),
            cost_estimate=reach_cost(x.size // 2),
        )(x.reshape(flat))
    result = pl.pallas_call(
        functools.partial(sum_kernel, chips),
        out_shape=jax.ShapeDtypeStruct(flat, jnp.bfloat16),
        in_specs=[WHOLE],
        out_specs=WHOLE,
        scratch_shapes=landing
        + [VMEM(flat, jnp.bfloat16)]
        + dmas(chips, 4),
        compiler_params=reach_params(0),
        cost_estimate=reach_cost(x.size),
    )(x.reshape(flat))
    return result.reshape(rows, width)


def gathered_over(blocks, near=None):
    n = lax.axis_size("fac")
    chips = n // 2
    parts, block, width = blocks.shape
    flat = (chips, 2, block, width)
    result, top = pl.pallas_call(
        functools.partial(gather_kernel, chips, parts),
        out_shape=(
            jax.ShapeDtypeStruct((parts + (near is not None),) + flat, jnp.bfloat16),
            jax.ShapeDtypeStruct((8, LANES), jnp.float32),
        ),
        in_specs=[WHOLE] * (1 if near is None else 2),
        out_specs=(WHOLE, WHOLE),
        scratch_shapes=[VMEM((parts,) + flat, jnp.bfloat16)]
        + dmas(parts * chips, 2)
        + [pltpu.SemaphoreType.DMA((parts,))],
        compiler_params=reach_params(2 if parts == 1 else 3),
        cost_estimate=reach_cost(block * width * parts * 8),
    )(blocks, *(() if near is None else (near.reshape(flat),)))
    return result.reshape(-1, width), top


def shards(right_side, factors, pair_weight, second_order, forward, backward):
    own, pairs, cols = right_side.shape
    nf = forward.shape[0]
    naux = factors.shape[1]
    parts = nf // own
    quarter = pairs // parts
    me = lax.axis_index("freq")

    def shift(x, by):
        if by == 0:
            return x
        return lax.ppermute(x, "freq", [(i, (i + by) % parts) for i in range(parts)])

    order = jnp.concatenate(
        [lax.rem(me - s + parts, parts) * own + jnp.arange(own) for s in range(parts)]
    )
    pick = jax.nn.one_hot(order, nf, dtype=jnp.float32)
    ahead = jnp.einsum("ts,sv,wv->tw", pick, forward, pick, precision=EXACT)
    back = jnp.einsum("ws,st,vt->wv", pick, backward, pick, precision=EXACT)
    coef = (back[:, None, :] * ahead.T[None, :, :]).reshape(nf * nf, nf)
    reach = jnp.max(
        jnp.sum(
            jnp.einsum("wt,tv->wv", jnp.abs(backward), jnp.abs(forward), precision=EXACT), axis=1
        )
    )

    both = jnp.stack([pair_weight, second_order])
    fine = HALF_TOP / 2.0
    slim = (both * fine).astype(jnp.float16)
    came = [shift(slim, s) for s in range(1, parts)]
    tables = [both] + [x.astype(jnp.float32) * (1.0 / fine) for x in came]
    weights, kernels = [jnp.concatenate([x[n] for x in tables]) for n in range(2)]
    size = tile_of(quarter) or quarter
    chunks = quarter // size
    early = max(chunks - 1, 1)
    groups = [(0, early)] + ([(early, chunks)] if early < chunks else [])
    calls = [(k, k + 1) for k in range(chunks)]
    tie = lax.optimization_barrier
    up = 8192.0

    def sliced(x, s, low, high):
        at = lax.rem(me + s, parts) * quarter + low * size
        return lax.dynamic_slice_in_dim(x, at, (high - low) * size, 1)

    def leaving(low, high):
        return [(sliced(right_side, s, low, high) * up).astype(jnp.float16) for s in range(1, parts)]

    def passed(blocks, back):
        return [
            shift(b, parts - 1 - s if back else s + 1) for s, b in enumerate(blocks)
        ]

    def first_projection():
        return jnp.einsum(
            "pa,fpc->fca",
            factors,
            right_side.astype(jnp.bfloat16),
            preferred_element_type=jnp.float32,
        ).reshape(own * cols, naux)

    def ladder(kept):
        total = kept
        for _ in range(INNER - 1):
            mine = summed(total, True)
            total = again(factors, pair_weight, mine, kept)
        block = summed(total, False)
        far = [shift(block, s) for s in range(1, parts)]
        return *gathered_over(block[None]), far

    def joined(blocks, near):
        blocks = jnp.stack(blocks)
        return gathered_over(blocks, near)

    leaves = []
    for g in groups:
        leaves.append(leaving(*g))
    right_late, leaves[-1] = tie((right_side, leaves[-1]))
    came = [passed(x, False) for x in leaves]
    near, near_top, blocks = ladder(first_projection())
    gathered, far_top = joined(blocks, near)
    height = jnp.sum(jnp.max(jnp.maximum(near_top, far_top), axis=0))
    u_top = jnp.maximum(1.01 * reach * (R_MAX + W_MAX * L_MAX * height), 1e-30)
    v_top = jnp.maximum(1.01 * reach * (R_MAX + u_top), 1e-30)

    def halved(far, top):
        blocks = [far[s * own : (s + 1) * own] for s in range(parts - 1)]
        return [(b * (HALF_TOP / top)).astype(jnp.float16) for b in blocks]

    def added(first, rest, top, group):
        rest = [b.astype(jnp.float32) * (top / HALF_TOP) for b in rest]
        return [sliced(right_late, s, *group) + b for s, b in enumerate([first] + rest)]

    us, vs, inward = [], [], []
    for n, (low, high) in enumerate(calls):
        at = next(g for g, (first, end) in enumerate(groups) if first <= low < end)
        moved = came[at]
        if n:
            moved, _ = tie((moved, us[-1][1]))
        start = (low - groups[at][0]) * size
        moved = [
            m[:, start : start + size].astype(jnp.float32) * (1.0 / up) for m in moved
        ]
        mine_u, far_u, mine_v, far_v = quarter_pass(
            me,
            low,
            factors,
            kernels,
            weights,
            coef,
            gathered,
            right_side,
            [(moved, 0)],
        )
        inward.append(passed(halved(far_u, u_top), True))
        us.append((mine_u, far_u))
        vs.append((mine_v, far_v))
    sources = []
    total = jnp.zeros((own * cols, naux), jnp.float32)
    for n, group in enumerate(calls):
        if n:
            inward[n], total = tie((inward[n], total))
        sources.append(added(us[n][0], inward[n], u_top, group))
        total = project(me, group[0], factors, sources[n], total)

    halves, back = [], {}
    for n in range(chunks):
        halves.append(halved(vs[n][1], v_top))

    def returned(n):
        back[n] = passed(halves[n], True)

    halves[0], total = tie((halves[0], total))
    returned(0)
    near, _, blocks = ladder(total)
    for n in range(1, chunks):
        returned(n)
    amplitudes = amplitude(me, factors, pair_weight, near, sources)
    gathered, _ = joined(blocks, near)
    outs = []
    for k in range(chunks):
        back[k], outs = tie((back[k], outs))
        base = added(vs[k][0], back[k], v_top, calls[k])
        outs = final(
            me,
            k,
            factors,
            kernels,
            weights,
            coef[: own * nf],
            gathered,
            base,
            outs,
        )
    return amplitudes, outs[0]


def solution(mesh):
    return jax.shard_map(
        shards,
        mesh=mesh,
        in_specs=(
            P("freq", "fac", None),
            P("fac", None),
            P("freq", "fac"),
            P("freq", "fac"),
            P(),
            P(),
        ),
        out_specs=(P("freq", "fac", None), P("freq", "fac", None)),
        check_vma=False,
    )
```

```python
import functools

import jax
import jax.numpy as jnp
from jax import lax
from jax.experimental import pallas as pl
from jax.experimental.pallas import tpu as pltpu
from jax.sharding import PartitionSpec as P


INNER = 2
LANES = 128
MESH = pl.DeviceIdType.MESH
CHUNK = 16
WIDE = 32
EXACT = lax.Precision.HIGHEST
R_MAX = 6.0
W_MAX = 2.0
L_MAX = 0.03125
HALF_TOP = 32768.0
VMEM = pltpu.VMEM


def tile_of(pairs):
    for blocks in (3, 4, 2, 1):
        if pairs % (blocks * LANES) == 0:
            return blocks * LANES
    return None


def wide_tile(pairs):
    for blocks in (9, 6, 4, 3, 2, 1):
        if pairs % (blocks * LANES) == 0:
            return blocks * LANES
    return None


def mix(table, lanes, outs, count, term):
    totals = [None] * outs
    for v in range(count):
        value = term(v)
        for w in range(outs):
            row = w * count + v
            product = table[row : row + 1, lanes] * value
            totals[w] = product if totals[w] is None else totals[w] + product
    return totals


def part(i, base, chunk):
    return pl.ds(pl.multiple_of(base + i * chunk, chunk), chunk)


def rows_times(p_ref, l_ref):
    return lax.dot_general(
        p_ref[...], l_ref[...], (((1,), (1,)), ((), ())), preferred_element_type=jnp.float32
    )


def dot_exact(a, b):
    return lax.dot_general(
        a, b, (((1,), (0,)), ((), ())), precision=EXACT, preferred_element_type=jnp.float32
    )


def resident(x):
    return pl.BlockSpec(x.shape, lambda i, *_: (0,) * x.ndim, pipeline_mode=pl.Buffered(1))


def quarter_kernel(nf, parts, sets, me_ref, l_ref, k_ref, wt_ref, coef_ref, p_ref, *rest):
    own_ref, rest = rest[0], rest[1:]
    came, rest = rest[: sets * (parts - 1)], rest[sets * (parts - 1) :]
    mine_u, far_u, mine_v, far_v, table, held, turned, mid, far = rest
    own = nf // parts
    cols = own_ref.shape[2]
    table[...] = dot_exact(coef_ref[...], k_ref[...])
    held[...] = rows_times(p_ref, l_ref)

    @pl.loop(0, table.shape[1] // LANES)
    def _(block):
        lanes = part(block, 0, LANES)
        for v in range(own):
            turned[v] = own_ref[v, lanes, :].T
        for j in range(sets):

            @pl.when(pl.program_id(0) == j)
            def _():
                for v in range(own, nf):
                    turned[v] = came[j * (parts - 1) + v // own - 1][v % own, lanes, :].T

        @pl.loop(0, cols // CHUNK)
        def _(i):
            rows = part(i, 0, CHUNK)
            got = mix(
                table,
                lanes,
                nf,
                nf,
                lambda v: turned[v, rows, :]
                + wt_ref[v : v + 1, lanes] * held[part(i, v * cols, CHUNK), lanes],
            )
            for w in range(nf):
                mid[w, rows, :] = got[w]
                turned[w, rows, :] = turned[w, rows, :] + got[w]
            got = mix(table, lanes, nf, nf, lambda v: turned[v, rows, :])
            for w in range(nf):
                far[w, rows, :] = got[w]

        for w in range(nf):
            u_ref, v_ref, row = (mine_u, mine_v, w) if w < own else (far_u, far_v, w - own)
            u_ref[row, lanes, :] = mid[w].T
            v_ref[row, lanes, :] = far[w].T


def quarter_pass(me, low, factors, kernels, weights, coef, gathered, right_side, moved):
    own, pairs, cols = right_side.shape
    nf = weights.shape[0]
    parts = nf // own
    quarter = pairs // parts
    naux = factors.shape[1]
    tile = tile_of(quarter)
    sets = len(moved)
    if tile is None:
        cut = lambda x, axis: lax.dynamic_slice_in_dim(x, me * quarter, quarter, axis)
        here = jnp.concatenate([cut(right_side, 1)] + moved[0][0])
        table = jnp.einsum("jt,tp->jp", coef, cut(kernels, 1), precision=EXACT)
        table = table.reshape(nf, nf, quarter)
        wide = jnp.einsum(
            "ja,pa->jp",
            gathered,
            cut(factors, 0),
            preferred_element_type=jnp.float32,
        )
        wide = jnp.transpose(wide.reshape(nf, cols, quarter), (0, 2, 1))
        wide = here + cut(weights, 1)[:, :, None] * wide
        u = jnp.einsum("wvp,vpc->wpc", table, wide, precision=EXACT)
        v = jnp.einsum("wvp,vpc->wpc", table, here + u, precision=EXACT)
        return u[:own], u[own:], v[:own], v[own:]
    steps = quarter // tile
    at = lambda i, m: m[0] * steps + low + i
    here = lambda n: pl.BlockSpec((own, tile, cols), lambda i, m: (0, n, 0))
    outs = [(rows, sets * tile, cols) for rows in (own, nf - own)]
    pieces = [pl.BlockSpec((x[0], tile, cols), lambda i, m: (0, i, 0)) for x in outs]
    return pl.pallas_call(
        functools.partial(quarter_kernel, nf, parts, sets),
        out_shape=[jax.ShapeDtypeStruct(x, jnp.float32) for x in outs]
        + [pltpu.HBM(x, jnp.float32) for x in outs],
        grid_spec=pltpu.PrefetchScalarGridSpec(
            num_scalar_prefetch=1,
            grid=(sets,),
            in_specs=[
                pl.BlockSpec((tile, naux), lambda i, m: (at(i, m), 0)),
                pl.BlockSpec((nf, tile), lambda i, m: (0, at(i, m))),
                pl.BlockSpec((nf, tile), lambda i, m: (0, at(i, m))),
                resident(coef),
                resident(gathered),
                pl.BlockSpec((own, tile, cols), lambda i, m: (0, at(i, m), 0)),
            ]
            + [here(n) for _, n in moved for _ in range(parts - 1)],
            out_specs=pieces * 2,
            scratch_shapes=[
                VMEM((nf * nf, tile), jnp.float32),
                VMEM((nf * cols, tile), jnp.float32),
            ]
            + [VMEM((nf, cols, LANES), jnp.float32)] * 3,
        ),
        compiler_params=pltpu.CompilerParams(vmem_limit_bytes=36 << 20),
        cost_estimate=pl.CostEstimate(
            flops=2 * nf * sets * tile * cols * (naux + 32 * nf),
            bytes_accessed=16 * nf * sets * tile * cols,
            transcendentals=0,
        ),
    )(
        me.reshape(1),
        factors,
        kernels,
        weights,
        coef,
        gathered,
        right_side,
        *[x for xs, _ in moved for x in xs],
    )


def project_kernel(parts, sets, me_ref, l_ref, *rest):
    s_refs, (x_ref, o_ref) = rest[:parts], rest[parts:]
    own, _, _ = s_refs[0].shape
    i = pl.program_id(0)

    @pl.when(i == 0)
    def _():
        o_ref[...] = x_ref[...]

    for s in range(parts):

        @pl.when(lax.div(i, sets) == s)
        def _():
            rounded = [s_refs[s][f].astype(jnp.bfloat16) for f in range(own)]
            o_ref[...] += lax.dot_general(
                jnp.concatenate(rounded, axis=1),
                l_ref[...],
                (((0,), (0,)), ((), ())),
                preferred_element_type=jnp.float32,
            )


def around(parts, steps, low, sets):
    return lambda i, m: lax.rem(m[0] + lax.div(i, sets), parts) * steps + low + lax.rem(i, sets)


def project(me, low, factors, pieces, total):
    own, size, cols = pieces[0].shape
    parts = len(pieces)
    pairs, naux = factors.shape
    quarter = pairs // parts
    tile = tile_of(quarter)
    if tile is None:
        for s, x in enumerate(pieces):
            rows = lax.dynamic_slice_in_dim(
                factors, lax.rem(me + s, parts) * quarter, quarter, 0
            )
            total = total + jnp.einsum(
                "pa,fpc->fca", rows, x.astype(jnp.bfloat16), preferred_element_type=jnp.float32
            ).reshape(total.shape)
        return total
    sets = size // tile
    at = around(parts, quarter // tile, low, sets)
    stay = lambda s: lambda i, m: (0, jnp.clip(i - s * sets, 0, sets - 1), 0)
    return pl.pallas_call(
        functools.partial(project_kernel, parts, sets),
        out_shape=jax.ShapeDtypeStruct(total.shape, jnp.float32),
        grid_spec=pltpu.PrefetchScalarGridSpec(
            num_scalar_prefetch=1,
            grid=(parts * sets,),
            in_specs=[pl.BlockSpec((tile, naux), lambda i, m: (at(i, m), 0))]
            + [pl.BlockSpec((own, tile, cols), stay(s)) for s in range(parts)]
            + [resident(total)],
            out_specs=pl.BlockSpec(total.shape, lambda i, m: (0, 0)),
        ),
        compiler_params=pltpu.CompilerParams(vmem_limit_bytes=18 << 20),
        cost_estimate=pl.CostEstimate(
            flops=2 * own * parts * size * cols * naux,
            bytes_accessed=8 * own * parts * size * cols,
            transcendentals=0,
        ),
    )(me.reshape(1), factors, *pieces, total)


def again_kernel(own, l_ref, wt_ref, p_ref, x_ref, o_ref):
    cols = p_ref.shape[0] // own

    @pl.when(pl.program_id(0) == 0)
    def _():
        o_ref[...] = x_ref[...]

    wide = lax.dot_general(
        p_ref[...], l_ref[...], (((1,), (1,)), ((), ())), preferred_element_type=jnp.float32
    )
    wide = [
        (wide[f * cols : (f + 1) * cols] * wt_ref[f : f + 1, :]).astype(jnp.bfloat16)
        for f in range(own)
    ]
    o_ref[...] += lax.dot_general(
        jnp.concatenate(wide, axis=0),
        l_ref[...],
        (((1,), (0,)), ((), ())),
        preferred_element_type=jnp.float32,
    )


def again(factors, pair_weight, projected, kept):
    pairs, naux = factors.shape
    own = pair_weight.shape[0]
    tile = wide_tile(pairs)
    return pl.pallas_call(
        functools.partial(again_kernel, own),
        out_shape=jax.ShapeDtypeStruct(kept.shape, jnp.float32),
        grid=(pairs // tile,),
        in_specs=[
            pl.BlockSpec((tile, naux), lambda i: (i, 0)),
            pl.BlockSpec((own, tile), lambda i: (0, i)),
            resident(projected),
            resident(kept),
        ],
        out_specs=pl.BlockSpec(kept.shape, lambda i: (0, 0)),
        compiler_params=pltpu.CompilerParams(vmem_limit_bytes=24 << 20),
        cost_estimate=pl.CostEstimate(
            flops=4 * kept.size * pairs, bytes_accessed=2 * factors.size, transcendentals=0
        ),
    )(factors, pair_weight, projected, kept)


class Stream:
    def __init__(self, refs, buffer, sems, step):
        tile = buffer.shape[2]
        refs = [
            ref.at[:, n : n + tile, :] for ref in refs for n in range(0, ref.shape[1], tile)
        ]
        self.refs, self.buffer, self.sems = refs, buffer, sems
        self.step = step
        self.slot = lax.rem(step + 2, 2)

    def copy(self, n):
        return pltpu.make_async_copy(self.refs[n], self.buffer.at[n % 2], self.sems.at[n % 2])

    def ahead(self):
        @pl.when(pl.program_id(0) == 0)
        def _():
            self.copy(0).start()

        for n in range(1, len(self.refs)):

            @pl.when(self.step == n - 1)
            def _():
                self.copy(n).start()

    def here(self):
        pltpu.make_async_copy(
            self.refs[0], self.buffer.at[self.slot], self.sems.at[self.slot]
        ).wait()
        return self.buffer.at[self.slot]


def stream_scratch(own, tile, cols):
    return [VMEM((2, own, tile, cols), jnp.float32), pltpu.SemaphoreType.DMA((2,))]


ANYWHERE = pl.BlockSpec(memory_space=pl.ANY)


def amplitude_kernel(pieces, me_ref, l_ref, wt_ref, p_ref, *rest):
    refs, (a_ref, buffer, sems) = rest[:pieces], rest[pieces:]
    own, tile, cols = a_ref.shape
    stream = Stream(refs, buffer, sems, pl.program_id(0))
    stream.ahead()
    wide = rows_times(p_ref, l_ref)
    here = stream.here()
    for f in range(own):
        scaled = wide[f * cols : (f + 1) * cols] * wt_ref[f : f + 1, :]
        for k in range(0, tile, LANES):
            lanes = slice(k, k + LANES)
            a_ref[f, lanes, :] = here[f, lanes, :] + scaled[:, lanes].T


def amplitude(me, factors, pair_weight, near, sources):
    own, _, cols = sources[0][0].shape
    parts = len(sources[0])
    pairs, naux = factors.shape
    quarter = pairs // parts
    size = tile_of(quarter)
    if size is None:
        wide = jnp.einsum("ja,pa->jp", near, factors, preferred_element_type=jnp.float32)
        wide = jnp.transpose(wide.reshape(own, cols, pairs), (0, 2, 1))
        result = wide * pair_weight[:, :, None]
        for s in range(parts):
            at = lax.rem(me + s, parts) * quarter
            part_of = lax.dynamic_slice_in_dim(result, at, quarter, 1) + sources[0][s]
            result = lax.dynamic_update_slice_in_dim(result, part_of, at, 1)
        return result
    steps = quarter // size
    pieces = [x for group in sources for x in group]
    at = lambda i, m: lax.rem(m[0] + lax.rem(i, parts), parts) * steps + lax.div(i, parts)
    return pl.pallas_call(
        functools.partial(amplitude_kernel, len(pieces)),
        out_shape=jax.ShapeDtypeStruct((own, pairs, cols), jnp.float32),
        grid_spec=pltpu.PrefetchScalarGridSpec(
            num_scalar_prefetch=1,
            grid=(parts * steps,),
            in_specs=[
                pl.BlockSpec((size, naux), lambda i, m: (at(i, m), 0)),
                pl.BlockSpec((own, size), lambda i, m: (0, at(i, m))),
                resident(near),
            ]
            + [ANYWHERE] * len(pieces),
            out_specs=pl.BlockSpec((own, size, cols), lambda i, m: (0, at(i, m), 0)),
            scratch_shapes=stream_scratch(own, size, cols),
        ),
        compiler_params=pltpu.CompilerParams(vmem_limit_bytes=13 << 20),
        cost_estimate=pl.CostEstimate(
            flops=2 * own * pairs * cols * naux,
            bytes_accessed=8 * own * pairs * cols,
            transcendentals=0,
        ),
    )(me.reshape(1), factors, pair_weight, near, *pieces)


def final_kernel(nf, parts, held_outs, me_ref, l_ref, k_ref, wt_ref, coef_ref, p_ref, *rest):
    b_refs, rest = rest[:parts], rest[parts + held_outs :]
    new_ref, table, held, mid, buffer, sems = rest
    own, _, cols = new_ref.shape
    stream = Stream(b_refs, buffer, sems, pl.program_id(0))
    stream.ahead()
    table[...] = dot_exact(coef_ref[...], k_ref[...])
    for w in range(own):
        rows = slice(w * nf, (w + 1) * nf)
        table[rows, :] = table[rows, :] * wt_ref[...]
    held[...] = rows_times(p_ref, l_ref)
    here = stream.here()

    @pl.loop(0, table.shape[1] // LANES)
    def _(block):
        lanes = part(block, 0, LANES)

        @pl.loop(0, cols // WIDE)
        def _(i):
            rows = part(i, 0, WIDE)
            got = mix(table, lanes, own, nf, lambda v: held[part(i, v * cols, WIDE), lanes])
            for w in range(own):
                mid[w, rows, :] = got[w]

        for w in range(own):
            new_ref[w, lanes, :] = here[w, lanes, :] + mid[w].T


def final(me, low, factors, kernels, weights, coef, gathered, base, outs):
    own, span, cols = base[0].shape
    parts = len(base)
    nf = weights.shape[0]
    pairs, naux = factors.shape
    quarter = pairs // parts
    tile = tile_of(quarter)
    if tile is None:
        wide = jnp.einsum(
            "ja,pa->jp",
            gathered,
            factors,
            preferred_element_type=jnp.float32,
        )
        wide = jnp.transpose(wide.reshape(nf, cols, pairs), (0, 2, 1)) * weights[:, :, None]
        table = jnp.einsum("jt,tp->jp", coef, kernels, precision=EXACT).reshape(own, nf, pairs)
        new = jnp.einsum("wvp,vpc->wpc", table, wide, precision=EXACT)
        for s in range(parts):
            at = lax.rem(me + s, parts) * quarter
            part_of = lax.dynamic_slice_in_dim(new, at, quarter, 1) + base[s]
            new = lax.dynamic_update_slice_in_dim(new, part_of, at, 1)
        return [new]
    size = tile
    sets = span // size
    at = around(parts, quarter // size, low, sets)
    result = pl.pallas_call(
        functools.partial(final_kernel, nf, parts, len(outs)),
        out_shape=jax.ShapeDtypeStruct((own, pairs, cols), jnp.float32),
        grid_spec=pltpu.PrefetchScalarGridSpec(
            num_scalar_prefetch=1,
            grid=(parts * sets,),
            in_specs=[
                pl.BlockSpec((size, naux), lambda i, m: (at(i, m), 0)),
                pl.BlockSpec((nf, size), lambda i, m: (0, at(i, m))),
                pl.BlockSpec((nf, size), lambda i, m: (0, at(i, m))),
                resident(coef),
                resident(gathered),
            ]
            + [ANYWHERE] * (parts + len(outs)),
            out_specs=pl.BlockSpec((own, size, cols), lambda i, m: (0, at(i, m), 0)),
            scratch_shapes=[
                VMEM((own * nf, size), jnp.float32),
                VMEM((nf * cols, size), jnp.float32),
                VMEM((own, cols, LANES), jnp.float32),
            ]
            + stream_scratch(own, size, cols),
        ),
        input_output_aliases={6 + parts + n: n for n in range(len(outs))},
        compiler_params=pltpu.CompilerParams(vmem_limit_bytes=18 << 20),
        cost_estimate=pl.CostEstimate(
            flops=2 * nf * parts * span * cols * naux,
            bytes_accessed=8 * own * parts * span * cols,
            transcendentals=0,
        ),
    )(me.reshape(1), factors, kernels, weights, coef, gathered, *base, *outs)
    return [result]


class Plane:
    def __init__(self, chips):
        self.chips = chips
        me = lax.axis_index("fac")
        self.core = lax.rem(me, 2)
        self.chip = lax.div(me, 2)
        self.pal = {"fac": me + 1 - 2 * self.core}
        self.started = []

    def on(self, d):
        return lax.rem(self.chip + d + self.chips, self.chips)

    def at(self, d):
        return {"fac": self.on(d) * 2 + self.core}

    def chip_at(self, chip):
        return {"fac": chip * 2 + self.core}

    def greet(self):
        barrier = pltpu.get_barrier_semaphore()
        for other in [self.pal] + [self.at(d) for d in range(1, self.chips)]:
            pl.semaphore_signal(barrier, inc=1, device_id=other, device_id_type=MESH)
        pl.semaphore_wait(barrier, self.chips)

    def send(self, src, dst, sems, at, to):
        copy = pltpu.make_async_remote_copy(
            src_ref=src,
            dst_ref=dst,
            send_sem=sems[0].at[at],
            recv_sem=sems[1].at[at],
            device_id=to,
            device_id_type=MESH,
        )
        copy.start()
        self.started.append(copy)
        return copy

    def end(self):
        for copy in self.started:
            copy.wait_send()


def reduced(plane, x_ref, near, red, land, mine, near_sems, red_sems):
    chips, chip, core, pal = plane.chips, plane.chip, plane.core, plane.pal
    nears = {}
    for d in list(range(1, chips)) + [0]:
        nears[d] = plane.send(x_ref.at[plane.on(d), 1 - core], near.at[d], near_sems, d, pal)
    block = mine.shape[0]
    step = min(block, 16)
    reds = []
    for d in range(1, chips):
        nears[d].wait_recv()
        for r in range(0, block, step):
            rows = slice(r, r + step)
            red[d, rows, :] = (x_ref[plane.on(d), core, rows, :] + near[d, rows, :]).astype(
                red.dtype
            )
        reds.append(plane.send(red.at[d], land.at[d], red_sems, d, plane.at(d)))
    nears[0].wait_recv()
    for copy in reds:
        copy.wait_recv()
    for r in range(0, block, step):
        rows = slice(r, r + step)
        total = x_ref[chip, core, rows, :] + near[0, rows, :]
        for d in range(1, chips):
            total = total + land[d, rows, :].astype(jnp.float32)
        mine[rows, :] = total.astype(mine.dtype)


def reduce_kernel(chips, x_ref, o_ref, near, red, land, *sems):
    plane = Plane(chips)
    plane.greet()
    reduced(plane, x_ref, near, red, land, o_ref, sems[0:2], sems[2:4])
    plane.end()


def sum_kernel(chips, x_ref, o_ref, near, red, land, joined, *sems):
    plane = Plane(chips)
    chip, core = plane.chip, plane.core
    plane.greet()
    here = joined.at[chip, core]
    reduced(plane, x_ref, near, red, land, here, sems[0:2], sems[2:4])
    wides = [plane.send(here, here, sems[4:6], d, plane.at(d)) for d in range(1, chips)]
    pairs = [plane.send(here, here, sems[6:8], 0, plane.pal)]
    for d, copy in enumerate(wides, 1):
        copy.wait_recv()
        there = joined.at[plane.on(-d), core]
        pairs.append(plane.send(there, there, sems[6:8], d, plane.pal))
    for copy in pairs:
        copy.wait_recv()
    plane.end()
    for c in range(chips):
        o_ref[c] = joined[c]


def gather_kernel(chips, parts, x_ref, *refs):
    near_ref = None
    if len(refs) > 8:
        near_ref, refs = refs[0], refs[1:]
    o_ref, top_ref, joined, *sems = refs
    skip = 0 if near_ref is None else 1
    x_refs = [x_ref.at[s] for s in range(parts)]
    kept = sems[4]
    plane = Plane(chips)
    chip, core, pal = plane.chip, plane.core, plane.pal
    plane.greet()
    wide_sems, pair_sems = sems[0:2], sems[2:4]
    pairs = []
    copies = []
    for s in range(parts):
        copies.append(
            pltpu.make_async_copy(x_refs[s], joined.at[s, chip, core], kept.at[s])
        )
        copies[-1].start()
    square = chips == 4
    column, row = lax.rem(chip, 2), lax.div(chip, 2)
    across, along = chip + 1 - 2 * column, chip + 2 - 4 * row
    corner = along + 1 - 2 * column
    wides = []
    for s in range(parts):
        src, dst = x_refs[s], joined.at[s, chip, core]
        if square:
            for n, to in enumerate((across, along)):
                copy = plane.send(src, dst, wide_sems, s * chips + n, plane.chip_at(to))
                wides.append((s, n, copy))
        else:
            for d in range(1, chips):
                copy = plane.send(src, dst, wide_sems, s * chips + d, plane.at(d))
                wides.append((s, d, copy))
    for s in range(parts):
        pairs.append(
            plane.send(x_refs[s], joined.at[s, chip, core], pair_sems, s * chips, pal)
        )
    late = []
    for s, d, copy in wides:
        copy.wait_recv()
        chip_from = (across, along)[d] if square else plane.on(-d)
        there = joined.at[s, chip_from, core]
        if square and d == s % 2:
            other = (along, across)[d]
            turned = plane.send(there, there, wide_sems, s * chips + 2, plane.chip_at(other))
            late.append((s, turned))
        at = s * chips + (1 + d if square else d)
        pairs.append(plane.send(there, there, pair_sems, at, pal))
    for s, copy in late:
        copy.wait_recv()
        there = joined.at[s, corner, core]
        pairs.append(plane.send(there, there, pair_sems, s * chips + 3, pal))
    for copy in pairs:
        copy.wait_recv()
    plane.end()
    for copy in copies:
        copy.wait()
    if skip:
        o_ref[0] = near_ref[...]
    top = jnp.zeros(top_ref.shape, jnp.float32)
    for s in range(parts):

        def fold(c, top):
            here = joined[s, c]
            o_ref[s + skip, c] = here
            here = jnp.abs(here.astype(jnp.float32))
            sums = here[..., :LANES]
            for k in range(LANES, here.shape[-1], LANES):
                sums = sums + here[..., k : k + LANES]
            return jnp.maximum(top, jnp.max(sums.reshape((-1,) + top.shape), axis=0))

        top = lax.fori_loop(0, chips, fold, top)
    top_ref[...] = top


def dmas(count, pairs):
    return [pltpu.SemaphoreType.DMA((count,))] * (2 * pairs)


def reach_params(cid):
    return pltpu.CompilerParams(
        collective_id=cid, has_side_effects=True, vmem_limit_bytes=24 << 20
    )


def reach_cost(size):
    return pl.CostEstimate(flops=40 * size, bytes_accessed=40 * size, transcendentals=0)


WHOLE = pl.BlockSpec(memory_space=VMEM)


def summed(x, all_blocks):
    n = lax.axis_size("fac")
    chips = n // 2
    rows, width = x.shape
    block = rows // n
    flat = (chips, 2, block, width)
    landing = [
        VMEM((chips, block, width), jnp.float32),
        VMEM((chips, block, width), jnp.bfloat16),
        VMEM((chips, block, width), jnp.bfloat16),
    ]
    if not all_blocks:
        return pl.pallas_call(
            functools.partial(reduce_kernel, chips),
            out_shape=jax.ShapeDtypeStruct((block, width), jnp.bfloat16),
            in_specs=[WHOLE],
            out_specs=WHOLE,
            scratch_shapes=landing + dmas(chips, 2),
            compiler_params=reach_params(1),
            cost_estimate=reach_cost(x.size // 2),
        )(x.reshape(flat))
    result = pl.pallas_call(
        functools.partial(sum_kernel, chips),
        out_shape=jax.ShapeDtypeStruct(flat, jnp.bfloat16),
        in_specs=[WHOLE],
        out_specs=WHOLE,
        scratch_shapes=landing
        + [VMEM(flat, jnp.bfloat16)]
        + dmas(chips, 4),
        compiler_params=reach_params(0),
        cost_estimate=reach_cost(x.size),
    )(x.reshape(flat))
    return result.reshape(rows, width)


def gathered_over(blocks, near=None):
    n = lax.axis_size("fac")
    chips = n // 2
    parts, block, width = blocks.shape
    flat = (chips, 2, block, width)
    result, top = pl.pallas_call(
        functools.partial(gather_kernel, chips, parts),
        out_shape=(
            jax.ShapeDtypeStruct((parts + (near is not None),) + flat, jnp.bfloat16),
            jax.ShapeDtypeStruct((8, LANES), jnp.float32),
        ),
        in_specs=[WHOLE] * (1 if near is None else 2),
        out_specs=(WHOLE, WHOLE),
        scratch_shapes=[VMEM((parts,) + flat, jnp.bfloat16)]
        + dmas(parts * chips, 2)
        + [pltpu.SemaphoreType.DMA((parts,))],
        compiler_params=reach_params(2 if parts == 1 else 3),
        cost_estimate=reach_cost(block * width * parts * 8),
    )(blocks, *(() if near is None else (near.reshape(flat),)))
    return result.reshape(-1, width), top


def shards(right_side, factors, pair_weight, second_order, forward, backward):
    own, pairs, cols = right_side.shape
    nf = forward.shape[0]
    naux = factors.shape[1]
    parts = nf // own
    quarter = pairs // parts
    me = lax.axis_index("freq")

    def shift(x, by):
        if by == 0:
            return x
        return lax.ppermute(x, "freq", [(i, (i + by) % parts) for i in range(parts)])

    order = jnp.concatenate(
        [lax.rem(me - s + parts, parts) * own + jnp.arange(own) for s in range(parts)]
    )
    pick = jax.nn.one_hot(order, nf, dtype=jnp.float32)
    ahead = jnp.einsum("ts,sv,wv->tw", pick, forward, pick, precision=EXACT)
    back = jnp.einsum("ws,st,vt->wv", pick, backward, pick, precision=EXACT)
    coef = (back[:, None, :] * ahead.T[None, :, :]).reshape(nf * nf, nf)
    reach = jnp.max(
        jnp.sum(
            jnp.einsum("wt,tv->wv", jnp.abs(backward), jnp.abs(forward), precision=EXACT), axis=1
        )
    )

    both = jnp.stack([pair_weight, second_order])
    fine = HALF_TOP / 2.0
    slim = (both * fine).astype(jnp.float16)
    came = [shift(slim, s) for s in range(1, parts)]
    tables = [both] + [x.astype(jnp.float32) * (1.0 / fine) for x in came]
    weights, kernels = [jnp.concatenate([x[n] for x in tables]) for n in range(2)]
    size = tile_of(quarter) or quarter
    chunks = quarter // size
    early = max(chunks - 1, 1)
    groups = [(0, early)] + ([(early, chunks)] if early < chunks else [])
    calls = [(k, k + 1) for k in range(chunks)]
    tie = lax.optimization_barrier
    up = 8192.0

    def sliced(x, s, low, high):
        at = lax.rem(me + s, parts) * quarter + low * size
        return lax.dynamic_slice_in_dim(x, at, (high - low) * size, 1)

    def leaving(low, high):
        return [(sliced(right_side, s, low, high) * up).astype(jnp.float16) for s in range(1, parts)]

    def passed(blocks, back):
        return [
            shift(b, parts - 1 - s if back else s + 1) for s, b in enumerate(blocks)
        ]

    def first_projection():
        return jnp.einsum(
            "pa,fpc->fca",
            factors,
            right_side.astype(jnp.bfloat16),
            preferred_element_type=jnp.float32,
        ).reshape(own * cols, naux)

    def ladder(kept):
        total = kept
        for _ in range(INNER - 1):
            mine = summed(total, True)
            total = again(factors, pair_weight, mine, kept)
        block = summed(total, False)
        far = [shift(block, s) for s in range(1, parts)]
        return *gathered_over(block[None]), far

    def joined(blocks, near):
        blocks = jnp.stack(blocks)
        return gathered_over(blocks, near)

    leaves = []
    for g in groups:
        leaves.append(leaving(*g))
    right_late, leaves[-1] = tie((right_side, leaves[-1]))
    came = [passed(x, False) for x in leaves]
    near, near_top, blocks = ladder(first_projection())
    gathered, far_top = joined(blocks, near)
    height = jnp.sum(jnp.max(jnp.maximum(near_top, far_top), axis=0))
    u_top = jnp.maximum(1.01 * reach * (R_MAX + W_MAX * L_MAX * height), 1e-30)
    v_top = jnp.maximum(1.01 * reach * (R_MAX + u_top), 1e-30)

    def halved(far, top):
        blocks = [far[s * own : (s + 1) * own] for s in range(parts - 1)]
        return [(b * (HALF_TOP / top)).astype(jnp.float16) for b in blocks]

    def added(first, rest, top, group):
        rest = [b.astype(jnp.float32) * (top / HALF_TOP) for b in rest]
        return [sliced(right_late, s, *group) + b for s, b in enumerate([first] + rest)]

    us, vs, inward = [], [], []
    for n, (low, high) in enumerate(calls):
        at = next(g for g, (first, end) in enumerate(groups) if first <= low < end)
        moved = came[at]
        if n:
            moved, _ = tie((moved, us[-1][1]))
        start = (low - groups[at][0]) * size
        moved = [
            m[:, start : start + size].astype(jnp.float32) * (1.0 / up) for m in moved
        ]
        mine_u, far_u, mine_v, far_v = quarter_pass(
            me,
            low,
            factors,
            kernels,
            weights,
            coef,
            gathered,
            right_side,
            [(moved, 0)],
        )
        inward.append(passed(halved(far_u, u_top), True))
        us.append((mine_u, far_u))
        vs.append((mine_v, far_v))
    sources = []
    total = jnp.zeros((own * cols, naux), jnp.float32)
    for n, group in enumerate(calls):
        if n:
            inward[n], total = tie((inward[n], total))
        sources.append(added(us[n][0], inward[n], u_top, group))
        total = project(me, group[0], factors, sources[n], total)

    last = max(chunks - 1, 1)
    lots = [list(range(last))] + ([[last]] if last < chunks else [])
    halves, back = [], {}
    for lot in lots:
        halves.append(halved(jnp.concatenate([vs[k][1] for k in lot], axis=1), v_top))

    def returned(n):
        back[n] = passed(halves[n], True)

    halves[0], total = tie((halves[0], total))
    returned(0)
    near, _, blocks = ladder(total)
    for n in range(1, len(lots)):
        returned(n)
    amplitudes = amplitude(me, factors, pair_weight, near, sources)
    gathered, _ = joined(blocks, near)
    outs = []
    for n, j, k in [(n, j, k) for n, lot in enumerate(lots) for j, k in enumerate(lot)]:
        back[n], outs = tie((back[n], outs))
        base = [m[:, j * size : (j + 1) * size] for m in back[n]]
        base = added(vs[k][0], base, v_top, calls[k])
        outs = final(
            me,
            k,
            factors,
            kernels,
            weights,
            coef[: own * nf],
            gathered,
            base,
            outs,
        )
    return amplitudes, outs[0]


def solution(mesh):
    return jax.shard_map(
        shards,
        mesh=mesh,
        in_specs=(
            P("freq", "fac", None),
            P("fac", None),
            P("freq", "fac"),
            P("freq", "fac"),
            P(),
            P(),
        ),
        out_specs=(P("freq", "fac", None), P("freq", "fac", None)),
        check_vma=False,
    )
```
